128 devices in a mesh: row: 8 (over y, core), col: 16 (over x, z).
Axes of the slice: x: 4, y: 4, z: 4, core: 2. Of those that a mesh axis runs over, the one named last changes fastest.
Arguments:
- theta: float32 [64, 256, 256], P('row', None, 'col'), may hold values from -6 to 6
- left_env: float32 [32, 32, 256, 256], P('row', 'col'), as said below
- right_env: float32 [8, 32, 256, 256], P(None, 'col'), as said below
- left_sector: int32 [64], replicated, may hold values from 0 to 31, as said below
- right_sector: int32 [64], P('row'), may hold values from 0 to 7
- term_on: int32 [64, 32], P('row', 'col'), may hold values 0 or 1
- left_size: int32 [32], replicated, may hold values from 1 to 256, 5120 in all
- right_size: int32 [8], replicated, may hold values from 1 to 256, 1280 in all
Outputs:
- new_theta: float32 [64, 256, 256], P('row', None, 'col')
- energy: float32 [], replicated
The draws below stay inside these ranges and needn't reach their ends.
Inputs may be any that keep to these rules, and one draw needn't show every extreme that they name: `left_sector`: left sector s belongs to row s // 4. Block k belongs to row k // 8. The 8 blocks of one row name distinct left sectors; they name either none or exactly 2 sectors belonging to any one row, and the blocks of every row name 2 sectors belonging to one common row. `left_env`: each tile is symmetric in its last two dimensions. `right_env`: each tile is symmetric in its last two dimensions.
All inputs are finite; a program needn't handle non-finite values. No bound on the sum of `term_on` on one device may be relied on, other than what follows from the above.
Results may differ from the reference program's by a relative error of at most 0.0001.
Values sent between devices are 32-bit elements; how exact they have to be, the bound alone decides.
No kernel may reach another device: no remote copies, remote signals or barrier semaphores. Data moves between devices by JAX's collectives and lax.ppermute only.
A program may use at most 128 MiB of HBM per device.

```python
import math
import jax
import jax.numpy as jnp
import numpy as np
from jax import lax

P_SIZE = 256
W = 32
BLK_DEV = 8
SR = 8
ITERS = 2
CAP = 2
SL_DEV = 4
SL = 32
K = 64
N_ROW = 8


def symmetric_tiles(key, count):
    shape = (count, W, P_SIZE, P_SIZE)
    base = jax.random.normal(key, shape, jnp.float32)
    return (base + jnp.swapaxes(base, 2, 3)) * 0.5 ** 0.5 * P_SIZE ** (-0.5)


def draw_left_env(key, part):
    return symmetric_tiles(jax.random.fold_in(key, 3), SL)


def draw_right_env(key, part):
    return symmetric_tiles(jax.random.fold_in(key, 5), SR)


def row_shuffle(key_one):
    return jax.random.permutation(key_one, N_ROW)


def sector_shuffle(key_one):
    return jax.random.permutation(key_one, SL_DEV)


def draw_left_sector(key, part):
    groups = BLK_DEV // CAP
    key_home = jax.random.fold_in(key, 11)
    key_common = jax.random.fold_in(key, 12)
    key_pick = jax.random.fold_in(key, 13)
    common = jax.random.randint(key_common, (), 0, N_ROW)
    row_perms = jax.vmap(row_shuffle)(jax.random.split(key_home, N_ROW))
    where_common = jnp.argmax((row_perms == common).astype(jnp.int32), axis=1)
    first_home = row_perms[:, 0]
    positions = jnp.arange(N_ROW)
    swapped = jnp.where(positions[None, :] == 0, common, jnp.where(positions[None, :] == where_common[:, None], first_home[:, None], row_perms))
    home_rows = swapped[:, :groups]
    local_picks = jax.vmap(sector_shuffle)(jax.random.split(key_pick, N_ROW * groups)).reshape(N_ROW, groups, SL_DEV)[:, :, :CAP]
    sector = home_rows[:, :, None] * SL_DEV + local_picks
    return sector.reshape(K).astype(jnp.int32)


def set_ends(array, stream_key, least, largest):
    dims = array.shape
    place = [jax.random.randint(jax.random.fold_in(stream_key, axis), (), 0, dims[axis]) for axis in range(len(dims))]
    array = array.at[tuple(place)].set(least)
    longest = dims.index(max(dims))
    place[longest] = (place[longest] + 1) % dims[longest]
    return array.at[tuple(place)].set(largest)


def block_levels(rng, dims, cuts, low, top_value):
    factor_of = 1.0
    for dim, blocks in cuts:
        draws = jax.random.uniform(jax.random.fold_in(jax.random.fold_in(rng, 6), dim), (blocks,), jnp.float32, low / len(cuts), top_value / len(cuts))
        factor_of = factor_of * jnp.repeat(jnp.exp(draws), dims[dim] // blocks).reshape((-1,) + (1,) * (len(dims) - 1 - dim))
    return factor_of


def split_up(number_of, total, most, slope):
    loads = [(1 << 20) // math.isqrt(grade ** slope) + 1 for grade in range(2, number_of + 1)]
    spare, given = total - most - (number_of - 1), [1] * (number_of - 1)
    while spare > 0:
        candidates = [i for i in range(number_of - 1) if given[i] < most]
        pool, remaining = sum([loads[i] for i in candidates]), spare
        for i in candidates:
            extra = min(most - given[i], max(1, remaining * loads[i] // pool), spare)
            given[i] = given[i] + extra
            spare = spare - extra
    return np.array([most] + given)


def uneven_parts(own_key, number_of, total, reach, skew):
    if number_of == 2:
        one = jax.random.randint(own_key, (), max(1, total - reach), min(reach, total - 1) + 1)
        return jnp.stack([one, total - one])
    tallies = jnp.asarray(split_up(number_of, total, reach, skew), jnp.int32)
    couples = (number_of - 1) // 2
    donor, sink = tallies[1:1 + 2 * couples:2], tallies[2:2 + 2 * couples:2]
    margin = jnp.minimum(donor - 1, reach - sink)
    moved = jax.random.randint(jax.random.fold_in(own_key, 1), (couples,), 0, 1 << 20) % (margin + 1)
    tallies = tallies.at[1:1 + 2 * couples:2].set(donor - moved).at[2:2 + 2 * couples:2].set(sink + moved)
    return tallies[jax.random.permutation(jax.random.fold_in(own_key, 2), number_of)]


def gaussian(rng, dims, width, reach, cuts=(), held_as=jnp.bfloat16):
    values = jax.random.normal(rng, dims, jnp.float32) * width
    if len(cuts) > 0:
        values = block_levels(rng, dims, cuts, -0.22, 0.18) * values
    return jnp.clip(values, min=-reach, max=reach).astype(held_as)


def setup_inputs(seed: int = 0) -> dict:
    arg_keys = jax.random.split(jax.random.key(seed), 9)
    return {
        "theta": gaussian(arg_keys[0], (K, P_SIZE, P_SIZE), 1.0, 6.0, ((0, 8), (2, 16)), jnp.float32),
        "left_env": draw_left_env(jax.random.fold_in(arg_keys[8], 71), 0),
        "right_env": draw_right_env(jax.random.fold_in(arg_keys[8], 71), 0),
        "left_sector": draw_left_sector(jax.random.fold_in(arg_keys[8], 71), 0),
        "right_sector": set_ends(jax.random.randint(arg_keys[4], (K,), 0, SR), jax.random.fold_in(arg_keys[4], 1), 0, SR - 1).astype(jnp.int32),
        "term_on": set_ends((jax.random.randint(arg_keys[5], (K, W), 0, 4) < 3).astype(jnp.int32), jax.random.fold_in(arg_keys[5], 1), 0, 1),
        "left_size": uneven_parts(arg_keys[6], SL, SL * P_SIZE * 5 // 8, P_SIZE, 1).astype(jnp.int32),
        "right_size": uneven_parts(arg_keys[7], SR, SR * P_SIZE * 5 // 8, P_SIZE, 1).astype(jnp.int32),
    }


highest = lax.Precision.HIGHEST

def reference(theta, left_env, right_env, left_sector, right_sector, term_on, left_size, right_size):
    tile_iota = jnp.arange(P_SIZE, dtype=jnp.int32)
    row_live = left_size[left_sector]
    col_live = right_size[right_sector]
    masks = ((tile_iota[None, :, None] < row_live[:, None, None]) & (tile_iota[None, None, :] < col_live[:, None, None])).astype(jnp.float32)
    weights = term_on.astype(jnp.float32)

    def operate(vector):

        def one_block(packed):
            block, left_id, right_id, block_weights = packed
            left_part = left_env[left_id]
            right_part = right_env[right_id]
            middle = jnp.einsum('wia,ab->wib', left_part, block, precision=highest) * block_weights[:, None, None]
            return jnp.einsum('wib,wjb->ij', middle, right_part, precision=highest)
        result = lax.map(one_block, (vector, left_sector, right_sector, weights))
        return result * masks
    start_vec = theta * masks
    image_vec = operate(start_vec)
    norm_sq = jnp.sum(start_vec * start_vec)
    correlation = jnp.sum(start_vec * image_vec)
    inv_norm = 1.0 / jnp.sqrt(norm_sq)
    basis_vec = start_vec * inv_norm
    applied = image_vec * inv_norm
    ritz_value = correlation / norm_sq
    for turn_index in range(ITERS):
        residual = applied - ritz_value * basis_vec
        res_sq = jnp.sum(residual * residual)
        length = jnp.sqrt(res_sq)
        fresh_vec = residual / length
        fresh_applied = operate(fresh_vec)
        curvature = jnp.sum(fresh_vec * fresh_applied)
        half_gap = 0.5 * (ritz_value - curvature)
        root_term = jnp.sqrt(half_gap * half_gap + res_sq)
        lowest = 0.5 * (ritz_value + curvature) - root_term
        first_coef = curvature - lowest
        pair_norm = jnp.sqrt(first_coef * first_coef + res_sq)
        basis_vec = (first_coef * basis_vec - length * fresh_vec) / pair_norm
        applied = (first_coef * applied - length * fresh_applied) / pair_norm
        ritz_value = lowest
    new_theta = basis_vec * jnp.sqrt(jnp.float32(K * P_SIZE * P_SIZE))
    return (new_theta, ritz_value)
```

```python
import jax
import jax.numpy as jnp
from jax import lax
from jax.sharding import Mesh, PartitionSpec as P

ITERS = 2
HALF = 128
COL = ("x", "z")
ALL = ("y", "c", "x", "z")
SWAP = [(0, 1), (1, 0)]
high = lax.Precision.HIGH


def grids():
    i = lax.broadcasted_iota(jnp.int32, (HALF, HALF), 0)
    j = lax.broadcasted_iota(jnp.int32, (HALF, HALF), 1)
    return i, j


def pack(tiles):
    i, j = grids()
    a00 = tiles[:, :HALF, :HALF]
    a01 = tiles[:, :HALF, HALF:]
    a11 = tiles[:, HALF:, HALF:]
    fold = jnp.where(i >= j, a00, a11)
    diag = jnp.sum(jnp.where(i == j, a11, 0.0), axis=1, keepdims=True)
    extra = jnp.pad(diag, ((0, 0), (0, 7), (0, HALF)))
    return jnp.concatenate([jnp.concatenate([fold, a01], axis=2), extra], axis=1)


def unpack(packed):
    i, j = grids()
    fold = packed[:, :HALF, :HALF]
    a01 = packed[:, :HALF, HALF:]
    diag = packed[:, HALF : HALF + 1, :HALF]
    flip = jnp.swapaxes(fold, 1, 2)
    a00 = jnp.where(i >= j, fold, flip)
    a11 = jnp.where(i == j, diag, jnp.where(i < j, fold, flip))
    top = jnp.concatenate([a00, a01], axis=2)
    low = jnp.concatenate([jnp.swapaxes(a01, 1, 2), a11], axis=2)
    return jnp.concatenate([top, low], axis=1)


def safe_div(value, norm):
    return jnp.where(norm > 0.0, value / jnp.where(norm > 0.0, norm, 1.0), 0.0)


def in_order(core, own, other):
    return jnp.where(
        core == 0, jnp.concatenate([own, other]), jnp.concatenate([other, own])
    )


def ritz_pair(stats):
    norm, a1, b1, a2, b2, a3 = [stats[:, m] for m in range(6)]

    def apply(x):
        return jnp.stack(
            [
                a1 * x[0] + b1 * x[1],
                b1 * x[0] + a2 * x[1] + b2 * x[2],
                b2 * x[1] + a3 * x[2],
            ]
        )

    zero = jnp.zeros_like(norm)
    start = jnp.stack([norm, zero, zero])
    image = apply(start)
    norm_sq = jnp.sum(start * start)
    correlation = jnp.sum(start * image)
    inv_norm = 1.0 / jnp.sqrt(norm_sq)
    basis = start * inv_norm
    applied = image * inv_norm
    ritz = correlation / norm_sq
    for _ in range(ITERS):
        residual = applied - ritz * basis
        res_sq = jnp.sum(residual * residual)
        length = jnp.sqrt(res_sq)
        fresh = residual / length
        fresh_applied = apply(fresh)
        curvature = jnp.sum(fresh * fresh_applied)
        half_gap = 0.5 * (ritz - curvature)
        root = jnp.sqrt(half_gap * half_gap + res_sq)
        lowest = 0.5 * (ritz + curvature) - root
        first = curvature - lowest
        pair = jnp.sqrt(first * first + res_sq)
        basis = (first * basis - length * fresh) / pair
        applied = (first * applied - length * fresh_applied) / pair
        ritz = lowest
    return basis, ritz


def local(theta, left_env, right_env, left_sector, right_sector, term_on, left_size, right_size):
    plane = lax.axis_index("y")
    core = lax.axis_index("c")
    place = lax.axis_index(COL)
    tile = theta.shape[1]
    blocks = theta.shape[0]
    thin = jnp.swapaxes(theta, 1, 2)

    about = jnp.concatenate([right_sector[:, None], term_on], axis=1)
    about16 = in_order(core, about, lax.ppermute(about, "c", SWAP))
    thin16 = in_order(core, thin, lax.ppermute(thin, "c", SWAP))
    right16 = about16[:, 0]
    on16 = jnp.where(core == 0, about16[:, 1], about16[:, 2]).astype(jnp.float32)
    left16 = lax.dynamic_slice_in_dim(left_sector, plane * 16, 16)

    mine = pack(lax.dynamic_index_in_dim(left_env, core, 1, keepdims=False))
    theirs = pack(lax.dynamic_index_in_dim(left_env, 1 - core, 1, keepdims=False))
    eight = in_order(core, mine, lax.ppermute(theirs, "c", SWAP))
    every = lax.all_gather(eight, "y", axis=0, tiled=True)

    right_term = lax.dynamic_index_in_dim(right_env, core, 1, keepdims=False)
    right_slots = pack(jnp.take(right_term, right16, axis=0) * on16[:, None, None])
    slots = jnp.concatenate([right_slots, thin16], axis=1)
    arrived = lax.all_to_all(slots, COL, 0, 0, tiled=True)
    right = unpack(arrived[:, :136])
    block = arrived[:, 136:].reshape(tile, tile)

    left = unpack(lax.all_to_all(jnp.take(every, left16, axis=0), COL, 0, 0, tiled=True))

    live_left = left_size[left16[place]]
    live_right = right_size[right16[place]]
    at = lax.broadcasted_iota(jnp.int32, (tile, tile), 0)
    along = lax.broadcasted_iota(jnp.int32, (tile, tile), 1)
    mask = ((at < live_right) & (along < live_left)).astype(jnp.float32)

    def half_image(u):
        middle = jnp.einsum("wjb,bi->wji", right, u, precision=high)
        return jnp.einsum("wja,wai->ji", middle, left, precision=high)

    def operate(u):
        part = half_image(u)
        return (part + lax.ppermute(part, "c", SWAP)) * mask

    start = block * mask
    norm = jnp.sqrt(jnp.sum(start * start))
    q1 = safe_div(start, norm)
    h1 = operate(q1)
    a1 = jnp.sum(q1 * h1)
    w1 = h1 - a1 * q1
    w1 = w1 - jnp.sum(q1 * w1) * q1
    b1 = jnp.sqrt(jnp.sum(w1 * w1))
    q2 = safe_div(w1, b1)
    h2 = operate(q2)
    a2 = jnp.sum(q2 * h2)
    w2 = h2 - a2 * q2 - b1 * q1
    w2 = w2 - jnp.sum(q2 * w2) * q2 - jnp.sum(q1 * w2) * q1
    b2 = jnp.sqrt(jnp.sum(w2 * w2))
    q3 = safe_div(w2, b2)
    a3 = jnp.sum(q3 * half_image(q3))

    sent = jnp.where(core == 0, q2, q3).reshape(16, theta.shape[2], tile)
    got = lax.all_to_all(sent, COL, 0, 0, tiled=True)
    keep = lax.dynamic_slice_in_dim(got, core * blocks, blocks)
    give = lax.dynamic_slice_in_dim(got, (1 - core) * blocks, blocks)
    back = lax.ppermute(give, "c", SWAP)
    thin2 = jnp.where(core == 0, keep, back)
    thin3 = jnp.where(core == 0, back, keep)

    zero = jnp.float32(0.0)
    mine_stats = jnp.stack([norm, a1, b1, a2, b2, a3, zero, zero])
    stats = lax.all_to_all(jnp.broadcast_to(mine_stats, (128, 8)), ALL, 0, 0, tiled=True)
    stats = stats.reshape(4, 2, 16, 8)
    both = jnp.concatenate([stats[:, 0, :, :5], stats[:, 0, :, 5:] + stats[:, 1, :, 5:]], axis=2)
    both = both.reshape(64, 8)
    basis, ritz = ritz_pair(both)

    scale = jnp.sqrt(jnp.float32(64 * tile * tile))
    row = plane * 2 + core
    first = safe_div(basis[0], both[:, 0])
    coef = jnp.stack([first, basis[1], basis[2]]) * scale
    coef = lax.dynamic_slice_in_dim(coef, row * blocks, blocks, axis=1)
    own_left = lax.dynamic_slice_in_dim(left16, core * blocks, blocks)
    rows_live = left_size[own_left]
    cols_live = right_size[right_sector]
    cols = place * theta.shape[2] + lax.broadcasted_iota(jnp.int32, thin.shape, 1)
    rows = lax.broadcasted_iota(jnp.int32, thin.shape, 2)
    live = (cols < cols_live[:, None, None]) & (rows < rows_live[:, None, None])
    out = (
        coef[0][:, None, None] * jnp.where(live, thin, 0.0)
        + coef[1][:, None, None] * thin2
        + coef[2][:, None, None] * thin3
    )
    return jnp.swapaxes(out, 1, 2), ritz


def solution(mesh):
    fine = Mesh(mesh.devices.reshape(4, 2, 4, 4), ALL)
    row = ("y", "c")
    placed = (
        P(row, None, COL),
        P(row, COL, None, None),
        P(None, COL, None, None),
        P(),
        P(row),
        P(row, COL),
        P(),
        P(),
    )
    return jax.shard_map(
        local, mesh=fine, in_specs=placed, out_specs=(P(row, None, COL), P()), check_vma=False
    )
```

```python
import jax
import jax.numpy as jnp
from jax import lax
from jax.experimental import pallas as pl
from jax.experimental.pallas import tpu as pltpu
from jax.sharding import Mesh, PartitionSpec as P

ITERS = 2
TILE = 256
HALF = 128
TERMS = 16
LEFT_ROWS = 136
SLOT_ROWS = 152
STEP = 2
COL = ("x", "z")
ALL = ("y", "c", "x", "z")
SWAP = [(0, 1), (1, 0)]
UP = [(i, (i + 1) % 4) for i in range(4)]
DOWN = [(i, (i - 1) % 4) for i in range(4)]
f32 = jnp.float32
bf16 = jnp.bfloat16
PARAMS = pltpu.CompilerParams(vmem_limit_bytes=48 * 1024 * 1024)


def vmem():
    return pl.BlockSpec(memory_space=pltpu.VMEM)


def grids(rows, cols):
    i = lax.broadcasted_iota(jnp.int32, (rows, cols), 0)
    j = lax.broadcasted_iota(jnp.int32, (rows, cols), 1)
    return i, j


def fold_tile(tile):
    i, j = grids(HALF, HALF)
    a00 = tile[:HALF, :HALF]
    a11 = tile[HALF:, HALF:]
    fold = jnp.where(i >= j, a00, a11)
    diag = jnp.sum(jnp.where(i == j, a11, 0.0), axis=0, keepdims=True)
    return fold, tile[:HALF, HALF:], diag


def diag_rows(diag):
    wide = jnp.concatenate([diag, jnp.zeros((1, HALF), f32)], axis=1)
    return jnp.broadcast_to(wide, (8, TILE))


def unfold_tile(fold, corner, diag):
    i, j = grids(HALF, HALF)
    flip = fold.T
    a00 = jnp.where(i >= j, fold, flip)
    a11 = jnp.where(i == j, diag, jnp.where(i < j, fold, flip))
    top = jnp.concatenate([a00, corner], axis=1)
    low = jnp.concatenate([corner.T, a11], axis=1)
    return jnp.concatenate([top, low], axis=0)


def split(x):
    hi = x.astype(bf16)
    return hi, (x - hi.astype(f32)).astype(bf16)


def dot3(a_hi, a_lo, b_hi, b_lo):
    def dot(a, b):
        return jnp.dot(a, b, preferred_element_type=f32)

    return dot(a_hi, b_hi) + (dot(a_hi, b_lo) + dot(a_lo, b_hi))


def total(x):
    return jnp.sum(jnp.sum(x, axis=0, keepdims=True), axis=1, keepdims=True)


def inverse(norm):
    good = norm > 0.0
    return jnp.where(good, 1.0 / jnp.where(good, norm, 1.0), 0.0)


def put(stats, lane, value):
    _, j = grids(8, HALF)
    return jnp.where(j == lane, value, stats)


def fold_left_body(pick, src, dst):
    fold, corner, diag = fold_tile(src[0, 0])
    dst[0, :HALF, :HALF] = fold
    dst[0, :HALF, HALF:] = corner
    dst[0, HALF:, :] = diag_rows(diag)


def fold_left(left_env, pick):
    count = left_env.shape[0]
    return pl.pallas_call(
        fold_left_body,
        grid_spec=pltpu.PrefetchScalarGridSpec(
            num_scalar_prefetch=1,
            grid=(count,),
            in_specs=[pl.BlockSpec((1, 1, TILE, TILE), lambda n, pick: (n, pick[0], 0, 0))],
            out_specs=pl.BlockSpec((1, LEFT_ROWS, TILE), lambda n, pick: (n, 0, 0)),
        ),
        out_shape=jax.ShapeDtypeStruct((count, LEFT_ROWS, TILE), f32),
        compiler_params=PARAMS,
        name="fold_left",
    )(pick, left_env)


def from_rows(ids, own, other, slot, field):
    at = (slot % 8) * 3 + field
    return jnp.where(slot // 8 == ids[1], own[at], other[at])


def right_slots_body(ids, own, other, right, thin, thin_other, dst):
    slot = pl.program_id(0)
    here = slot // 8 == ids[1]
    on = from_rows(ids, own, other, slot, 1 + ids[1]).astype(f32)
    row = slot % 8
    fold, corner, diag = fold_tile(right[0, 0] * on)
    dst[0, :16, :] = jnp.where(here, thin[row], thin_other[row])
    dst[0, 16 : 16 + HALF, :HALF] = fold
    dst[0, 16 : 16 + HALF, HALF:] = corner
    dst[0, 16 + HALF :, :] = diag_rows(diag)


def right_slots(ids, own, other, right_env, thin, thin_other):
    def right_at(slot, ids, own, other):
        return (from_rows(ids, own, other, slot, 0), ids[1], 0, 0)

    whole = pl.BlockSpec((8, 16, TILE), lambda slot, ids, own, other: (0, 0, 0))
    return pl.pallas_call(
        right_slots_body,
        grid_spec=pltpu.PrefetchScalarGridSpec(
            num_scalar_prefetch=3,
            grid=(TERMS,),
            in_specs=[pl.BlockSpec((1, 1, TILE, TILE), right_at), whole, whole],
            out_specs=pl.BlockSpec(
                (1, SLOT_ROWS, TILE), lambda slot, ids, own, other: (slot, 0, 0)
            ),
        ),
        out_shape=jax.ShapeDtypeStruct((TERMS, SLOT_ROWS, TILE), f32),
        compiler_params=PARAMS,
        name="right_slots",
    )(ids, own, other, right_env, thin, thin_other)


def left_slots_body(ids, left_sector, *refs):
    pieces, dst, sem = refs[:8], refs[8], refs[9]

    def copy(src, slot):
        return pltpu.make_async_copy(src, dst.at[slot], sem.at[slot])

    def start(slot, carry):
        sector = left_sector[ids[0] * 16 + slot]
        home = sector // 4
        which = ((home // 2 - ids[0] + 4) % 4) * 2 + (home % 2 + ids[1]) % 2
        for n in range(8):

            @pl.when(which == n)
            def _():
                copy(pieces[n].at[sector % 4], slot).start()

        return carry

    def finish(slot, carry):
        copy(pieces[0].at[0], slot).wait()
        return carry

    lax.fori_loop(0, TERMS, start, 0)
    lax.fori_loop(0, TERMS, finish, 0)


def left_slots(ids, left_sector, pieces):
    smem = pl.BlockSpec(memory_space=pltpu.SMEM)
    anywhere = pl.BlockSpec(memory_space=pl.ANY)
    return pl.pallas_call(
        left_slots_body,
        in_specs=[smem, smem] + [anywhere] * 8,
        out_specs=anywhere,
        out_shape=jax.ShapeDtypeStruct((TERMS,) + pieces[0].shape[1:], f32),
        scratch_shapes=[pltpu.SemaphoreType.DMA((TERMS,))],
        name="left_slots",
    )(ids, left_sector, *pieces)


def live_sizes(ids, own, other, left_sector, left_size, right_size):
    live_left = left_size[left_sector[ids[0] * 16 + ids[2]]]
    live_right = right_size[from_rows(ids, own, other, ids[2], 0)]
    return live_right, live_left


def mask_of(live_right, live_left):
    i, j = grids(TILE, TILE)
    return (i < live_right) & (j < live_left)


def first_body(ids, own, other, sector, lsize, rsize, arrived, r_hi, r_lo, mid, q1, stats):
    live_right, live_left = live_sizes(ids, own, other, sector, lsize, rsize)
    block = jnp.concatenate([arrived[n, :16, :] for n in range(TERMS)], axis=0)
    start = jnp.where(mask_of(live_right, live_left), block, 0.0)
    norm = jnp.sqrt(total(start * start))
    vec = start * inverse(norm)
    q1[...] = vec
    stats[...] = put(jnp.zeros((8, HALF), f32), 0, norm)
    q_hi, q_lo = split(vec)

    def term(n, carry):
        full = unfold_tile(
            arrived[n, 16 : 16 + HALF, :HALF],
            arrived[n, 16 : 16 + HALF, HALF:],
            arrived[n, 16 + HALF : 17 + HALF, :HALF],
        )
        hi, lo = split(full)
        r_hi[n] = hi
        r_lo[n] = lo
        mid[n] = dot3(hi, lo, q_hi, q_lo)
        return carry

    lax.fori_loop(0, TERMS, term, 0)


def first_vector(scalars, arrived):
    smem = pl.BlockSpec(memory_space=pltpu.SMEM)
    stack = (TERMS, TILE, TILE)
    return pl.pallas_call(
        first_body,
        in_specs=[smem] * 6 + [vmem()],
        out_specs=[vmem()] * 5,
        out_shape=[
            jax.ShapeDtypeStruct(stack, bf16),
            jax.ShapeDtypeStruct(stack, bf16),
            jax.ShapeDtypeStruct(stack, f32),
            jax.ShapeDtypeStruct((TILE, TILE), f32),
            jax.ShapeDtypeStruct((8, HALF), f32),
        ],
        compiler_params=PARAMS,
        name="first_vector",
    )(*scalars, arrived)


def image_one_body(arrived, mid, l_hi, l_lo, part):
    @pl.when(pl.program_id(0) == 0)
    def _():
        part[...] = jnp.zeros_like(part)

    acc = part[...]
    for t in range(STEP):
        full = unfold_tile(
            arrived[t, :HALF, :HALF], arrived[t, :HALF, HALF:], arrived[t, HALF : HALF + 1, :HALF]
        )
        hi, lo = split(full)
        l_hi[t] = hi
        l_lo[t] = lo
        m_hi, m_lo = split(mid[t])
        acc = acc + dot3(m_hi, m_lo, hi, lo)
    part[...] = acc


def image_one(arrived, mid):
    stack = (TERMS, TILE, TILE)
    tiles = pl.BlockSpec((STEP, TILE, TILE), lambda n: (n, 0, 0))
    return pl.pallas_call(
        image_one_body,
        grid=(TERMS // STEP,),
        in_specs=[pl.BlockSpec((STEP, LEFT_ROWS, TILE), lambda n: (n, 0, 0)), tiles],
        out_specs=[tiles, tiles, pl.BlockSpec((TILE, TILE), lambda n: (0, 0))],
        out_shape=[
            jax.ShapeDtypeStruct(stack, bf16),
            jax.ShapeDtypeStruct(stack, bf16),
            jax.ShapeDtypeStruct((TILE, TILE), f32),
        ],
        compiler_params=PARAMS,
        name="image_one",
    )(arrived, mid)


def lanczos(image, last, before, beta):
    alpha = total(last * image)
    rest = image - alpha * last
    if before is not None:
        rest = rest - beta * before
    again = rest - total(last * rest) * last
    if before is not None:
        again = again - total(before * rest) * before
    norm = jnp.sqrt(total(again * again))
    return alpha, norm, again * inverse(norm)


def add_terms(q_hi, q_lo, r_hi, r_lo, l_hi, l_lo, acc):
    for t in range(STEP):
        m_hi, m_lo = split(dot3(r_hi[t], r_lo[t], q_hi, q_lo))
        acc = acc + dot3(m_hi, m_lo, l_hi[t], l_lo[t])
    return acc


def image_two_body(
    ids, own, other, sector, lsize, rsize,
    part_a, part_b, q1, stats_in, r_hi, r_lo, l_hi, l_lo,
    part, q2, stats, q_hi, q_lo,
):
    @pl.when(pl.program_id(0) == 0)
    def _():
        mask = mask_of(*live_sizes(ids, own, other, sector, lsize, rsize))
        image = jnp.where(mask, part_a[...] + part_b[...], 0.0)
        alpha, norm, vec = lanczos(image, q1[...], None, None)
        q2[...] = vec
        stats[...] = put(put(stats_in[...], 1, alpha), 2, norm)
        hi, lo = split(vec)
        q_hi[...] = hi
        q_lo[...] = lo
        part[...] = jnp.zeros_like(part)

    part[...] = add_terms(q_hi[...], q_lo[...], r_hi, r_lo, l_hi, l_lo, part[...])


def image_two(scalars, part, part_other, q1, stats, stacks):
    flat = pl.BlockSpec((TILE, TILE), lambda n, *_: (0, 0))
    line = pl.BlockSpec((8, HALF), lambda n, *_: (0, 0))
    tiles = pl.BlockSpec((STEP, TILE, TILE), lambda n, *_: (n, 0, 0))
    return pl.pallas_call(
        image_two_body,
        grid_spec=pltpu.PrefetchScalarGridSpec(
            num_scalar_prefetch=6,
            grid=(TERMS // STEP,),
            in_specs=[flat, flat, flat, line] + [tiles] * 4,
            out_specs=[flat, flat, line],
            scratch_shapes=[pltpu.VMEM((TILE, TILE), bf16)] * 2,
        ),
        out_shape=[
            jax.ShapeDtypeStruct((TILE, TILE), f32),
            jax.ShapeDtypeStruct((TILE, TILE), f32),
            jax.ShapeDtypeStruct((8, HALF), f32),
        ],
        compiler_params=PARAMS,
        name="image_two",
    )(*scalars, part, part_other, q1, stats, *stacks)


def third_body(
    ids, own, other, sector, lsize, rsize, part_a, part_b, q1, q2, stats_in, q3, sent, stats
):
    mask = mask_of(*live_sizes(ids, own, other, sector, lsize, rsize))
    image = jnp.where(mask, part_a[...] + part_b[...], 0.0)
    _, j = grids(8, HALF)
    beta = total(jnp.where((j == 2) & (grids(8, HALF)[0] == 0), stats_in[...], 0.0))
    alpha, norm, vec = lanczos(image, q2[...], q1[...], beta)
    q3[...] = vec
    pick = jnp.where(ids[1] == 0, q2[...], vec)
    for n in range(16):
        sent[n] = pick[16 * n : 16 * n + 16]
    stats[...] = put(put(stats_in[...], 3, alpha), 4, norm)


def third_vector(scalars, part, part_other, q1, q2, stats):
    smem = pl.BlockSpec(memory_space=pltpu.SMEM)
    return pl.pallas_call(
        third_body,
        in_specs=[smem] * 6 + [vmem()] * 5,
        out_specs=[vmem()] * 3,
        out_shape=[
            jax.ShapeDtypeStruct((TILE, TILE), f32),
            jax.ShapeDtypeStruct((16, 16, TILE), f32),
            jax.ShapeDtypeStruct((8, HALF), f32),
        ],
        compiler_params=PARAMS,
        name="third_vector",
    )(*scalars, part, part_other, q1, q2, stats)


def image_three_body(q3, stats_in, r_hi, r_lo, l_hi, l_lo, stats, part, q_hi, q_lo):
    @pl.when(pl.program_id(0) == 0)
    def _():
        hi, lo = split(q3[...])
        q_hi[...] = hi
        q_lo[...] = lo
        part[...] = jnp.zeros_like(part)

    part[...] = add_terms(q_hi[...], q_lo[...], r_hi, r_lo, l_hi, l_lo, part[...])

    @pl.when(pl.program_id(0) == pl.num_programs(0) - 1)
    def _():
        alpha = total(q3[...] * part[...])
        mine = put(stats_in[...], 5, alpha)
        stats[...] = jnp.broadcast_to(mine[0:1, :], (128, HALF))


def image_three(q3, stats, stacks):
    flat = pl.BlockSpec((TILE, TILE), lambda n: (0, 0))
    line = pl.BlockSpec((8, HALF), lambda n: (0, 0))
    tiles = pl.BlockSpec((STEP, TILE, TILE), lambda n: (n, 0, 0))
    return pl.pallas_call(
        image_three_body,
        grid=(TERMS // STEP,),
        in_specs=[flat, line] + [tiles] * 4,
        out_specs=pl.BlockSpec((128, HALF), lambda n: (0, 0)),
        out_shape=jax.ShapeDtypeStruct((128, HALF), f32),
        scratch_shapes=[
            pltpu.VMEM((TILE, TILE), f32),
            pltpu.VMEM((TILE, TILE), bf16),
            pltpu.VMEM((TILE, TILE), bf16),
        ],
        compiler_params=PARAMS,
        name="image_three",
    )(q3, stats, *stacks)


def ritz_pair(norm, a1, b1, a2, b2, a3):
    def apply(x):
        return [a1 * x[0] + b1 * x[1], b1 * x[0] + a2 * x[1] + b2 * x[2], b2 * x[1] + a3 * x[2]]

    def dot(x, y):
        return 0.5 * jnp.sum(x[0] * y[0] + x[1] * y[1] + x[2] * y[2], axis=1, keepdims=True)

    zero = jnp.zeros_like(norm)
    start = [norm, zero, zero]
    image = apply(start)
    norm_sq = dot(start, start)
    correlation = dot(start, image)
    inv_norm = 1.0 / jnp.sqrt(norm_sq)
    basis = [x * inv_norm for x in start]
    applied = [x * inv_norm for x in image]
    ritz = correlation / norm_sq
    for _ in range(ITERS):
        residual = [x - ritz * y for x, y in zip(applied, basis)]
        res_sq = dot(residual, residual)
        length = jnp.sqrt(res_sq)
        fresh = [x / length for x in residual]
        fresh_applied = apply(fresh)
        curvature = dot(fresh, fresh_applied)
        half_gap = 0.5 * (ritz - curvature)
        root = jnp.sqrt(half_gap * half_gap + res_sq)
        lowest = 0.5 * (ritz + curvature) - root
        first = curvature - lowest
        pair = jnp.sqrt(first * first + res_sq)
        basis = [(first * x - length * y) / pair for x, y in zip(basis, fresh)]
        applied = [(first * x - length * y) / pair for x, y in zip(applied, fresh_applied)]
        ritz = lowest
    return basis, ritz


def finish_body(
    ids, sector, rsector, lsize, rsize, stats, thin, got, back, out, energy, coef
):
    flip = stats[...].T
    norm, a1, b1, a2, b2, part = [flip[m : m + 1, :] for m in range(6)]
    _, lane = grids(1, HALF)
    core_of = (lane // 16) % 2
    a3 = part + jnp.where(core_of == 0, pltpu.roll(part, HALF - 16, 1), pltpu.roll(part, 16, 1))
    basis, ritz = ritz_pair(norm, a1, b1, a2, b2, a3)
    energy[...] = jnp.broadcast_to(ritz, (8, HALF))
    scale = jnp.sqrt(jnp.full((1, HALF), 64 * TILE * TILE, f32))
    i, _ = grids(HALF, HALF)
    c1 = basis[0] * inverse(norm) * scale
    c2 = basis[1] * scale
    c3 = basis[2] * scale
    coef[...] = jnp.where(i == 0, c1, jnp.where(i == 1, c2, jnp.where(i == 2, c3, 0.0))).T
    core = ids[1]
    own = coef[pl.ds(pl.multiple_of(ids[0] * 32 + core * 8, 8), 8), :]
    jcol, irow = grids(16, TILE)
    for b in range(8):
        live_left = lsize[sector[ids[0] * 16 + core * 8 + b]]
        live_right = rsize[rsector[b]]
        live = (jcol + ids[2] * 16 < live_right) & (irow < live_left)
        keep = got[core * 8 + b]
        recv = back[b]
        second = jnp.where(core == 0, keep, recv)
        third = jnp.where(core == 0, recv, keep)
        out[b] = (
            own[b : b + 1, 0:1] * jnp.where(live, thin[b], 0.0)
            + own[b : b + 1, 1:2] * second
            + own[b : b + 1, 2:3] * third
        )


def finish(ids, sector, rsector, lsize, rsize, stats, thin, got, back):
    smem = pl.BlockSpec(memory_space=pltpu.SMEM)
    return pl.pallas_call(
        finish_body,
        in_specs=[smem] * 5 + [vmem()] * 4,
        out_specs=[vmem()] * 2,
        out_shape=[
            jax.ShapeDtypeStruct(thin.shape, f32),
            jax.ShapeDtypeStruct((8, HALF), f32),
        ],
        scratch_shapes=[pltpu.VMEM((HALF, HALF), f32)],
        compiler_params=PARAMS,
        name="finish",
    )(ids, sector, rsector, lsize, rsize, stats, thin, got, back)


def local(theta, left_env, right_env, left_sector, right_sector, term_on, left_size, right_size):
    plane = lax.axis_index("y").astype(jnp.int32)
    core = lax.axis_index("c").astype(jnp.int32)
    place = lax.axis_index(COL).astype(jnp.int32)
    ids = jnp.stack([plane, core, place])
    thin = jnp.swapaxes(theta, 1, 2)

    theirs = lax.ppermute(fold_left(left_env, (1 - core).reshape(1)), "c", SWAP)
    mine = fold_left(left_env, core.reshape(1))
    mine_up = lax.ppermute(mine, "y", UP)
    mine_down = lax.ppermute(mine, "y", DOWN)
    theirs_up = lax.ppermute(theirs, "y", UP)
    theirs_down = lax.ppermute(theirs, "y", DOWN)
    mine_far = lax.ppermute(mine_up, "y", UP)
    theirs_far = lax.ppermute(theirs_down, "y", DOWN)
    pieces = [mine, theirs, mine_down, theirs_down, mine_far, theirs_far, mine_up, theirs_up]

    own = jnp.concatenate([right_sector[:, None], term_on], axis=1).reshape(-1)
    other = lax.ppermute(own, "c", SWAP)
    thin_other = lax.ppermute(thin, "c", SWAP)
    slots = right_slots(ids, own, other, right_env, thin, thin_other)
    arrived = lax.all_to_all(slots, COL, 0, 0, tiled=True)
    scalars = (ids, own, other, left_sector, left_size, right_size)
    r_hi, r_lo, mid, q1, stats = first_vector(scalars, arrived)

    left_arrived = lax.all_to_all(left_slots(ids, left_sector, pieces), COL, 0, 0, tiled=True)
    l_hi, l_lo, part = image_one(left_arrived, mid)
    stacks = (r_hi, r_lo, l_hi, l_lo)
    part, q2, stats = image_two(scalars, part, lax.ppermute(part, "c", SWAP), q1, stats, stacks)
    q3, sent, stats = third_vector(scalars, part, lax.ppermute(part, "c", SWAP), q1, q2, stats)

    got = lax.all_to_all(sent, COL, 0, 0, tiled=True)
    give = lax.dynamic_slice_in_dim(got, (1 - core) * 8, 8)
    back = lax.ppermute(give, "c", SWAP)

    stats = lax.all_to_all(image_three(q3, stats, stacks), ALL, 0, 0, tiled=True)
    out, energy = finish(
        ids, left_sector, right_sector, left_size, right_size, stats, thin, got, back
    )
    return jnp.swapaxes(out, 1, 2), energy[0, 0]


def solution(mesh):
    fine = Mesh(mesh.devices.reshape(4, 2, 4, 4), ALL)
    row = ("y", "c")
    placed = (
        P(row, None, COL),
        P(row, COL, None, None),
        P(None, COL, None, None),
        P(),
        P(row),
        P(row, COL),
        P(),
        P(),
    )
    return jax.shard_map(
        local, mesh=fine, in_specs=placed, out_specs=(P(row, None, COL), P()), check_vma=False
    )
```

```python
import jax
import jax.numpy as jnp
from jax import lax
from jax.experimental import pallas as pl
from jax.experimental.pallas import tpu as pltpu
from jax.sharding import Mesh, PartitionSpec as P

ITERS = 2
TILE = 256
HALF = 128
TERMS = 16
LEFT_ROWS = 136
SLOT_ROWS = 152
COL = ("x", "z")
ALL = ("y", "c", "x", "z")
SWAP = [(0, 1), (1, 0)]
UP = [(i, (i + 1) % 4) for i in range(4)]
DOWN = [(i, (i - 1) % 4) for i in range(4)]
f32 = jnp.float32
bf16 = jnp.bfloat16


def params(mib):
    return pltpu.CompilerParams(vmem_limit_bytes=mib * 1024 * 1024)


def cost(flops, nbytes):
    return pl.CostEstimate(flops=flops, transcendentals=0, bytes_accessed=nbytes)


def vmem():
    return pl.BlockSpec(memory_space=pltpu.VMEM)


def grids(rows, cols):
    i = lax.broadcasted_iota(jnp.int32, (rows, cols), 0)
    j = lax.broadcasted_iota(jnp.int32, (rows, cols), 1)
    return i, j


def fold_tile(tile):
    i, j = grids(HALF, HALF)
    a00 = tile[:HALF, :HALF]
    a11 = tile[HALF:, HALF:]
    fold = jnp.where(i >= j, a00, a11)
    diag = jnp.sum(jnp.where(i == j, a11, 0.0), axis=0, keepdims=True)
    return fold, tile[:HALF, HALF:], diag


def diag_rows(diag):
    wide = jnp.concatenate([diag, jnp.zeros((1, HALF), f32)], axis=1)
    return jnp.broadcast_to(wide, (8, TILE))


def unfold_tile(fold, corner, diag):
    i, j = grids(HALF, HALF)
    flip = fold.T
    a00 = jnp.where(i >= j, fold, flip)
    a11 = jnp.where(i == j, diag, jnp.where(i < j, fold, flip))
    top = jnp.concatenate([a00, corner], axis=1)
    low = jnp.concatenate([corner.T, a11], axis=1)
    return jnp.concatenate([top, low], axis=0)


def split(x):
    hi = x.astype(bf16)
    return hi, (x - hi.astype(f32)).astype(bf16)


def dot3(a_hi, a_lo, b_hi, b_lo):
    def dot(a, b):
        return jnp.dot(a, b, preferred_element_type=f32)

    return dot(a_hi, b_hi) + (dot(a_hi, b_lo) + dot(a_lo, b_hi))


def total(x):
    return jnp.sum(jnp.sum(x, axis=0, keepdims=True), axis=1, keepdims=True)


def inverse(norm):
    good = norm > 0.0
    return jnp.where(good, 1.0 / jnp.where(good, norm, 1.0), 0.0)


def put(stats, lane, value):
    _, j = grids(8, HALF)
    return jnp.where(j == lane, value, stats)


def fold_left_body(ids, src, keep, give):
    for dst, term in ((give, 1 - ids[1]), (keep, ids[1])):
        fold, corner, diag = fold_tile(src[0, term])
        dst[0, :HALF, :HALF] = fold
        dst[0, :HALF, HALF:] = corner
        dst[0, HALF:, :] = diag_rows(diag)


def fold_left(ids, left_env):
    count = left_env.shape[0]
    folded = pl.BlockSpec((1, LEFT_ROWS, TILE), lambda n, ids: (n, 0, 0))
    return pl.pallas_call(
        fold_left_body,
        grid_spec=pltpu.PrefetchScalarGridSpec(
            num_scalar_prefetch=1,
            grid=(count,),
            in_specs=[pl.BlockSpec((1, 2, TILE, TILE), lambda n, ids: (n, 0, 0, 0))],
            out_specs=[folded, folded],
        ),
        out_shape=[jax.ShapeDtypeStruct((count, LEFT_ROWS, TILE), f32)] * 2,
        compiler_params=params(4),
        cost_estimate=cost(1_000_000, 4_000_000),
        name="fold_left",
    )(ids, left_env)


def from_rows(ids, own, other, slot, field):
    at = (slot % 8) * 3 + field
    return jnp.where(slot // 8 == ids[1], own[at], other[at])


def right_slots_body(ids, own, other, thin, thin_other, right_env, dst, right, sem):
    def fetch(sector):
        return pltpu.make_async_copy(right_env.at[sector, ids[1]], right.at[sector], sem.at[sector])

    for sector in range(8):
        fetch(sector).start()
    for slot in range(TERMS):
        here = slot // 8 == ids[1]
        dst[slot, :16, :] = jnp.where(here, thin[slot % 8], thin_other[slot % 8])
    for sector in range(8):
        fetch(sector).wait()

    def one(slot, carry):
        on = from_rows(ids, own, other, slot, 1 + ids[1]).astype(f32)
        fold, corner, diag = fold_tile(right[from_rows(ids, own, other, slot, 0)] * on)
        dst[slot, 16 : 16 + HALF, :HALF] = fold
        dst[slot, 16 : 16 + HALF, HALF:] = corner
        dst[slot, 16 + HALF :, :] = diag_rows(diag)
        return carry

    lax.fori_loop(0, TERMS, one, 0)


def right_slots(ids, own, other, right_env, thin, thin_other):
    smem = pl.BlockSpec(memory_space=pltpu.SMEM)
    return pl.pallas_call(
        right_slots_body,
        in_specs=[smem] * 3 + [vmem()] * 2 + [pl.BlockSpec(memory_space=pl.ANY)],
        out_specs=vmem(),
        out_shape=jax.ShapeDtypeStruct((TERMS, SLOT_ROWS, TILE), f32),
        scratch_shapes=[pltpu.VMEM((8, TILE, TILE), f32), pltpu.SemaphoreType.DMA((8,))],
        compiler_params=params(10),
        cost_estimate=cost(4_000_000, 10_000_000),
        name="right_slots",
    )(ids, own, other, thin, thin_other, right_env)


def left_slots_body(ids, left_sector, *refs):
    pieces, dst = refs[:8], refs[8]

    def one(slot, carry):
        sector = left_sector[ids[0] * 16 + slot]
        home = sector // 4
        which = ((home // 2 - ids[0] + 4) % 4) * 2 + (home % 2 + ids[1]) % 2
        for n in range(8):

            @pl.when(which == n)
            def _():
                dst[slot] = pieces[n][sector % 4]

        return carry

    lax.fori_loop(0, TERMS, one, 0)


def left_slots(ids, left_sector, pieces):
    smem = pl.BlockSpec(memory_space=pltpu.SMEM)
    return pl.pallas_call(
        left_slots_body,
        in_specs=[smem, smem] + [vmem()] * 8,
        out_specs=vmem(),
        out_shape=jax.ShapeDtypeStruct((TERMS,) + pieces[0].shape[1:], f32),
        compiler_params=params(10),
        cost_estimate=cost(0, 4_000_000),
        name="left_slots",
    )(ids, left_sector, *pieces)


def live_sizes(ids, own, other, left_sector, left_size, right_size):
    live_left = left_size[left_sector[ids[0] * 16 + ids[2]]]
    live_right = right_size[from_rows(ids, own, other, ids[2], 0)]
    return live_right, live_left


def mask_of(live_right, live_left):
    i, j = grids(TILE, TILE)
    return (i < live_right) & (j < live_left)


def right_times(r_hi, r_lo, q_hi, q_lo, m_hi, m_lo):
    for n in range(TERMS):
        rows = pl.ds(n * TILE, TILE)
        hi, lo = split(dot3(r_hi[rows, :], r_lo[rows, :], q_hi, q_lo))
        m_hi[:, rows] = hi
        m_lo[:, rows] = lo


def first_body(ids, own, other, sector, lsize, rsize, arrived, r_hi, r_lo, m_hi, m_lo, q1, stats):
    live_right, live_left = live_sizes(ids, own, other, sector, lsize, rsize)
    block = jnp.concatenate([arrived[n, :16, :] for n in range(TERMS)], axis=0)
    start = jnp.where(mask_of(live_right, live_left), block, 0.0)
    norm = jnp.sqrt(total(start * start))
    vec = start * inverse(norm)
    q1[...] = vec
    stats[...] = put(jnp.zeros((8, HALF), f32), 0, norm)

    def term(n, carry):
        full = unfold_tile(
            arrived[n, 16 : 16 + HALF, :HALF],
            arrived[n, 16 : 16 + HALF, HALF:],
            arrived[n, 16 + HALF : 17 + HALF, :HALF],
        )
        hi, lo = split(full)
        rows = pl.ds(pl.multiple_of(n * TILE, TILE), TILE)
        r_hi[rows, :] = hi
        r_lo[rows, :] = lo
        return carry

    lax.fori_loop(0, TERMS, term, 0)
    q_hi, q_lo = split(vec)
    right_times(r_hi, r_lo, q_hi, q_lo, m_hi, m_lo)


def first_vector(scalars, arrived):
    smem = pl.BlockSpec(memory_space=pltpu.SMEM)
    return pl.pallas_call(
        first_body,
        in_specs=[smem] * 6 + [vmem()],
        out_specs=[vmem()] * 6,
        out_shape=[
            jax.ShapeDtypeStruct((TERMS * TILE, TILE), bf16),
            jax.ShapeDtypeStruct((TERMS * TILE, TILE), bf16),
            jax.ShapeDtypeStruct((TILE, TERMS * TILE), bf16),
            jax.ShapeDtypeStruct((TILE, TERMS * TILE), bf16),
            jax.ShapeDtypeStruct((TILE, TILE), f32),
            jax.ShapeDtypeStruct((8, HALF), f32),
        ],
        compiler_params=params(10),
        cost_estimate=cost(1_700_000_000, 12_000_000),
        name="first_vector",
    )(*scalars, arrived)


def image_one_body(arrived, m_hi, m_lo, l_hi, l_lo, part):
    for n in range(TERMS):
        full = unfold_tile(
            arrived[n, :HALF, :HALF], arrived[n, :HALF, HALF:], arrived[n, HALF : HALF + 1, :HALF]
        )
        hi, lo = split(full)
        rows = pl.ds(n * TILE, TILE)
        l_hi[rows, :] = hi
        l_lo[rows, :] = lo
    part[...] = dot3(m_hi[...], m_lo[...], l_hi[...], l_lo[...])


def image_one(arrived, m_hi, m_lo):
    return pl.pallas_call(
        image_one_body,
        in_specs=[vmem()] * 3,
        out_specs=[vmem()] * 3,
        out_shape=[
            jax.ShapeDtypeStruct((TERMS * TILE, TILE), bf16),
            jax.ShapeDtypeStruct((TERMS * TILE, TILE), bf16),
            jax.ShapeDtypeStruct((TILE, TILE), f32),
        ],
        compiler_params=params(10),
        cost_estimate=cost(1_700_000_000, 10_000_000),
        name="image_one",
    )(arrived, m_hi, m_lo)


def lanczos(image, last, before, beta):
    alpha = total(last * image)
    rest = image - alpha * last
    if before is not None:
        rest = rest - beta * before
    again = rest - total(last * rest) * last
    if before is not None:
        again = again - total(before * rest) * before
    norm = jnp.sqrt(total(again * again))
    return alpha, norm, again * inverse(norm)


def image_two_body(
    ids, own, other, sector, lsize, rsize,
    part_a, part_b, q1, stats_in, r_hi, r_lo, l_hi, l_lo,
    part, q2, stats, m_hi, m_lo,
):
    mask = mask_of(*live_sizes(ids, own, other, sector, lsize, rsize))
    image = jnp.where(mask, part_a[...] + part_b[...], 0.0)
    alpha, norm, vec = lanczos(image, q1[...], None, None)
    q2[...] = vec
    stats[...] = put(put(stats_in[...], 1, alpha), 2, norm)
    q_hi, q_lo = split(vec)
    right_times(r_hi, r_lo, q_hi, q_lo, m_hi, m_lo)
    part[...] = dot3(m_hi[...], m_lo[...], l_hi[...], l_lo[...])


def image_two(scalars, part, part_other, q1, stats, stacks):
    smem = pl.BlockSpec(memory_space=pltpu.SMEM)
    return pl.pallas_call(
        image_two_body,
        in_specs=[smem] * 6 + [vmem()] * 8,
        out_specs=[vmem()] * 3,
        out_shape=[
            jax.ShapeDtypeStruct((TILE, TILE), f32),
            jax.ShapeDtypeStruct((TILE, TILE), f32),
            jax.ShapeDtypeStruct((8, HALF), f32),
        ],
        scratch_shapes=[pltpu.VMEM((TILE, TERMS * TILE), bf16)] * 2,
        compiler_params=params(10),
        cost_estimate=cost(3_300_000_000, 9_000_000),
        name="image_two",
    )(*scalars, part, part_other, q1, stats, *stacks)


def third_body(
    ids, own, other, sector, lsize, rsize, part_a, part_b, q1, q2, stats_in, q3, sent, stats
):
    mask = mask_of(*live_sizes(ids, own, other, sector, lsize, rsize))
    image = jnp.where(mask, part_a[...] + part_b[...], 0.0)
    _, j = grids(8, HALF)
    beta = total(jnp.where((j == 2) & (grids(8, HALF)[0] == 0), stats_in[...], 0.0))
    alpha, norm, vec = lanczos(image, q2[...], q1[...], beta)
    q3[...] = vec
    pick = jnp.where(ids[1] == 0, q2[...], vec)
    for n in range(16):
        sent[n] = pick[16 * n : 16 * n + 16]
    stats[...] = put(put(stats_in[...], 3, alpha), 4, norm)


def third_vector(scalars, part, part_other, q1, q2, stats):
    smem = pl.BlockSpec(memory_space=pltpu.SMEM)
    return pl.pallas_call(
        third_body,
        in_specs=[smem] * 6 + [vmem()] * 5,
        out_specs=[vmem()] * 3,
        out_shape=[
            jax.ShapeDtypeStruct((TILE, TILE), f32),
            jax.ShapeDtypeStruct((16, 16, TILE), f32),
            jax.ShapeDtypeStruct((8, HALF), f32),
        ],
        compiler_params=params(4),
        name="third_vector",
    )(*scalars, part, part_other, q1, q2, stats)


def image_three_body(q3, stats_in, r_hi, r_lo, l_hi, l_lo, stats, m_hi, m_lo):
    vec = q3[...]
    q_hi, q_lo = split(vec)
    right_times(r_hi, r_lo, q_hi, q_lo, m_hi, m_lo)
    alpha = total(vec * dot3(m_hi[...], m_lo[...], l_hi[...], l_lo[...]))
    mine = put(stats_in[...], 5, alpha)
    stats[...] = jnp.broadcast_to(mine[0:1, :], (128, HALF))


def image_three(q3, stats, stacks):
    return pl.pallas_call(
        image_three_body,
        in_specs=[vmem()] * 6,
        out_specs=vmem(),
        out_shape=jax.ShapeDtypeStruct((128, HALF), f32),
        scratch_shapes=[pltpu.VMEM((TILE, TERMS * TILE), bf16)] * 2,
        compiler_params=params(10),
        cost_estimate=cost(3_300_000_000, 9_000_000),
        name="image_three",
    )(q3, stats, *stacks)


def ritz_pair(norm, a1, b1, a2, b2, a3):
    def apply(x):
        return [a1 * x[0] + b1 * x[1], b1 * x[0] + a2 * x[1] + b2 * x[2], b2 * x[1] + a3 * x[2]]

    def dot(x, y):
        return 0.5 * jnp.sum(x[0] * y[0] + x[1] * y[1] + x[2] * y[2], axis=1, keepdims=True)

    zero = jnp.zeros_like(norm)
    start = [norm, zero, zero]
    image = apply(start)
    norm_sq = dot(start, start)
    correlation = dot(start, image)
    inv_norm = 1.0 / jnp.sqrt(norm_sq)
    basis = [x * inv_norm for x in start]
    applied = [x * inv_norm for x in image]
    ritz = correlation / norm_sq
    for _ in range(ITERS):
        residual = [x - ritz * y for x, y in zip(applied, basis)]
        res_sq = dot(residual, residual)
        length = jnp.sqrt(res_sq)
        fresh = [x / length for x in residual]
        fresh_applied = apply(fresh)
        curvature = dot(fresh, fresh_applied)
        half_gap = 0.5 * (ritz - curvature)
        root = jnp.sqrt(half_gap * half_gap + res_sq)
        lowest = 0.5 * (ritz + curvature) - root
        first = curvature - lowest
        pair = jnp.sqrt(first * first + res_sq)
        basis = [(first * x - length * y) / pair for x, y in zip(basis, fresh)]
        applied = [(first * x - length * y) / pair for x, y in zip(applied, fresh_applied)]
        ritz = lowest
    return basis, ritz


def finish_body(
    ids, sector, rsector, lsize, rsize, stats, thin, got, back, out, energy, coef
):
    flip = stats[...].T
    norm, a1, b1, a2, b2, part = [flip[m : m + 1, :] for m in range(6)]
    _, lane = grids(1, HALF)
    core_of = (lane // 16) % 2
    a3 = part + jnp.where(core_of == 0, pltpu.roll(part, HALF - 16, 1), pltpu.roll(part, 16, 1))
    basis, ritz = ritz_pair(norm, a1, b1, a2, b2, a3)
    energy[...] = jnp.broadcast_to(ritz, (8, HALF))
    scale = jnp.sqrt(jnp.full((1, HALF), 64 * TILE * TILE, f32))
    i, _ = grids(HALF, HALF)
    c1 = basis[0] * inverse(norm) * scale
    c2 = basis[1] * scale
    c3 = basis[2] * scale
    coef[...] = jnp.where(i == 0, c1, jnp.where(i == 1, c2, jnp.where(i == 2, c3, 0.0))).T
    core = ids[1]
    own = coef[pl.ds(pl.multiple_of(ids[0] * 32 + core * 8, 8), 8), :]
    jcol, irow = grids(16, TILE)
    for b in range(8):
        live_left = lsize[sector[ids[0] * 16 + core * 8 + b]]
        live_right = rsize[rsector[b]]
        live = (jcol + ids[2] * 16 < live_right) & (irow < live_left)
        keep = got[core * 8 + b]
        recv = back[b]
        second = jnp.where(core == 0, keep, recv)
        third = jnp.where(core == 0, recv, keep)
        out[b] = (
            own[b : b + 1, 0:1] * jnp.where(live, thin[b], 0.0)
            + own[b : b + 1, 1:2] * second
            + own[b : b + 1, 2:3] * third
        )


def finish(ids, sector, rsector, lsize, rsize, stats, thin, got, back):
    smem = pl.BlockSpec(memory_space=pltpu.SMEM)
    return pl.pallas_call(
        finish_body,
        in_specs=[smem] * 5 + [vmem()] * 4,
        out_specs=[vmem()] * 2,
        out_shape=[
            jax.ShapeDtypeStruct(thin.shape, f32),
            jax.ShapeDtypeStruct((8, HALF), f32),
        ],
        scratch_shapes=[pltpu.VMEM((HALF, HALF), f32)],
        compiler_params=params(4),
        name="finish",
    )(ids, sector, rsector, lsize, rsize, stats, thin, got, back)


def local(theta, left_env, right_env, left_sector, right_sector, term_on, left_size, right_size):
    plane = lax.axis_index("y").astype(jnp.int32)
    core = lax.axis_index("c").astype(jnp.int32)
    place = lax.axis_index(COL).astype(jnp.int32)
    ids = jnp.stack([plane, core, place])
    thin = jnp.swapaxes(theta, 1, 2)

    own = jnp.concatenate([right_sector[:, None], term_on], axis=1).reshape(-1)
    mine, folded = fold_left(ids, left_env)
    theirs = lax.ppermute(folded, "c", SWAP)
    mine_up = lax.ppermute(mine, "y", UP)
    mine_down = lax.ppermute(mine, "y", DOWN)
    theirs_up = lax.ppermute(theirs, "y", UP)
    theirs_down = lax.ppermute(theirs, "y", DOWN)

    other = lax.ppermute(own, "c", SWAP)
    thin_other = lax.ppermute(thin, "c", SWAP)
    thin_late, _ = lax.optimization_barrier((thin, mine))
    slots = right_slots(ids, own, other, right_env, thin_late, thin_other)
    arrived = lax.all_to_all(slots, COL, 0, 0, tiled=True)
    scalars = (ids, own, other, left_sector, left_size, right_size)
    r_hi, r_lo, m_hi, m_lo, q1, stats = first_vector(scalars, arrived)

    mine_far = lax.ppermute(mine_up, "y", UP)
    theirs_far = lax.ppermute(theirs_down, "y", DOWN)
    pieces = [mine, theirs, mine_down, theirs_down, mine_far, theirs_far, mine_up, theirs_up]
    left_arrived = lax.all_to_all(left_slots(ids, left_sector, pieces), COL, 0, 0, tiled=True)
    l_hi, l_lo, part = image_one(left_arrived, m_hi, m_lo)
    stacks = (r_hi, r_lo, l_hi, l_lo)
    part, q2, stats = image_two(scalars, part, lax.ppermute(part, "c", SWAP), q1, stats, stacks)
    q3, sent, stats = third_vector(scalars, part, lax.ppermute(part, "c", SWAP), q1, q2, stats)

    stats = image_three(q3, stats, stacks)
    sent, stats = lax.optimization_barrier((sent, stats))
    stats = lax.all_to_all(stats, ALL, 0, 0, tiled=True)
    got = lax.all_to_all(sent, COL, 0, 0, tiled=True)
    give = lax.dynamic_slice_in_dim(got, (1 - core) * 8, 8)
    back = lax.ppermute(give, "c", SWAP)
    out, energy = finish(
        ids, left_sector, right_sector, left_size, right_size, stats, thin, got, back
    )
    return jnp.swapaxes(out, 1, 2), energy[0, 0]


def solution(mesh):
    fine = Mesh(mesh.devices.reshape(4, 2, 4, 4), ALL)
    row = ("y", "c")
    placed = (
        P(row, None, COL),
        P(row, COL, None, None),
        P(None, COL, None, None),
        P(),
        P(row),
        P(row, COL),
        P(),
        P(),
    )
    return jax.shard_map(
        local, mesh=fine, in_specs=placed, out_specs=(P(row, None, COL), P()), check_vma=False
    )
```

```python
import jax
import jax.numpy as jnp
from jax import lax
from jax.experimental import pallas as pl
from jax.experimental.pallas import tpu as pltpu
from jax.sharding import Mesh, PartitionSpec as P

ITERS = 2
TILE = 256
HALF = 128
TERMS = 16
LEFT_ROWS = 136
SLOT_ROWS = 152
COL = ("x", "z")
ALL = ("y", "c", "x", "z")
SWAP = [(0, 1), (1, 0)]
UP = [(i, (i + 1) % 4) for i in range(4)]
DOWN = [(i, (i - 1) % 4) for i in range(4)]
f32 = jnp.float32
bf16 = jnp.bfloat16


def params(mib):
    return pltpu.CompilerParams(vmem_limit_bytes=mib * 1024 * 1024)


def hbm():
    return pl.BlockSpec(memory_space=pltpu.HBM)


def in_hbm(x):
    return pltpu.with_memory_space_constraint(x, pltpu.HBM)


def smem():
    return pl.BlockSpec(memory_space=pltpu.SMEM)


def cost(flops, nbytes):
    return pl.CostEstimate(flops=flops, transcendentals=0, bytes_accessed=nbytes)


def vmem():
    return pl.BlockSpec(memory_space=pltpu.VMEM)


def grids(rows, cols):
    i = lax.broadcasted_iota(jnp.int32, (rows, cols), 0)
    j = lax.broadcasted_iota(jnp.int32, (rows, cols), 1)
    return i, j


def fold_tile(tile):
    i, j = grids(HALF, HALF)
    a00 = tile[:HALF, :HALF]
    a11 = tile[HALF:, HALF:]
    fold = jnp.where(i >= j, a00, a11)
    diag = jnp.sum(jnp.where(i == j, a11, 0.0), axis=0, keepdims=True)
    return fold, tile[:HALF, HALF:], diag


def diag_rows(diag):
    wide = jnp.concatenate([diag, jnp.zeros((1, HALF), f32)], axis=1)
    return jnp.broadcast_to(wide, (8, TILE))


def unfold_tile(fold, corner, diag):
    i, j = grids(HALF, HALF)
    flip = fold.T
    a00 = jnp.where(i >= j, fold, flip)
    a11 = jnp.where(i == j, diag, jnp.where(i < j, fold, flip))
    top = jnp.concatenate([a00, corner], axis=1)
    low = jnp.concatenate([corner.T, a11], axis=1)
    return jnp.concatenate([top, low], axis=0)


def split(x):
    hi = x.astype(bf16)
    return hi, (x - hi.astype(f32)).astype(bf16)


def dot3(a_hi, a_lo, b_hi, b_lo):
    def dot(a, b):
        return jnp.dot(a, b, preferred_element_type=f32)

    return dot(a_hi, b_hi) + (dot(a_hi, b_lo) + dot(a_lo, b_hi))


def total(x):
    return jnp.sum(jnp.sum(x, axis=0, keepdims=True), axis=1, keepdims=True)


def inverse(norm):
    good = norm > 0.0
    return jnp.where(good, 1.0 / jnp.where(good, norm, 1.0), 0.0)


def put(stats, lane, value):
    _, j = grids(8, HALF)
    return jnp.where(j == lane, value, stats)


def put_folded(dst, at, row, tile):
    fold, corner, diag = fold_tile(tile)
    dst[at, row : row + HALF, :HALF] = fold
    dst[at, row : row + HALF, HALF:] = corner
    dst[at, row + HALF : row + HALF + 8, :] = diag_rows(diag)


def fold_left_body(ids, src, keep, give, tiles, folded, sem_in, sem_out):
    def fetch(t, n):
        term = ids[1] if t else 1 - ids[1]
        at = 4 * t + n
        return pltpu.make_async_copy(src.at[n, term], tiles.at[at], sem_in.at[at])

    def store(t, n):
        at = 4 * t + n
        dst = keep if t else give
        return pltpu.make_async_copy(folded.at[at], dst.at[n], sem_out.at[at])

    order = [(t, n) for t in range(2) for n in range(4)]
    for t, n in order:
        fetch(t, n).start()
    for t, n in order:
        fetch(t, n).wait()
        put_folded(folded, 4 * t + n, 0, tiles[4 * t + n])
        store(t, n).start()
    for t, n in order:
        store(t, n).wait()


def fold_left(ids, left_env):
    count = left_env.shape[0]
    return pl.pallas_call(
        fold_left_body,
        in_specs=[smem(), hbm()],
        out_specs=[hbm(), hbm()],
        out_shape=[pltpu.HBM((count, LEFT_ROWS, TILE), f32)] * 2,
        scratch_shapes=[
            pltpu.VMEM((2 * count, TILE, TILE), f32),
            pltpu.VMEM((2 * count, LEFT_ROWS, TILE), f32),
            pltpu.SemaphoreType.DMA((2 * count,)),
            pltpu.SemaphoreType.DMA((2 * count,)),
        ],
        compiler_params=params(8),
        cost_estimate=cost(1_000_000, 4_000_000),
        name="fold_left",
    )(ids, in_hbm(left_env))


def sector_of(ids, rsector, rsector_other, slot):
    return jnp.where(slot // 8 == ids[1], rsector[slot % 8], rsector_other[slot % 8])


def right_slots_body(
    ids, rsector, rsector_other, on, on_other, thin, thin_other, right_env,
    out, right, dst, sem_in, sem_out,
):
    def fetch(sector):
        return pltpu.make_async_copy(
            right_env.at[sector, ids[1]], right.at[sector], sem_in.at[sector]
        )

    def store(slot):
        return pltpu.make_async_copy(dst.at[slot], out.at[slot], sem_out.at[slot])

    for sector in range(8):
        fetch(sector).start()
    for slot in range(TERMS):
        here = slot // 8 == ids[1]
        dst[slot, :16, :] = jnp.where(here, thin[slot % 8], thin_other[slot % 8])
    for sector in range(8):
        fetch(sector).wait()

    def one(slot, carry):
        here = slot // 8 == ids[1]
        weight = jnp.where(here, on[slot % 8, ids[1]], on_other[slot % 8, ids[1]]).astype(f32)
        put_folded(dst, slot, 16, right[sector_of(ids, rsector, rsector_other, slot)] * weight)
        store(slot).start()
        return carry

    def finished(slot, carry):
        store(slot).wait()
        return carry

    lax.fori_loop(0, TERMS, one, 0)
    lax.fori_loop(0, TERMS, finished, 0)


def right_slots(ids, rsector, rsector_other, on, on_other, thin, thin_other, right_env):
    slots = (TERMS, SLOT_ROWS, TILE)
    return pl.pallas_call(
        right_slots_body,
        in_specs=[smem()] * 5 + [vmem()] * 2 + [hbm()],
        out_specs=hbm(),
        out_shape=pltpu.HBM(slots, f32),
        scratch_shapes=[
            pltpu.VMEM((8, TILE, TILE), f32),
            pltpu.VMEM(slots, f32),
            pltpu.SemaphoreType.DMA((8,)),
            pltpu.SemaphoreType.DMA((TERMS,)),
        ],
        compiler_params=params(10),
        cost_estimate=cost(4_000_000, 10_000_000),
        name="right_slots",
    )(ids, rsector, rsector_other, on, on_other, thin, thin_other, in_hbm(right_env))


def left_slots_body(ids, left_sector, kept, theirs, below, above, far_a, far_b, out, *scratch):
    dst, sem_in, sem_out = scratch

    def fetch(src, slot):
        return pltpu.make_async_copy(src, dst.at[slot], sem_in.at[slot])

    def store(slot):
        return pltpu.make_async_copy(dst.at[slot], out.at[slot], sem_out.at[slot])

    def start(slot, carry):
        sector = left_sector[ids[0] * 16 + slot]
        home = sector // 4
        tile = sector % 4
        away = (home // 2 - ids[0] + 4) % 4
        same = home % 2 == ids[1]
        cases = [
            (same, kept, (home // 2) * 4 + tile),
            (~same & (away == 0), theirs, tile),
            (~same & (away == 1), above, tile),
            (~same & (away == 2) & (tile < 2), far_a, tile),
            (~same & (away == 2) & (tile >= 2), far_b, tile - 2),
            (~same & (away == 3), below, tile),
        ]
        for case, src, at in cases:

            @pl.when(case)
            def _():
                fetch(src.at[at], slot).start()

        return carry

    def forward(slot, carry):
        fetch(kept.at[0], slot).wait()
        store(slot).start()
        return carry

    def finished(slot, carry):
        store(slot).wait()
        return carry

    lax.fori_loop(0, TERMS, start, 0)
    lax.fori_loop(0, TERMS, forward, 0)
    lax.fori_loop(0, TERMS, finished, 0)


def left_slots(ids, left_sector, pieces):
    slots = (TERMS, LEFT_ROWS, TILE)
    return pl.pallas_call(
        left_slots_body,
        in_specs=[smem(), smem()] + [hbm()] * 6,
        out_specs=hbm(),
        out_shape=pltpu.HBM(slots, f32),
        scratch_shapes=[
            pltpu.VMEM(slots, f32),
            pltpu.SemaphoreType.DMA((TERMS,)),
            pltpu.SemaphoreType.DMA((TERMS,)),
        ],
        compiler_params=params(6),
        cost_estimate=cost(0, 4_000_000),
        name="left_slots",
    )(ids, left_sector, *[in_hbm(x) for x in pieces])


def live_sizes(ids, rsector, rsector_other, left_sector, left_size, right_size):
    live_left = left_size[left_sector[ids[0] * 16 + ids[2]]]
    live_right = right_size[sector_of(ids, rsector, rsector_other, ids[2])]
    return live_right, live_left


def mask_of(live_right, live_left):
    i, j = grids(TILE, TILE)
    return (i < live_right) & (j < live_left)


def first_body(
    ids, rsector, rsector_other, sector, lsize, rsize, slots,
    r_hi, r_lo, m_hi, m_lo, q1, stats, arrived, sem,
):
    live_right, live_left = live_sizes(ids, rsector, rsector_other, sector, lsize, rsize)

    def fetch(n):
        return pltpu.make_async_copy(slots.at[n], arrived.at[n], sem.at[n])

    for n in range(TERMS):
        fetch(n).start()
    for n in range(TERMS):
        fetch(n).wait()
        full = unfold_tile(
            arrived[n, 16 : 16 + HALF, :HALF],
            arrived[n, 16 : 16 + HALF, HALF:],
            arrived[n, 16 + HALF : 17 + HALF, :HALF],
        )
        hi, lo = split(full)
        r_hi[n * TILE : (n + 1) * TILE, :] = hi
        r_lo[n * TILE : (n + 1) * TILE, :] = lo
    block = jnp.concatenate([arrived[n, :16, :] for n in range(TERMS)], axis=0)
    start = jnp.where(mask_of(live_right, live_left), block, 0.0)
    norm = jnp.sqrt(total(start * start))
    vec = start * inverse(norm)
    q1[...] = vec
    stats[...] = put(jnp.zeros((8, HALF), f32), 0, norm)
    q_hi, q_lo = split(vec)
    for n in range(TERMS):
        rows = pl.ds(n * TILE, TILE)
        hi, lo = split(dot3(r_hi[rows, :], r_lo[rows, :], q_hi, q_lo))
        m_hi[:, rows] = hi
        m_lo[:, rows] = lo


def first_vector(scalars, slots):
    return pl.pallas_call(
        first_body,
        in_specs=[smem()] * 6 + [hbm()],
        out_specs=[vmem()] * 6,
        out_shape=[
            jax.ShapeDtypeStruct((TERMS * TILE, TILE), bf16),
            jax.ShapeDtypeStruct((TERMS * TILE, TILE), bf16),
            jax.ShapeDtypeStruct((TILE, TERMS * TILE), bf16),
            jax.ShapeDtypeStruct((TILE, TERMS * TILE), bf16),
            jax.ShapeDtypeStruct((TILE, TILE), f32),
            jax.ShapeDtypeStruct((8, HALF), f32),
        ],
        scratch_shapes=[
            pltpu.VMEM((TERMS, SLOT_ROWS, TILE), f32),
            pltpu.SemaphoreType.DMA((TERMS,)),
        ],
        compiler_params=params(10),
        cost_estimate=cost(1_700_000_000, 12_000_000),
        name="first_vector",
    )(*scalars, in_hbm(slots))


def image_one_body(arrived, m_hi, m_lo, l_hi, l_lo, part, here, sem):
    chunk = TERMS // 4

    def fetch(p, c):
        cols = pl.ds(c * chunk * TILE, chunk * TILE)
        src = (m_hi, m_lo)[p]
        return pltpu.make_async_copy(src.at[:, cols], here.at[p, :, cols], sem.at[p, c])

    for c in range(4):
        for p in range(2):
            fetch(p, c).start()
    for n in range(TERMS):
        full = unfold_tile(
            arrived[n, :HALF, :HALF], arrived[n, :HALF, HALF:], arrived[n, HALF : HALF + 1, :HALF]
        )
        hi, lo = split(full)
        l_hi[n * TILE : (n + 1) * TILE, :] = hi
        l_lo[n * TILE : (n + 1) * TILE, :] = lo
    acc = jnp.zeros((TILE, TILE), f32)
    for c in range(4):
        for p in range(2):
            fetch(p, c).wait()
        cols = pl.ds(c * chunk * TILE, chunk * TILE)
        acc = acc + dot3(here[0, :, cols], here[1, :, cols], l_hi[cols, :], l_lo[cols, :])
    part[...] = acc


def image_one(arrived, m_hi, m_lo):
    return pl.pallas_call(
        image_one_body,
        in_specs=[vmem(), hbm(), hbm()],
        out_specs=[vmem()] * 3,
        out_shape=[
            jax.ShapeDtypeStruct((TERMS * TILE, TILE), bf16),
            jax.ShapeDtypeStruct((TERMS * TILE, TILE), bf16),
            jax.ShapeDtypeStruct((TILE, TILE), f32),
        ],
        scratch_shapes=[
            pltpu.VMEM((2, TILE, TERMS * TILE), bf16),
            pltpu.SemaphoreType.DMA((2, 4)),
        ],
        compiler_params=params(10),
        cost_estimate=cost(1_700_000_000, 10_000_000),
        name="image_one",
    )(arrived, in_hbm(m_hi), in_hbm(m_lo))


def lanczos(image, last, before, beta):
    alpha = total(last * image)
    rest = image - alpha * last
    if before is not None:
        rest = rest - beta * before
    again = rest - total(last * rest) * last
    if before is not None:
        again = again - total(before * rest) * before
    norm = jnp.sqrt(total(again * again))
    return alpha, norm, again * inverse(norm)


def half_image(vec, r_hi, r_lo, l_hi, l_lo):
    q_hi, q_lo = split(vec)
    acc = jnp.zeros((TILE, TILE), f32)
    for n in range(TERMS):
        rows = pl.ds(n * TILE, TILE)
        hi, lo = split(dot3(r_hi[rows, :], r_lo[rows, :], q_hi, q_lo))
        acc = acc + dot3(hi, lo, l_hi[rows, :], l_lo[rows, :])
    return acc


def image_two_body(
    ids, rsector, rsector_other, sector, lsize, rsize,
    part_a, part_b, q1, stats_in, r_hi, r_lo, l_hi, l_lo,
    part, q2, stats,
):
    mask = mask_of(*live_sizes(ids, rsector, rsector_other, sector, lsize, rsize))
    image = jnp.where(mask, part_a[...] + part_b[...], 0.0)
    alpha, norm, vec = lanczos(image, q1[...], None, None)
    q2[...] = vec
    stats[...] = put(put(stats_in[...], 1, alpha), 2, norm)
    part[...] = half_image(vec, r_hi, r_lo, l_hi, l_lo)


def image_two(scalars, part, part_other, q1, stats, stacks):
    return pl.pallas_call(
        image_two_body,
        in_specs=[smem()] * 6 + [vmem()] * 8,
        out_specs=[vmem()] * 3,
        out_shape=[
            jax.ShapeDtypeStruct((TILE, TILE), f32),
            jax.ShapeDtypeStruct((TILE, TILE), f32),
            jax.ShapeDtypeStruct((8, HALF), f32),
        ],
        compiler_params=params(6),
        cost_estimate=cost(3_300_000_000, 9_000_000),
        name="image_two",
    )(*scalars, part, part_other, q1, stats, *stacks)


def image_three_body(
    ids, rsector, rsector_other, sector, lsize, rsize,
    part_a, part_b, q1, q2, stats_in, r_hi, r_lo, l_hi, l_lo, slots,
):
    mask = mask_of(*live_sizes(ids, rsector, rsector_other, sector, lsize, rsize))
    image = jnp.where(mask, part_a[...] + part_b[...], 0.0)
    i, j = grids(8, HALF)
    beta = total(jnp.where((j == 2) & (i == 0), stats_in[...], 0.0))
    alpha, norm, vec = lanczos(image, q2[...], q1[...], beta)
    pick = jnp.where(ids[1] == 0, q2[...], vec)
    for n in range(16):
        slots[n, :16, :] = pick[16 * n : 16 * n + 16]
    stats = put(put(stats_in[...], 3, alpha), 4, norm)
    alpha = total(vec * half_image(vec, r_hi, r_lo, l_hi, l_lo))
    stats = put(stats, 5, alpha)
    wide = jnp.concatenate([stats, jnp.zeros((8, HALF), f32)], axis=1)
    for n in range(16):
        slots[n, 16:24, :] = wide


def image_three(scalars, part, part_other, q1, q2, stats, stacks):
    return pl.pallas_call(
        image_three_body,
        in_specs=[smem()] * 6 + [vmem()] * 9,
        out_specs=vmem(),
        out_shape=jax.ShapeDtypeStruct((16, 24, TILE), f32),
        compiler_params=params(6),
        cost_estimate=cost(3_300_000_000, 9_000_000),
        name="image_three",
    )(*scalars, part, part_other, q1, q2, stats, *stacks)


def ritz_pair(norm, a1, b1, a2, b2, a3):
    def apply(x):
        return [a1 * x[0] + b1 * x[1], b1 * x[0] + a2 * x[1] + b2 * x[2], b2 * x[1] + a3 * x[2]]

    def dot(x, y):
        return jnp.sum(x[0] * y[0] + x[1] * y[1] + x[2] * y[2], axis=1, keepdims=True)

    zero = jnp.zeros_like(norm)
    start = [norm, zero, zero]
    image = apply(start)
    norm_sq = dot(start, start)
    correlation = dot(start, image)
    inv_norm = 1.0 / jnp.sqrt(norm_sq)
    basis = [x * inv_norm for x in start]
    applied = [x * inv_norm for x in image]
    ritz = correlation / norm_sq
    for _ in range(ITERS):
        residual = [x - ritz * y for x, y in zip(applied, basis)]
        res_sq = dot(residual, residual)
        length = jnp.sqrt(res_sq)
        fresh = [x / length for x in residual]
        fresh_applied = apply(fresh)
        curvature = dot(fresh, fresh_applied)
        half_gap = 0.5 * (ritz - curvature)
        root = jnp.sqrt(half_gap * half_gap + res_sq)
        lowest = 0.5 * (ritz + curvature) - root
        first = curvature - lowest
        pair = jnp.sqrt(first * first + res_sq)
        basis = [(first * x - length * y) / pair for x, y in zip(basis, fresh)]
        applied = [(first * x - length * y) / pair for x, y in zip(applied, fresh_applied)]
        ritz = lowest
    return basis, ritz


def finish_body(
    ids, sector, rsector, lsize, rsize, own_stats, other_stats, thin, got, back,
    out, energy, coef,
):
    _, lane = grids(64, HALF)
    stats = own_stats[...] + jnp.where(lane == 5, other_stats[...], 0.0)
    flip = jnp.concatenate([stats, jnp.zeros((64, HALF), f32)], axis=0).T
    norm, a1, b1, a2, b2, a3 = [flip[m : m + 1, :] for m in range(6)]
    basis, ritz = ritz_pair(norm, a1, b1, a2, b2, a3)
    energy[0, 0] = jnp.sum(ritz)
    scale = jnp.sqrt(jnp.full((1, HALF), 64 * TILE * TILE, f32))
    i, _ = grids(HALF, HALF)
    c1 = basis[0] * inverse(norm) * scale
    c2 = basis[1] * scale
    c3 = basis[2] * scale
    coef[...] = jnp.where(i == 0, c1, jnp.where(i == 1, c2, jnp.where(i == 2, c3, 0.0))).T
    core = ids[1]
    own = coef[pl.ds(pl.multiple_of(core * 8, 8), 8), :]
    jcol, irow = grids(16, TILE)
    for b in range(8):
        live_left = lsize[sector[ids[0] * 16 + core * 8 + b]]
        live_right = rsize[rsector[b]]
        live = (jcol + ids[2] * 16 < live_right) & (irow < live_left)
        keep = got[core * 8 + b, :16, :]
        recv = back[b, :16, :]
        second = jnp.where(core == 0, keep, recv)
        third = jnp.where(core == 0, recv, keep)
        out[b] = (
            own[b : b + 1, 0:1] * jnp.where(live, thin[b], 0.0)
            + own[b : b + 1, 1:2] * second
            + own[b : b + 1, 2:3] * third
        )


def finish(ids, sector, rsector, lsize, rsize, own_stats, other_stats, thin, got, back):
    return pl.pallas_call(
        finish_body,
        in_specs=[smem()] * 5 + [vmem()] * 5,
        out_specs=[vmem(), smem()],
        out_shape=[
            jax.ShapeDtypeStruct(thin.shape, f32),
            jax.ShapeDtypeStruct((1, 1), f32),
        ],
        scratch_shapes=[pltpu.VMEM((HALF, HALF), f32)],
        compiler_params=params(4),
        name="finish",
    )(ids, sector, rsector, lsize, rsize, own_stats, other_stats, thin, got, back)


def local(theta, left_env, right_env, left_sector, right_sector, term_on, left_size, right_size):
    plane = lax.axis_index("y").astype(jnp.int32)
    core = lax.axis_index("c").astype(jnp.int32)
    place = lax.axis_index(COL).astype(jnp.int32)
    ids = jnp.stack([plane, core, place])
    thin = jnp.swapaxes(theta, 1, 2)

    mine, folded = fold_left(ids, left_env)
    kept = lax.all_gather(mine, "y", axis=0, tiled=True)
    theirs = lax.ppermute(folded, "c", SWAP)
    below = lax.ppermute(theirs, "y", UP)
    above = lax.ppermute(theirs, "y", DOWN)
    far_a = lax.ppermute(below[:2], "y", UP)
    far_b = lax.ppermute(above[2:], "y", DOWN)

    rsector_other = lax.ppermute(right_sector, "c", SWAP)
    on_other = lax.ppermute(term_on, "c", SWAP)
    thin_other = lax.ppermute(thin, "c", SWAP)
    thin_late, _ = lax.optimization_barrier((thin, mine))
    slots = right_slots(
        ids, right_sector, rsector_other, term_on, on_other, thin_late, thin_other, right_env
    )
    arrived = lax.all_to_all(slots, COL, 0, 0, tiled=True)
    scalars = (ids, right_sector, rsector_other, left_sector, left_size, right_size)
    r_hi, r_lo, m_hi, m_lo, q1, stats = first_vector(scalars, arrived)

    pieces = [kept, theirs, below, above, far_a, far_b]
    left_arrived = lax.all_to_all(left_slots(ids, left_sector, pieces), COL, 0, 0, tiled=True)
    l_hi, l_lo, part = image_one(left_arrived, m_hi, m_lo)
    stacks = (r_hi, r_lo, l_hi, l_lo)
    part, q2, stats = image_two(scalars, part, lax.ppermute(part, "c", SWAP), q1, stats, stacks)
    sent = image_three(scalars, part, lax.ppermute(part, "c", SWAP), q1, q2, stats, stacks)

    got = lax.all_to_all(sent, COL, 0, 0, tiled=True)
    plane_stats = got[:, 16, :HALF]
    turned = [
        lax.ppermute(plane_stats, "y", [(i, (i + k) % 4) for i in range(4)]) for k in (1, 2, 3)
    ]
    back = lax.ppermute(lax.dynamic_slice_in_dim(got, (1 - core) * 8, 8), "c", SWAP)
    own_stats = jnp.concatenate([plane_stats] + turned)
    other_stats = lax.ppermute(own_stats, "c", SWAP)
    out, energy = finish(
        ids, left_sector, right_sector, left_size, right_size,
        own_stats, other_stats, thin, got, back,
    )
    return jnp.swapaxes(out, 1, 2), energy[0, 0]


def solution(mesh):
    fine = Mesh(mesh.devices.reshape(4, 2, 4, 4), ALL)
    row = ("y", "c")
    placed = (
        P(row, None, COL),
        P(row, COL, None, None),
        P(None, COL, None, None),
        P(),
        P(row),
        P(row, COL),
        P(),
        P(),
    )
    return jax.shard_map(
        local, mesh=fine, in_specs=placed, out_specs=(P(row, None, COL), P()), check_vma=False
    )
```

```python
import jax
import jax.numpy as jnp
from jax import lax
from jax.experimental import pallas as pl
from jax.experimental.pallas import tpu as pltpu
from jax.sharding import Mesh, PartitionSpec as P

ITERS = 2
TILE = 256
HALF = 128
TERMS = 16
LEFT_ROWS = 136
SLOT_ROWS = 152
LEFT_BYTES = 4_000_000
COL = ("x", "z")
ALL = ("y", "c", "x", "z")
SWAP = [(0, 1), (1, 0)]
UP = [(i, (i + 1) % 4) for i in range(4)]
DOWN = [(i, (i - 1) % 4) for i in range(4)]
f32 = jnp.float32
bf16 = jnp.bfloat16


def params(mib):
    return pltpu.CompilerParams(vmem_limit_bytes=mib * 1024 * 1024)


def hbm():
    return pl.BlockSpec(memory_space=pltpu.HBM)


def in_hbm(x):
    return pltpu.with_memory_space_constraint(x, pltpu.HBM)


def smem():
    return pl.BlockSpec(memory_space=pltpu.SMEM)


def cost(flops, nbytes):
    return pl.CostEstimate(flops=flops, transcendentals=0, bytes_accessed=nbytes)


def vmem():
    return pl.BlockSpec(memory_space=pltpu.VMEM)


def grids(rows, cols):
    i = lax.broadcasted_iota(jnp.int32, (rows, cols), 0)
    j = lax.broadcasted_iota(jnp.int32, (rows, cols), 1)
    return i, j


def fold_tile(tile):
    i, j = grids(HALF, HALF)
    a00 = tile[:HALF, :HALF]
    a11 = tile[HALF:, HALF:]
    fold = jnp.where(i >= j, a00, a11)
    diag = jnp.sum(jnp.where(i == j, a11, 0.0), axis=0, keepdims=True)
    return fold, tile[:HALF, HALF:], diag


def diag_rows(diag):
    wide = jnp.concatenate([diag, jnp.zeros((1, HALF), f32)], axis=1)
    return jnp.broadcast_to(wide, (8, TILE))


def unfold_tile(fold, corner, diag):
    i, j = grids(HALF, HALF)
    flip = fold.T
    a00 = jnp.where(i >= j, fold, flip)
    a11 = jnp.where(i == j, diag, jnp.where(i < j, fold, flip))
    top = jnp.concatenate([a00, corner], axis=1)
    low = jnp.concatenate([corner.T, a11], axis=1)
    return jnp.concatenate([top, low], axis=0)


def split(x):
    hi = x.astype(bf16)
    return hi, (x - hi.astype(f32)).astype(bf16)


def dot3(a_hi, a_lo, b_hi, b_lo):
    def dot(a, b):
        return jnp.dot(a, b, preferred_element_type=f32)

    return dot(a_hi, b_hi) + (dot(a_hi, b_lo) + dot(a_lo, b_hi))


def total(x):
    return jnp.sum(jnp.sum(x, axis=0, keepdims=True), axis=1, keepdims=True)


def inverse(norm):
    good = norm > 0.0
    return jnp.where(good, 1.0 / jnp.where(good, norm, 1.0), 0.0)


def put(stats, lane, value):
    _, j = grids(8, HALF)
    return jnp.where(j == lane, value, stats)


def put_folded(dst, at, row, tile):
    fold, corner, diag = fold_tile(tile)
    dst[at, row : row + HALF, :HALF] = fold
    dst[at, row : row + HALF, HALF:] = corner
    dst[at, row + HALF : row + HALF + 8, :] = diag_rows(diag)


def fold_left_body(term, src, dst, tiles, folded, sem_in, sem_out):
    def fetch(n):
        return pltpu.make_async_copy(src.at[n, term[0]], tiles.at[n], sem_in.at[n])

    def store(n):
        return pltpu.make_async_copy(folded.at[n], dst.at[n], sem_out.at[n])

    for n in range(4):
        fetch(n).start()
    for n in range(4):
        fetch(n).wait()
        put_folded(folded, n, 0, tiles[n])
        store(n).start()
    for n in range(4):
        store(n).wait()


def fold_left(term, left_env):
    return pl.pallas_call(
        fold_left_body,
        in_specs=[smem(), hbm()],
        out_specs=hbm(),
        out_shape=pltpu.HBM((4, LEFT_ROWS, TILE), f32),
        scratch_shapes=[
            pltpu.VMEM((4, TILE, TILE), f32),
            pltpu.VMEM((4, LEFT_ROWS, TILE), f32),
            pltpu.SemaphoreType.DMA((4,)),
            pltpu.SemaphoreType.DMA((4,)),
        ],
        compiler_params=params(4),
        cost_estimate=cost(1_000_000, 4_000_000),
        name="fold_left",
    )(term.reshape(1), in_hbm(left_env))


def sector_of(ids, rsector, rsector_other, slot):
    return jnp.where(slot // 8 == ids[1], rsector[slot % 8], rsector_other[slot % 8])


def right_slots_body(
    ids, rsector, rsector_other, on, on_other, thin, thin_other, right_env,
    out, right, dst, sem_in, sem_out,
):
    def fetch(sector):
        return pltpu.make_async_copy(
            right_env.at[sector, ids[1]], right.at[sector], sem_in.at[sector]
        )

    def store(slot):
        return pltpu.make_async_copy(dst.at[slot], out.at[slot], sem_out.at[slot])

    for sector in range(8):
        fetch(sector).start()
    for slot in range(TERMS):
        here = slot // 8 == ids[1]
        dst[slot, :16, :] = jnp.where(here, thin[slot % 8], thin_other[slot % 8])
    for sector in range(8):
        fetch(sector).wait()

    def one(slot, carry):
        here = slot // 8 == ids[1]
        weight = jnp.where(here, on[slot % 8, ids[1]], on_other[slot % 8, ids[1]]).astype(f32)
        put_folded(dst, slot, 16, right[sector_of(ids, rsector, rsector_other, slot)] * weight)
        store(slot).start()
        return carry

    def finished(slot, carry):
        store(slot).wait()
        return carry

    lax.fori_loop(0, TERMS, one, 0)
    lax.fori_loop(0, TERMS, finished, 0)


def right_slots(ids, rsector, rsector_other, on, on_other, thin, thin_other, right_env):
    slots = (TERMS, SLOT_ROWS, TILE)
    return pl.pallas_call(
        right_slots_body,
        in_specs=[smem()] * 5 + [vmem()] * 2 + [hbm()],
        out_specs=hbm(),
        out_shape=pltpu.HBM(slots, f32),
        scratch_shapes=[
            pltpu.VMEM((8, TILE, TILE), f32),
            pltpu.VMEM(slots, f32),
            pltpu.SemaphoreType.DMA((8,)),
            pltpu.SemaphoreType.DMA((TERMS,)),
        ],
        compiler_params=params(10),
        cost_estimate=cost(4_000_000, 10_000_000),
        name="right_slots",
    )(ids, rsector, rsector_other, on, on_other, thin, thin_other, in_hbm(right_env))


def left_slots_body(ids, left_sector, *refs):
    mine, theirs = refs[:2]
    above, far, below = refs[2:4], refs[4:6], refs[6:8]
    out, dst, sem_in, sem_out = refs[8:]

    def fetch(src, slot):
        return pltpu.make_async_copy(src, dst.at[slot], sem_in.at[slot])

    def store(slot):
        return pltpu.make_async_copy(dst.at[slot], out.at[slot], sem_out.at[slot])

    def start(slot, carry):
        sector = left_sector[ids[0] * 16 + slot]
        home = sector // 4
        tile = sector % 4
        away = (home // 2 - ids[0] + 4) % 4
        same = home % 2 == ids[1]
        cases = [(same, mine, tile), (~same, theirs, tile)]
        cases = [(case & (away == 0), src, at) for case, src, at in cases]
        for n, half in ((0, same), (1, ~same)):
            cases.append((half & (away == 1), above[n], tile))
            cases.append((half & (away == 2), far[n], tile))
            cases.append((half & (away == 3), below[n], tile))
        for case, src, at in cases:

            @pl.when(case)
            def _():
                fetch(src.at[at], slot).start()

        return carry

    def forward(slot, carry):
        fetch(mine.at[0], slot).wait()
        store(slot).start()
        return carry

    def finished(slot, carry):
        store(slot).wait()
        return carry

    lax.fori_loop(0, TERMS, start, 0)
    lax.fori_loop(0, TERMS, forward, 0)
    lax.fori_loop(0, TERMS, finished, 0)


def left_slots(ids, left_sector, pieces):
    slots = (TERMS, LEFT_ROWS, TILE)
    return pl.pallas_call(
        left_slots_body,
        in_specs=[smem(), smem()] + [hbm()] * 8,
        out_specs=hbm(),
        out_shape=pltpu.HBM(slots, f32),
        scratch_shapes=[
            pltpu.VMEM(slots, f32),
            pltpu.SemaphoreType.DMA((TERMS,)),
            pltpu.SemaphoreType.DMA((TERMS,)),
        ],
        compiler_params=params(6),
        cost_estimate=cost(0, LEFT_BYTES),
        name="left_slots",
    )(ids, left_sector, *[in_hbm(x) for x in pieces])


def live_sizes(ids, rsector, rsector_other, left_sector, left_size, right_size):
    live_left = left_size[left_sector[ids[0] * 16 + ids[2]]]
    live_right = right_size[sector_of(ids, rsector, rsector_other, ids[2])]
    return live_right, live_left


def mask_of(live_right, live_left):
    i, j = grids(TILE, TILE)
    return (i < live_right) & (j < live_left)


def first_body(
    ids, rsector, rsector_other, sector, lsize, rsize, slots,
    r_hi, r_lo, m_hi, m_lo, q1, stats, arrived, sem,
):
    live_right, live_left = live_sizes(ids, rsector, rsector_other, sector, lsize, rsize)

    def fetch(n):
        return pltpu.make_async_copy(slots.at[n], arrived.at[n], sem.at[n])

    for n in range(TERMS):
        fetch(n).start()
    for n in range(TERMS):
        fetch(n).wait()
        full = unfold_tile(
            arrived[n, 16 : 16 + HALF, :HALF],
            arrived[n, 16 : 16 + HALF, HALF:],
            arrived[n, 16 + HALF : 17 + HALF, :HALF],
        )
        hi, lo = split(full)
        r_hi[n * TILE : (n + 1) * TILE, :] = hi
        r_lo[n * TILE : (n + 1) * TILE, :] = lo
    block = jnp.concatenate([arrived[n, :16, :] for n in range(TERMS)], axis=0)
    start = jnp.where(mask_of(live_right, live_left), block, 0.0)
    norm = jnp.sqrt(total(start * start))
    vec = start * inverse(norm)
    q1[...] = vec
    stats[...] = put(jnp.zeros((8, HALF), f32), 0, norm)
    q_hi, q_lo = split(vec)
    for n in range(TERMS):
        rows = pl.ds(n * TILE, TILE)
        hi, lo = split(dot3(r_hi[rows, :], r_lo[rows, :], q_hi, q_lo))
        m_hi[:, rows] = hi
        m_lo[:, rows] = lo


def first_vector(scalars, slots):
    return pl.pallas_call(
        first_body,
        in_specs=[smem()] * 6 + [hbm()],
        out_specs=[vmem()] * 6,
        out_shape=[
            jax.ShapeDtypeStruct((TERMS * TILE, TILE), bf16),
            jax.ShapeDtypeStruct((TERMS * TILE, TILE), bf16),
            jax.ShapeDtypeStruct((TILE, TERMS * TILE), bf16),
            jax.ShapeDtypeStruct((TILE, TERMS * TILE), bf16),
            jax.ShapeDtypeStruct((TILE, TILE), f32),
            jax.ShapeDtypeStruct((8, HALF), f32),
        ],
        scratch_shapes=[
            pltpu.VMEM((TERMS, SLOT_ROWS, TILE), f32),
            pltpu.SemaphoreType.DMA((TERMS,)),
        ],
        compiler_params=params(10),
        cost_estimate=cost(1_700_000_000, 12_000_000),
        name="first_vector",
    )(*scalars, in_hbm(slots))


def image_one_body(arrived, m_hi, m_lo, l_hi, l_lo, part, here, sem):
    chunk = TERMS // 4

    def fetch(p, c):
        cols = pl.ds(c * chunk * TILE, chunk * TILE)
        src = (m_hi, m_lo)[p]
        return pltpu.make_async_copy(src.at[:, cols], here.at[p, :, cols], sem.at[p, c])

    for c in range(4):
        for p in range(2):
            fetch(p, c).start()
    for n in range(TERMS):
        full = unfold_tile(
            arrived[n, :HALF, :HALF], arrived[n, :HALF, HALF:], arrived[n, HALF : HALF + 1, :HALF]
        )
        hi, lo = split(full)
        l_hi[n * TILE : (n + 1) * TILE, :] = hi
        l_lo[n * TILE : (n + 1) * TILE, :] = lo
    acc = jnp.zeros((TILE, TILE), f32)
    for c in range(4):
        for p in range(2):
            fetch(p, c).wait()
        cols = pl.ds(c * chunk * TILE, chunk * TILE)
        acc = acc + dot3(here[0, :, cols], here[1, :, cols], l_hi[cols, :], l_lo[cols, :])
    part[...] = acc


def image_one(arrived, m_hi, m_lo):
    return pl.pallas_call(
        image_one_body,
        in_specs=[vmem(), hbm(), hbm()],
        out_specs=[vmem()] * 3,
        out_shape=[
            jax.ShapeDtypeStruct((TERMS * TILE, TILE), bf16),
            jax.ShapeDtypeStruct((TERMS * TILE, TILE), bf16),
            jax.ShapeDtypeStruct((TILE, TILE), f32),
        ],
        scratch_shapes=[
            pltpu.VMEM((2, TILE, TERMS * TILE), bf16),
            pltpu.SemaphoreType.DMA((2, 4)),
        ],
        compiler_params=params(10),
        cost_estimate=cost(1_700_000_000, 10_000_000),
        name="image_one",
    )(arrived, in_hbm(m_hi), in_hbm(m_lo))


def lanczos(image, last, before, beta):
    alpha = total(last * image)
    rest = image - alpha * last
    if before is not None:
        rest = rest - beta * before
    again = rest - total(last * rest) * last
    if before is not None:
        again = again - total(before * rest) * before
    norm = jnp.sqrt(total(again * again))
    return alpha, norm, again * inverse(norm)


def half_image(vec, r_hi, r_lo, l_hi, l_lo):
    q_hi, q_lo = split(vec)
    acc = jnp.zeros((TILE, TILE), f32)
    for n in range(TERMS):
        rows = pl.ds(n * TILE, TILE)
        hi, lo = split(dot3(r_hi[rows, :], r_lo[rows, :], q_hi, q_lo))
        acc = acc + dot3(hi, lo, l_hi[rows, :], l_lo[rows, :])
    return acc


def image_two_body(
    ids, rsector, rsector_other, sector, lsize, rsize,
    part_a, part_b, q1, stats_in, r_hi, r_lo, l_hi, l_lo,
    part, q2, stats,
):
    mask = mask_of(*live_sizes(ids, rsector, rsector_other, sector, lsize, rsize))
    image = jnp.where(mask, part_a[...] + part_b[...], 0.0)
    alpha, norm, vec = lanczos(image, q1[...], None, None)
    q2[...] = vec
    stats[...] = put(put(stats_in[...], 1, alpha), 2, norm)
    part[...] = half_image(vec, r_hi, r_lo, l_hi, l_lo)


def image_two(scalars, part, part_other, q1, stats, stacks):
    return pl.pallas_call(
        image_two_body,
        in_specs=[smem()] * 6 + [vmem()] * 8,
        out_specs=[vmem()] * 3,
        out_shape=[
            jax.ShapeDtypeStruct((TILE, TILE), f32),
            jax.ShapeDtypeStruct((TILE, TILE), f32),
            jax.ShapeDtypeStruct((8, HALF), f32),
        ],
        compiler_params=params(6),
        cost_estimate=cost(3_300_000_000, 9_000_000),
        name="image_two",
    )(*scalars, part, part_other, q1, stats, *stacks)


def image_three_body(
    ids, rsector, rsector_other, sector, lsize, rsize,
    part_a, part_b, q1, q2, stats_in, r_hi, r_lo, l_hi, l_lo, slots,
):
    mask = mask_of(*live_sizes(ids, rsector, rsector_other, sector, lsize, rsize))
    image = jnp.where(mask, part_a[...] + part_b[...], 0.0)
    i, j = grids(8, HALF)
    beta = total(jnp.where((j == 2) & (i == 0), stats_in[...], 0.0))
    alpha, norm, vec = lanczos(image, q2[...], q1[...], beta)
    pick = jnp.where(ids[1] == 0, q2[...], vec)
    for n in range(16):
        slots[n, :16, :] = pick[16 * n : 16 * n + 16]
    stats = put(put(stats_in[...], 3, alpha), 4, norm)
    alpha = total(vec * half_image(vec, r_hi, r_lo, l_hi, l_lo))
    stats = put(stats, 5, alpha)
    wide = jnp.concatenate([stats, jnp.zeros((8, HALF), f32)], axis=1)
    for n in range(16):
        slots[n, 16:24, :] = wide


def image_three(scalars, part, part_other, q1, q2, stats, stacks):
    return pl.pallas_call(
        image_three_body,
        in_specs=[smem()] * 6 + [vmem()] * 9,
        out_specs=vmem(),
        out_shape=jax.ShapeDtypeStruct((16, 24, TILE), f32),
        compiler_params=params(6),
        cost_estimate=cost(3_300_000_000, 9_000_000),
        name="image_three",
    )(*scalars, part, part_other, q1, q2, stats, *stacks)


def ritz_pair(norm, a1, b1, a2, b2, a3):
    def apply(x):
        return [a1 * x[0] + b1 * x[1], b1 * x[0] + a2 * x[1] + b2 * x[2], b2 * x[1] + a3 * x[2]]

    def dot(x, y):
        return jnp.sum(x[0] * y[0] + x[1] * y[1] + x[2] * y[2], axis=1, keepdims=True)

    zero = jnp.zeros_like(norm)
    start = [norm, zero, zero]
    image = apply(start)
    norm_sq = dot(start, start)
    correlation = dot(start, image)
    inv_norm = 1.0 / jnp.sqrt(norm_sq)
    basis = [x * inv_norm for x in start]
    applied = [x * inv_norm for x in image]
    ritz = correlation / norm_sq
    for _ in range(ITERS):
        residual = [x - ritz * y for x, y in zip(applied, basis)]
        res_sq = dot(residual, residual)
        length = jnp.sqrt(res_sq)
        fresh = [x / length for x in residual]
        fresh_applied = apply(fresh)
        curvature = dot(fresh, fresh_applied)
        half_gap = 0.5 * (ritz - curvature)
        root = jnp.sqrt(half_gap * half_gap + res_sq)
        lowest = 0.5 * (ritz + curvature) - root
        first = curvature - lowest
        pair = jnp.sqrt(first * first + res_sq)
        basis = [(first * x - length * y) / pair for x, y in zip(basis, fresh)]
        applied = [(first * x - length * y) / pair for x, y in zip(applied, fresh_applied)]
        ritz = lowest
    return basis, ritz


def finish_body(
    ids, sector, rsector, lsize, rsize, own_stats, other_stats, thin, got, back,
    out, energy, coef,
):
    _, lane = grids(64, HALF)
    stats = own_stats[...] + jnp.where(lane == 5, other_stats[...], 0.0)
    flip = jnp.concatenate([stats, jnp.zeros((64, HALF), f32)], axis=0).T
    norm, a1, b1, a2, b2, a3 = [flip[m : m + 1, :] for m in range(6)]
    basis, ritz = ritz_pair(norm, a1, b1, a2, b2, a3)
    energy[0, 0] = jnp.sum(ritz)
    scale = jnp.sqrt(jnp.full((1, HALF), 64 * TILE * TILE, f32))
    i, _ = grids(HALF, HALF)
    c1 = basis[0] * inverse(norm) * scale
    c2 = basis[1] * scale
    c3 = basis[2] * scale
    coef[...] = jnp.where(i == 0, c1, jnp.where(i == 1, c2, jnp.where(i == 2, c3, 0.0))).T
    core = ids[1]
    own = coef[pl.ds(pl.multiple_of(core * 8, 8), 8), :]
    jcol, irow = grids(16, TILE)
    for b in range(8):
        live_left = lsize[sector[ids[0] * 16 + core * 8 + b]]
        live_right = rsize[rsector[b]]
        live = (jcol + ids[2] * 16 < live_right) & (irow < live_left)
        keep = got[core * 8 + b, :16, :]
        recv = back[b, :16, :]
        second = jnp.where(core == 0, keep, recv)
        third = jnp.where(core == 0, recv, keep)
        out[b] = (
            own[b : b + 1, 0:1] * jnp.where(live, thin[b], 0.0)
            + own[b : b + 1, 1:2] * second
            + own[b : b + 1, 2:3] * third
        )


def finish(ids, sector, rsector, lsize, rsize, own_stats, other_stats, thin, got, back):
    return pl.pallas_call(
        finish_body,
        in_specs=[smem()] * 5 + [vmem()] * 5,
        out_specs=[vmem(), smem()],
        out_shape=[
            jax.ShapeDtypeStruct(thin.shape, f32),
            jax.ShapeDtypeStruct((1, 1), f32),
        ],
        scratch_shapes=[pltpu.VMEM((HALF, HALF), f32)],
        compiler_params=params(4),
        name="finish",
    )(ids, sector, rsector, lsize, rsize, own_stats, other_stats, thin, got, back)


def local(theta, left_env, right_env, left_sector, right_sector, term_on, left_size, right_size):
    plane = lax.axis_index("y").astype(jnp.int32)
    core = lax.axis_index("c").astype(jnp.int32)
    place = lax.axis_index(COL).astype(jnp.int32)
    ids = jnp.stack([plane, core, place])
    thin = jnp.swapaxes(theta, 1, 2)

    mine = fold_left(core, left_env)
    other_core, mine = lax.optimization_barrier((1 - core, mine))
    folded = fold_left(other_core, left_env)
    theirs = lax.ppermute(folded, "c", SWAP)
    below = [lax.ppermute(mine, "y", UP)]
    above = [lax.ppermute(mine, "y", DOWN)]

    rsector_other = lax.ppermute(right_sector, "c", SWAP)
    on_other = lax.ppermute(term_on, "c", SWAP)
    thin_other = lax.ppermute(thin, "c", SWAP)
    thin_late, _ = lax.optimization_barrier((thin, folded))
    slots = right_slots(
        ids, right_sector, rsector_other, term_on, on_other, thin_late, thin_other, right_env
    )
    slots, theirs, first_below, first_above = lax.optimization_barrier(
        (slots, theirs, below[0], above[0])
    )
    arrived = lax.all_to_all(slots, COL, 0, 0, tiled=True)
    scalars = (ids, right_sector, rsector_other, left_sector, left_size, right_size)
    r_hi, r_lo, m_hi, m_lo, q1, stats = first_vector(scalars, arrived)

    below = [first_below, lax.ppermute(theirs, "y", UP)]
    above = [first_above, lax.ppermute(theirs, "y", DOWN)]
    far = [lax.ppermute(below[0], "y", UP), lax.ppermute(above[1], "y", DOWN)]
    pieces = [mine, theirs] + above + far + below
    left_arrived = lax.all_to_all(left_slots(ids, left_sector, pieces), COL, 0, 0, tiled=True)
    l_hi, l_lo, part = image_one(left_arrived, m_hi, m_lo)
    stacks = (r_hi, r_lo, l_hi, l_lo)
    part, q2, stats = image_two(scalars, part, lax.ppermute(part, "c", SWAP), q1, stats, stacks)
    sent = image_three(scalars, part, lax.ppermute(part, "c", SWAP), q1, q2, stats, stacks)

    got = lax.all_to_all(sent, COL, 0, 0, tiled=True)
    plane_stats = got[:, 16, :HALF]
    turned = [
        lax.ppermute(plane_stats, "y", [(i, (i + k) % 4) for i in range(4)]) for k in (1, 2, 3)
    ]
    back = lax.ppermute(lax.dynamic_slice_in_dim(got, (1 - core) * 8, 8), "c", SWAP)
    own_stats = jnp.concatenate([plane_stats] + turned)
    other_stats = lax.ppermute(own_stats, "c", SWAP)
    out, energy = finish(
        ids, left_sector, right_sector, left_size, right_size,
        own_stats, other_stats, thin, got, back,
    )
    return jnp.swapaxes(out, 1, 2), energy[0, 0]


def solution(mesh):
    fine = Mesh(mesh.devices.reshape(4, 2, 4, 4), ALL)
    row = ("y", "c")
    placed = (
        P(row, None, COL),
        P(row, COL, None, None),
        P(None, COL, None, None),
        P(),
        P(row),
        P(row, COL),
        P(),
        P(),
    )
    return jax.shard_map(
        local, mesh=fine, in_specs=placed, out_specs=(P(row, None, COL), P()), check_vma=False
    )
```

```python
import jax
import jax.numpy as jnp
from jax import lax
from jax.experimental import pallas as pl
from jax.experimental.pallas import tpu as pltpu
from jax.sharding import Mesh, PartitionSpec as P

ITERS = 2
TILE = 256
HALF = 128
TERMS = 16
LEFT_ROWS = 136
SLOT_ROWS = 152
COL = ("x", "z")
ALL = ("y", "c", "x", "z")
SWAP = [(0, 1), (1, 0)]
UP = [(i, (i + 1) % 4) for i in range(4)]
DOWN = [(i, (i - 1) % 4) for i in range(4)]
f32 = jnp.float32
bf16 = jnp.bfloat16


def params(mib):
    return pltpu.CompilerParams(vmem_limit_bytes=mib * 1024 * 1024)


def hbm():
    return pl.BlockSpec(memory_space=pltpu.HBM)


def in_hbm(x):
    return pltpu.with_memory_space_constraint(x, pltpu.HBM)


def smem():
    return pl.BlockSpec(memory_space=pltpu.SMEM)


def cost(flops, nbytes):
    return pl.CostEstimate(flops=flops, transcendentals=0, bytes_accessed=nbytes)


def vmem():
    return pl.BlockSpec(memory_space=pltpu.VMEM)


def grids(rows, cols):
    i = lax.broadcasted_iota(jnp.int32, (rows, cols), 0)
    j = lax.broadcasted_iota(jnp.int32, (rows, cols), 1)
    return i, j


def fold_tile(tile):
    i, j = grids(HALF, HALF)
    a00 = tile[:HALF, :HALF]
    a11 = tile[HALF:, HALF:]
    fold = jnp.where(i >= j, a00, a11)
    diag = jnp.sum(jnp.where(i == j, a11, 0.0), axis=0, keepdims=True)
    return fold, tile[:HALF, HALF:], diag


def diag_rows(diag):
    wide = jnp.concatenate([diag, jnp.zeros((1, HALF), f32)], axis=1)
    return jnp.broadcast_to(wide, (8, TILE))


def unfold_tile(fold, corner, diag):
    i, j = grids(HALF, HALF)
    flip = fold.T
    a00 = jnp.where(i >= j, fold, flip)
    a11 = jnp.where(i == j, diag, jnp.where(i < j, fold, flip))
    top = jnp.concatenate([a00, corner], axis=1)
    low = jnp.concatenate([corner.T, a11], axis=1)
    return jnp.concatenate([top, low], axis=0)


def split(x):
    hi = x.astype(bf16)
    return hi, (x - hi.astype(f32)).astype(bf16)


def dot3(a_hi, a_lo, b_hi, b_lo):
    def dot(a, b):
        return jnp.dot(a, b, preferred_element_type=f32)

    return dot(a_hi, b_hi) + (dot(a_hi, b_lo) + dot(a_lo, b_hi))


def total(x):
    return jnp.sum(jnp.sum(x, axis=0, keepdims=True), axis=1, keepdims=True)


def inverse(norm):
    good = norm > 0.0
    return jnp.where(good, 1.0 / jnp.where(good, norm, 1.0), 0.0)


def put(stats, lane, value):
    _, j = grids(8, HALF)
    return jnp.where(j == lane, value, stats)


def put_folded(dst, at, row, tile):
    fold, corner, diag = fold_tile(tile)
    dst[at, row : row + HALF, :HALF] = fold
    dst[at, row : row + HALF, HALF:] = corner
    dst[at, row + HALF : row + HALF + 8, :] = diag_rows(diag)


def fold_left_body(ids, src, keep, give, tiles, folded, sem_in, sem_out):
    def fetch(t, n):
        term = ids[1] if t else 1 - ids[1]
        at = 4 * t + n
        return pltpu.make_async_copy(src.at[n, term], tiles.at[at], sem_in.at[at])

    def store(t, n):
        at = 4 * t + n
        dst = keep if t else give
        return pltpu.make_async_copy(folded.at[at], dst.at[n], sem_out.at[at])

    order = [(t, n) for t in range(2) for n in range(4)]
    for t, n in order:
        fetch(t, n).start()
    for t, n in order:
        fetch(t, n).wait()
        put_folded(folded, 4 * t + n, 0, tiles[4 * t + n])
        store(t, n).start()
    for t, n in order:
        store(t, n).wait()


def fold_left(ids, left_env):
    return pl.pallas_call(
        fold_left_body,
        in_specs=[smem(), hbm()],
        out_specs=[hbm(), hbm()],
        out_shape=[pltpu.HBM((4, LEFT_ROWS, TILE), f32)] * 2,
        scratch_shapes=[
            pltpu.VMEM((8, TILE, TILE), f32),
            pltpu.VMEM((8, LEFT_ROWS, TILE), f32),
            pltpu.SemaphoreType.DMA((8,)),
            pltpu.SemaphoreType.DMA((8,)),
        ],
        compiler_params=params(8),
        cost_estimate=cost(1_000_000, 4_000_000),
        name="fold_left",
    )(ids, in_hbm(left_env))


def sector_of(ids, rsector, rsector_other, slot):
    return jnp.where(slot // 8 == ids[1], rsector[slot % 8], rsector_other[slot % 8])


def right_slots_body(
    ids, rsector, rsector_other, on, on_other, thin, thin_other, right_env,
    out, right, dst, sem_in, sem_out,
):
    def fetch(sector):
        return pltpu.make_async_copy(
            right_env.at[sector, ids[1]], right.at[sector], sem_in.at[sector]
        )

    def store(slot):
        return pltpu.make_async_copy(dst.at[slot], out.at[slot], sem_out.at[slot])

    for sector in range(8):
        fetch(sector).start()
    for slot in range(TERMS):
        here = slot // 8 == ids[1]
        dst[slot, :16, :] = jnp.where(here, thin[slot % 8], thin_other[slot % 8])
    for sector in range(8):
        fetch(sector).wait()

    def one(slot, carry):
        here = slot // 8 == ids[1]
        weight = jnp.where(here, on[slot % 8, ids[1]], on_other[slot % 8, ids[1]]).astype(f32)
        put_folded(dst, slot, 16, right[sector_of(ids, rsector, rsector_other, slot)] * weight)
        store(slot).start()
        return carry

    def finished(slot, carry):
        store(slot).wait()
        return carry

    lax.fori_loop(0, TERMS, one, 0)
    lax.fori_loop(0, TERMS, finished, 0)


def right_slots(ids, rsector, rsector_other, on, on_other, thin, thin_other, right_env):
    slots = (TERMS, SLOT_ROWS, TILE)
    return pl.pallas_call(
        right_slots_body,
        in_specs=[smem()] * 5 + [vmem()] * 2 + [hbm()],
        out_specs=hbm(),
        out_shape=pltpu.HBM(slots, f32),
        scratch_shapes=[
            pltpu.VMEM((8, TILE, TILE), f32),
            pltpu.VMEM(slots, f32),
            pltpu.SemaphoreType.DMA((8,)),
            pltpu.SemaphoreType.DMA((TERMS,)),
        ],
        compiler_params=params(10),
        cost_estimate=cost(4_000_000, 10_000_000),
        name="right_slots",
    )(ids, rsector, rsector_other, on, on_other, thin, thin_other, in_hbm(right_env))


def left_slots_body(ids, left_sector, *refs):
    mine, theirs = refs[:2]
    above, far, below = refs[2:4], refs[4:6], refs[6:8]
    out, dst, sem_in, sem_out = refs[8:]

    def fetch(src, slot):
        return pltpu.make_async_copy(src, dst.at[slot], sem_in.at[slot])

    def store(slot):
        return pltpu.make_async_copy(dst.at[slot], out.at[slot], sem_out.at[slot])

    def start(slot, carry):
        sector = left_sector[ids[0] * 16 + slot]
        home = sector // 4
        tile = sector % 4
        away = (home // 2 - ids[0] + 4) % 4
        same = home % 2 == ids[1]
        cases = [(same, mine, tile), (~same, theirs, tile)]
        cases = [(case & (away == 0), src, at) for case, src, at in cases]
        for n, half in ((0, same), (1, ~same)):
            cases.append((half & (away == 1), above[n], tile))
            cases.append((half & (away == 2), far[n], tile))
            cases.append((half & (away == 3), below[n], tile))
        for case, src, at in cases:

            @pl.when(case)
            def _():
                fetch(src.at[at], slot).start()

        return carry

    def forward(slot, carry):
        fetch(mine.at[0], slot).wait()
        store(slot).start()
        return carry

    def finished(slot, carry):
        store(slot).wait()
        return carry

    lax.fori_loop(0, TERMS, start, 0)
    lax.fori_loop(0, TERMS, forward, 0)
    lax.fori_loop(0, TERMS, finished, 0)


def left_slots(ids, left_sector, pieces):
    slots = (TERMS, LEFT_ROWS, TILE)
    return pl.pallas_call(
        left_slots_body,
        in_specs=[smem(), smem()] + [hbm()] * 8,
        out_specs=hbm(),
        out_shape=pltpu.HBM(slots, f32),
        scratch_shapes=[
            pltpu.VMEM(slots, f32),
            pltpu.SemaphoreType.DMA((TERMS,)),
            pltpu.SemaphoreType.DMA((TERMS,)),
        ],
        compiler_params=params(6),
        cost_estimate=cost(15_000_000_000, 4_000_000),
        name="left_slots",
    )(ids, left_sector, *[in_hbm(x) for x in pieces])


def live_sizes(ids, rsector, rsector_other, left_sector, left_size, right_size):
    live_left = left_size[left_sector[ids[0] * 16 + ids[2]]]
    live_right = right_size[sector_of(ids, rsector, rsector_other, ids[2])]
    return live_right, live_left


def mask_of(live_right, live_left):
    i, j = grids(TILE, TILE)
    return (i < live_right) & (j < live_left)


def first_body(
    ids, rsector, rsector_other, sector, lsize, rsize, slots,
    r_hi, r_lo, m_hi, m_lo, q1, stats, arrived, sem,
):
    live_right, live_left = live_sizes(ids, rsector, rsector_other, sector, lsize, rsize)

    def fetch(n):
        return pltpu.make_async_copy(slots.at[n], arrived.at[n], sem.at[n])

    for n in range(TERMS):
        fetch(n).start()
    for n in range(TERMS):
        fetch(n).wait()
        full = unfold_tile(
            arrived[n, 16 : 16 + HALF, :HALF],
            arrived[n, 16 : 16 + HALF, HALF:],
            arrived[n, 16 + HALF : 17 + HALF, :HALF],
        )
        hi, lo = split(full)
        r_hi[n * TILE : (n + 1) * TILE, :] = hi
        r_lo[n * TILE : (n + 1) * TILE, :] = lo
    block = jnp.concatenate([arrived[n, :16, :] for n in range(TERMS)], axis=0)
    start = jnp.where(mask_of(live_right, live_left), block, 0.0)
    norm = jnp.sqrt(total(start * start))
    vec = start * inverse(norm)
    q1[...] = vec
    stats[...] = put(jnp.zeros((8, HALF), f32), 0, norm)
    q_hi, q_lo = split(vec)
    for n in range(TERMS):
        rows = pl.ds(n * TILE, TILE)
        hi, lo = split(dot3(r_hi[rows, :], r_lo[rows, :], q_hi, q_lo))
        m_hi[:, rows] = hi
        m_lo[:, rows] = lo


def first_vector(scalars, slots):
    return pl.pallas_call(
        first_body,
        in_specs=[smem()] * 6 + [hbm()],
        out_specs=[vmem()] * 6,
        out_shape=[
            jax.ShapeDtypeStruct((TERMS * TILE, TILE), bf16),
            jax.ShapeDtypeStruct((TERMS * TILE, TILE), bf16),
            jax.ShapeDtypeStruct((TILE, TERMS * TILE), bf16),
            jax.ShapeDtypeStruct((TILE, TERMS * TILE), bf16),
            jax.ShapeDtypeStruct((TILE, TILE), f32),
            jax.ShapeDtypeStruct((8, HALF), f32),
        ],
        scratch_shapes=[
            pltpu.VMEM((TERMS, SLOT_ROWS, TILE), f32),
            pltpu.SemaphoreType.DMA((TERMS,)),
        ],
        compiler_params=params(10),
        cost_estimate=cost(1_700_000_000, 12_000_000),
        name="first_vector",
    )(*scalars, in_hbm(slots))


def image_one_body(arrived, m_hi, m_lo, l_hi, l_lo, part, here, sem):
    chunk = TERMS // 4

    def fetch(p, c):
        cols = pl.ds(c * chunk * TILE, chunk * TILE)
        src = (m_hi, m_lo)[p]
        return pltpu.make_async_copy(src.at[:, cols], here.at[p, :, cols], sem.at[p, c])

    for c in range(4):
        for p in range(2):
            fetch(p, c).start()
    for n in range(TERMS):
        full = unfold_tile(
            arrived[n, :HALF, :HALF], arrived[n, :HALF, HALF:], arrived[n, HALF : HALF + 1, :HALF]
        )
        hi, lo = split(full)
        l_hi[n * TILE : (n + 1) * TILE, :] = hi
        l_lo[n * TILE : (n + 1) * TILE, :] = lo
    acc = jnp.zeros((TILE, TILE), f32)
    for c in range(4):
        for p in range(2):
            fetch(p, c).wait()
        cols = pl.ds(c * chunk * TILE, chunk * TILE)
        acc = acc + dot3(here[0, :, cols], here[1, :, cols], l_hi[cols, :], l_lo[cols, :])
    part[...] = acc


def image_one(arrived, m_hi, m_lo):
    return pl.pallas_call(
        image_one_body,
        in_specs=[vmem(), hbm(), hbm()],
        out_specs=[vmem()] * 3,
        out_shape=[
            jax.ShapeDtypeStruct((TERMS * TILE, TILE), bf16),
            jax.ShapeDtypeStruct((TERMS * TILE, TILE), bf16),
            jax.ShapeDtypeStruct((TILE, TILE), f32),
        ],
        scratch_shapes=[
            pltpu.VMEM((2, TILE, TERMS * TILE), bf16),
            pltpu.SemaphoreType.DMA((2, 4)),
        ],
        compiler_params=params(10),
        cost_estimate=cost(1_700_000_000, 10_000_000),
        name="image_one",
    )(arrived, in_hbm(m_hi), in_hbm(m_lo))


def lanczos(image, last, before, beta):
    alpha = total(last * image)
    rest = image - alpha * last
    if before is not None:
        rest = rest - beta * before
    again = rest - total(last * rest) * last
    if before is not None:
        again = again - total(before * rest) * before
    norm = jnp.sqrt(total(again * again))
    return alpha, norm, again * inverse(norm)


def half_image(vec, r_hi, r_lo, l_hi, l_lo):
    q_hi, q_lo = split(vec)
    acc = jnp.zeros((TILE, TILE), f32)
    for n in range(TERMS):
        rows = pl.ds(n * TILE, TILE)
        hi, lo = split(dot3(r_hi[rows, :], r_lo[rows, :], q_hi, q_lo))
        acc = acc + dot3(hi, lo, l_hi[rows, :], l_lo[rows, :])
    return acc


def image_two_body(
    ids, rsector, rsector_other, sector, lsize, rsize,
    part_a, part_b, q1, stats_in, r_hi, r_lo, l_hi, l_lo,
    part, q2, stats,
):
    mask = mask_of(*live_sizes(ids, rsector, rsector_other, sector, lsize, rsize))
    image = jnp.where(mask, part_a[...] + part_b[...], 0.0)
    alpha, norm, vec = lanczos(image, q1[...], None, None)
    q2[...] = vec
    stats[...] = put(put(stats_in[...], 1, alpha), 2, norm)
    part[...] = half_image(vec, r_hi, r_lo, l_hi, l_lo)


def image_two(scalars, part, part_other, q1, stats, stacks):
    return pl.pallas_call(
        image_two_body,
        in_specs=[smem()] * 6 + [vmem()] * 8,
        out_specs=[vmem()] * 3,
        out_shape=[
            jax.ShapeDtypeStruct((TILE, TILE), f32),
            jax.ShapeDtypeStruct((TILE, TILE), f32),
            jax.ShapeDtypeStruct((8, HALF), f32),
        ],
        compiler_params=params(6),
        cost_estimate=cost(3_300_000_000, 9_000_000),
        name="image_two",
    )(*scalars, part, part_other, q1, stats, *stacks)


def image_three_body(
    ids, rsector, rsector_other, sector, lsize, rsize,
    part_a, part_b, q1, q2, stats_in, r_hi, r_lo, l_hi, l_lo, slots,
):
    mask = mask_of(*live_sizes(ids, rsector, rsector_other, sector, lsize, rsize))
    image = jnp.where(mask, part_a[...] + part_b[...], 0.0)
    i, j = grids(8, HALF)
    beta = total(jnp.where((j == 2) & (i == 0), stats_in[...], 0.0))
    alpha, norm, vec = lanczos(image, q2[...], q1[...], beta)
    pick = jnp.where(ids[1] == 0, q2[...], vec)
    for n in range(16):
        slots[n, :16, :] = pick[16 * n : 16 * n + 16]
    stats = put(put(stats_in[...], 3, alpha), 4, norm)
    alpha = total(vec * half_image(vec, r_hi, r_lo, l_hi, l_lo))
    stats = put(stats, 5, alpha)
    wide = jnp.concatenate([stats, jnp.zeros((8, HALF), f32)], axis=1)
    for n in range(16):
        slots[n, 16:24, :] = wide


def image_three(scalars, part, part_other, q1, q2, stats, stacks):
    return pl.pallas_call(
        image_three_body,
        in_specs=[smem()] * 6 + [vmem()] * 9,
        out_specs=vmem(),
        out_shape=jax.ShapeDtypeStruct((16, 24, TILE), f32),
        compiler_params=params(6),
        cost_estimate=cost(3_300_000_000, 9_000_000),
        name="image_three",
    )(*scalars, part, part_other, q1, q2, stats, *stacks)


def ritz_pair(norm, a1, b1, a2, b2, a3):
    def apply(x):
        return [a1 * x[0] + b1 * x[1], b1 * x[0] + a2 * x[1] + b2 * x[2], b2 * x[1] + a3 * x[2]]

    def dot(x, y):
        return jnp.sum(x[0] * y[0] + x[1] * y[1] + x[2] * y[2], axis=1, keepdims=True)

    zero = jnp.zeros_like(norm)
    start = [norm, zero, zero]
    image = apply(start)
    norm_sq = dot(start, start)
    correlation = dot(start, image)
    inv_norm = 1.0 / jnp.sqrt(norm_sq)
    basis = [x * inv_norm for x in start]
    applied = [x * inv_norm for x in image]
    ritz = correlation / norm_sq
    for _ in range(ITERS):
        residual = [x - ritz * y for x, y in zip(applied, basis)]
        res_sq = dot(residual, residual)
        length = jnp.sqrt(res_sq)
        fresh = [x / length for x in residual]
        fresh_applied = apply(fresh)
        curvature = dot(fresh, fresh_applied)
        half_gap = 0.5 * (ritz - curvature)
        root = jnp.sqrt(half_gap * half_gap + res_sq)
        lowest = 0.5 * (ritz + curvature) - root
        first = curvature - lowest
        pair = jnp.sqrt(first * first + res_sq)
        basis = [(first * x - length * y) / pair for x, y in zip(basis, fresh)]
        applied = [(first * x - length * y) / pair for x, y in zip(applied, fresh_applied)]
        ritz = lowest
    return basis, ritz


def finish_body(
    ids, sector, rsector, lsize, rsize, own_stats, other_stats, thin, got, back,
    out, energy, coef,
):
    _, lane = grids(64, HALF)
    stats = own_stats[...] + jnp.where(lane == 5, other_stats[...], 0.0)
    flip = jnp.concatenate([stats, jnp.zeros((64, HALF), f32)], axis=0).T
    norm, a1, b1, a2, b2, a3 = [flip[m : m + 1, :] for m in range(6)]
    basis, ritz = ritz_pair(norm, a1, b1, a2, b2, a3)
    energy[0, 0] = jnp.sum(ritz)
    scale = jnp.sqrt(jnp.full((1, HALF), 64 * TILE * TILE, f32))
    i, _ = grids(HALF, HALF)
    c1 = basis[0] * inverse(norm) * scale
    c2 = basis[1] * scale
    c3 = basis[2] * scale
    coef[...] = jnp.where(i == 0, c1, jnp.where(i == 1, c2, jnp.where(i == 2, c3, 0.0))).T
    core = ids[1]
    own = coef[pl.ds(pl.multiple_of(core * 8, 8), 8), :]
    jcol, irow = grids(16, TILE)
    for b in range(8):
        live_left = lsize[sector[ids[0] * 16 + core * 8 + b]]
        live_right = rsize[rsector[b]]
        live = (jcol + ids[2] * 16 < live_right) & (irow < live_left)
        keep = got[core * 8 + b, :16, :]
        recv = back[b, :16, :]
        second = jnp.where(core == 0, keep, recv)
        third = jnp.where(core == 0, recv, keep)
        out[b] = (
            own[b : b + 1, 0:1] * jnp.where(live, thin[b], 0.0)
            + own[b : b + 1, 1:2] * second
            + own[b : b + 1, 2:3] * third
        )


def finish(ids, sector, rsector, lsize, rsize, own_stats, other_stats, thin, got, back):
    return pl.pallas_call(
        finish_body,
        in_specs=[smem()] * 5 + [vmem()] * 5,
        out_specs=[vmem(), smem()],
        out_shape=[
            jax.ShapeDtypeStruct(thin.shape, f32),
            jax.ShapeDtypeStruct((1, 1), f32),
        ],
        scratch_shapes=[pltpu.VMEM((HALF, HALF), f32)],
        compiler_params=params(4),
        name="finish",
    )(ids, sector, rsector, lsize, rsize, own_stats, other_stats, thin, got, back)


def local(theta, left_env, right_env, left_sector, right_sector, term_on, left_size, right_size):
    plane = lax.axis_index("y").astype(jnp.int32)
    core = lax.axis_index("c").astype(jnp.int32)
    place = lax.axis_index(COL).astype(jnp.int32)
    ids = jnp.stack([plane, core, place])
    thin = jnp.swapaxes(theta, 1, 2)

    rsector_other = lax.ppermute(right_sector, "c", SWAP)
    on_other = lax.ppermute(term_on, "c", SWAP)
    thin_other = lax.ppermute(thin, "c", SWAP)

    mine, folded = fold_left(ids, left_env)
    theirs = lax.ppermute(folded, "c", SWAP)
    below = [lax.ppermute(x, "y", UP) for x in (mine, theirs)]
    above = [lax.ppermute(x, "y", DOWN) for x in (mine, theirs)]
    far = [lax.ppermute(below[0], "y", UP), lax.ppermute(above[1], "y", DOWN)]

    thin_late, _ = lax.optimization_barrier((thin, folded))
    slots = right_slots(
        ids, right_sector, rsector_other, term_on, on_other, thin_late, thin_other, right_env
    )
    slots, theirs_now = lax.optimization_barrier((slots, theirs))
    arrived = lax.all_to_all(slots, COL, 0, 0, tiled=True)
    scalars = (ids, right_sector, rsector_other, left_sector, left_size, right_size)
    r_hi, r_lo, m_hi, m_lo, q1, stats = first_vector(scalars, arrived)

    pieces = [mine, theirs] + above + far + below
    left_sent = left_slots(ids, left_sector, pieces)
    left_arrived = lax.all_to_all(left_sent, COL, 0, 0, tiled=True)
    l_hi, l_lo, part = image_one(left_arrived, m_hi, m_lo)
    stacks = (r_hi, r_lo, l_hi, l_lo)
    part, q2, stats = image_two(scalars, part, lax.ppermute(part, "c", SWAP), q1, stats, stacks)
    sent = image_three(scalars, part, lax.ppermute(part, "c", SWAP), q1, q2, stats, stacks)

    got = lax.all_to_all(sent, COL, 0, 0, tiled=True)
    plane_stats = got[:, 16, :HALF]
    turned = [
        lax.ppermute(plane_stats, "y", [(i, (i + k) % 4) for i in range(4)]) for k in (1, 2, 3)
    ]
    back = lax.ppermute(lax.dynamic_slice_in_dim(got, (1 - core) * 8, 8), "c", SWAP)
    own_stats = jnp.concatenate([plane_stats] + turned)
    other_stats = lax.ppermute(own_stats, "c", SWAP)
    out, energy = finish(
        ids, left_sector, right_sector, left_size, right_size,
        own_stats, other_stats, thin, got, back,
    )
    return jnp.swapaxes(out, 1, 2), energy[0, 0]


def solution(mesh):
    fine = Mesh(mesh.devices.reshape(4, 2, 4, 4), ALL)
    row = ("y", "c")
    placed = (
        P(row, None, COL),
        P(row, COL, None, None),
        P(None, COL, None, None),
        P(),
        P(row),
        P(row, COL),
        P(),
        P(),
    )
    return jax.shard_map(
        local, mesh=fine, in_specs=placed, out_specs=(P(row, None, COL), P()), check_vma=False
    )
```

```python
import jax
import jax.numpy as jnp
from jax import lax
from jax.experimental import pallas as pl
from jax.experimental.pallas import tpu as pltpu
from jax.sharding import Mesh, PartitionSpec as P

ITERS = 2
LEFT_FLOPS = 15_000_000_000
TILE = 256
HALF = 128
TERMS = 16
FOLDED = 264
THIN = 32
SLOT = THIN + FOLDED
COL = ("x", "z")
ALL = ("y", "c", "x", "z")
SWAP = [(0, 1), (1, 0)]
UP = [(i, (i + 1) % 4) for i in range(4)]
DOWN = [(i, (i - 1) % 4) for i in range(4)]
f32 = jnp.float32
bf16 = jnp.bfloat16


def params(mib):
    return pltpu.CompilerParams(vmem_limit_bytes=mib * 1024 * 1024)


def hbm():
    return pl.BlockSpec(memory_space=pltpu.HBM)


def in_hbm(x):
    return pltpu.with_memory_space_constraint(x, pltpu.HBM)


def smem():
    return pl.BlockSpec(memory_space=pltpu.SMEM)


def cost(flops, nbytes):
    return pl.CostEstimate(flops=flops, transcendentals=0, bytes_accessed=nbytes)


def vmem():
    return pl.BlockSpec(memory_space=pltpu.VMEM)


def grids(rows, cols):
    i = lax.broadcasted_iota(jnp.int32, (rows, cols), 0)
    j = lax.broadcasted_iota(jnp.int32, (rows, cols), 1)
    return i, j


def fold_tile(tile):
    i, j = grids(HALF, HALF)
    a00 = tile[:HALF, :HALF]
    a11 = tile[HALF:, HALF:]
    fold = jnp.where(i >= j, a00, a11)
    diag = jnp.sum(jnp.where(i == j, a11, 0.0), axis=0, keepdims=True)
    return fold, tile[:HALF, HALF:], diag


def put_folded(dst, at, tile):
    fold, corner, diag = fold_tile(tile)
    dst[at, :HALF, :] = fold
    dst[at, HALF:TILE, :] = corner
    dst[at, TILE:, :] = jnp.broadcast_to(diag, (FOLDED - TILE, HALF))


def get_folded(src, at, row):
    return unfold_tile(
        src[at, row : row + HALF, :],
        src[at, row + HALF : row + TILE, :],
        src[at, row + TILE : row + TILE + 1, :],
    )


def unfold_tile(fold, corner, diag):
    i, j = grids(HALF, HALF)
    flip = fold.T
    a00 = jnp.where(i >= j, fold, flip)
    a11 = jnp.where(i == j, diag, jnp.where(i < j, fold, flip))
    top = jnp.concatenate([a00, corner], axis=1)
    low = jnp.concatenate([corner.T, a11], axis=1)
    return jnp.concatenate([top, low], axis=0)


def split(x):
    hi = x.astype(bf16)
    return hi, (x - hi.astype(f32)).astype(bf16)


def dot3(a_hi, a_lo, b_hi, b_lo):
    def dot(a, b):
        return jnp.dot(a, b, preferred_element_type=f32)

    return dot(a_hi, b_hi) + (dot(a_hi, b_lo) + dot(a_lo, b_hi))


def total(x):
    return jnp.sum(jnp.sum(x, axis=0, keepdims=True), axis=1, keepdims=True)


def inverse(norm):
    good = norm > 0.0
    return jnp.where(good, 1.0 / jnp.where(good, norm, 1.0), 0.0)


def put(stats, lane, value):
    _, j = grids(8, HALF)
    return jnp.where(j == lane, value, stats)


def fold_left_body(ids, src, keep, give, tiles, folded, sem_in, sem_out):
    def fetch(t, n):
        term = ids[1] if t else 1 - ids[1]
        at = 4 * t + n
        return pltpu.make_async_copy(src.at[n, term], tiles.at[at], sem_in.at[at])

    def store(t, n):
        at = 4 * t + n
        dst = keep if t else give
        return pltpu.make_async_copy(folded.at[at], dst.at[n], sem_out.at[at])

    order = [(t, n) for t in range(2) for n in range(4)]
    for t, n in order:
        fetch(t, n).start()
    for t, n in order:
        fetch(t, n).wait()
        put_folded(folded, 4 * t + n, tiles[4 * t + n])
        store(t, n).start()
    for t, n in order:
        store(t, n).wait()


def fold_left(ids, left_env):
    return pl.pallas_call(
        fold_left_body,
        in_specs=[smem(), hbm()],
        out_specs=[hbm(), hbm()],
        out_shape=[pltpu.HBM((4, FOLDED, HALF), f32)] * 2,
        scratch_shapes=[
            pltpu.VMEM((8, TILE, TILE), f32),
            pltpu.VMEM((8, FOLDED, HALF), f32),
            pltpu.SemaphoreType.DMA((8,)),
            pltpu.SemaphoreType.DMA((8,)),
        ],
        compiler_params=params(8),
        cost_estimate=cost(1_000_000, 4_000_000),
        name="fold_left",
    )(ids, in_hbm(left_env))


def sector_of(ids, rsector, rsector_other, slot):
    return jnp.where(slot // 8 == ids[1], rsector[slot % 8], rsector_other[slot % 8])


def right_slots_body(
    ids, rsector, rsector_other, on, on_other, thin, thin_other, right_env,
    out, right, folded, cols, sem_in, sem_out, sem_thin,
):
    def fetch(sector):
        return pltpu.make_async_copy(
            right_env.at[sector, ids[1]], right.at[sector], sem_in.at[sector]
        )

    def store_thin(slot):
        return pltpu.make_async_copy(
            cols.at[slot], out.at[slot, pl.ds(0, THIN), :], sem_thin.at[slot]
        )

    def store(slot, sector):
        return pltpu.make_async_copy(
            folded.at[sector], out.at[slot, pl.ds(THIN, FOLDED), :], sem_out.at[slot]
        )

    for sector in range(8):
        fetch(sector).start()
    for slot in range(TERMS):
        here = slot // 8 == ids[1]
        block = jnp.where(here, thin[slot % 8], thin_other[slot % 8])
        cols[slot, :16, :] = block[:, :HALF]
        cols[slot, 16:, :] = block[:, HALF:]
        store_thin(slot).start()
    folded[8] = jnp.zeros((FOLDED, HALF), f32)
    for sector in range(8):
        fetch(sector).wait()
        put_folded(folded, sector, right[sector])

    def one(slot, carry):
        here = slot // 8 == ids[1]
        weight = jnp.where(here, on[slot % 8, ids[1]], on_other[slot % 8, ids[1]])
        sector = sector_of(ids, rsector, rsector_other, slot)
        store(slot, jnp.where(weight == 0, 8, sector)).start()
        return carry

    def finished(slot, carry):
        store_thin(slot).wait()
        store(slot, 0).wait()
        return carry

    lax.fori_loop(0, TERMS, one, 0)
    lax.fori_loop(0, TERMS, finished, 0)


def right_slots(ids, rsector, rsector_other, on, on_other, thin, thin_other, right_env):
    return pl.pallas_call(
        right_slots_body,
        in_specs=[smem()] * 5 + [vmem()] * 2 + [hbm()],
        out_specs=hbm(),
        out_shape=pltpu.HBM((TERMS, SLOT, HALF), f32),
        scratch_shapes=[
            pltpu.VMEM((8, TILE, TILE), f32),
            pltpu.VMEM((9, FOLDED, HALF), f32),
            pltpu.VMEM((TERMS, THIN, HALF), f32),
            pltpu.SemaphoreType.DMA((8,)),
            pltpu.SemaphoreType.DMA((TERMS,)),
            pltpu.SemaphoreType.DMA((TERMS,)),
        ],
        compiler_params=params(10),
        cost_estimate=cost(4_000_000, 10_000_000),
        name="right_slots",
    )(ids, rsector, rsector_other, on, on_other, thin, thin_other, in_hbm(right_env))


def left_slots_body(ids, left_sector, *refs):
    mine, theirs = refs[:2]
    above, far, below = refs[2:4], refs[4:6], refs[6:8]
    out, sem = refs[8:]

    def store(src, slot):
        return pltpu.make_async_copy(src, out.at[slot], sem.at[slot])

    def start(slot, carry):
        sector = left_sector[ids[0] * 16 + slot]
        home = sector // 4
        tile = sector % 4
        away = (home // 2 - ids[0] + 4) % 4
        same = home % 2 == ids[1]
        cases = [(same, mine, tile), (~same, theirs, tile)]
        cases = [(case & (away == 0), src, at) for case, src, at in cases]
        for n, half in ((0, same), (1, ~same)):
            cases.append((half & (away == 1), above[n], tile))
            cases.append((half & (away == 2), far[n], tile))
            cases.append((half & (away == 3), below[n], tile))
        for case, src, at in cases:

            @pl.when(case)
            def _():
                store(src.at[at], slot).start()

        return carry

    def finished(slot, carry):
        store(mine.at[0], slot).wait()
        return carry

    lax.fori_loop(0, TERMS, start, 0)
    lax.fori_loop(0, TERMS, finished, 0)


def left_slots(ids, left_sector, pieces):
    return pl.pallas_call(
        left_slots_body,
        in_specs=[smem(), smem()] + [vmem()] * 8,
        out_specs=hbm(),
        out_shape=pltpu.HBM((TERMS, FOLDED, HALF), f32),
        scratch_shapes=[pltpu.SemaphoreType.DMA((TERMS,))],
        compiler_params=params(8),
        cost_estimate=cost(LEFT_FLOPS, 4_000_000),
        name="left_slots",
    )(ids, left_sector, *pieces)


def live_sizes(ids, rsector, rsector_other, left_sector, left_size, right_size):
    live_left = left_size[left_sector[ids[0] * 16 + ids[2]]]
    live_right = right_size[sector_of(ids, rsector, rsector_other, ids[2])]
    return live_right, live_left


def mask_of(live_right, live_left):
    i, j = grids(TILE, TILE)
    return (i < live_right) & (j < live_left)


def first_body(
    ids, rsector, rsector_other, sector, lsize, rsize, slots,
    r_hi, r_lo, m_hi, m_lo, q1, stats, arrived, sem,
):
    live_right, live_left = live_sizes(ids, rsector, rsector_other, sector, lsize, rsize)

    def fetch(n):
        return pltpu.make_async_copy(slots.at[n], arrived.at[n], sem.at[n])

    for n in range(TERMS):
        fetch(n).start()
    for n in range(TERMS):
        fetch(n).wait()
        full = get_folded(arrived, n, THIN)
        hi, lo = split(full)
        r_hi[n * TILE : (n + 1) * TILE, :] = hi
        r_lo[n * TILE : (n + 1) * TILE, :] = lo
    block = jnp.concatenate(
        [
            jnp.concatenate([arrived[n, :16, :], arrived[n, 16:THIN, :]], axis=1)
            for n in range(TERMS)
        ],
        axis=0,
    )
    start = jnp.where(mask_of(live_right, live_left), block, 0.0)
    norm = jnp.sqrt(total(start * start))
    vec = start * inverse(norm)
    q1[...] = vec
    stats[...] = put(jnp.zeros((8, HALF), f32), 0, norm)
    q_hi, q_lo = split(vec)
    for n in range(TERMS):
        rows = pl.ds(n * TILE, TILE)
        hi, lo = split(dot3(r_hi[rows, :], r_lo[rows, :], q_hi, q_lo))
        m_hi[:, rows] = hi
        m_lo[:, rows] = lo


def first_vector(scalars, slots):
    return pl.pallas_call(
        first_body,
        in_specs=[smem()] * 6 + [hbm()],
        out_specs=[vmem()] * 6,
        out_shape=[
            jax.ShapeDtypeStruct((TERMS * TILE, TILE), bf16),
            jax.ShapeDtypeStruct((TERMS * TILE, TILE), bf16),
            jax.ShapeDtypeStruct((TILE, TERMS * TILE), bf16),
            jax.ShapeDtypeStruct((TILE, TERMS * TILE), bf16),
            jax.ShapeDtypeStruct((TILE, TILE), f32),
            jax.ShapeDtypeStruct((8, HALF), f32),
        ],
        scratch_shapes=[
            pltpu.VMEM((TERMS, SLOT, HALF), f32),
            pltpu.SemaphoreType.DMA((TERMS,)),
        ],
        compiler_params=params(10),
        cost_estimate=cost(1_700_000_000, 12_000_000),
        name="first_vector",
    )(*scalars, in_hbm(slots))


def image_one_body(
    arrived, m_hi, m_lo, r_hi_in, r_lo_in, l_hi, l_lo, part, r_hi, r_lo, here, sem, sem_r
):
    chunk = TERMS // 4

    def fetch(p, c):
        cols = pl.ds(c * chunk * TILE, chunk * TILE)
        src = (m_hi, m_lo)[p]
        return pltpu.make_async_copy(src.at[:, cols], here.at[p, :, cols], sem.at[p, c])

    def fetch_right(p):
        src, dst = ((r_hi_in, r_hi), (r_lo_in, r_lo))[p]
        return pltpu.make_async_copy(src, dst, sem_r.at[p])

    for c in range(4):
        for p in range(2):
            fetch(p, c).start()
    for p in range(2):
        fetch_right(p).start()
    acc = jnp.zeros((TILE, TILE), f32)
    for c in range(4):
        for n in range(c * chunk, (c + 1) * chunk):
            hi, lo = split(get_folded(arrived, n, 0))
            l_hi[n * TILE : (n + 1) * TILE, :] = hi
            l_lo[n * TILE : (n + 1) * TILE, :] = lo
        for p in range(2):
            fetch(p, c).wait()
        cols = pl.ds(c * chunk * TILE, chunk * TILE)
        acc = acc + dot3(here[0, :, cols], here[1, :, cols], l_hi[cols, :], l_lo[cols, :])
    part[...] = acc
    for p in range(2):
        fetch_right(p).wait()


def image_one(arrived, m_hi, m_lo, r_hi, r_lo):
    stack = jax.ShapeDtypeStruct((TERMS * TILE, TILE), bf16)
    return pl.pallas_call(
        image_one_body,
        in_specs=[vmem()] + [hbm()] * 4,
        out_specs=[vmem()] * 5,
        out_shape=[stack, stack, jax.ShapeDtypeStruct((TILE, TILE), f32), stack, stack],
        scratch_shapes=[
            pltpu.VMEM((2, TILE, TERMS * TILE), bf16),
            pltpu.SemaphoreType.DMA((2, 4)),
            pltpu.SemaphoreType.DMA((2,)),
        ],
        compiler_params=params(10),
        cost_estimate=cost(1_700_000_000, 10_000_000),
        name="image_one",
    )(arrived, in_hbm(m_hi), in_hbm(m_lo), in_hbm(r_hi), in_hbm(r_lo))


def lanczos(image, last, before, beta):
    alpha = total(last * image)
    rest = image - alpha * last
    if before is not None:
        rest = rest - beta * before
    again = rest - total(last * rest) * last
    if before is not None:
        again = again - total(before * rest) * before
    norm = jnp.sqrt(total(again * again))
    return alpha, norm, again * inverse(norm)


def half_image(vec, r_hi, r_lo, l_hi, l_lo):
    q_hi, q_lo = split(vec)
    acc = jnp.zeros((TILE, TILE), f32)
    for n in range(TERMS):
        rows = pl.ds(n * TILE, TILE)
        hi, lo = split(dot3(r_hi[rows, :], r_lo[rows, :], q_hi, q_lo))
        acc = acc + dot3(hi, lo, l_hi[rows, :], l_lo[rows, :])
    return acc


def image_two_body(
    ids, rsector, rsector_other, sector, lsize, rsize,
    part_a, part_b, q1, stats_in, r_hi, r_lo, l_hi, l_lo,
    part, q2, stats,
):
    mask = mask_of(*live_sizes(ids, rsector, rsector_other, sector, lsize, rsize))
    image = jnp.where(mask, part_a[...] + part_b[...], 0.0)
    alpha, norm, vec = lanczos(image, q1[...], None, None)
    q2[...] = vec
    stats[...] = put(put(stats_in[...], 1, alpha), 2, norm)
    part[...] = half_image(vec, r_hi, r_lo, l_hi, l_lo)


def image_two(scalars, part, part_other, q1, stats, stacks):
    return pl.pallas_call(
        image_two_body,
        in_specs=[smem()] * 6 + [vmem()] * 8,
        out_specs=[vmem()] * 3,
        out_shape=[
            jax.ShapeDtypeStruct((TILE, TILE), f32),
            jax.ShapeDtypeStruct((TILE, TILE), f32),
            jax.ShapeDtypeStruct((8, HALF), f32),
        ],
        compiler_params=params(6),
        cost_estimate=cost(3_300_000_000, 9_000_000),
        name="image_two",
    )(*scalars, part, part_other, q1, stats, *stacks)


def image_three_body(
    ids, rsector, rsector_other, sector, lsize, rsize,
    part_a, part_b, q1, q2, stats_in, r_hi, r_lo, l_hi, l_lo, slots,
):
    mask = mask_of(*live_sizes(ids, rsector, rsector_other, sector, lsize, rsize))
    image = jnp.where(mask, part_a[...] + part_b[...], 0.0)
    i, j = grids(8, HALF)
    beta = total(jnp.where((j == 2) & (i == 0), stats_in[...], 0.0))
    alpha, norm, vec = lanczos(image, q2[...], q1[...], beta)
    pick = jnp.where(ids[1] == 0, q2[...], vec)
    for n in range(16):
        slots[n, :16, :] = pick[16 * n : 16 * n + 16]
    stats = put(put(stats_in[...], 3, alpha), 4, norm)
    alpha = total(vec * half_image(vec, r_hi, r_lo, l_hi, l_lo))
    stats = put(stats, 5, alpha)
    wide = jnp.concatenate([stats, jnp.zeros((8, HALF), f32)], axis=1)
    for n in range(16):
        slots[n, 16:24, :] = wide


def image_three(scalars, part, part_other, q1, q2, stats, stacks):
    return pl.pallas_call(
        image_three_body,
        in_specs=[smem()] * 6 + [vmem()] * 9,
        out_specs=vmem(),
        out_shape=jax.ShapeDtypeStruct((16, 24, TILE), f32),
        compiler_params=params(6),
        cost_estimate=cost(3_300_000_000, 9_000_000),
        name="image_three",
    )(*scalars, part, part_other, q1, q2, stats, *stacks)


def ritz_pair(norm, a1, b1, a2, b2, a3):
    def apply(x):
        return [a1 * x[0] + b1 * x[1], b1 * x[0] + a2 * x[1] + b2 * x[2], b2 * x[1] + a3 * x[2]]

    def dot(x, y):
        return jnp.sum(x[0] * y[0] + x[1] * y[1] + x[2] * y[2], axis=1, keepdims=True)

    zero = jnp.zeros_like(norm)
    start = [norm, zero, zero]
    image = apply(start)
    norm_sq = dot(start, start)
    correlation = dot(start, image)
    inv_norm = 1.0 / jnp.sqrt(norm_sq)
    basis = [x * inv_norm for x in start]
    applied = [x * inv_norm for x in image]
    ritz = correlation / norm_sq
    for _ in range(ITERS):
        residual = [x - ritz * y for x, y in zip(applied, basis)]
        res_sq = dot(residual, residual)
        length = jnp.sqrt(res_sq)
        fresh = [x / length for x in residual]
        fresh_applied = apply(fresh)
        curvature = dot(fresh, fresh_applied)
        half_gap = 0.5 * (ritz - curvature)
        root = jnp.sqrt(half_gap * half_gap + res_sq)
        lowest = 0.5 * (ritz + curvature) - root
        first = curvature - lowest
        pair = jnp.sqrt(first * first + res_sq)
        basis = [(first * x - length * y) / pair for x, y in zip(basis, fresh)]
        applied = [(first * x - length * y) / pair for x, y in zip(applied, fresh_applied)]
        ritz = lowest
    return basis, ritz


def finish_body(
    ids, sector, rsector, lsize, rsize, own_stats, other_stats, thin, got, back,
    out, energy, coef,
):
    _, lane = grids(64, HALF)
    stats = own_stats[...] + jnp.where(lane == 5, other_stats[...], 0.0)
    flip = jnp.concatenate([stats, jnp.zeros((64, HALF), f32)], axis=0).T
    norm, a1, b1, a2, b2, a3 = [flip[m : m + 1, :] for m in range(6)]
    basis, ritz = ritz_pair(norm, a1, b1, a2, b2, a3)
    energy[0, 0] = jnp.sum(ritz)
    scale = jnp.sqrt(jnp.full((1, HALF), 64 * TILE * TILE, f32))
    i, _ = grids(HALF, HALF)
    c1 = basis[0] * inverse(norm) * scale
    c2 = basis[1] * scale
    c3 = basis[2] * scale
    coef[...] = jnp.where(i == 0, c1, jnp.where(i == 1, c2, jnp.where(i == 2, c3, 0.0))).T
    core = ids[1]
    own = coef[pl.ds(pl.multiple_of(core * 8, 8), 8), :]
    jcol, irow = grids(16, TILE)
    for b in range(8):
        live_left = lsize[sector[ids[0] * 16 + core * 8 + b]]
        live_right = rsize[rsector[b]]
        live = (jcol + ids[2] * 16 < live_right) & (irow < live_left)
        keep = got[core * 8 + b, :16, :]
        recv = back[b, :16, :]
        second = jnp.where(core == 0, keep, recv)
        third = jnp.where(core == 0, recv, keep)
        out[b] = (
            own[b : b + 1, 0:1] * jnp.where(live, thin[b], 0.0)
            + own[b : b + 1, 1:2] * second
            + own[b : b + 1, 2:3] * third
        )


def finish(ids, sector, rsector, lsize, rsize, own_stats, other_stats, thin, got, back):
    return pl.pallas_call(
        finish_body,
        in_specs=[smem()] * 5 + [vmem()] * 5,
        out_specs=[vmem(), smem()],
        out_shape=[
            jax.ShapeDtypeStruct(thin.shape, f32),
            jax.ShapeDtypeStruct((1, 1), f32),
        ],
        scratch_shapes=[pltpu.VMEM((HALF, HALF), f32)],
        compiler_params=params(4),
        name="finish",
    )(ids, sector, rsector, lsize, rsize, own_stats, other_stats, thin, got, back)


def local(theta, left_env, right_env, left_sector, right_sector, term_on, left_size, right_size):
    plane = lax.axis_index("y").astype(jnp.int32)
    core = lax.axis_index("c").astype(jnp.int32)
    place = lax.axis_index(COL).astype(jnp.int32)
    ids = jnp.stack([plane, core, place])
    thin = jnp.swapaxes(theta, 1, 2)

    rsector_other = lax.ppermute(right_sector, "c", SWAP)
    on_other = lax.ppermute(term_on, "c", SWAP)
    thin_other = lax.ppermute(thin, "c", SWAP)

    mine, folded = fold_left(ids, left_env)
    theirs = lax.ppermute(folded, "c", SWAP)
    below = [lax.ppermute(x, "y", UP) for x in (mine, theirs)]
    above = [lax.ppermute(x, "y", DOWN) for x in (mine, theirs)]
    far = [lax.ppermute(below[0], "y", UP), lax.ppermute(above[1], "y", DOWN)]

    thin_late, _ = lax.optimization_barrier((thin, folded))
    slots = right_slots(
        ids, right_sector, rsector_other, term_on, on_other, thin_late, thin_other, right_env
    )
    slots, theirs_now = lax.optimization_barrier((slots, theirs))
    arrived = lax.all_to_all(slots, COL, 0, 0, tiled=True)
    scalars = (ids, right_sector, rsector_other, left_sector, left_size, right_size)
    r_hi, r_lo, m_hi, m_lo, q1, stats = first_vector(scalars, arrived)

    pieces = [mine, theirs] + above + far + below
    left_sent = left_slots(ids, left_sector, pieces)
    left_arrived = lax.all_to_all(left_sent, COL, 0, 0, tiled=True)
    l_hi, l_lo, part, r_hi, r_lo = image_one(left_arrived, m_hi, m_lo, r_hi, r_lo)
    stacks = (r_hi, r_lo, l_hi, l_lo)
    part, q2, stats = image_two(scalars, part, lax.ppermute(part, "c", SWAP), q1, stats, stacks)
    sent = image_three(scalars, part, lax.ppermute(part, "c", SWAP), q1, q2, stats, stacks)

    got = lax.all_to_all(sent, COL, 0, 0, tiled=True)
    plane_stats = got[:, 16, :HALF]
    turned = [
        lax.ppermute(plane_stats, "y", [(i, (i + k) % 4) for i in range(4)]) for k in (1, 2, 3)
    ]
    back = lax.ppermute(lax.dynamic_slice_in_dim(got, (1 - core) * 8, 8), "c", SWAP)
    own_stats = jnp.concatenate([plane_stats] + turned)
    other_stats = lax.ppermute(own_stats, "c", SWAP)
    out, energy = finish(
        ids, left_sector, right_sector, left_size, right_size,
        own_stats, other_stats, thin, got, back,
    )
    return jnp.swapaxes(out, 1, 2), energy[0, 0]


def solution(mesh):
    fine = Mesh(mesh.devices.reshape(4, 2, 4, 4), ALL)
    row = ("y", "c")
    placed = (
        P(row, None, COL),
        P(row, COL, None, None),
        P(None, COL, None, None),
        P(),
        P(row),
        P(row, COL),
        P(),
        P(),
    )
    return jax.shard_map(
        local, mesh=fine, in_specs=placed, out_specs=(P(row, None, COL), P()), check_vma=False
    )
```

```python
import jax
import jax.numpy as jnp
from jax import lax
from jax.experimental import pallas as pl
from jax.experimental.pallas import tpu as pltpu
from jax.sharding import Mesh, PartitionSpec as P

ITERS = 2
LEFT_FLOPS = 15_000_000_000
TILE = 256
HALF = 128
TERMS = 16
FOLDED = 264
THIN = 32
GROUP = 4
SLOT = THIN + FOLDED
COL = ("x", "z")
ALL = ("y", "c", "x", "z")
SWAP = [(0, 1), (1, 0)]
UP = [(i, (i + 1) % 4) for i in range(4)]
DOWN = [(i, (i - 1) % 4) for i in range(4)]
f32 = jnp.float32
bf16 = jnp.bfloat16


def params(mib):
    return pltpu.CompilerParams(vmem_limit_bytes=mib * 1024 * 1024)


def hbm():
    return pl.BlockSpec(memory_space=pltpu.HBM)


def in_hbm(x):
    return pltpu.with_memory_space_constraint(x, pltpu.HBM)


def smem():
    return pl.BlockSpec(memory_space=pltpu.SMEM)


def cost(flops, nbytes):
    return pl.CostEstimate(flops=flops, transcendentals=0, bytes_accessed=nbytes)


def vmem():
    return pl.BlockSpec(memory_space=pltpu.VMEM)


def grids(rows, cols):
    i = lax.broadcasted_iota(jnp.int32, (rows, cols), 0)
    j = lax.broadcasted_iota(jnp.int32, (rows, cols), 1)
    return i, j


def fold_tile(tile):
    i, j = grids(HALF, HALF)
    a00 = tile[:HALF, :HALF]
    a11 = tile[HALF:, HALF:]
    fold = jnp.where(i >= j, a00, a11)
    diag = jnp.sum(jnp.where(i == j, a11, 0.0), axis=0, keepdims=True)
    return fold, tile[:HALF, HALF:], diag


def put_folded(dst, at, tile):
    fold, corner, diag = fold_tile(tile)
    dst[at, :HALF, :] = fold
    dst[at, HALF:TILE, :] = corner
    dst[at, TILE:, :] = jnp.broadcast_to(diag, (FOLDED - TILE, HALF))


def get_folded(src, at, row):
    return unfold_tile(
        src[at, row : row + HALF, :],
        src[at, row + HALF : row + TILE, :],
        src[at, row + TILE : row + TILE + 1, :],
    )


def unfold_tile(fold, corner, diag):
    i, j = grids(HALF, HALF)
    flip = fold.T
    a00 = jnp.where(i >= j, fold, flip)
    a11 = jnp.where(i == j, diag, jnp.where(i < j, fold, flip))
    top = jnp.concatenate([a00, corner], axis=1)
    low = jnp.concatenate([corner.T, a11], axis=1)
    return jnp.concatenate([top, low], axis=0)


def split(x):
    hi = x.astype(bf16)
    return hi, (x - hi.astype(f32)).astype(bf16)


def dot3(a_hi, a_lo, b_hi, b_lo):
    def dot(a, b):
        return jnp.dot(a, b, preferred_element_type=f32)

    return dot(a_hi, b_hi) + (dot(a_hi, b_lo) + dot(a_lo, b_hi))


def total(x):
    return jnp.sum(jnp.sum(x, axis=0, keepdims=True), axis=1, keepdims=True)


def inverse(norm):
    good = norm > 0.0
    return jnp.where(good, 1.0 / jnp.where(good, norm, 1.0), 0.0)


def put(stats, lane, value):
    _, j = grids(8, HALF)
    return jnp.where(j == lane, value, stats)


def fold_left_body(ids, src, keep, give, tiles, folded, sem_in, sem_out):
    def fetch(t, n):
        term = ids[1] if t else 1 - ids[1]
        at = 4 * t + n
        return pltpu.make_async_copy(src.at[n, term], tiles.at[at], sem_in.at[at])

    def store(t, n):
        at = 4 * t + n
        dst = keep if t else give
        return pltpu.make_async_copy(folded.at[at], dst.at[n], sem_out.at[at])

    order = [(t, n) for t in range(2) for n in range(4)]
    for t, n in order:
        fetch(t, n).start()
    for t, n in order:
        fetch(t, n).wait()
        put_folded(folded, 4 * t + n, tiles[4 * t + n])
        store(t, n).start()
    for t, n in order:
        store(t, n).wait()


def fold_left(ids, left_env):
    return pl.pallas_call(
        fold_left_body,
        in_specs=[smem(), hbm()],
        out_specs=[hbm(), hbm()],
        out_shape=[pltpu.HBM((4, FOLDED, HALF), f32)] * 2,
        scratch_shapes=[
            pltpu.VMEM((8, TILE, TILE), f32),
            pltpu.VMEM((8, FOLDED, HALF), f32),
            pltpu.SemaphoreType.DMA((8,)),
            pltpu.SemaphoreType.DMA((8,)),
        ],
        compiler_params=params(8),
        cost_estimate=cost(1_000_000, 4_000_000),
        name="fold_left",
    )(ids, in_hbm(left_env))


def sector_of(ids, rsector, rsector_other, slot):
    return jnp.where(slot // 8 == ids[1], rsector[slot % 8], rsector_other[slot % 8])


def right_slots_body(
    ids, rsector, rsector_other, on, on_other, thin, thin_other, right_env,
    out, right, folded, cols, sem_in, sem_out, sem_thin,
):
    def fetch(sector):
        return pltpu.make_async_copy(
            right_env.at[sector, ids[1]], right.at[sector], sem_in.at[sector]
        )

    def store_thin(slot):
        return pltpu.make_async_copy(
            cols.at[slot], out.at[slot, pl.ds(0, THIN), :], sem_thin.at[slot]
        )

    def store(slot, sector):
        return pltpu.make_async_copy(
            folded.at[sector], out.at[slot, pl.ds(THIN, FOLDED), :], sem_out.at[slot]
        )

    for sector in range(8):
        fetch(sector).start()
    for slot in range(TERMS):
        here = slot // 8 == ids[1]
        block = jnp.where(here, thin[slot % 8], thin_other[slot % 8])
        cols[slot, :16, :] = block[:, :HALF]
        cols[slot, 16:, :] = block[:, HALF:]
        store_thin(slot).start()
    folded[8] = jnp.zeros((FOLDED, HALF), f32)
    for sector in range(8):
        fetch(sector).wait()
        put_folded(folded, sector, right[sector])

        def one(slot, carry):
            @pl.when(sector_of(ids, rsector, rsector_other, slot) == sector)
            def _():
                here = slot // 8 == ids[1]
                weight = jnp.where(here, on[slot % 8, ids[1]], on_other[slot % 8, ids[1]])
                store(slot, jnp.where(weight == 0, 8, sector)).start()

            return carry

        lax.fori_loop(0, TERMS, one, 0)

    def finished(slot, carry):
        store_thin(slot).wait()
        store(slot, 0).wait()
        return carry

    lax.fori_loop(0, TERMS, finished, 0)


def right_slots(ids, rsector, rsector_other, on, on_other, thin, thin_other, right_env):
    return pl.pallas_call(
        right_slots_body,
        in_specs=[smem()] * 5 + [vmem()] * 2 + [hbm()],
        out_specs=hbm(),
        out_shape=pltpu.HBM((TERMS, SLOT, HALF), f32),
        scratch_shapes=[
            pltpu.VMEM((8, TILE, TILE), f32),
            pltpu.VMEM((9, FOLDED, HALF), f32),
            pltpu.VMEM((TERMS, THIN, HALF), f32),
            pltpu.SemaphoreType.DMA((8,)),
            pltpu.SemaphoreType.DMA((TERMS,)),
            pltpu.SemaphoreType.DMA((TERMS,)),
        ],
        compiler_params=params(10),
        cost_estimate=cost(4_000_000, 10_000_000),
        name="right_slots",
    )(ids, rsector, rsector_other, on, on_other, thin, thin_other, in_hbm(right_env))


def left_slots_body(ids, left_sector, *refs):
    mine, theirs = refs[:2]
    above, far, below = refs[2:4], refs[4:6], refs[6:8]
    out, sem = refs[8:]

    def store(src, slot):
        return pltpu.make_async_copy(src, out.at[slot], sem.at[slot])

    def start(slot, carry):
        sector = left_sector[ids[0] * 16 + slot]
        home = sector // 4
        tile = sector % 4
        away = (home // 2 - ids[0] + 4) % 4
        same = home % 2 == ids[1]
        cases = [(same, mine, tile), (~same, theirs, tile)]
        cases = [(case & (away == 0), src, at) for case, src, at in cases]
        for n, half in ((0, same), (1, ~same)):
            cases.append((half & (away == 1), above[n], tile))
            cases.append((half & (away == 2), far[n], tile))
            cases.append((half & (away == 3), below[n], tile))
        for case, src, at in cases:

            @pl.when(case)
            def _():
                store(src.at[at], slot).start()

        return carry

    def finished(slot, carry):
        store(mine.at[0], slot).wait()
        return carry

    lax.fori_loop(0, TERMS, start, 0)
    lax.fori_loop(0, TERMS, finished, 0)


def left_slots(ids, left_sector, pieces):
    return pl.pallas_call(
        left_slots_body,
        in_specs=[smem(), smem()] + [vmem()] * 8,
        out_specs=hbm(),
        out_shape=pltpu.HBM((TERMS, FOLDED, HALF), f32),
        scratch_shapes=[pltpu.SemaphoreType.DMA((TERMS,))],
        compiler_params=params(8),
        cost_estimate=cost(LEFT_FLOPS, 4_000_000),
        name="left_slots",
    )(ids, left_sector, *pieces)


def live_sizes(ids, rsector, rsector_other, left_sector, left_size, right_size):
    live_left = left_size[left_sector[ids[0] * 16 + ids[2]]]
    live_right = right_size[sector_of(ids, rsector, rsector_other, ids[2])]
    return live_right, live_left


def mask_of(live_right, live_left):
    i, j = grids(TILE, TILE)
    return (i < live_right) & (j < live_left)


def first_body(
    ids, rsector, rsector_other, sector, lsize, rsize, slots,
    r_hi, r_lo, q1, stats, arrived, sem,
):
    live_right, live_left = live_sizes(ids, rsector, rsector_other, sector, lsize, rsize)

    def fetch(n):
        return pltpu.make_async_copy(slots.at[n], arrived.at[n], sem.at[n])

    for n in range(TERMS):
        fetch(n).start()
    for n in range(TERMS):
        fetch(n).wait()
        full = get_folded(arrived, n, THIN)
        hi, lo = split(full)
        r_hi[n * TILE : (n + 1) * TILE, :] = hi
        r_lo[n * TILE : (n + 1) * TILE, :] = lo
    block = jnp.concatenate(
        [
            jnp.concatenate([arrived[n, :16, :], arrived[n, 16:THIN, :]], axis=1)
            for n in range(TERMS)
        ],
        axis=0,
    )
    start = jnp.where(mask_of(live_right, live_left), block, 0.0)
    norm = jnp.sqrt(total(start * start))
    vec = start * inverse(norm)
    q1[...] = vec
    stats[...] = put(jnp.zeros((8, HALF), f32), 0, norm)


def first_vector(scalars, slots):
    return pl.pallas_call(
        first_body,
        in_specs=[smem()] * 6 + [hbm()],
        out_specs=[vmem()] * 4,
        out_shape=[
            jax.ShapeDtypeStruct((TERMS * TILE, TILE), bf16),
            jax.ShapeDtypeStruct((TERMS * TILE, TILE), bf16),
            jax.ShapeDtypeStruct((TILE, TILE), f32),
            jax.ShapeDtypeStruct((8, HALF), f32),
        ],
        scratch_shapes=[
            pltpu.VMEM((TERMS, SLOT, HALF), f32),
            pltpu.SemaphoreType.DMA((TERMS,)),
        ],
        compiler_params=params(10),
        cost_estimate=cost(1_700_000_000, 8_000_000),
        name="first_vector",
    )(*scalars, in_hbm(slots))


def image_one_body(arrived, q1, r_hi_in, r_lo_in, l_hi, l_lo, part, r_hi, r_lo, sem):
    def fetch(n, p):
        rows = pl.ds(n * TILE, TILE)
        src, dst = ((r_hi_in, r_hi), (r_lo_in, r_lo))[p]
        return pltpu.make_async_copy(src.at[rows, :], dst.at[rows, :], sem.at[n, p])

    pairs = [(n, p) for n in range(TERMS) for p in range(2)]
    for n, p in pairs:
        fetch(n, p).start()
    q_hi, q_lo = split(q1[...])
    acc = jnp.zeros((TILE, TILE), f32)
    for c in range(0, TERMS, GROUP):
        for n in range(c, c + GROUP):
            for p in range(2):
                fetch(n, p).wait()
        for n in range(c, c + GROUP):
            rows = pl.ds(n * TILE, TILE)
            left_hi, left_lo = split(get_folded(arrived, n, 0))
            l_hi[rows, :] = left_hi
            l_lo[rows, :] = left_lo
            hi, lo = split(dot3(r_hi[rows, :], r_lo[rows, :], q_hi, q_lo))
            acc = acc + dot3(hi, lo, left_hi, left_lo)
    part[...] = acc


def image_one(arrived, q1, r_hi, r_lo):
    stack = jax.ShapeDtypeStruct((TERMS * TILE, TILE), bf16)
    return pl.pallas_call(
        image_one_body,
        in_specs=[vmem(), vmem(), hbm(), hbm()],
        out_specs=[vmem()] * 5,
        out_shape=[stack, stack, jax.ShapeDtypeStruct((TILE, TILE), f32), stack, stack],
        scratch_shapes=[pltpu.SemaphoreType.DMA((TERMS, 2))],
        compiler_params=params(10),
        cost_estimate=cost(3_300_000_000, 10_000_000),
        name="image_one",
    )(arrived, q1, in_hbm(r_hi), in_hbm(r_lo))


def lanczos(image, last, before, beta):
    alpha = total(last * image)
    rest = image - alpha * last
    if before is not None:
        rest = rest - beta * before
    again = rest - total(last * rest) * last
    if before is not None:
        again = again - total(before * rest) * before
    norm = jnp.sqrt(total(again * again))
    return alpha, norm, again * inverse(norm)


def half_image(vec, r_hi, r_lo, l_hi, l_lo):
    q_hi, q_lo = split(vec)
    acc = jnp.zeros((TILE, TILE), f32)
    for n in range(TERMS):
        rows = pl.ds(n * TILE, TILE)
        hi, lo = split(dot3(r_hi[rows, :], r_lo[rows, :], q_hi, q_lo))
        acc = acc + dot3(hi, lo, l_hi[rows, :], l_lo[rows, :])
    return acc


def image_two_body(
    ids, rsector, rsector_other, sector, lsize, rsize,
    part_a, part_b, q1, stats_in, r_hi, r_lo, l_hi, l_lo,
    part, q2, stats,
):
    mask = mask_of(*live_sizes(ids, rsector, rsector_other, sector, lsize, rsize))
    image = jnp.where(mask, part_a[...] + part_b[...], 0.0)
    alpha, norm, vec = lanczos(image, q1[...], None, None)
    q2[...] = vec
    stats[...] = put(put(stats_in[...], 1, alpha), 2, norm)
    part[...] = half_image(vec, r_hi, r_lo, l_hi, l_lo)


def image_two(scalars, part, part_other, q1, stats, stacks):
    return pl.pallas_call(
        image_two_body,
        in_specs=[smem()] * 6 + [vmem()] * 8,
        out_specs=[vmem()] * 3,
        out_shape=[
            jax.ShapeDtypeStruct((TILE, TILE), f32),
            jax.ShapeDtypeStruct((TILE, TILE), f32),
            jax.ShapeDtypeStruct((8, HALF), f32),
        ],
        compiler_params=params(6),
        cost_estimate=cost(3_300_000_000, 9_000_000),
        name="image_two",
    )(*scalars, part, part_other, q1, stats, *stacks)


def image_three_body(
    ids, rsector, rsector_other, sector, lsize, rsize,
    part_a, part_b, q1, q2, stats_in, r_hi, r_lo, l_hi, l_lo, slots,
):
    mask = mask_of(*live_sizes(ids, rsector, rsector_other, sector, lsize, rsize))
    image = jnp.where(mask, part_a[...] + part_b[...], 0.0)
    i, j = grids(8, HALF)
    beta = total(jnp.where((j == 2) & (i == 0), stats_in[...], 0.0))
    alpha, norm, vec = lanczos(image, q2[...], q1[...], beta)
    pick = jnp.where(ids[1] == 0, q2[...], vec)
    for n in range(16):
        slots[n, :16, :] = pick[16 * n : 16 * n + 16]
    stats = put(put(stats_in[...], 3, alpha), 4, norm)
    alpha = total(vec * half_image(vec, r_hi, r_lo, l_hi, l_lo))
    stats = put(stats, 5, alpha)
    wide = jnp.concatenate([stats, jnp.zeros((8, HALF), f32)], axis=1)
    for n in range(16):
        slots[n, 16:24, :] = wide


def image_three(scalars, part, part_other, q1, q2, stats, stacks):
    return pl.pallas_call(
        image_three_body,
        in_specs=[smem()] * 6 + [vmem()] * 9,
        out_specs=vmem(),
        out_shape=jax.ShapeDtypeStruct((16, 24, TILE), f32),
        compiler_params=params(6),
        cost_estimate=cost(3_300_000_000, 9_000_000),
        name="image_three",
    )(*scalars, part, part_other, q1, q2, stats, *stacks)


def ritz_pair(norm, a1, b1, a2, b2, a3):
    def apply(x):
        return [a1 * x[0] + b1 * x[1], b1 * x[0] + a2 * x[1] + b2 * x[2], b2 * x[1] + a3 * x[2]]

    def dot(x, y):
        return jnp.sum(x[0] * y[0] + x[1] * y[1] + x[2] * y[2], axis=1, keepdims=True)

    zero = jnp.zeros_like(norm)
    start = [norm, zero, zero]
    image = apply(start)
    norm_sq = dot(start, start)
    correlation = dot(start, image)
    inv_norm = 1.0 / jnp.sqrt(norm_sq)
    basis = [x * inv_norm for x in start]
    applied = [x * inv_norm for x in image]
    ritz = correlation / norm_sq
    for _ in range(ITERS):
        residual = [x - ritz * y for x, y in zip(applied, basis)]
        res_sq = dot(residual, residual)
        length = jnp.sqrt(res_sq)
        fresh = [x / length for x in residual]
        fresh_applied = apply(fresh)
        curvature = dot(fresh, fresh_applied)
        half_gap = 0.5 * (ritz - curvature)
        root = jnp.sqrt(half_gap * half_gap + res_sq)
        lowest = 0.5 * (ritz + curvature) - root
        first = curvature - lowest
        pair = jnp.sqrt(first * first + res_sq)
        basis = [(first * x - length * y) / pair for x, y in zip(basis, fresh)]
        applied = [(first * x - length * y) / pair for x, y in zip(applied, fresh_applied)]
        ritz = lowest
    return basis, ritz


def finish_body(
    ids, sector, rsector, lsize, rsize, own_stats, other_stats, thin, got, back,
    out, energy, coef,
):
    _, lane = grids(64, HALF)
    stats = own_stats[...] + jnp.where(lane == 5, other_stats[...], 0.0)
    flip = jnp.concatenate([stats, jnp.zeros((64, HALF), f32)], axis=0).T
    norm, a1, b1, a2, b2, a3 = [flip[m : m + 1, :] for m in range(6)]
    basis, ritz = ritz_pair(norm, a1, b1, a2, b2, a3)
    energy[0, 0] = jnp.sum(ritz)
    scale = jnp.sqrt(jnp.full((1, HALF), 64 * TILE * TILE, f32))
    i, _ = grids(HALF, HALF)
    c1 = basis[0] * inverse(norm) * scale
    c2 = basis[1] * scale
    c3 = basis[2] * scale
    coef[...] = jnp.where(i == 0, c1, jnp.where(i == 1, c2, jnp.where(i == 2, c3, 0.0))).T
    core = ids[1]
    own = coef[pl.ds(pl.multiple_of(core * 8, 8), 8), :]
    jcol, irow = grids(16, TILE)
    for b in range(8):
        live_left = lsize[sector[ids[0] * 16 + core * 8 + b]]
        live_right = rsize[rsector[b]]
        live = (jcol + ids[2] * 16 < live_right) & (irow < live_left)
        keep = got[core * 8 + b, :16, :]
        recv = back[b, :16, :]
        second = jnp.where(core == 0, keep, recv)
        third = jnp.where(core == 0, recv, keep)
        out[b] = (
            own[b : b + 1, 0:1] * jnp.where(live, thin[b], 0.0)
            + own[b : b + 1, 1:2] * second
            + own[b : b + 1, 2:3] * third
        )


def finish(ids, sector, rsector, lsize, rsize, own_stats, other_stats, thin, got, back):
    return pl.pallas_call(
        finish_body,
        in_specs=[smem()] * 5 + [vmem()] * 5,
        out_specs=[vmem(), smem()],
        out_shape=[
            jax.ShapeDtypeStruct(thin.shape, f32),
            jax.ShapeDtypeStruct((1, 1), f32),
        ],
        scratch_shapes=[pltpu.VMEM((HALF, HALF), f32)],
        compiler_params=params(4),
        name="finish",
    )(ids, sector, rsector, lsize, rsize, own_stats, other_stats, thin, got, back)


def local(theta, left_env, right_env, left_sector, right_sector, term_on, left_size, right_size):
    plane = lax.axis_index("y").astype(jnp.int32)
    core = lax.axis_index("c").astype(jnp.int32)
    place = lax.axis_index(COL).astype(jnp.int32)
    ids = jnp.stack([plane, core, place])
    thin = jnp.swapaxes(theta, 1, 2)

    rsector_other = lax.ppermute(right_sector, "c", SWAP)
    on_other = lax.ppermute(term_on, "c", SWAP)
    thin_other = lax.ppermute(thin, "c", SWAP)

    mine, folded = fold_left(ids, left_env)
    theirs = lax.ppermute(folded, "c", SWAP)
    below = [lax.ppermute(x, "y", UP) for x in (mine, theirs)]
    above = [lax.ppermute(x, "y", DOWN) for x in (mine, theirs)]
    far = [lax.ppermute(below[0], "y", UP), lax.ppermute(above[1], "y", DOWN)]

    thin_late, _ = lax.optimization_barrier((thin, folded))
    slots = right_slots(
        ids, right_sector, rsector_other, term_on, on_other, thin_late, thin_other, right_env
    )
    slots, theirs_now = lax.optimization_barrier((slots, theirs))
    arrived = lax.all_to_all(slots, COL, 0, 0, tiled=True)
    scalars = (ids, right_sector, rsector_other, left_sector, left_size, right_size)
    r_hi, r_lo, q1, stats = first_vector(scalars, arrived)

    pieces = [mine, theirs] + above + far + below
    left_sent = left_slots(ids, left_sector, pieces)
    left_arrived = lax.all_to_all(left_sent, COL, 0, 0, tiled=True)
    l_hi, l_lo, part, r_hi, r_lo = image_one(left_arrived, q1, r_hi, r_lo)
    stacks = (r_hi, r_lo, l_hi, l_lo)
    part, q2, stats = image_two(scalars, part, lax.ppermute(part, "c", SWAP), q1, stats, stacks)
    sent = image_three(scalars, part, lax.ppermute(part, "c", SWAP), q1, q2, stats, stacks)

    got = lax.all_to_all(sent, COL, 0, 0, tiled=True)
    plane_stats = got[:, 16, :HALF]
    turned = [
        lax.ppermute(plane_stats, "y", [(i, (i + k) % 4) for i in range(4)]) for k in (1, 2, 3)
    ]
    back = lax.ppermute(lax.dynamic_slice_in_dim(got, (1 - core) * 8, 8), "c", SWAP)
    own_stats = jnp.concatenate([plane_stats] + turned)
    other_stats = lax.ppermute(own_stats, "c", SWAP)
    out, energy = finish(
        ids, left_sector, right_sector, left_size, right_size,
        own_stats, other_stats, thin, got, back,
    )
    return jnp.swapaxes(out, 1, 2), energy[0, 0]


def solution(mesh):
    fine = Mesh(mesh.devices.reshape(4, 2, 4, 4), ALL)
    row = ("y", "c")
    placed = (
        P(row, None, COL),
        P(row, COL, None, None),
        P(None, COL, None, None),
        P(),
        P(row),
        P(row, COL),
        P(),
        P(),
    )
    return jax.shard_map(
        local, mesh=fine, in_specs=placed, out_specs=(P(row, None, COL), P()), check_vma=False
    )
```

```python
import jax
import jax.numpy as jnp
from jax import lax
from jax.experimental import pallas as pl
from jax.experimental.pallas import tpu as pltpu
from jax.sharding import Mesh, PartitionSpec as P

ITERS = 2
LEFT_FLOPS = 15_000_000_000
TILE = 256
HALF = 128
TERMS = 16
FOLDED = 264
THIN = 32
SLOT = THIN + FOLDED
COL = ("x", "z")
ALL = ("y", "c", "x", "z")
SWAP = [(0, 1), (1, 0)]
UP = [(i, (i + 1) % 4) for i in range(4)]
DOWN = [(i, (i - 1) % 4) for i in range(4)]
f32 = jnp.float32
bf16 = jnp.bfloat16


def params(mib):
    return pltpu.CompilerParams(vmem_limit_bytes=mib * 1024 * 1024)


def hbm():
    return pl.BlockSpec(memory_space=pltpu.HBM)


def in_hbm(x):
    return pltpu.with_memory_space_constraint(x, pltpu.HBM)


def smem():
    return pl.BlockSpec(memory_space=pltpu.SMEM)


def cost(flops, nbytes):
    return pl.CostEstimate(flops=flops, transcendentals=0, bytes_accessed=nbytes)


def vmem():
    return pl.BlockSpec(memory_space=pltpu.VMEM)


def grids(rows, cols):
    i = lax.broadcasted_iota(jnp.int32, (rows, cols), 0)
    j = lax.broadcasted_iota(jnp.int32, (rows, cols), 1)
    return i, j


def fold_tile(tile):
    i, j = grids(HALF, HALF)
    a00 = tile[:HALF, :HALF]
    a11 = tile[HALF:, HALF:]
    fold = jnp.where(i >= j, a00, a11)
    diag = jnp.sum(jnp.where(i == j, a11, 0.0), axis=0, keepdims=True)
    return fold, tile[:HALF, HALF:], diag


def put_folded(dst, at, tile):
    fold, corner, diag = fold_tile(tile)
    dst[at, :HALF, :] = fold
    dst[at, HALF:TILE, :] = corner
    dst[at, TILE:, :] = jnp.broadcast_to(diag, (FOLDED - TILE, HALF))


def get_folded(src, at, row):
    return unfold_tile(
        src[at, row : row + HALF, :],
        src[at, row + HALF : row + TILE, :],
        src[at, row + TILE : row + TILE + 1, :],
    )


def unfold_tile(fold, corner, diag):
    i, j = grids(HALF, HALF)
    flip = fold.T
    a00 = jnp.where(i >= j, fold, flip)
    a11 = jnp.where(i == j, diag, jnp.where(i < j, fold, flip))
    top = jnp.concatenate([a00, corner], axis=1)
    low = jnp.concatenate([corner.T, a11], axis=1)
    return jnp.concatenate([top, low], axis=0)


def split(x):
    hi = x.astype(bf16)
    return hi, (x - hi.astype(f32)).astype(bf16)


def dot3(a_hi, a_lo, b_hi, b_lo):
    def dot(a, b):
        return jnp.dot(a, b, preferred_element_type=f32)

    return dot(a_hi, b_hi) + (dot(a_hi, b_lo) + dot(a_lo, b_hi))


def total(x):
    return jnp.sum(jnp.sum(x, axis=0, keepdims=True), axis=1, keepdims=True)


def inverse(norm):
    good = norm > 0.0
    return jnp.where(good, 1.0 / jnp.where(good, norm, 1.0), 0.0)


def put(stats, lane, value):
    _, j = grids(8, HALF)
    return jnp.where(j == lane, value, stats)


def fold_body(
    ids, left_env, right_env, keep, give, right, tiles, folded, others, sem_in, sem_out, sem_right
):
    def fetch(t, n):
        term = ids[1] if t else 1 - ids[1]
        at = 4 * t + n
        return pltpu.make_async_copy(left_env.at[n, term], tiles.at[at], sem_in.at[at])

    def fetch_right(n):
        return pltpu.make_async_copy(right_env.at[n, ids[1]], others.at[n], sem_right.at[n])

    def store(t, n):
        at = 4 * t + n
        dst = keep if t else give
        return pltpu.make_async_copy(folded.at[at], dst.at[n], sem_out.at[at])

    order = [(t, n) for t in range(2) for n in range(4)]
    for t, n in order:
        fetch(t, n).start()
    for n in range(8):
        fetch_right(n).start()
    right[8] = jnp.zeros((FOLDED, HALF), f32)
    for t, n in order:
        fetch(t, n).wait()
        put_folded(folded, 4 * t + n, tiles[4 * t + n])
        store(t, n).start()
    for n in range(8):
        fetch_right(n).wait()
        put_folded(right, n, others[n])
    for t, n in order:
        store(t, n).wait()


def fold(ids, left_env, right_env):
    return pl.pallas_call(
        fold_body,
        in_specs=[smem(), hbm(), hbm()],
        out_specs=[hbm(), hbm(), vmem()],
        out_shape=[pltpu.HBM((4, FOLDED, HALF), f32)] * 2
        + [jax.ShapeDtypeStruct((9, FOLDED, HALF), f32)],
        scratch_shapes=[
            pltpu.VMEM((8, TILE, TILE), f32),
            pltpu.VMEM((8, FOLDED, HALF), f32),
            pltpu.VMEM((8, TILE, TILE), f32),
            pltpu.SemaphoreType.DMA((8,)),
            pltpu.SemaphoreType.DMA((8,)),
            pltpu.SemaphoreType.DMA((8,)),
        ],
        compiler_params=params(10),
        cost_estimate=cost(1_000_000, 6_000_000),
        name="fold",
    )(ids, in_hbm(left_env), in_hbm(right_env))


def sector_of(ids, rsector, rsector_other, slot):
    return jnp.where(slot // 8 == ids[1], rsector[slot % 8], rsector_other[slot % 8])


def right_slots_body(
    ids, rsector, rsector_other, on, on_other, thin, thin_other, folded, out, cols, sem_out, sem_thin
):
    def store_thin(slot):
        return pltpu.make_async_copy(
            cols.at[slot], out.at[slot, pl.ds(0, THIN), :], sem_thin.at[slot]
        )

    def store(slot, sector):
        return pltpu.make_async_copy(
            folded.at[sector], out.at[slot, pl.ds(THIN, FOLDED), :], sem_out.at[slot]
        )

    for slot in range(TERMS):
        here = slot // 8 == ids[1]
        weight = jnp.where(here, on[slot % 8, ids[1]], on_other[slot % 8, ids[1]])
        sector = sector_of(ids, rsector, rsector_other, slot)
        store(slot, jnp.where(weight == 0, 8, sector)).start()
    for slot in range(TERMS):
        here = slot // 8 == ids[1]
        block = jnp.where(here, thin[slot % 8], thin_other[slot % 8])
        cols[slot, :16, :] = block[:, :HALF]
        cols[slot, 16:, :] = block[:, HALF:]
        store_thin(slot).start()
    for slot in range(TERMS):
        store_thin(slot).wait()
        store(slot, 0).wait()


def right_slots(ids, rsector, rsector_other, on, on_other, thin, thin_other, folded):
    return pl.pallas_call(
        right_slots_body,
        in_specs=[smem()] * 5 + [vmem()] * 3,
        out_specs=hbm(),
        out_shape=pltpu.HBM((TERMS, SLOT, HALF), f32),
        scratch_shapes=[
            pltpu.VMEM((TERMS, THIN, HALF), f32),
            pltpu.SemaphoreType.DMA((TERMS,)),
            pltpu.SemaphoreType.DMA((TERMS,)),
        ],
        compiler_params=params(6),
        cost_estimate=cost(4_000_000, 6_000_000),
        name="right_slots",
    )(ids, rsector, rsector_other, on, on_other, thin, thin_other, folded)


def left_slots_body(ids, left_sector, *refs):
    mine, theirs = refs[:2]
    above, far, below = refs[2:4], refs[4:6], refs[6:8]
    out, sem = refs[8:]

    def store(src, slot):
        return pltpu.make_async_copy(src, out.at[slot], sem.at[slot])

    def start(slot, carry):
        sector = left_sector[ids[0] * 16 + slot]
        home = sector // 4
        tile = sector % 4
        away = (home // 2 - ids[0] + 4) % 4
        same = home % 2 == ids[1]
        cases = [(same, mine, tile), (~same, theirs, tile)]
        cases = [(case & (away == 0), src, at) for case, src, at in cases]
        for n, half in ((0, same), (1, ~same)):
            cases.append((half & (away == 1), above[n], tile))
            cases.append((half & (away == 2), far[n], tile))
            cases.append((half & (away == 3), below[n], tile))
        for case, src, at in cases:

            @pl.when(case)
            def _():
                store(src.at[at], slot).start()

        return carry

    def finished(slot, carry):
        store(mine.at[0], slot).wait()
        return carry

    lax.fori_loop(0, TERMS, start, 0)
    lax.fori_loop(0, TERMS, finished, 0)


def left_slots(ids, left_sector, pieces):
    return pl.pallas_call(
        left_slots_body,
        in_specs=[smem(), smem()] + [vmem()] * 8,
        out_specs=hbm(),
        out_shape=pltpu.HBM((TERMS, FOLDED, HALF), f32),
        scratch_shapes=[pltpu.SemaphoreType.DMA((TERMS,))],
        compiler_params=params(8),
        cost_estimate=cost(LEFT_FLOPS, 4_000_000),
        name="left_slots",
    )(ids, left_sector, *pieces)


def live_sizes(ids, rsector, rsector_other, left_sector, left_size, right_size):
    live_left = left_size[left_sector[ids[0] * 16 + ids[2]]]
    live_right = right_size[sector_of(ids, rsector, rsector_other, ids[2])]
    return live_right, live_left


def mask_of(live_right, live_left):
    i, j = grids(TILE, TILE)
    return (i < live_right) & (j < live_left)


def first_body(
    ids, rsector, rsector_other, sector, lsize, rsize, slots,
    r_hi, r_lo, m_hi, m_lo, q1, stats, arrived, sem,
):
    live_right, live_left = live_sizes(ids, rsector, rsector_other, sector, lsize, rsize)

    def fetch(n):
        return pltpu.make_async_copy(slots.at[n], arrived.at[n], sem.at[n])

    for n in range(TERMS):
        fetch(n).start()
    for n in range(TERMS):
        fetch(n).wait()
        full = get_folded(arrived, n, THIN)
        hi, lo = split(full)
        r_hi[n * TILE : (n + 1) * TILE, :] = hi
        r_lo[n * TILE : (n + 1) * TILE, :] = lo
    block = jnp.concatenate(
        [
            jnp.concatenate([arrived[n, :16, :], arrived[n, 16:THIN, :]], axis=1)
            for n in range(TERMS)
        ],
        axis=0,
    )
    start = jnp.where(mask_of(live_right, live_left), block, 0.0)
    norm = jnp.sqrt(total(start * start))
    vec = start * inverse(norm)
    q1[...] = vec
    stats[...] = put(jnp.zeros((8, HALF), f32), 0, norm)
    q_hi, q_lo = split(vec)
    for n in range(TERMS):
        rows = pl.ds(n * TILE, TILE)
        hi, lo = split(dot3(r_hi[rows, :], r_lo[rows, :], q_hi, q_lo))
        m_hi[:, rows] = hi
        m_lo[:, rows] = lo


def first_vector(scalars, slots):
    return pl.pallas_call(
        first_body,
        in_specs=[smem()] * 6 + [hbm()],
        out_specs=[vmem()] * 6,
        out_shape=[
            jax.ShapeDtypeStruct((TERMS * TILE, TILE), bf16),
            jax.ShapeDtypeStruct((TERMS * TILE, TILE), bf16),
            jax.ShapeDtypeStruct((TILE, TERMS * TILE), bf16),
            jax.ShapeDtypeStruct((TILE, TERMS * TILE), bf16),
            jax.ShapeDtypeStruct((TILE, TILE), f32),
            jax.ShapeDtypeStruct((8, HALF), f32),
        ],
        scratch_shapes=[
            pltpu.VMEM((TERMS, SLOT, HALF), f32),
            pltpu.SemaphoreType.DMA((TERMS,)),
        ],
        compiler_params=params(10),
        cost_estimate=cost(1_700_000_000, 12_000_000),
        name="first_vector",
    )(*scalars, in_hbm(slots))


def image_one_body(arrived, m_hi, m_lo, l_hi, l_lo, part, here, sem):
    chunk = TERMS // 4

    def fetch(p, c):
        cols = pl.ds(c * chunk * TILE, chunk * TILE)
        src = (m_hi, m_lo)[p]
        return pltpu.make_async_copy(src.at[:, cols], here.at[p, :, cols], sem.at[p, c])

    for c in range(4):
        for p in range(2):
            fetch(p, c).start()
    for n in range(TERMS):
        hi, lo = split(get_folded(arrived, n, 0))
        l_hi[n * TILE : (n + 1) * TILE, :] = hi
        l_lo[n * TILE : (n + 1) * TILE, :] = lo
    acc = jnp.zeros((TILE, TILE), f32)
    for c in range(4):
        for p in range(2):
            fetch(p, c).wait()
        cols = pl.ds(c * chunk * TILE, chunk * TILE)
        acc = acc + dot3(here[0, :, cols], here[1, :, cols], l_hi[cols, :], l_lo[cols, :])
    part[...] = acc


def image_one(arrived, m_hi, m_lo):
    stack = jax.ShapeDtypeStruct((TERMS * TILE, TILE), bf16)
    return pl.pallas_call(
        image_one_body,
        in_specs=[vmem(), hbm(), hbm()],
        out_specs=[vmem()] * 3,
        out_shape=[stack, stack, jax.ShapeDtypeStruct((TILE, TILE), f32)],
        scratch_shapes=[
            pltpu.VMEM((2, TILE, TERMS * TILE), bf16),
            pltpu.SemaphoreType.DMA((2, 4)),
        ],
        compiler_params=params(10),
        cost_estimate=cost(1_700_000_000, 10_000_000),
        name="image_one",
    )(arrived, in_hbm(m_hi), in_hbm(m_lo))


def lanczos(image, last, before, beta):
    alpha = total(last * image)
    rest = image - alpha * last
    if before is not None:
        rest = rest - beta * before
    again = rest - total(last * rest) * last
    if before is not None:
        again = again - total(before * rest) * before
    norm = jnp.sqrt(total(again * again))
    return alpha, norm, again * inverse(norm)


def half_image(vec, r_hi, r_lo, l_hi, l_lo):
    q_hi, q_lo = split(vec)
    acc = jnp.zeros((TILE, TILE), f32)
    for n in range(TERMS):
        rows = pl.ds(n * TILE, TILE)
        hi, lo = split(dot3(r_hi[rows, :], r_lo[rows, :], q_hi, q_lo))
        acc = acc + dot3(hi, lo, l_hi[rows, :], l_lo[rows, :])
    return acc


def image_two_body(
    ids, rsector, rsector_other, sector, lsize, rsize,
    part_a, part_b, q1, stats_in, r_hi, r_lo, l_hi, l_lo,
    part, q2, stats,
):
    mask = mask_of(*live_sizes(ids, rsector, rsector_other, sector, lsize, rsize))
    image = jnp.where(mask, part_a[...] + part_b[...], 0.0)
    alpha, norm, vec = lanczos(image, q1[...], None, None)
    q2[...] = vec
    stats[...] = put(put(stats_in[...], 1, alpha), 2, norm)
    part[...] = half_image(vec, r_hi, r_lo, l_hi, l_lo)


def image_two(scalars, part, part_other, q1, stats, stacks):
    return pl.pallas_call(
        image_two_body,
        in_specs=[smem()] * 6 + [vmem()] * 8,
        out_specs=[vmem()] * 3,
        out_shape=[
            jax.ShapeDtypeStruct((TILE, TILE), f32),
            jax.ShapeDtypeStruct((TILE, TILE), f32),
            jax.ShapeDtypeStruct((8, HALF), f32),
        ],
        compiler_params=params(6),
        cost_estimate=cost(3_300_000_000, 9_000_000),
        name="image_two",
    )(*scalars, part, part_other, q1, stats, *stacks)


def image_three_body(
    ids, rsector, rsector_other, sector, lsize, rsize,
    part_a, part_b, q1, q2, stats_in, r_hi, r_lo, l_hi, l_lo, slots,
):
    mask = mask_of(*live_sizes(ids, rsector, rsector_other, sector, lsize, rsize))
    image = jnp.where(mask, part_a[...] + part_b[...], 0.0)
    i, j = grids(8, HALF)
    beta = total(jnp.where((j == 2) & (i == 0), stats_in[...], 0.0))
    alpha, norm, vec = lanczos(image, q2[...], q1[...], beta)
    pick = jnp.where(ids[1] == 0, q2[...], vec)
    for n in range(16):
        slots[n, :16, :] = pick[16 * n : 16 * n + 16]
    stats = put(put(stats_in[...], 3, alpha), 4, norm)
    alpha = total(vec * half_image(vec, r_hi, r_lo, l_hi, l_lo))
    stats = put(stats, 5, alpha)
    wide = jnp.concatenate([stats, jnp.zeros((8, HALF), f32)], axis=1)
    for n in range(16):
        slots[n, 16:24, :] = wide


def image_three(scalars, part, part_other, q1, q2, stats, stacks):
    return pl.pallas_call(
        image_three_body,
        in_specs=[smem()] * 6 + [vmem()] * 9,
        out_specs=vmem(),
        out_shape=jax.ShapeDtypeStruct((16, 24, TILE), f32),
        compiler_params=params(6),
        cost_estimate=cost(3_300_000_000, 9_000_000),
        name="image_three",
    )(*scalars, part, part_other, q1, q2, stats, *stacks)


def ritz_pair(norm, a1, b1, a2, b2, a3):
    def apply(x):
        return [a1 * x[0] + b1 * x[1], b1 * x[0] + a2 * x[1] + b2 * x[2], b2 * x[1] + a3 * x[2]]

    def dot(x, y):
        return jnp.sum(x[0] * y[0] + x[1] * y[1] + x[2] * y[2], axis=1, keepdims=True)

    zero = jnp.zeros_like(norm)
    start = [norm, zero, zero]
    image = apply(start)
    norm_sq = dot(start, start)
    correlation = dot(start, image)
    inv_norm = 1.0 / jnp.sqrt(norm_sq)
    basis = [x * inv_norm for x in start]
    applied = [x * inv_norm for x in image]
    ritz = correlation / norm_sq
    for _ in range(ITERS):
        residual = [x - ritz * y for x, y in zip(applied, basis)]
        res_sq = dot(residual, residual)
        length = jnp.sqrt(res_sq)
        fresh = [x / length for x in residual]
        fresh_applied = apply(fresh)
        curvature = dot(fresh, fresh_applied)
        half_gap = 0.5 * (ritz - curvature)
        root = jnp.sqrt(half_gap * half_gap + res_sq)
        lowest = 0.5 * (ritz + curvature) - root
        first = curvature - lowest
        pair = jnp.sqrt(first * first + res_sq)
        basis = [(first * x - length * y) / pair for x, y in zip(basis, fresh)]
        applied = [(first * x - length * y) / pair for x, y in zip(applied, fresh_applied)]
        ritz = lowest
    return basis, ritz


def finish_body(
    ids, sector, rsector, lsize, rsize, own_stats, other_stats, thin, got, back,
    out, energy, coef,
):
    _, lane = grids(64, HALF)
    stats = own_stats[...] + jnp.where(lane == 5, other_stats[...], 0.0)
    flip = jnp.concatenate([stats, jnp.zeros((64, HALF), f32)], axis=0).T
    norm, a1, b1, a2, b2, a3 = [flip[m : m + 1, :] for m in range(6)]
    basis, ritz = ritz_pair(norm, a1, b1, a2, b2, a3)
    energy[0, 0] = jnp.sum(ritz)
    scale = jnp.sqrt(jnp.full((1, HALF), 64 * TILE * TILE, f32))
    i, _ = grids(HALF, HALF)
    c1 = basis[0] * inverse(norm) * scale
    c2 = basis[1] * scale
    c3 = basis[2] * scale
    coef[...] = jnp.where(i == 0, c1, jnp.where(i == 1, c2, jnp.where(i == 2, c3, 0.0))).T
    core = ids[1]
    own = coef[pl.ds(pl.multiple_of(core * 8, 8), 8), :]
    jcol, irow = grids(16, TILE)
    for b in range(8):
        live_left = lsize[sector[ids[0] * 16 + core * 8 + b]]
        live_right = rsize[rsector[b]]
        live = (jcol + ids[2] * 16 < live_right) & (irow < live_left)
        keep = got[core * 8 + b, :16, :]
        recv = back[b, :16, :]
        second = jnp.where(core == 0, keep, recv)
        third = jnp.where(core == 0, recv, keep)
        out[b] = (
            own[b : b + 1, 0:1] * jnp.where(live, thin[b], 0.0)
            + own[b : b + 1, 1:2] * second
            + own[b : b + 1, 2:3] * third
        )


def finish(ids, sector, rsector, lsize, rsize, own_stats, other_stats, thin, got, back):
    return pl.pallas_call(
        finish_body,
        in_specs=[smem()] * 5 + [vmem()] * 5,
        out_specs=[vmem(), smem()],
        out_shape=[
            jax.ShapeDtypeStruct(thin.shape, f32),
            jax.ShapeDtypeStruct((1, 1), f32),
        ],
        scratch_shapes=[pltpu.VMEM((HALF, HALF), f32)],
        compiler_params=params(4),
        name="finish",
    )(ids, sector, rsector, lsize, rsize, own_stats, other_stats, thin, got, back)


def local(theta, left_env, right_env, left_sector, right_sector, term_on, left_size, right_size):
    plane = lax.axis_index("y").astype(jnp.int32)
    core = lax.axis_index("c").astype(jnp.int32)
    place = lax.axis_index(COL).astype(jnp.int32)
    ids = jnp.stack([plane, core, place])
    thin = jnp.swapaxes(theta, 1, 2)

    rsector_other = lax.ppermute(right_sector, "c", SWAP)
    on_other = lax.ppermute(term_on, "c", SWAP)
    thin_other = lax.ppermute(thin, "c", SWAP)

    mine, folded, right_folded = fold(ids, left_env, right_env)
    theirs = lax.ppermute(folded, "c", SWAP)
    below = [lax.ppermute(x, "y", UP) for x in (mine, theirs)]
    above = [lax.ppermute(x, "y", DOWN) for x in (mine, theirs)]
    far = [lax.ppermute(below[0], "y", UP), lax.ppermute(above[1], "y", DOWN)]

    slots = right_slots(
        ids, right_sector, rsector_other, term_on, on_other, thin, thin_other, right_folded
    )
    slots, theirs_now = lax.optimization_barrier((slots, theirs))
    arrived = lax.all_to_all(slots, COL, 0, 0, tiled=True)
    scalars = (ids, right_sector, rsector_other, left_sector, left_size, right_size)
    r_hi, r_lo, m_hi, m_lo, q1, stats = first_vector(scalars, arrived)

    pieces = [mine, theirs] + above + far + below
    left_sent = left_slots(ids, left_sector, pieces)
    left_arrived = lax.all_to_all(left_sent, COL, 0, 0, tiled=True)
    l_hi, l_lo, part = image_one(left_arrived, m_hi, m_lo)
    stacks = (r_hi, r_lo, l_hi, l_lo)
    part, q2, stats = image_two(scalars, part, lax.ppermute(part, "c", SWAP), q1, stats, stacks)
    sent = image_three(scalars, part, lax.ppermute(part, "c", SWAP), q1, q2, stats, stacks)

    got = lax.all_to_all(sent, COL, 0, 0, tiled=True)
    plane_stats = got[:, 16, :HALF]
    turned = [
        lax.ppermute(plane_stats, "y", [(i, (i + k) % 4) for i in range(4)]) for k in (1, 2, 3)
    ]
    back = lax.ppermute(lax.dynamic_slice_in_dim(got, (1 - core) * 8, 8), "c", SWAP)
    own_stats = jnp.concatenate([plane_stats] + turned)
    other_stats = lax.ppermute(own_stats, "c", SWAP)
    out, energy = finish(
        ids, left_sector, right_sector, left_size, right_size,
        own_stats, other_stats, thin, got, back,
    )
    return jnp.swapaxes(out, 1, 2), energy[0, 0]


def solution(mesh):
    fine = Mesh(mesh.devices.reshape(4, 2, 4, 4), ALL)
    row = ("y", "c")
    placed = (
        P(row, None, COL),
        P(row, COL, None, None),
        P(None, COL, None, None),
        P(),
        P(row),
        P(row, COL),
        P(),
        P(),
    )
    return jax.shard_map(
        local, mesh=fine, in_specs=placed, out_specs=(P(row, None, COL), P()), check_vma=False
    )
```

```python
import jax
import jax.numpy as jnp
from jax import lax
from jax.experimental import pallas as pl
from jax.experimental.pallas import tpu as pltpu
from jax.sharding import Mesh, PartitionSpec as P

ITERS = 2
LEFT_FLOPS = 15_000_000_000
TILE = 256
HALF = 128
TERMS = 16
FOLDED = 264
THIN = 32
SLOT = THIN + FOLDED
COL = ("x", "z")
ALL = ("y", "c", "x", "z")
SWAP = [(0, 1), (1, 0)]
UP = [(i, (i + 1) % 4) for i in range(4)]
DOWN = [(i, (i - 1) % 4) for i in range(4)]
f32 = jnp.float32
bf16 = jnp.bfloat16


def params(mib):
    return pltpu.CompilerParams(vmem_limit_bytes=mib * 1024 * 1024)


def hbm():
    return pl.BlockSpec(memory_space=pltpu.HBM)


def in_hbm(x):
    return pltpu.with_memory_space_constraint(x, pltpu.HBM)


def smem():
    return pl.BlockSpec(memory_space=pltpu.SMEM)


def cost(flops, nbytes):
    return pl.CostEstimate(flops=flops, transcendentals=0, bytes_accessed=nbytes)


def vmem():
    return pl.BlockSpec(memory_space=pltpu.VMEM)


def grids(rows, cols):
    i = lax.broadcasted_iota(jnp.int32, (rows, cols), 0)
    j = lax.broadcasted_iota(jnp.int32, (rows, cols), 1)
    return i, j


def fold_tile(tile):
    i, j = grids(HALF, HALF)
    a00 = tile[:HALF, :HALF]
    a11 = tile[HALF:, HALF:]
    fold = jnp.where(i >= j, a00, a11)
    diag = jnp.sum(jnp.where(i == j, a11, 0.0), axis=0, keepdims=True)
    return fold, tile[:HALF, HALF:], diag


def put_folded(dst, at, tile):
    fold, corner, diag = fold_tile(tile)
    dst[at, :HALF, :] = fold
    dst[at, HALF:TILE, :] = corner
    dst[at, TILE:, :] = jnp.broadcast_to(diag, (FOLDED - TILE, HALF))


def get_folded(src, at, row):
    return unfold_tile(
        src[at, row : row + HALF, :],
        src[at, row + HALF : row + TILE, :],
        src[at, row + TILE : row + TILE + 1, :],
    )


def unfold_tile(fold, corner, diag):
    i, j = grids(HALF, HALF)
    flip = fold.T
    a00 = jnp.where(i >= j, fold, flip)
    a11 = jnp.where(i == j, diag, jnp.where(i < j, fold, flip))
    top = jnp.concatenate([a00, corner], axis=1)
    low = jnp.concatenate([corner.T, a11], axis=1)
    return jnp.concatenate([top, low], axis=0)


def split(x):
    hi = x.astype(bf16)
    return hi, (x - hi.astype(f32)).astype(bf16)


def dot3(a_hi, a_lo, b_hi, b_lo):
    def dot(a, b):
        return jnp.dot(a, b, preferred_element_type=f32)

    return dot(a_hi, b_hi) + (dot(a_hi, b_lo) + dot(a_lo, b_hi))


def total(x):
    return jnp.sum(jnp.sum(x, axis=0, keepdims=True), axis=1, keepdims=True)


def inverse(norm):
    good = norm > 0.0
    return jnp.where(good, 1.0 / jnp.where(good, norm, 1.0), 0.0)


def put(stats, lane, value):
    _, j = grids(8, HALF)
    return jnp.where(j == lane, value, stats)


def fold_body(
    ids, left_env, right_env, keep, give, right, tiles, folded, others, sem_in, sem_out, sem_right
):
    def fetch(t):
        term = ids[1] if t else 1 - ids[1]
        return pltpu.make_async_copy(left_env.at[:, term], tiles.at[t], sem_in.at[t])

    def store(t):
        dst = keep if t else give
        return pltpu.make_async_copy(folded.at[t], dst, sem_out.at[t])

    rights = pltpu.make_async_copy(right_env.at[:, ids[1]], others, sem_right)
    for t in range(2):
        fetch(t).start()
    rights.start()
    right[8] = jnp.zeros((FOLDED, HALF), f32)
    for t in range(2):
        fetch(t).wait()
        for n in range(4):
            put_folded(folded.at[t], n, tiles[t, n])
        store(t).start()
    rights.wait()
    for n in range(8):
        put_folded(right, n, others[n])
    for t in range(2):
        store(t).wait()


def fold(ids, left_env, right_env):
    return pl.pallas_call(
        fold_body,
        in_specs=[smem(), hbm(), hbm()],
        out_specs=[hbm(), hbm(), vmem()],
        out_shape=[pltpu.HBM((4, FOLDED, HALF), f32)] * 2
        + [jax.ShapeDtypeStruct((9, FOLDED, HALF), f32)],
        scratch_shapes=[
            pltpu.VMEM((2, 4, TILE, TILE), f32),
            pltpu.VMEM((2, 4, FOLDED, HALF), f32),
            pltpu.VMEM((8, TILE, TILE), f32),
            pltpu.SemaphoreType.DMA((2,)),
            pltpu.SemaphoreType.DMA((2,)),
            pltpu.SemaphoreType.DMA(()),
        ],
        compiler_params=params(10),
        cost_estimate=cost(1_000_000, 6_000_000),
        name="fold",
    )(ids, in_hbm(left_env), in_hbm(right_env))


def sector_of(ids, rsector, rsector_other, slot):
    return jnp.where(slot // 8 == ids[1], rsector[slot % 8], rsector_other[slot % 8])


def right_slots_body(
    ids, rsector, rsector_other, on, on_other, thin, thin_other, folded, out, cols, sem
):
    for slot in range(TERMS):
        here = slot // 8 == ids[1]
        weight = jnp.where(here, on[slot % 8, ids[1]], on_other[slot % 8, ids[1]])
        sector = sector_of(ids, rsector, rsector_other, slot)
        src = folded.at[jnp.where(weight == 0, 8, sector)]
        pltpu.make_async_copy(src, out.at[slot, pl.ds(THIN, FOLDED), :], sem).start()
    for slot in range(TERMS):
        here = slot // 8 == ids[1]
        block = jnp.where(here, thin[slot % 8], thin_other[slot % 8])
        cols[slot, :16, :] = block[:, :HALF]
        cols[slot, 16:, :] = block[:, HALF:]
    pltpu.make_async_copy(cols, out.at[:, pl.ds(0, THIN), :], sem).start()
    pltpu.make_async_copy(out, out, sem).wait()


def right_slots(ids, rsector, rsector_other, on, on_other, thin, thin_other, folded):
    return pl.pallas_call(
        right_slots_body,
        in_specs=[smem()] * 5 + [vmem()] * 3,
        out_specs=hbm(),
        out_shape=pltpu.HBM((TERMS, SLOT, HALF), f32),
        scratch_shapes=[
            pltpu.VMEM((TERMS, THIN, HALF), f32),
            pltpu.SemaphoreType.DMA(()),
        ],
        compiler_params=params(6),
        cost_estimate=cost(4_000_000, 6_000_000),
        name="right_slots",
    )(ids, rsector, rsector_other, on, on_other, thin, thin_other, folded)


def left_slots_body(ids, left_sector, *refs):
    mine, theirs = refs[:2]
    above, far, below = refs[2:4], refs[4:6], refs[6:8]
    out, sem = refs[8:]

    def store(src, slot):
        return pltpu.make_async_copy(src, out.at[slot], sem)

    def start(slot, carry):
        sector = left_sector[ids[0] * 16 + slot]
        home = sector // 4
        tile = sector % 4
        away = (home // 2 - ids[0] + 4) % 4
        same = home % 2 == ids[1]
        cases = [(same, mine, tile), (~same, theirs, tile)]
        cases = [(case & (away == 0), src, at) for case, src, at in cases]
        for n, half in ((0, same), (1, ~same)):
            cases.append((half & (away == 1), above[n], tile))
            cases.append((half & (away == 2), far[n], tile))
            cases.append((half & (away == 3), below[n], tile))
        for case, src, at in cases:

            @pl.when(case)
            def _():
                store(src.at[at], slot).start()

        return carry

    lax.fori_loop(0, TERMS, start, 0)
    pltpu.make_async_copy(out, out, sem).wait()


def left_slots(ids, left_sector, pieces):
    return pl.pallas_call(
        left_slots_body,
        in_specs=[smem(), smem()] + [vmem()] * 8,
        out_specs=hbm(),
        out_shape=pltpu.HBM((TERMS, FOLDED, HALF), f32),
        scratch_shapes=[pltpu.SemaphoreType.DMA(())],
        compiler_params=params(8),
        cost_estimate=cost(LEFT_FLOPS, 4_000_000),
        name="left_slots",
    )(ids, left_sector, *pieces)


def live_sizes(ids, rsector, rsector_other, left_sector, left_size, right_size):
    live_left = left_size[left_sector[ids[0] * 16 + ids[2]]]
    live_right = right_size[sector_of(ids, rsector, rsector_other, ids[2])]
    return live_right, live_left


def mask_of(live_right, live_left):
    i, j = grids(TILE, TILE)
    return (i < live_right) & (j < live_left)


def first_body(
    ids, rsector, rsector_other, sector, lsize, rsize, slots,
    r_hi, r_lo, m_hi, m_lo, q1, stats, arrived, sem,
):
    live_right, live_left = live_sizes(ids, rsector, rsector_other, sector, lsize, rsize)

    def fetch(n):
        return pltpu.make_async_copy(slots.at[n], arrived.at[n], sem.at[n])

    for n in range(TERMS):
        fetch(n).start()
    for n in range(TERMS):
        fetch(n).wait()
        full = get_folded(arrived, n, THIN)
        hi, lo = split(full)
        r_hi[n * TILE : (n + 1) * TILE, :] = hi
        r_lo[n * TILE : (n + 1) * TILE, :] = lo
    block = jnp.concatenate(
        [
            jnp.concatenate([arrived[n, :16, :], arrived[n, 16:THIN, :]], axis=1)
            for n in range(TERMS)
        ],
        axis=0,
    )
    start = jnp.where(mask_of(live_right, live_left), block, 0.0)
    norm = jnp.sqrt(total(start * start))
    vec = start * inverse(norm)
    q1[...] = vec
    stats[...] = put(jnp.zeros((8, HALF), f32), 0, norm)
    q_hi, q_lo = split(vec)
    for n in range(TERMS):
        rows = pl.ds(n * TILE, TILE)
        hi, lo = split(dot3(r_hi[rows, :], r_lo[rows, :], q_hi, q_lo))
        m_hi[:, rows] = hi
        m_lo[:, rows] = lo


def first_vector(scalars, slots):
    return pl.pallas_call(
        first_body,
        in_specs=[smem()] * 6 + [hbm()],
        out_specs=[vmem()] * 6,
        out_shape=[
            jax.ShapeDtypeStruct((TERMS * TILE, TILE), bf16),
            jax.ShapeDtypeStruct((TERMS * TILE, TILE), bf16),
            jax.ShapeDtypeStruct((TILE, TERMS * TILE), bf16),
            jax.ShapeDtypeStruct((TILE, TERMS * TILE), bf16),
            jax.ShapeDtypeStruct((TILE, TILE), f32),
            jax.ShapeDtypeStruct((8, HALF), f32),
        ],
        scratch_shapes=[
            pltpu.VMEM((TERMS, SLOT, HALF), f32),
            pltpu.SemaphoreType.DMA((TERMS,)),
        ],
        compiler_params=params(10),
        cost_estimate=cost(1_700_000_000, 12_000_000),
        name="first_vector",
    )(*scalars, in_hbm(slots))


def image_one_body(arrived, m_hi, m_lo, l_hi, l_lo, part, here_hi, here_lo, sem):
    fetches = [
        pltpu.make_async_copy(m_hi, here_hi, sem.at[0]),
        pltpu.make_async_copy(m_lo, here_lo, sem.at[1]),
    ]
    for fetch in fetches:
        fetch.start()
    for n in range(TERMS):
        hi, lo = split(get_folded(arrived, n, 0))
        l_hi[n * TILE : (n + 1) * TILE, :] = hi
        l_lo[n * TILE : (n + 1) * TILE, :] = lo
    for fetch in fetches:
        fetch.wait()
    part[...] = dot3(here_hi[...], here_lo[...], l_hi[...], l_lo[...])


def image_one(arrived, m_hi, m_lo):
    stack = jax.ShapeDtypeStruct((TERMS * TILE, TILE), bf16)
    return pl.pallas_call(
        image_one_body,
        in_specs=[vmem(), hbm(), hbm()],
        out_specs=[vmem()] * 3,
        out_shape=[stack, stack, jax.ShapeDtypeStruct((TILE, TILE), f32)],
        scratch_shapes=[
            pltpu.VMEM((TILE, TERMS * TILE), bf16),
            pltpu.VMEM((TILE, TERMS * TILE), bf16),
            pltpu.SemaphoreType.DMA((2,)),
        ],
        compiler_params=params(10),
        cost_estimate=cost(1_700_000_000, 10_000_000),
        name="image_one",
    )(arrived, in_hbm(m_hi), in_hbm(m_lo))


def lanczos(image, last, before, beta):
    alpha = total(last * image)
    rest = image - alpha * last
    if before is not None:
        rest = rest - beta * before
    again = rest - total(last * rest) * last
    if before is not None:
        again = again - total(before * rest) * before
    norm = jnp.sqrt(total(again * again))
    return alpha, norm, again * inverse(norm)


def half_image(vec, r_hi, r_lo, l_hi, l_lo):
    q_hi, q_lo = split(vec)
    acc = jnp.zeros((TILE, TILE), f32)
    for n in range(TERMS):
        rows = pl.ds(n * TILE, TILE)
        hi, lo = split(dot3(r_hi[rows, :], r_lo[rows, :], q_hi, q_lo))
        acc = acc + dot3(hi, lo, l_hi[rows, :], l_lo[rows, :])
    return acc


def image_two_body(
    ids, rsector, rsector_other, sector, lsize, rsize,
    part_a, part_b, q1, stats_in, r_hi, r_lo, l_hi, l_lo,
    part, q2, stats,
):
    mask = mask_of(*live_sizes(ids, rsector, rsector_other, sector, lsize, rsize))
    image = jnp.where(mask, part_a[...] + part_b[...], 0.0)
    alpha, norm, vec = lanczos(image, q1[...], None, None)
    q2[...] = vec
    stats[...] = put(put(stats_in[...], 1, alpha), 2, norm)
    part[...] = half_image(vec, r_hi, r_lo, l_hi, l_lo)


def image_two(scalars, part, part_other, q1, stats, stacks):
    return pl.pallas_call(
        image_two_body,
        in_specs=[smem()] * 6 + [vmem()] * 8,
        out_specs=[vmem()] * 3,
        out_shape=[
            jax.ShapeDtypeStruct((TILE, TILE), f32),
            jax.ShapeDtypeStruct((TILE, TILE), f32),
            jax.ShapeDtypeStruct((8, HALF), f32),
        ],
        compiler_params=params(6),
        cost_estimate=cost(3_300_000_000, 9_000_000),
        name="image_two",
    )(*scalars, part, part_other, q1, stats, *stacks)


def image_three_body(
    ids, rsector, rsector_other, sector, lsize, rsize,
    part_a, part_b, q1, q2, stats_in, r_hi, r_lo, l_hi, l_lo, slots,
):
    mask = mask_of(*live_sizes(ids, rsector, rsector_other, sector, lsize, rsize))
    image = jnp.where(mask, part_a[...] + part_b[...], 0.0)
    i, j = grids(8, HALF)
    beta = total(jnp.where((j == 2) & (i == 0), stats_in[...], 0.0))
    alpha, norm, vec = lanczos(image, q2[...], q1[...], beta)
    pick = jnp.where(ids[1] == 0, q2[...], vec)
    for n in range(16):
        slots[n, :16, :] = pick[16 * n : 16 * n + 16]
    stats = put(put(stats_in[...], 3, alpha), 4, norm)
    alpha = total(vec * half_image(vec, r_hi, r_lo, l_hi, l_lo))
    stats = put(stats, 5, alpha)
    wide = jnp.concatenate([stats, jnp.zeros((8, HALF), f32)], axis=1)
    for n in range(16):
        slots[n, 16:24, :] = wide


def image_three(scalars, part, part_other, q1, q2, stats, stacks):
    return pl.pallas_call(
        image_three_body,
        in_specs=[smem()] * 6 + [vmem()] * 9,
        out_specs=vmem(),
        out_shape=jax.ShapeDtypeStruct((16, 24, TILE), f32),
        compiler_params=params(6),
        cost_estimate=cost(3_300_000_000, 9_000_000),
        name="image_three",
    )(*scalars, part, part_other, q1, q2, stats, *stacks)


def ritz_pair(norm, a1, b1, a2, b2, a3):
    def apply(x):
        return [a1 * x[0] + b1 * x[1], b1 * x[0] + a2 * x[1] + b2 * x[2], b2 * x[1] + a3 * x[2]]

    def dot(x, y):
        return jnp.sum(x[0] * y[0] + x[1] * y[1] + x[2] * y[2], axis=1, keepdims=True)

    zero = jnp.zeros_like(norm)
    start = [norm, zero, zero]
    image = apply(start)
    norm_sq = dot(start, start)
    correlation = dot(start, image)
    inv_norm = 1.0 / jnp.sqrt(norm_sq)
    basis = [x * inv_norm for x in start]
    applied = [x * inv_norm for x in image]
    ritz = correlation / norm_sq
    for _ in range(ITERS):
        residual = [x - ritz * y for x, y in zip(applied, basis)]
        res_sq = dot(residual, residual)
        length = jnp.sqrt(res_sq)
        fresh = [x / length for x in residual]
        fresh_applied = apply(fresh)
        curvature = dot(fresh, fresh_applied)
        half_gap = 0.5 * (ritz - curvature)
        root = jnp.sqrt(half_gap * half_gap + res_sq)
        lowest = 0.5 * (ritz + curvature) - root
        first = curvature - lowest
        pair = jnp.sqrt(first * first + res_sq)
        basis = [(first * x - length * y) / pair for x, y in zip(basis, fresh)]
        applied = [(first * x - length * y) / pair for x, y in zip(applied, fresh_applied)]
        ritz = lowest
    return basis, ritz


def finish_body(
    ids, sector, rsector, lsize, rsize, own_stats, other_stats, thin, got, back,
    out, energy, coef,
):
    _, lane = grids(64, HALF)
    stats = own_stats[...] + jnp.where(lane == 5, other_stats[...], 0.0)
    flip = jnp.concatenate([stats, jnp.zeros((64, HALF), f32)], axis=0).T
    norm, a1, b1, a2, b2, a3 = [flip[m : m + 1, :] for m in range(6)]
    basis, ritz = ritz_pair(norm, a1, b1, a2, b2, a3)
    energy[0, 0] = jnp.sum(ritz)
    scale = jnp.sqrt(jnp.full((1, HALF), 64 * TILE * TILE, f32))
    i, _ = grids(HALF, HALF)
    c1 = basis[0] * inverse(norm) * scale
    c2 = basis[1] * scale
    c3 = basis[2] * scale
    coef[...] = jnp.where(i == 0, c1, jnp.where(i == 1, c2, jnp.where(i == 2, c3, 0.0))).T
    core = ids[1]
    own = coef[pl.ds(pl.multiple_of(core * 8, 8), 8), :]
    jcol, irow = grids(16, TILE)
    for b in range(8):
        live_left = lsize[sector[ids[0] * 16 + core * 8 + b]]
        live_right = rsize[rsector[b]]
        live = (jcol + ids[2] * 16 < live_right) & (irow < live_left)
        keep = got[core * 8 + b, :16, :]
        recv = back[b, :16, :]
        second = jnp.where(core == 0, keep, recv)
        third = jnp.where(core == 0, recv, keep)
        out[b] = (
            own[b : b + 1, 0:1] * jnp.where(live, thin[b], 0.0)
            + own[b : b + 1, 1:2] * second
            + own[b : b + 1, 2:3] * third
        )


def finish(ids, sector, rsector, lsize, rsize, own_stats, other_stats, thin, got, back):
    return pl.pallas_call(
        finish_body,
        in_specs=[smem()] * 5 + [vmem()] * 5,
        out_specs=[vmem(), smem()],
        out_shape=[
            jax.ShapeDtypeStruct(thin.shape, f32),
            jax.ShapeDtypeStruct((1, 1), f32),
        ],
        scratch_shapes=[pltpu.VMEM((HALF, HALF), f32)],
        compiler_params=params(4),
        name="finish",
    )(ids, sector, rsector, lsize, rsize, own_stats, other_stats, thin, got, back)


def local(theta, left_env, right_env, left_sector, right_sector, term_on, left_size, right_size):
    plane = lax.axis_index("y").astype(jnp.int32)
    core = lax.axis_index("c").astype(jnp.int32)
    place = lax.axis_index(COL).astype(jnp.int32)
    ids = jnp.stack([plane, core, place])
    thin = jnp.swapaxes(theta, 1, 2)

    rsector_other = lax.ppermute(right_sector, "c", SWAP)
    on_other = lax.ppermute(term_on, "c", SWAP)
    thin_other = lax.ppermute(thin, "c", SWAP)

    mine, folded, right_folded = fold(ids, left_env, right_env)
    theirs = lax.ppermute(folded, "c", SWAP)
    below = [lax.ppermute(x, "y", UP) for x in (mine, theirs)]
    above = [lax.ppermute(x, "y", DOWN) for x in (mine, theirs)]
    far = [lax.ppermute(below[0], "y", UP), lax.ppermute(above[1], "y", DOWN)]

    slots = right_slots(
        ids, right_sector, rsector_other, term_on, on_other, thin, thin_other, right_folded
    )
    slots, theirs_now = lax.optimization_barrier((slots, theirs))
    arrived = lax.all_to_all(slots, COL, 0, 0, tiled=True)
    scalars = (ids, right_sector, rsector_other, left_sector, left_size, right_size)
    r_hi, r_lo, m_hi, m_lo, q1, stats = first_vector(scalars, arrived)

    pieces = [mine, theirs] + above + far + below
    left_sent = left_slots(ids, left_sector, pieces)
    left_arrived = lax.all_to_all(left_sent, COL, 0, 0, tiled=True)
    l_hi, l_lo, part = image_one(left_arrived, m_hi, m_lo)
    stacks = (r_hi, r_lo, l_hi, l_lo)
    part, q2, stats = image_two(scalars, part, lax.ppermute(part, "c", SWAP), q1, stats, stacks)
    sent = image_three(scalars, part, lax.ppermute(part, "c", SWAP), q1, q2, stats, stacks)

    got = lax.all_to_all(sent, COL, 0, 0, tiled=True)
    plane_stats = got[:, 16, :HALF]
    turned = [
        lax.ppermute(plane_stats, "y", [(i, (i + k) % 4) for i in range(4)]) for k in (1, 2, 3)
    ]
    back = lax.ppermute(lax.dynamic_slice_in_dim(got, (1 - core) * 8, 8), "c", SWAP)
    own_stats = jnp.concatenate([plane_stats] + turned)
    other_stats = lax.ppermute(own_stats, "c", SWAP)
    out, energy = finish(
        ids, left_sector, right_sector, left_size, right_size,
        own_stats, other_stats, thin, got, back,
    )
    return jnp.swapaxes(out, 1, 2), energy[0, 0]


def solution(mesh):
    fine = Mesh(mesh.devices.reshape(4, 2, 4, 4), ALL)
    row = ("y", "c")
    placed = (
        P(row, None, COL),
        P(row, COL, None, None),
        P(None, COL, None, None),
        P(),
        P(row),
        P(row, COL),
        P(),
        P(),
    )
    return jax.shard_map(
        local, mesh=fine, in_specs=placed, out_specs=(P(row, None, COL), P()), check_vma=False
    )
```

```python
import jax
import jax.numpy as jnp
from jax import lax
from jax.experimental import pallas as pl
from jax.experimental.pallas import tpu as pltpu
from jax.sharding import Mesh, PartitionSpec as P

ITERS = 2
LEFT_FLOPS = 15_000_000_000
TILE = 256
HALF = 128
TERMS = 16
FOLDED = 264
THIN = 32
SLOT = THIN + FOLDED
COL = ("x", "z")
ALL = ("y", "c", "x", "z")
SWAP = [(0, 1), (1, 0)]
UP = [(i, (i + 1) % 4) for i in range(4)]
DOWN = [(i, (i - 1) % 4) for i in range(4)]
f32 = jnp.float32
bf16 = jnp.bfloat16


def params(mib):
    return pltpu.CompilerParams(vmem_limit_bytes=mib * 1024 * 1024)


def hbm():
    return pl.BlockSpec(memory_space=pltpu.HBM)


def in_hbm(x):
    return pltpu.with_memory_space_constraint(x, pltpu.HBM)


def smem():
    return pl.BlockSpec(memory_space=pltpu.SMEM)


def cost(flops, nbytes):
    return pl.CostEstimate(flops=flops, transcendentals=0, bytes_accessed=nbytes)


def vmem():
    return pl.BlockSpec(memory_space=pltpu.VMEM)


def grids(rows, cols):
    i = lax.broadcasted_iota(jnp.int32, (rows, cols), 0)
    j = lax.broadcasted_iota(jnp.int32, (rows, cols), 1)
    return i, j


def fold_tile(tile):
    i, j = grids(HALF, HALF)
    a00 = tile[:HALF, :HALF]
    a11 = tile[HALF:, HALF:]
    fold = jnp.where(i >= j, a00, a11)
    diag = jnp.sum(jnp.where(i == j, a11, 0.0), axis=0, keepdims=True)
    return fold, tile[:HALF, HALF:], diag


def put_folded(dst, at, tile):
    fold, corner, diag = fold_tile(tile)
    dst[at, :HALF, :] = fold
    dst[at, HALF:TILE, :] = corner
    dst[at, TILE:, :] = jnp.broadcast_to(diag, (FOLDED - TILE, HALF))


def get_folded(src, at, row):
    return unfold_tile(
        src[at, row : row + HALF, :],
        src[at, row + HALF : row + TILE, :],
        src[at, row + TILE : row + TILE + 1, :],
    )


def unfold_tile(fold, corner, diag):
    i, j = grids(HALF, HALF)
    flip = fold.T
    a00 = jnp.where(i >= j, fold, flip)
    a11 = jnp.where(i == j, diag, jnp.where(i < j, fold, flip))
    top = jnp.concatenate([a00, corner], axis=1)
    low = jnp.concatenate([corner.T, a11], axis=1)
    return jnp.concatenate([top, low], axis=0)


def split(x):
    hi = x.astype(bf16)
    return hi, (x - hi.astype(f32)).astype(bf16)


def dot3(a_hi, a_lo, b_hi, b_lo):
    def dot(a, b):
        return jnp.dot(a, b, preferred_element_type=f32)

    return dot(a_hi, b_hi) + (dot(a_hi, b_lo) + dot(a_lo, b_hi))


def total(x):
    return jnp.sum(jnp.sum(x, axis=0, keepdims=True), axis=1, keepdims=True)


def inverse(norm):
    good = norm > 0.0
    return jnp.where(good, 1.0 / jnp.where(good, norm, 1.0), 0.0)


def put(stats, lane, value):
    _, j = grids(8, HALF)
    return jnp.where(j == lane, value, stats)


def fold_body(
    ids, left_env, right_env, keep, give, right, tiles, folded, others, sem_in, sem_out, sem_right
):
    def fetch(t):
        term = ids[1] if t else 1 - ids[1]
        return pltpu.make_async_copy(left_env.at[:, term], tiles.at[t], sem_in.at[t])

    def store(t):
        dst = keep if t else give
        return pltpu.make_async_copy(folded.at[t], dst, sem_out.at[t])

    rights = pltpu.make_async_copy(right_env.at[:, ids[1]], others, sem_right)
    for t in range(2):
        fetch(t).start()
    rights.start()
    right[8] = jnp.zeros((FOLDED, HALF), f32)
    for t in range(2):
        fetch(t).wait()
        for n in range(4):
            put_folded(folded.at[t], n, tiles[t, n])
        store(t).start()
    rights.wait()
    for n in range(8):
        put_folded(right, n, others[n])
    for t in range(2):
        store(t).wait()


def fold(ids, left_env, right_env):
    return pl.pallas_call(
        fold_body,
        in_specs=[smem(), hbm(), hbm()],
        out_specs=[hbm(), hbm(), vmem()],
        out_shape=[pltpu.HBM((4, FOLDED, HALF), f32)] * 2
        + [jax.ShapeDtypeStruct((9, FOLDED, HALF), f32)],
        scratch_shapes=[
            pltpu.VMEM((2, 4, TILE, TILE), f32),
            pltpu.VMEM((2, 4, FOLDED, HALF), f32),
            pltpu.VMEM((8, TILE, TILE), f32),
            pltpu.SemaphoreType.DMA((2,)),
            pltpu.SemaphoreType.DMA((2,)),
            pltpu.SemaphoreType.DMA(()),
        ],
        compiler_params=params(10),
        cost_estimate=cost(1_000_000, 6_000_000),
        name="fold",
    )(ids, in_hbm(left_env), in_hbm(right_env))


def sector_of(ids, rsector, rsector_other, slot):
    return jnp.where(slot // 8 == ids[1], rsector[slot % 8], rsector_other[slot % 8])


def right_slots_body(
    ids, rsector, rsector_other, on, on_other, thin, thin_other, folded, out, cols, sem
):
    for slot in range(TERMS):
        here = slot // 8 == ids[1]
        weight = jnp.where(here, on[slot % 8, ids[1]], on_other[slot % 8, ids[1]])
        sector = sector_of(ids, rsector, rsector_other, slot)
        src = folded.at[jnp.where(weight == 0, 8, sector)]
        pltpu.make_async_copy(src, out.at[slot, pl.ds(THIN, FOLDED), :], sem).start()
    for slot in range(TERMS):
        here = slot // 8 == ids[1]
        block = jnp.where(here, thin[slot % 8], thin_other[slot % 8])
        cols[slot, :16, :] = block[:, :HALF]
        cols[slot, 16:, :] = block[:, HALF:]
    pltpu.make_async_copy(cols, out.at[:, pl.ds(0, THIN), :], sem).start()
    pltpu.make_async_copy(out, out, sem).wait()


def right_slots(ids, rsector, rsector_other, on, on_other, thin, thin_other, folded):
    return pl.pallas_call(
        right_slots_body,
        in_specs=[smem()] * 5 + [vmem()] * 3,
        out_specs=hbm(),
        out_shape=pltpu.HBM((TERMS, SLOT, HALF), f32),
        scratch_shapes=[
            pltpu.VMEM((TERMS, THIN, HALF), f32),
            pltpu.SemaphoreType.DMA(()),
        ],
        compiler_params=params(6),
        cost_estimate=cost(4_000_000, 6_000_000),
        name="right_slots",
    )(ids, rsector, rsector_other, on, on_other, thin, thin_other, folded)


def left_slots_body(ids, left_sector, *refs):
    mine, theirs = refs[:2]
    above, far, below = refs[2:4], refs[4:6], refs[6:8]
    out, sem = refs[8:]

    def store(src, slot):
        return pltpu.make_async_copy(src, out.at[slot], sem)

    def start(slot, carry):
        sector = left_sector[ids[0] * 16 + slot]
        home = sector // 4
        tile = sector % 4
        away = (home // 2 - ids[0] + 4) % 4
        same = home % 2 == ids[1]
        cases = [(same, mine, tile), (~same, theirs, tile)]
        cases = [(case & (away == 0), src, at) for case, src, at in cases]
        for n, half in ((0, same), (1, ~same)):
            cases.append((half & (away == 1), above[n], tile))
            cases.append((half & (away == 2), far[n], tile))
            cases.append((half & (away == 3), below[n], tile))
        for case, src, at in cases:

            @pl.when(case)
            def _():
                store(src.at[at], slot).start()

        return carry

    lax.fori_loop(0, TERMS, start, 0)
    pltpu.make_async_copy(out, out, sem).wait()


def left_slots(ids, left_sector, pieces):
    return pl.pallas_call(
        left_slots_body,
        in_specs=[smem(), smem()] + [vmem()] * 8,
        out_specs=hbm(),
        out_shape=pltpu.HBM((TERMS, FOLDED, HALF), f32),
        scratch_shapes=[pltpu.SemaphoreType.DMA(())],
        compiler_params=params(8),
        cost_estimate=cost(LEFT_FLOPS, 4_000_000),
        name="left_slots",
    )(ids, left_sector, *pieces)


def live_sizes(ids, rsector, rsector_other, left_sector, left_size, right_size):
    live_left = left_size[left_sector[ids[0] * 16 + ids[2]]]
    live_right = right_size[sector_of(ids, rsector, rsector_other, ids[2])]
    return live_right, live_left


def mask_of(live_right, live_left):
    i, j = grids(TILE, TILE)
    return (i < live_right) & (j < live_left)


def first_body(
    ids, rsector, rsector_other, sector, lsize, rsize, slots,
    r_hi, r_lo, m_hi, m_lo, q1, stats, arrived, sem,
):
    live_right, live_left = live_sizes(ids, rsector, rsector_other, sector, lsize, rsize)

    def fetch(n):
        return pltpu.make_async_copy(slots.at[n], arrived.at[n], sem.at[n])

    for n in range(TERMS):
        fetch(n).start()
    for n in range(TERMS):
        fetch(n).wait()
        full = get_folded(arrived, n, THIN)
        hi, lo = split(full)
        r_hi[n * TILE : (n + 1) * TILE, :] = hi
        r_lo[n * TILE : (n + 1) * TILE, :] = lo
    block = jnp.concatenate(
        [
            jnp.concatenate([arrived[n, :16, :], arrived[n, 16:THIN, :]], axis=1)
            for n in range(TERMS)
        ],
        axis=0,
    )
    start = jnp.where(mask_of(live_right, live_left), block, 0.0)
    norm = jnp.sqrt(total(start * start))
    vec = start * inverse(norm)
    q1[...] = vec
    stats[...] = put(jnp.zeros((8, HALF), f32), 0, norm)
    q_hi, q_lo = split(vec)
    for n in range(TERMS):
        rows = pl.ds(n * TILE, TILE)
        hi, lo = split(dot3(r_hi[rows, :], r_lo[rows, :], q_hi, q_lo))
        m_hi[:, rows] = hi
        m_lo[:, rows] = lo


def first_vector(scalars, slots):
    return pl.pallas_call(
        first_body,
        in_specs=[smem()] * 6 + [hbm()],
        out_specs=[vmem()] * 6,
        out_shape=[
            jax.ShapeDtypeStruct((TERMS * TILE, TILE), bf16),
            jax.ShapeDtypeStruct((TERMS * TILE, TILE), bf16),
            jax.ShapeDtypeStruct((TILE, TERMS * TILE), bf16),
            jax.ShapeDtypeStruct((TILE, TERMS * TILE), bf16),
            jax.ShapeDtypeStruct((TILE, TILE), f32),
            jax.ShapeDtypeStruct((8, HALF), f32),
        ],
        scratch_shapes=[
            pltpu.VMEM((TERMS, SLOT, HALF), f32),
            pltpu.SemaphoreType.DMA((TERMS,)),
        ],
        compiler_params=params(10),
        cost_estimate=cost(1_700_000_000, 12_000_000),
        name="first_vector",
    )(*scalars, in_hbm(slots))


def image_one_body(arrived, m_hi, m_lo, l_hi, l_lo, part, here_hi, here_lo, sem):
    fetches = [
        pltpu.make_async_copy(m_hi, here_hi, sem.at[0]),
        pltpu.make_async_copy(m_lo, here_lo, sem.at[1]),
    ]
    for fetch in fetches:
        fetch.start()
    for n in range(TERMS):
        hi, lo = split(get_folded(arrived, n, 0))
        l_hi[n * TILE : (n + 1) * TILE, :] = hi
        l_lo[n * TILE : (n + 1) * TILE, :] = lo
    for fetch in fetches:
        fetch.wait()
    part[...] = dot3(here_hi[...], here_lo[...], l_hi[...], l_lo[...])


def image_one(arrived, m_hi, m_lo):
    stack = jax.ShapeDtypeStruct((TERMS * TILE, TILE), bf16)
    return pl.pallas_call(
        image_one_body,
        in_specs=[vmem(), hbm(), hbm()],
        out_specs=[vmem()] * 3,
        out_shape=[stack, stack, jax.ShapeDtypeStruct((TILE, TILE), f32)],
        scratch_shapes=[
            pltpu.VMEM((TILE, TERMS * TILE), bf16),
            pltpu.VMEM((TILE, TERMS * TILE), bf16),
            pltpu.SemaphoreType.DMA((2,)),
        ],
        compiler_params=params(10),
        cost_estimate=cost(1_700_000_000, 10_000_000),
        name="image_one",
    )(arrived, in_hbm(m_hi), in_hbm(m_lo))


def lanczos(image, last, before, beta):
    alpha = total(last * image)
    rest = image - alpha * last
    if before is not None:
        rest = rest - beta * before
    again = rest - total(last * rest) * last
    if before is not None:
        again = again - total(before * rest) * before
    norm = jnp.sqrt(total(again * again))
    return alpha, norm, again * inverse(norm)


def half_image(vec, r_hi, r_lo, l_hi, l_lo):
    q_hi, q_lo = split(vec)
    acc = jnp.zeros((TILE, TILE), f32)
    for n in range(TERMS):
        rows = pl.ds(n * TILE, TILE)
        hi, lo = split(dot3(r_hi[rows, :], r_lo[rows, :], q_hi, q_lo))
        acc = acc + dot3(hi, lo, l_hi[rows, :], l_lo[rows, :])
    return acc


def image_two_body(
    ids, rsector, rsector_other, sector, lsize, rsize,
    part_a, part_b, q1, stats_in, r_hi, r_lo, l_hi, l_lo,
    part, q2, stats,
):
    mask = mask_of(*live_sizes(ids, rsector, rsector_other, sector, lsize, rsize))
    image = jnp.where(mask, part_a[...] + part_b[...], 0.0)
    alpha, norm, vec = lanczos(image, q1[...], None, None)
    q2[...] = vec
    stats[...] = put(put(stats_in[...], 1, alpha), 2, norm)
    part[...] = half_image(vec, r_hi, r_lo, l_hi, l_lo)


def image_two(scalars, part, part_other, q1, stats, stacks):
    return pl.pallas_call(
        image_two_body,
        in_specs=[smem()] * 6 + [vmem()] * 8,
        out_specs=[vmem()] * 3,
        out_shape=[
            jax.ShapeDtypeStruct((TILE, TILE), f32),
            jax.ShapeDtypeStruct((TILE, TILE), f32),
            jax.ShapeDtypeStruct((8, HALF), f32),
        ],
        compiler_params=params(6),
        cost_estimate=cost(3_300_000_000, 9_000_000),
        name="image_two",
    )(*scalars, part, part_other, q1, stats, *stacks)


def image_three_body(
    ids, rsector, rsector_other, sector, lsize, rsize,
    part_a, part_b, q1, q2, stats_in, r_hi, r_lo, l_hi, l_lo, slots,
):
    mask = mask_of(*live_sizes(ids, rsector, rsector_other, sector, lsize, rsize))
    image = jnp.where(mask, part_a[...] + part_b[...], 0.0)
    i, j = grids(8, HALF)
    beta = total(jnp.where((j == 2) & (i == 0), stats_in[...], 0.0))
    alpha, norm, vec = lanczos(image, q2[...], q1[...], beta)
    pick = jnp.where(ids[1] == 0, q2[...], vec)
    for n in range(16):
        slots[n, :16, :] = pick[16 * n : 16 * n + 16, :HALF]
        slots[n, 16:THIN, :] = pick[16 * n : 16 * n + 16, HALF:]
    stats = put(put(stats_in[...], 3, alpha), 4, norm)
    alpha = total(vec * half_image(vec, r_hi, r_lo, l_hi, l_lo))
    stats = put(stats, 5, alpha)
    for n in range(16):
        slots[n, THIN:, :] = stats


def image_three(scalars, part, part_other, q1, q2, stats, stacks):
    return pl.pallas_call(
        image_three_body,
        in_specs=[smem()] * 6 + [vmem()] * 9,
        out_specs=vmem(),
        out_shape=jax.ShapeDtypeStruct((16, THIN + 8, HALF), f32),
        compiler_params=params(6),
        cost_estimate=cost(3_300_000_000, 9_000_000),
        name="image_three",
    )(*scalars, part, part_other, q1, q2, stats, *stacks)


def ritz_pair(norm, a1, b1, a2, b2, a3):
    def apply(x):
        return [a1 * x[0] + b1 * x[1], b1 * x[0] + a2 * x[1] + b2 * x[2], b2 * x[1] + a3 * x[2]]

    def dot(x, y):
        return jnp.sum(x[0] * y[0] + x[1] * y[1] + x[2] * y[2], axis=1, keepdims=True)

    zero = jnp.zeros_like(norm)
    start = [norm, zero, zero]
    image = apply(start)
    norm_sq = dot(start, start)
    correlation = dot(start, image)
    inv_norm = 1.0 / jnp.sqrt(norm_sq)
    basis = [x * inv_norm for x in start]
    applied = [x * inv_norm for x in image]
    ritz = correlation / norm_sq
    for _ in range(ITERS):
        residual = [x - ritz * y for x, y in zip(applied, basis)]
        res_sq = dot(residual, residual)
        length = jnp.sqrt(res_sq)
        fresh = [x / length for x in residual]
        fresh_applied = apply(fresh)
        curvature = dot(fresh, fresh_applied)
        half_gap = 0.5 * (ritz - curvature)
        root = jnp.sqrt(half_gap * half_gap + res_sq)
        lowest = 0.5 * (ritz + curvature) - root
        first = curvature - lowest
        pair = jnp.sqrt(first * first + res_sq)
        basis = [(first * x - length * y) / pair for x, y in zip(basis, fresh)]
        applied = [(first * x - length * y) / pair for x, y in zip(applied, fresh_applied)]
        ritz = lowest
    return basis, ritz


def finish_body(
    ids, sector, rsector, lsize, rsize, own_stats, other_stats, thin, got, back,
    out, energy, coef,
):
    _, lane = grids(64, HALF)
    stats = own_stats[...] + jnp.where(lane == 5, other_stats[...], 0.0)
    flip = jnp.concatenate([stats, jnp.zeros((64, HALF), f32)], axis=0).T
    norm, a1, b1, a2, b2, a3 = [flip[m : m + 1, :] for m in range(6)]
    basis, ritz = ritz_pair(norm, a1, b1, a2, b2, a3)
    energy[0, 0] = jnp.sum(ritz)
    scale = jnp.sqrt(jnp.full((1, HALF), 64 * TILE * TILE, f32))
    i, _ = grids(HALF, HALF)
    c1 = basis[0] * inverse(norm) * scale
    c2 = basis[1] * scale
    c3 = basis[2] * scale
    coef[...] = jnp.where(i == 0, c1, jnp.where(i == 1, c2, jnp.where(i == 2, c3, 0.0))).T
    core = ids[1]
    own = coef[pl.ds(pl.multiple_of(core * 8, 8), 8), :]
    jcol, irow = grids(16, TILE)
    for b in range(8):
        live_left = lsize[sector[ids[0] * 16 + core * 8 + b]]
        live_right = rsize[rsector[b]]
        live = (jcol + ids[2] * 16 < live_right) & (irow < live_left)
        at = core * 8 + b
        keep = jnp.concatenate([got[at, :16, :], got[at, 16:THIN, :]], axis=1)
        recv = jnp.concatenate([back[b, :16, :], back[b, 16:THIN, :]], axis=1)
        second = jnp.where(core == 0, keep, recv)
        third = jnp.where(core == 0, recv, keep)
        out[b] = (
            own[b : b + 1, 0:1] * jnp.where(live, thin[b], 0.0)
            + own[b : b + 1, 1:2] * second
            + own[b : b + 1, 2:3] * third
        )


def finish(ids, sector, rsector, lsize, rsize, own_stats, other_stats, thin, got, back):
    return pl.pallas_call(
        finish_body,
        in_specs=[smem()] * 5 + [vmem()] * 5,
        out_specs=[vmem(), smem()],
        out_shape=[
            jax.ShapeDtypeStruct(thin.shape, f32),
            jax.ShapeDtypeStruct((1, 1), f32),
        ],
        scratch_shapes=[pltpu.VMEM((HALF, HALF), f32)],
        compiler_params=params(4),
        name="finish",
    )(ids, sector, rsector, lsize, rsize, own_stats, other_stats, thin, got, back)


def local(theta, left_env, right_env, left_sector, right_sector, term_on, left_size, right_size):
    plane = lax.axis_index("y").astype(jnp.int32)
    core = lax.axis_index("c").astype(jnp.int32)
    place = lax.axis_index(COL).astype(jnp.int32)
    ids = jnp.stack([plane, core, place])
    thin = jnp.swapaxes(theta, 1, 2)

    rsector_other = lax.ppermute(right_sector, "c", SWAP)
    on_other = lax.ppermute(term_on, "c", SWAP)
    thin_other = lax.ppermute(thin, "c", SWAP)

    mine, folded, right_folded = fold(ids, left_env, right_env)
    theirs = lax.ppermute(folded, "c", SWAP)
    theirs, rsector_other, on_other, thin_other = lax.optimization_barrier(
        (theirs, rsector_other, on_other, thin_other)
    )
    below = [lax.ppermute(x, "y", UP) for x in (mine, theirs)]
    above = [lax.ppermute(x, "y", DOWN) for x in (mine, theirs)]
    far = [lax.ppermute(below[0], "y", UP), lax.ppermute(above[1], "y", DOWN)]

    slots = right_slots(
        ids, right_sector, rsector_other, term_on, on_other, thin, thin_other, right_folded
    )
    slots, theirs_now = lax.optimization_barrier((slots, theirs))
    arrived = lax.all_to_all(slots, COL, 0, 0, tiled=True)
    scalars = (ids, right_sector, rsector_other, left_sector, left_size, right_size)
    r_hi, r_lo, m_hi, m_lo, q1, stats = first_vector(scalars, arrived)

    pieces = [mine, theirs] + above + far + below
    left_sent = left_slots(ids, left_sector, pieces)
    left_arrived = lax.all_to_all(left_sent, COL, 0, 0, tiled=True)
    l_hi, l_lo, part = image_one(left_arrived, m_hi, m_lo)
    stacks = (r_hi, r_lo, l_hi, l_lo)
    part, q2, stats = image_two(scalars, part, lax.ppermute(part, "c", SWAP), q1, stats, stacks)
    sent = image_three(scalars, part, lax.ppermute(part, "c", SWAP), q1, q2, stats, stacks)

    got = lax.all_to_all(sent, COL, 0, 0, tiled=True)
    plane_stats = got[:, THIN, :]
    turned = [
        lax.ppermute(plane_stats, "y", [(i, (i + k) % 4) for i in range(4)]) for k in (1, 2, 3)
    ]
    give = lax.dynamic_slice(got, ((1 - core) * 8, 0, 0), (8, THIN, HALF))
    back = lax.ppermute(give, "c", SWAP)
    own_stats = jnp.concatenate([plane_stats] + turned)
    other_stats = lax.ppermute(own_stats, "c", SWAP)
    out, energy = finish(
        ids, left_sector, right_sector, left_size, right_size,
        own_stats, other_stats, thin, got, back,
    )
    return jnp.swapaxes(out, 1, 2), energy[0, 0]


def solution(mesh):
    fine = Mesh(mesh.devices.reshape(4, 2, 4, 4), ALL)
    row = ("y", "c")
    placed = (
        P(row, None, COL),
        P(row, COL, None, None),
        P(None, COL, None, None),
        P(),
        P(row),
        P(row, COL),
        P(),
        P(),
    )
    return jax.shard_map(
        local, mesh=fine, in_specs=placed, out_specs=(P(row, None, COL), P()), check_vma=False
    )
```

```python
import jax
import jax.numpy as jnp
from jax import lax
from jax.experimental import pallas as pl
from jax.experimental.pallas import tpu as pltpu
from jax.sharding import Mesh, PartitionSpec as P

ITERS = 2
LEFT_FLOPS = 15_000_000_000
TILE = 256
HALF = 128
TERMS = 16
FOLDED = 264
THIN = 32
SLOT = THIN + FOLDED
COL = ("x", "z")
ALL = ("y", "c", "x", "z")
SWAP = [(0, 1), (1, 0)]
UP = [(i, (i + 1) % 4) for i in range(4)]
DOWN = [(i, (i - 1) % 4) for i in range(4)]
f32 = jnp.float32
bf16 = jnp.bfloat16


def params(mib):
    return pltpu.CompilerParams(vmem_limit_bytes=mib * 1024 * 1024)


def hbm():
    return pl.BlockSpec(memory_space=pltpu.HBM)


def in_hbm(x):
    return pltpu.with_memory_space_constraint(x, pltpu.HBM)


def smem():
    return pl.BlockSpec(memory_space=pltpu.SMEM)


def cost(flops, nbytes):
    return pl.CostEstimate(flops=flops, transcendentals=0, bytes_accessed=nbytes)


def vmem():
    return pl.BlockSpec(memory_space=pltpu.VMEM)


def grids(rows, cols):
    i = lax.broadcasted_iota(jnp.int32, (rows, cols), 0)
    j = lax.broadcasted_iota(jnp.int32, (rows, cols), 1)
    return i, j


def fold_tile(tile):
    i, j = grids(HALF, HALF)
    a00 = tile[:HALF, :HALF]
    a11 = tile[HALF:, HALF:]
    fold = jnp.where(i >= j, a00, a11)
    diag = jnp.sum(jnp.where(i == j, a11, 0.0), axis=0, keepdims=True)
    return fold, tile[:HALF, HALF:], diag


def put_folded(dst, at, tile):
    fold, corner, diag = fold_tile(tile)
    dst[at, :HALF, :] = fold
    dst[at, HALF:TILE, :] = corner
    dst[at, TILE:, :] = jnp.broadcast_to(diag, (FOLDED - TILE, HALF))


def get_folded(src, at, row):
    return unfold_tile(
        src[at, row : row + HALF, :],
        src[at, row + HALF : row + TILE, :],
        src[at, row + TILE : row + TILE + 1, :],
    )


def unfold_tile(fold, corner, diag):
    i, j = grids(HALF, HALF)
    flip = fold.T
    a00 = jnp.where(i >= j, fold, flip)
    a11 = jnp.where(i == j, diag, jnp.where(i < j, fold, flip))
    top = jnp.concatenate([a00, corner], axis=1)
    low = jnp.concatenate([corner.T, a11], axis=1)
    return jnp.concatenate([top, low], axis=0)


def split(x):
    hi = x.astype(bf16)
    return hi, (x - hi.astype(f32)).astype(bf16)


def dot(a, b):
    return jnp.dot(a, b, preferred_element_type=f32)


def dot3(a_hi, a_lo, b_hi, b_lo):
    return dot(a_hi, b_hi) + (dot(a_hi, b_lo) + dot(a_lo, b_hi))


def total(x):
    return jnp.sum(jnp.sum(x, axis=0, keepdims=True), axis=1, keepdims=True)


def inverse(norm):
    good = norm > 0.0
    return jnp.where(good, 1.0 / jnp.where(good, norm, 1.0), 0.0)


def put(stats, lane, value):
    _, j = grids(8, HALF)
    return jnp.where(j == lane, value, stats)


def fold_body(
    ids, left_env, right_env, keep, give, right, tiles, folded, others, sem_in, sem_out, sem_right
):
    def fetch(t):
        term = ids[1] if t else 1 - ids[1]
        return pltpu.make_async_copy(left_env.at[:, term], tiles.at[t], sem_in.at[t])

    def store(t):
        dst = keep if t else give
        return pltpu.make_async_copy(folded.at[t], dst, sem_out.at[t])

    rights = pltpu.make_async_copy(right_env.at[:, ids[1]], others, sem_right)
    for t in range(2):
        fetch(t).start()
    rights.start()
    right[8] = jnp.zeros((FOLDED, HALF), f32)
    for t in range(2):
        fetch(t).wait()
        for n in range(4):
            put_folded(folded.at[t], n, tiles[t, n])
        store(t).start()
    rights.wait()
    for n in range(8):
        put_folded(right, n, others[n])
    for t in range(2):
        store(t).wait()


def fold(ids, left_env, right_env):
    return pl.pallas_call(
        fold_body,
        in_specs=[smem(), hbm(), hbm()],
        out_specs=[hbm(), hbm(), vmem()],
        out_shape=[pltpu.HBM((4, FOLDED, HALF), f32)] * 2
        + [jax.ShapeDtypeStruct((9, FOLDED, HALF), f32)],
        scratch_shapes=[
            pltpu.VMEM((2, 4, TILE, TILE), f32),
            pltpu.VMEM((2, 4, FOLDED, HALF), f32),
            pltpu.VMEM((8, TILE, TILE), f32),
            pltpu.SemaphoreType.DMA((2,)),
            pltpu.SemaphoreType.DMA((2,)),
            pltpu.SemaphoreType.DMA(()),
        ],
        compiler_params=params(10),
        cost_estimate=cost(1_000_000, 6_000_000),
        name="fold",
    )(ids, in_hbm(left_env), in_hbm(right_env))


def sector_of(ids, rsector, rsector_other, slot):
    return jnp.where(slot // 8 == ids[1], rsector[slot % 8], rsector_other[slot % 8])


def right_slots_body(
    ids, rsector, rsector_other, on, on_other, thin, thin_other, folded, out, cols, sem
):
    for slot in range(TERMS):
        here = slot // 8 == ids[1]
        weight = jnp.where(here, on[slot % 8, ids[1]], on_other[slot % 8, ids[1]])
        sector = sector_of(ids, rsector, rsector_other, slot)
        src = folded.at[jnp.where(weight == 0, 8, sector)]
        pltpu.make_async_copy(src, out.at[slot, pl.ds(THIN, FOLDED), :], sem).start()
    for slot in range(TERMS):
        here = slot // 8 == ids[1]
        block = jnp.where(here, thin[slot % 8], thin_other[slot % 8])
        cols[slot, :16, :] = block[:, :HALF]
        cols[slot, 16:, :] = block[:, HALF:]
    pltpu.make_async_copy(cols, out.at[:, pl.ds(0, THIN), :], sem).start()
    pltpu.make_async_copy(out, out, sem).wait()


def right_slots(ids, rsector, rsector_other, on, on_other, thin, thin_other, folded):
    return pl.pallas_call(
        right_slots_body,
        in_specs=[smem()] * 5 + [vmem()] * 3,
        out_specs=hbm(),
        out_shape=pltpu.HBM((TERMS, SLOT, HALF), f32),
        scratch_shapes=[
            pltpu.VMEM((TERMS, THIN, HALF), f32),
            pltpu.SemaphoreType.DMA(()),
        ],
        compiler_params=params(6),
        cost_estimate=cost(4_000_000, 6_000_000),
        name="right_slots",
    )(ids, rsector, rsector_other, on, on_other, thin, thin_other, folded)


def left_slots_body(ids, left_sector, *refs):
    mine, theirs = refs[:2]
    above, far, below = refs[2:4], refs[4:6], refs[6:8]
    out, sem = refs[8:]

    def store(src, slot):
        return pltpu.make_async_copy(src, out.at[slot], sem)

    def start(slot, carry):
        sector = left_sector[ids[0] * 16 + slot]
        home = sector // 4
        tile = sector % 4
        away = (home // 2 - ids[0] + 4) % 4
        same = home % 2 == ids[1]
        cases = [(same, mine, tile), (~same, theirs, tile)]
        cases = [(case & (away == 0), src, at) for case, src, at in cases]
        for n, half in ((0, same), (1, ~same)):
            cases.append((half & (away == 1), above[n], tile))
            cases.append((half & (away == 2), far[n], tile))
            cases.append((half & (away == 3), below[n], tile))
        for case, src, at in cases:

            @pl.when(case)
            def _():
                store(src.at[at], slot).start()

        return carry

    lax.fori_loop(0, TERMS, start, 0)
    pltpu.make_async_copy(out, out, sem).wait()


def left_slots(ids, left_sector, pieces):
    return pl.pallas_call(
        left_slots_body,
        in_specs=[smem(), smem()] + [vmem()] * 8,
        out_specs=hbm(),
        out_shape=pltpu.HBM((TERMS, FOLDED, HALF), f32),
        scratch_shapes=[pltpu.SemaphoreType.DMA(())],
        compiler_params=params(8),
        cost_estimate=cost(LEFT_FLOPS, 4_000_000),
        name="left_slots",
    )(ids, left_sector, *pieces)


def live_sizes(ids, rsector, rsector_other, left_sector, left_size, right_size):
    live_left = left_size[left_sector[ids[0] * 16 + ids[2]]]
    live_right = right_size[sector_of(ids, rsector, rsector_other, ids[2])]
    return live_right, live_left


def mask_of(live_right, live_left):
    i, j = grids(TILE, TILE)
    return (i < live_right) & (j < live_left)


def first_body(
    ids, rsector, rsector_other, sector, lsize, rsize, slots,
    r_hi, r_lo, m_hi, m_lo, q1, stats, arrived, sem,
):
    live_right, live_left = live_sizes(ids, rsector, rsector_other, sector, lsize, rsize)

    def fetch(n):
        return pltpu.make_async_copy(slots.at[n], arrived.at[n], sem.at[n])

    for n in range(TERMS):
        fetch(n).start()
    for n in range(TERMS):
        fetch(n).wait()
        full = get_folded(arrived, n, THIN)
        hi, lo = split(full)
        r_hi[n * TILE : (n + 1) * TILE, :] = hi
        r_lo[n * TILE : (n + 1) * TILE, :] = lo
    block = jnp.concatenate(
        [
            jnp.concatenate([arrived[n, :16, :], arrived[n, 16:THIN, :]], axis=1)
            for n in range(TERMS)
        ],
        axis=0,
    )
    start = jnp.where(mask_of(live_right, live_left), block, 0.0)
    norm = jnp.sqrt(total(start * start))
    vec = start * inverse(norm)
    q1[...] = vec
    stats[...] = put(jnp.zeros((8, HALF), f32), 0, norm)
    q_hi, q_lo = split(vec)
    for n in range(TERMS):
        rows = pl.ds(n * TILE, TILE)
        hi, lo = split(dot3(r_hi[rows, :], r_lo[rows, :], q_hi, q_lo))
        m_hi[:, rows] = hi
        m_lo[:, rows] = lo


def first_vector(scalars, slots):
    return pl.pallas_call(
        first_body,
        in_specs=[smem()] * 6 + [hbm()],
        out_specs=[vmem()] * 6,
        out_shape=[
            jax.ShapeDtypeStruct((TERMS * TILE, TILE), bf16),
            jax.ShapeDtypeStruct((TERMS * TILE, TILE), bf16),
            jax.ShapeDtypeStruct((TILE, TERMS * TILE), bf16),
            jax.ShapeDtypeStruct((TILE, TERMS * TILE), bf16),
            jax.ShapeDtypeStruct((TILE, TILE), f32),
            jax.ShapeDtypeStruct((8, HALF), f32),
        ],
        scratch_shapes=[
            pltpu.VMEM((TERMS, SLOT, HALF), f32),
            pltpu.SemaphoreType.DMA((TERMS,)),
        ],
        compiler_params=params(10),
        cost_estimate=cost(1_700_000_000, 12_000_000),
        name="first_vector",
    )(*scalars, in_hbm(slots))


def image_one_body(arrived, m_hi, m_lo, l_hi, l_lo, part, here_hi, here_lo, sem):
    high = pltpu.make_async_copy(m_hi, here_hi, sem.at[0])
    low = pltpu.make_async_copy(m_lo, here_lo, sem.at[1])
    high.start()
    for n in range(TERMS):
        hi, lo = split(get_folded(arrived, n, 0))
        l_hi[n * TILE : (n + 1) * TILE, :] = hi
        l_lo[n * TILE : (n + 1) * TILE, :] = lo
    high.wait()
    low.start()
    acc = dot(here_hi[...], l_lo[...]) + dot(here_hi[...], l_hi[...])
    low.wait()
    part[...] = acc + dot(here_lo[...], l_hi[...])


def image_one(arrived, m_hi, m_lo):
    stack = jax.ShapeDtypeStruct((TERMS * TILE, TILE), bf16)
    return pl.pallas_call(
        image_one_body,
        in_specs=[vmem(), hbm(), hbm()],
        out_specs=[vmem()] * 3,
        out_shape=[stack, stack, jax.ShapeDtypeStruct((TILE, TILE), f32)],
        scratch_shapes=[
            pltpu.VMEM((TILE, TERMS * TILE), bf16),
            pltpu.VMEM((TILE, TERMS * TILE), bf16),
            pltpu.SemaphoreType.DMA((2,)),
        ],
        compiler_params=params(10),
        cost_estimate=cost(1_700_000_000, 10_000_000),
        name="image_one",
    )(arrived, in_hbm(m_hi), in_hbm(m_lo))


def lanczos(image, last, before, beta):
    alpha = total(last * image)
    rest = image - alpha * last
    if before is not None:
        rest = rest - beta * before
    again = rest - total(last * rest) * last
    if before is not None:
        again = again - total(before * rest) * before
    norm = jnp.sqrt(total(again * again))
    return alpha, norm, again * inverse(norm)


def half_image(vec, r_hi, r_lo, l_hi, l_lo):
    q_hi, q_lo = split(vec)
    acc = jnp.zeros((TILE, TILE), f32)
    for n in range(TERMS):
        rows = pl.ds(n * TILE, TILE)
        hi, lo = split(dot3(r_hi[rows, :], r_lo[rows, :], q_hi, q_lo))
        acc = acc + dot3(hi, lo, l_hi[rows, :], l_lo[rows, :])
    return acc


def image_two_body(
    ids, rsector, rsector_other, sector, lsize, rsize,
    part_a, part_b, q1, stats_in, r_hi, r_lo, l_hi, l_lo,
    part, q2, stats,
):
    mask = mask_of(*live_sizes(ids, rsector, rsector_other, sector, lsize, rsize))
    image = jnp.where(mask, part_a[...] + part_b[...], 0.0)
    alpha, norm, vec = lanczos(image, q1[...], None, None)
    q2[...] = vec
    stats[...] = put(put(stats_in[...], 1, alpha), 2, norm)
    part[...] = half_image(vec, r_hi, r_lo, l_hi, l_lo)


def image_two(scalars, part, part_other, q1, stats, stacks):
    return pl.pallas_call(
        image_two_body,
        in_specs=[smem()] * 6 + [vmem()] * 8,
        out_specs=[vmem()] * 3,
        out_shape=[
            jax.ShapeDtypeStruct((TILE, TILE), f32),
            jax.ShapeDtypeStruct((TILE, TILE), f32),
            jax.ShapeDtypeStruct((8, HALF), f32),
        ],
        compiler_params=params(6),
        cost_estimate=cost(3_300_000_000, 9_000_000),
        name="image_two",
    )(*scalars, part, part_other, q1, stats, *stacks)


def image_three_body(
    ids, rsector, rsector_other, sector, lsize, rsize,
    part_a, part_b, q1, q2, stats_in, r_hi, r_lo, l_hi, l_lo, out, cols, tail, sem,
):
    mask = mask_of(*live_sizes(ids, rsector, rsector_other, sector, lsize, rsize))
    image = jnp.where(mask, part_a[...] + part_b[...], 0.0)
    i, j = grids(8, HALF)
    beta = total(jnp.where((j == 2) & (i == 0), stats_in[...], 0.0))
    alpha, norm, vec = lanczos(image, q2[...], q1[...], beta)
    pick = jnp.where(ids[1] == 0, q2[...], vec)
    for n in range(16):
        cols[n, :16, :] = pick[16 * n : 16 * n + 16, :HALF]
        cols[n, 16:, :] = pick[16 * n : 16 * n + 16, HALF:]
    columns = pltpu.make_async_copy(cols, out.at[:, pl.ds(0, THIN), :], sem.at[0])
    columns.start()
    stats = put(put(stats_in[...], 3, alpha), 4, norm)
    alpha = total(vec * half_image(vec, r_hi, r_lo, l_hi, l_lo))
    stats = put(stats, 5, alpha)
    for n in range(16):
        tail[n] = stats
    numbers = pltpu.make_async_copy(tail, out.at[:, pl.ds(THIN, 8), :], sem.at[1])
    numbers.start()
    numbers.wait()
    columns.wait()


def image_three(scalars, part, part_other, q1, q2, stats, stacks):
    return pl.pallas_call(
        image_three_body,
        in_specs=[smem()] * 6 + [vmem()] * 9,
        out_specs=hbm(),
        out_shape=pltpu.HBM((16, THIN + 8, HALF), f32),
        scratch_shapes=[
            pltpu.VMEM((16, THIN, HALF), f32),
            pltpu.VMEM((16, 8, HALF), f32),
            pltpu.SemaphoreType.DMA((2,)),
        ],
        compiler_params=params(6),
        cost_estimate=cost(3_300_000_000, 9_000_000),
        name="image_three",
    )(*scalars, part, part_other, q1, q2, stats, *stacks)


def ritz_pair(norm, a1, b1, a2, b2, a3):
    def apply(x):
        return [a1 * x[0] + b1 * x[1], b1 * x[0] + a2 * x[1] + b2 * x[2], b2 * x[1] + a3 * x[2]]

    def dot(x, y):
        return jnp.sum(x[0] * y[0] + x[1] * y[1] + x[2] * y[2], axis=1, keepdims=True)

    zero = jnp.zeros_like(norm)
    start = [norm, zero, zero]
    image = apply(start)
    norm_sq = dot(start, start)
    correlation = dot(start, image)
    inv_norm = 1.0 / jnp.sqrt(norm_sq)
    basis = [x * inv_norm for x in start]
    applied = [x * inv_norm for x in image]
    ritz = correlation / norm_sq
    for _ in range(ITERS):
        residual = [x - ritz * y for x, y in zip(applied, basis)]
        res_sq = dot(residual, residual)
        length = jnp.sqrt(res_sq)
        fresh = [x / length for x in residual]
        fresh_applied = apply(fresh)
        curvature = dot(fresh, fresh_applied)
        half_gap = 0.5 * (ritz - curvature)
        root = jnp.sqrt(half_gap * half_gap + res_sq)
        lowest = 0.5 * (ritz + curvature) - root
        first = curvature - lowest
        pair = jnp.sqrt(first * first + res_sq)
        basis = [(first * x - length * y) / pair for x, y in zip(basis, fresh)]
        applied = [(first * x - length * y) / pair for x, y in zip(applied, fresh_applied)]
        ritz = lowest
    return basis, ritz


def finish_body(
    ids, sector, rsector, lsize, rsize, own_stats, other_stats, thin, got, back,
    out, energy, coef,
):
    _, lane = grids(64, HALF)
    stats = own_stats[...] + jnp.where(lane == 5, other_stats[...], 0.0)
    flip = jnp.concatenate([stats, jnp.zeros((64, HALF), f32)], axis=0).T
    norm, a1, b1, a2, b2, a3 = [flip[m : m + 1, :] for m in range(6)]
    basis, ritz = ritz_pair(norm, a1, b1, a2, b2, a3)
    energy[0, 0] = jnp.sum(ritz)
    scale = jnp.sqrt(jnp.full((1, HALF), 64 * TILE * TILE, f32))
    i, _ = grids(HALF, HALF)
    c1 = basis[0] * inverse(norm) * scale
    c2 = basis[1] * scale
    c3 = basis[2] * scale
    coef[...] = jnp.where(i == 0, c1, jnp.where(i == 1, c2, jnp.where(i == 2, c3, 0.0))).T
    core = ids[1]
    own = coef[pl.ds(pl.multiple_of(core * 8, 8), 8), :]
    jcol, irow = grids(16, TILE)
    for b in range(8):
        live_left = lsize[sector[ids[0] * 16 + core * 8 + b]]
        live_right = rsize[rsector[b]]
        live = (jcol + ids[2] * 16 < live_right) & (irow < live_left)
        at = core * 8 + b
        keep = jnp.concatenate([got[at, :16, :], got[at, 16:THIN, :]], axis=1)
        recv = jnp.concatenate([back[b, :16, :], back[b, 16:THIN, :]], axis=1)
        second = jnp.where(core == 0, keep, recv)
        third = jnp.where(core == 0, recv, keep)
        out[b] = (
            own[b : b + 1, 0:1] * jnp.where(live, thin[b], 0.0)
            + own[b : b + 1, 1:2] * second
            + own[b : b + 1, 2:3] * third
        )


def finish(ids, sector, rsector, lsize, rsize, own_stats, other_stats, thin, got, back):
    return pl.pallas_call(
        finish_body,
        in_specs=[smem()] * 5 + [vmem()] * 5,
        out_specs=[vmem(), smem()],
        out_shape=[
            jax.ShapeDtypeStruct(thin.shape, f32),
            jax.ShapeDtypeStruct((1, 1), f32),
        ],
        scratch_shapes=[pltpu.VMEM((HALF, HALF), f32)],
        compiler_params=params(4),
        name="finish",
    )(ids, sector, rsector, lsize, rsize, own_stats, other_stats, thin, got, back)


def local(theta, left_env, right_env, left_sector, right_sector, term_on, left_size, right_size):
    plane = lax.axis_index("y").astype(jnp.int32)
    core = lax.axis_index("c").astype(jnp.int32)
    place = lax.axis_index(COL).astype(jnp.int32)
    ids = jnp.stack([plane, core, place])
    thin = jnp.swapaxes(theta, 1, 2)

    rsector_other = lax.ppermute(right_sector, "c", SWAP)
    on_other = lax.ppermute(term_on, "c", SWAP)
    thin_other = lax.ppermute(thin, "c", SWAP)

    mine, folded, right_folded = fold(ids, left_env, right_env)
    theirs = lax.ppermute(folded, "c", SWAP)
    theirs, rsector_other, on_other, thin_other = lax.optimization_barrier(
        (theirs, rsector_other, on_other, thin_other)
    )
    below = [lax.ppermute(x, "y", UP) for x in (mine, theirs)]
    above = [lax.ppermute(x, "y", DOWN) for x in (mine, theirs)]
    far = [lax.ppermute(below[0], "y", UP), lax.ppermute(above[1], "y", DOWN)]

    slots = right_slots(
        ids, right_sector, rsector_other, term_on, on_other, thin, thin_other, right_folded
    )
    slots, theirs_now = lax.optimization_barrier((slots, theirs))
    arrived = lax.all_to_all(slots, COL, 0, 0, tiled=True)
    scalars = (ids, right_sector, rsector_other, left_sector, left_size, right_size)
    r_hi, r_lo, m_hi, m_lo, q1, stats = first_vector(scalars, arrived)

    pieces = [mine, theirs] + above + far + below
    left_sent = left_slots(ids, left_sector, pieces)
    left_arrived = lax.all_to_all(left_sent, COL, 0, 0, tiled=True)
    l_hi, l_lo, part = image_one(left_arrived, m_hi, m_lo)
    stacks = (r_hi, r_lo, l_hi, l_lo)
    part, q2, stats = image_two(scalars, part, lax.ppermute(part, "c", SWAP), q1, stats, stacks)
    sent = image_three(scalars, part, lax.ppermute(part, "c", SWAP), q1, q2, stats, stacks)

    got = lax.all_to_all(sent, COL, 0, 0, tiled=True)
    plane_stats = got[:, THIN, :]
    turned = [
        lax.ppermute(plane_stats, "y", [(i, (i + k) % 4) for i in range(4)]) for k in (1, 2, 3)
    ]
    give = lax.dynamic_slice(got, ((1 - core) * 8, 0, 0), (8, THIN, HALF))
    back = lax.ppermute(give, "c", SWAP)
    own_stats = jnp.concatenate([plane_stats] + turned)
    other_stats = lax.ppermute(own_stats, "c", SWAP)
    out, energy = finish(
        ids, left_sector, right_sector, left_size, right_size,
        own_stats, other_stats, thin, got, back,
    )
    return jnp.swapaxes(out, 1, 2), energy[0, 0]


def solution(mesh):
    fine = Mesh(mesh.devices.reshape(4, 2, 4, 4), ALL)
    row = ("y", "c")
    placed = (
        P(row, None, COL),
        P(row, COL, None, None),
        P(None, COL, None, None),
        P(),
        P(row),
        P(row, COL),
        P(),
        P(),
    )
    return jax.shard_map(
        local, mesh=fine, in_specs=placed, out_specs=(P(row, None, COL), P()), check_vma=False
    )
```

```python
import jax
import jax.numpy as jnp
from jax import lax
from jax.experimental import pallas as pl
from jax.experimental.pallas import tpu as pltpu
from jax.sharding import Mesh, PartitionSpec as P

ITERS = 2
LEFT_FLOPS = 15_000_000_000
TILE = 256
HALF = 128
TERMS = 16
FOLDED = 264
THIN = 16
COLS = 32
SLOT = THIN + FOLDED
COL = ("x", "z")
ALL = ("y", "c", "x", "z")
SWAP = [(0, 1), (1, 0)]
UP = [(i, (i + 1) % 4) for i in range(4)]
DOWN = [(i, (i - 1) % 4) for i in range(4)]
f32 = jnp.float32
bf16 = jnp.bfloat16


def params(mib):
    return pltpu.CompilerParams(vmem_limit_bytes=mib * 1024 * 1024)


def hbm():
    return pl.BlockSpec(memory_space=pltpu.HBM)


def in_hbm(x):
    return pltpu.with_memory_space_constraint(x, pltpu.HBM)


def smem():
    return pl.BlockSpec(memory_space=pltpu.SMEM)


def cost(flops, nbytes):
    return pl.CostEstimate(flops=flops, transcendentals=0, bytes_accessed=nbytes)


def vmem():
    return pl.BlockSpec(memory_space=pltpu.VMEM)


def grids(rows, cols):
    i = lax.broadcasted_iota(jnp.int32, (rows, cols), 0)
    j = lax.broadcasted_iota(jnp.int32, (rows, cols), 1)
    return i, j


def fold_tile(tile):
    i, j = grids(HALF, HALF)
    a00 = tile[:HALF, :HALF]
    a11 = tile[HALF:, HALF:]
    fold = jnp.where(i >= j, a00, a11)
    diag = jnp.sum(jnp.where(i == j, a11, 0.0), axis=0, keepdims=True)
    return fold, tile[:HALF, HALF:], diag


def put_folded(dst, at, tile):
    fold, corner, diag = fold_tile(tile)
    dst[at, :HALF, :] = fold
    dst[at, HALF:TILE, :] = corner
    dst[at, TILE:, :] = jnp.broadcast_to(diag, (FOLDED - TILE, HALF))


def get_folded(src, at, row):
    return unfold_tile(
        src[at, row : row + HALF, :],
        src[at, row + HALF : row + TILE, :],
        src[at, row + TILE : row + TILE + 1, :],
    )


def unfold_tile(fold, corner, diag):
    i, j = grids(HALF, HALF)
    flip = fold.T
    a00 = jnp.where(i >= j, fold, flip)
    a11 = jnp.where(i == j, diag, jnp.where(i < j, fold, flip))
    top = jnp.concatenate([a00, corner], axis=1)
    low = jnp.concatenate([corner.T, a11], axis=1)
    return jnp.concatenate([top, low], axis=0)


def split(x):
    hi = x.astype(bf16)
    return hi, (x - hi.astype(f32)).astype(bf16)


def dot3(a_hi, a_lo, b_hi, b_lo):
    def dot(a, b):
        return jnp.dot(a, b, preferred_element_type=f32)

    return dot(a_hi, b_hi) + (dot(a_hi, b_lo) + dot(a_lo, b_hi))


def total(x):
    return jnp.sum(jnp.sum(x, axis=0, keepdims=True), axis=1, keepdims=True)


def inverse(norm):
    good = norm > 0.0
    return jnp.where(good, 1.0 / jnp.where(good, norm, 1.0), 0.0)


def put(stats, lane, value):
    _, j = grids(8, HALF)
    return jnp.where(j == lane, value, stats)


def fold_body(
    ids, left_env, right_env, keep, give, right, tiles, folded, others, sem_in, sem_out, sem_right
):
    def fetch(t):
        term = ids[1] if t else 1 - ids[1]
        return pltpu.make_async_copy(left_env.at[:, term], tiles.at[t], sem_in.at[t])

    def store(t):
        dst = keep if t else give
        return pltpu.make_async_copy(folded.at[t], dst, sem_out.at[t])

    rights = pltpu.make_async_copy(right_env.at[:, ids[1]], others, sem_right)
    for t in range(2):
        fetch(t).start()
    rights.start()
    right[8] = jnp.zeros((FOLDED, HALF), f32)
    for t in range(2):
        fetch(t).wait()
        for n in range(4):
            put_folded(folded.at[t], n, tiles[t, n])
        store(t).start()
    rights.wait()
    for n in range(8):
        put_folded(right, n, others[n])
    for t in range(2):
        store(t).wait()


def fold(ids, left_env, right_env):
    return pl.pallas_call(
        fold_body,
        in_specs=[smem(), hbm(), hbm()],
        out_specs=[hbm(), hbm(), vmem()],
        out_shape=[pltpu.HBM((4, FOLDED, HALF), f32)] * 2
        + [jax.ShapeDtypeStruct((9, FOLDED, HALF), f32)],
        scratch_shapes=[
            pltpu.VMEM((2, 4, TILE, TILE), f32),
            pltpu.VMEM((2, 4, FOLDED, HALF), f32),
            pltpu.VMEM((8, TILE, TILE), f32),
            pltpu.SemaphoreType.DMA((2,)),
            pltpu.SemaphoreType.DMA((2,)),
            pltpu.SemaphoreType.DMA(()),
        ],
        compiler_params=params(10),
        cost_estimate=cost(1_000_000, 6_000_000),
        name="fold",
    )(ids, in_hbm(left_env), in_hbm(right_env))


def sector_of(ids, rsector, rsector_other, slot):
    return jnp.where(slot // 8 == ids[1], rsector[slot % 8], rsector_other[slot % 8])


def right_slots_body(
    ids, rsector, rsector_other, on, on_other, thin, thin_other, folded, out, cols, sem
):
    for slot in range(TERMS):
        here = slot // 8 == ids[1]
        weight = jnp.where(here, on[slot % 8, ids[1]], on_other[slot % 8, ids[1]])
        sector = sector_of(ids, rsector, rsector_other, slot)
        src = folded.at[jnp.where(weight == 0, 8, sector)]
        pltpu.make_async_copy(src, out.at[slot, pl.ds(THIN, FOLDED), :], sem).start()
    for slot in range(TERMS):
        here = slot // 8 == ids[1]
        block = jnp.where(here, thin[slot % 8], thin_other[slot % 8])
        cols[slot] = jnp.where(ids[1] == 0, block[:, :HALF], block[:, HALF:])
    pltpu.make_async_copy(cols, out.at[:, pl.ds(0, THIN), :], sem).start()
    pltpu.make_async_copy(out, out, sem).wait()


def right_slots(ids, rsector, rsector_other, on, on_other, thin, thin_other, folded):
    return pl.pallas_call(
        right_slots_body,
        in_specs=[smem()] * 5 + [vmem()] * 3,
        out_specs=hbm(),
        out_shape=pltpu.HBM((TERMS, SLOT, HALF), f32),
        scratch_shapes=[
            pltpu.VMEM((TERMS, THIN, HALF), f32),
            pltpu.SemaphoreType.DMA(()),
        ],
        compiler_params=params(6),
        cost_estimate=cost(4_000_000, 6_000_000),
        name="right_slots",
    )(ids, rsector, rsector_other, on, on_other, thin, thin_other, folded)


def left_slots_body(ids, left_sector, *refs):
    mine, theirs = refs[:2]
    above, far, below = refs[2:4], refs[4:6], refs[6:8]
    out, sem = refs[8:]

    def store(src, slot):
        return pltpu.make_async_copy(src, out.at[slot], sem)

    def start(slot, carry):
        sector = left_sector[ids[0] * 16 + slot]
        home = sector // 4
        tile = sector % 4
        away = (home // 2 - ids[0] + 4) % 4
        same = home % 2 == ids[1]
        cases = [(same, mine, tile), (~same, theirs, tile)]
        cases = [(case & (away == 0), src, at) for case, src, at in cases]
        for n, half in ((0, same), (1, ~same)):
            cases.append((half & (away == 1), above[n], tile))
            cases.append((half & (away == 2), far[n], tile))
            cases.append((half & (away == 3), below[n], tile))
        for case, src, at in cases:

            @pl.when(case)
            def _():
                store(src.at[at], slot).start()

        return carry

    lax.fori_loop(0, TERMS, start, 0)
    pltpu.make_async_copy(out, out, sem).wait()


def left_slots(ids, left_sector, pieces):
    return pl.pallas_call(
        left_slots_body,
        in_specs=[smem(), smem()] + [vmem()] * 8,
        out_specs=hbm(),
        out_shape=pltpu.HBM((TERMS, FOLDED, HALF), f32),
        scratch_shapes=[pltpu.SemaphoreType.DMA(())],
        compiler_params=params(8),
        cost_estimate=cost(LEFT_FLOPS, 4_000_000),
        name="left_slots",
    )(ids, left_sector, *pieces)


def live_sizes(ids, rsector, rsector_other, left_sector, left_size, right_size):
    live_left = left_size[left_sector[ids[0] * 16 + ids[2]]]
    live_right = right_size[sector_of(ids, rsector, rsector_other, ids[2])]
    return live_right, live_left


def mask_of(live_right, live_left):
    i, j = grids(TILE, TILE)
    return (i < live_right) & (j < live_left)


def first_body(
    ids, rsector, rsector_other, sector, lsize, rsize, halves, slots,
    r_hi, r_lo, m_hi, m_lo, q1, stats, arrived, sem,
):
    live_right, live_left = live_sizes(ids, rsector, rsector_other, sector, lsize, rsize)

    def fetch(n):
        return pltpu.make_async_copy(slots.at[n], arrived.at[n], sem.at[n])

    for n in range(TERMS):
        fetch(n).start()
    for n in range(TERMS):
        fetch(n).wait()
        full = get_folded(arrived, n, THIN)
        hi, lo = split(full)
        r_hi[n * TILE : (n + 1) * TILE, :] = hi
        r_lo[n * TILE : (n + 1) * TILE, :] = lo
    mine = jnp.concatenate([arrived[n, :THIN, :] for n in range(TERMS)], axis=0)
    theirs = jnp.concatenate([halves[n] for n in range(TERMS)], axis=0)
    first = ids[1] == 0
    block = jnp.concatenate(
        [jnp.where(first, mine, theirs), jnp.where(first, theirs, mine)], axis=1
    )
    start = jnp.where(mask_of(live_right, live_left), block, 0.0)
    norm = jnp.sqrt(total(start * start))
    vec = start * inverse(norm)
    q1[...] = vec
    stats[...] = put(jnp.zeros((8, HALF), f32), 0, norm)
    q_hi, q_lo = split(vec)
    for n in range(TERMS):
        rows = pl.ds(n * TILE, TILE)
        hi, lo = split(dot3(r_hi[rows, :], r_lo[rows, :], q_hi, q_lo))
        m_hi[:, rows] = hi
        m_lo[:, rows] = lo


def first_vector(scalars, halves, slots):
    return pl.pallas_call(
        first_body,
        in_specs=[smem()] * 6 + [vmem(), hbm()],
        out_specs=[vmem()] * 6,
        out_shape=[
            jax.ShapeDtypeStruct((TERMS * TILE, TILE), bf16),
            jax.ShapeDtypeStruct((TERMS * TILE, TILE), bf16),
            jax.ShapeDtypeStruct((TILE, TERMS * TILE), bf16),
            jax.ShapeDtypeStruct((TILE, TERMS * TILE), bf16),
            jax.ShapeDtypeStruct((TILE, TILE), f32),
            jax.ShapeDtypeStruct((8, HALF), f32),
        ],
        scratch_shapes=[
            pltpu.VMEM((TERMS, SLOT, HALF), f32),
            pltpu.SemaphoreType.DMA((TERMS,)),
        ],
        compiler_params=params(10),
        cost_estimate=cost(1_700_000_000, 12_000_000),
        name="first_vector",
    )(*scalars, halves, in_hbm(slots))


def image_one_body(arrived, m_hi, m_lo, l_hi, l_lo, part, here_hi, here_lo, sem):
    fetches = [
        pltpu.make_async_copy(m_hi, here_hi, sem.at[0]),
        pltpu.make_async_copy(m_lo, here_lo, sem.at[1]),
    ]
    for fetch in fetches:
        fetch.start()
    for n in range(TERMS):
        hi, lo = split(get_folded(arrived, n, 0))
        l_hi[n * TILE : (n + 1) * TILE, :] = hi
        l_lo[n * TILE : (n + 1) * TILE, :] = lo
    for fetch in fetches:
        fetch.wait()
    part[...] = dot3(here_hi[...], here_lo[...], l_hi[...], l_lo[...])


def image_one(arrived, m_hi, m_lo):
    stack = jax.ShapeDtypeStruct((TERMS * TILE, TILE), bf16)
    return pl.pallas_call(
        image_one_body,
        in_specs=[vmem(), hbm(), hbm()],
        out_specs=[vmem()] * 3,
        out_shape=[stack, stack, jax.ShapeDtypeStruct((TILE, TILE), f32)],
        scratch_shapes=[
            pltpu.VMEM((TILE, TERMS * TILE), bf16),
            pltpu.VMEM((TILE, TERMS * TILE), bf16),
            pltpu.SemaphoreType.DMA((2,)),
        ],
        compiler_params=params(10),
        cost_estimate=cost(1_700_000_000, 10_000_000),
        name="image_one",
    )(arrived, in_hbm(m_hi), in_hbm(m_lo))


def lanczos(image, last, before, beta):
    alpha = total(last * image)
    rest = image - alpha * last
    if before is not None:
        rest = rest - beta * before
    again = rest - total(last * rest) * last
    if before is not None:
        again = again - total(before * rest) * before
    norm = jnp.sqrt(total(again * again))
    return alpha, norm, again * inverse(norm)


def half_image(vec, r_hi, r_lo, l_hi, l_lo):
    q_hi, q_lo = split(vec)
    acc = jnp.zeros((TILE, TILE), f32)
    for n in range(TERMS):
        rows = pl.ds(n * TILE, TILE)
        hi, lo = split(dot3(r_hi[rows, :], r_lo[rows, :], q_hi, q_lo))
        acc = acc + dot3(hi, lo, l_hi[rows, :], l_lo[rows, :])
    return acc


def image_two_body(
    ids, rsector, rsector_other, sector, lsize, rsize,
    part_a, part_b, q1, stats_in, r_hi, r_lo, l_hi, l_lo,
    part, q2, stats,
):
    mask = mask_of(*live_sizes(ids, rsector, rsector_other, sector, lsize, rsize))
    image = jnp.where(mask, part_a[...] + part_b[...], 0.0)
    alpha, norm, vec = lanczos(image, q1[...], None, None)
    q2[...] = vec
    stats[...] = put(put(stats_in[...], 1, alpha), 2, norm)
    part[...] = half_image(vec, r_hi, r_lo, l_hi, l_lo)


def image_two(scalars, part, part_other, q1, stats, stacks):
    return pl.pallas_call(
        image_two_body,
        in_specs=[smem()] * 6 + [vmem()] * 8,
        out_specs=[vmem()] * 3,
        out_shape=[
            jax.ShapeDtypeStruct((TILE, TILE), f32),
            jax.ShapeDtypeStruct((TILE, TILE), f32),
            jax.ShapeDtypeStruct((8, HALF), f32),
        ],
        compiler_params=params(6),
        cost_estimate=cost(3_300_000_000, 9_000_000),
        name="image_two",
    )(*scalars, part, part_other, q1, stats, *stacks)


def image_three_body(
    ids, rsector, rsector_other, sector, lsize, rsize,
    part_a, part_b, q1, q2, stats_in, r_hi, r_lo, l_hi, l_lo, slots,
):
    mask = mask_of(*live_sizes(ids, rsector, rsector_other, sector, lsize, rsize))
    image = jnp.where(mask, part_a[...] + part_b[...], 0.0)
    i, j = grids(8, HALF)
    beta = total(jnp.where((j == 2) & (i == 0), stats_in[...], 0.0))
    alpha, norm, vec = lanczos(image, q2[...], q1[...], beta)
    pick = jnp.where(ids[1] == 0, q2[...], vec)
    for n in range(16):
        slots[n, :16, :] = pick[16 * n : 16 * n + 16, :HALF]
        slots[n, 16:COLS, :] = pick[16 * n : 16 * n + 16, HALF:]
    stats = put(put(stats_in[...], 3, alpha), 4, norm)
    alpha = total(vec * half_image(vec, r_hi, r_lo, l_hi, l_lo))
    stats = put(stats, 5, alpha)
    for n in range(16):
        slots[n, COLS:, :] = stats


def image_three(scalars, part, part_other, q1, q2, stats, stacks):
    return pl.pallas_call(
        image_three_body,
        in_specs=[smem()] * 6 + [vmem()] * 9,
        out_specs=vmem(),
        out_shape=jax.ShapeDtypeStruct((16, COLS + 8, HALF), f32),
        compiler_params=params(6),
        cost_estimate=cost(3_300_000_000, 9_000_000),
        name="image_three",
    )(*scalars, part, part_other, q1, q2, stats, *stacks)


def ritz_pair(norm, a1, b1, a2, b2, a3):
    def apply(x):
        return [a1 * x[0] + b1 * x[1], b1 * x[0] + a2 * x[1] + b2 * x[2], b2 * x[1] + a3 * x[2]]

    def dot(x, y):
        return jnp.sum(x[0] * y[0] + x[1] * y[1] + x[2] * y[2], axis=1, keepdims=True)

    zero = jnp.zeros_like(norm)
    start = [norm, zero, zero]
    image = apply(start)
    norm_sq = dot(start, start)
    correlation = dot(start, image)
    inv_norm = 1.0 / jnp.sqrt(norm_sq)
    basis = [x * inv_norm for x in start]
    applied = [x * inv_norm for x in image]
    ritz = correlation / norm_sq
    for _ in range(ITERS):
        residual = [x - ritz * y for x, y in zip(applied, basis)]
        res_sq = dot(residual, residual)
        length = jnp.sqrt(res_sq)
        fresh = [x / length for x in residual]
        fresh_applied = apply(fresh)
        curvature = dot(fresh, fresh_applied)
        half_gap = 0.5 * (ritz - curvature)
        root = jnp.sqrt(half_gap * half_gap + res_sq)
        lowest = 0.5 * (ritz + curvature) - root
        first = curvature - lowest
        pair = jnp.sqrt(first * first + res_sq)
        basis = [(first * x - length * y) / pair for x, y in zip(basis, fresh)]
        applied = [(first * x - length * y) / pair for x, y in zip(applied, fresh_applied)]
        ritz = lowest
    return basis, ritz


def finish_body(
    ids, sector, rsector, lsize, rsize, own_stats, other_stats, thin, got, back,
    out, energy, coef,
):
    _, lane = grids(64, HALF)
    stats = own_stats[...] + jnp.where(lane == 5, other_stats[...], 0.0)
    flip = jnp.concatenate([stats, jnp.zeros((64, HALF), f32)], axis=0).T
    norm, a1, b1, a2, b2, a3 = [flip[m : m + 1, :] for m in range(6)]
    basis, ritz = ritz_pair(norm, a1, b1, a2, b2, a3)
    energy[0, 0] = jnp.sum(ritz)
    scale = jnp.sqrt(jnp.full((1, HALF), 64 * TILE * TILE, f32))
    i, _ = grids(HALF, HALF)
    c1 = basis[0] * inverse(norm) * scale
    c2 = basis[1] * scale
    c3 = basis[2] * scale
    coef[...] = jnp.where(i == 0, c1, jnp.where(i == 1, c2, jnp.where(i == 2, c3, 0.0))).T
    core = ids[1]
    own = coef[pl.ds(pl.multiple_of(core * 8, 8), 8), :]
    jcol, irow = grids(16, TILE)
    for b in range(8):
        live_left = lsize[sector[ids[0] * 16 + core * 8 + b]]
        live_right = rsize[rsector[b]]
        live = (jcol + ids[2] * 16 < live_right) & (irow < live_left)
        at = core * 8 + b
        keep = jnp.concatenate([got[at, :16, :], got[at, 16:COLS, :]], axis=1)
        recv = jnp.concatenate([back[b, :16, :], back[b, 16:COLS, :]], axis=1)
        second = jnp.where(core == 0, keep, recv)
        third = jnp.where(core == 0, recv, keep)
        out[b] = (
            own[b : b + 1, 0:1] * jnp.where(live, thin[b], 0.0)
            + own[b : b + 1, 1:2] * second
            + own[b : b + 1, 2:3] * third
        )


def finish(ids, sector, rsector, lsize, rsize, own_stats, other_stats, thin, got, back):
    return pl.pallas_call(
        finish_body,
        in_specs=[smem()] * 5 + [vmem()] * 5,
        out_specs=[vmem(), smem()],
        out_shape=[
            jax.ShapeDtypeStruct(thin.shape, f32),
            jax.ShapeDtypeStruct((1, 1), f32),
        ],
        scratch_shapes=[pltpu.VMEM((HALF, HALF), f32)],
        compiler_params=params(4),
        name="finish",
    )(ids, sector, rsector, lsize, rsize, own_stats, other_stats, thin, got, back)


def local(theta, left_env, right_env, left_sector, right_sector, term_on, left_size, right_size):
    plane = lax.axis_index("y").astype(jnp.int32)
    core = lax.axis_index("c").astype(jnp.int32)
    place = lax.axis_index(COL).astype(jnp.int32)
    ids = jnp.stack([plane, core, place])
    thin = jnp.swapaxes(theta, 1, 2)

    rsector_other = lax.ppermute(right_sector, "c", SWAP)
    on_other = lax.ppermute(term_on, "c", SWAP)
    thin_other = lax.ppermute(thin, "c", SWAP)

    mine, folded, right_folded = fold(ids, left_env, right_env)
    theirs = lax.ppermute(folded, "c", SWAP)
    theirs, rsector_other, on_other, thin_other = lax.optimization_barrier(
        (theirs, rsector_other, on_other, thin_other)
    )
    below = [lax.ppermute(x, "y", UP) for x in (mine, theirs)]
    above = [lax.ppermute(x, "y", DOWN) for x in (mine, theirs)]
    far = [lax.ppermute(below[0], "y", UP), lax.ppermute(above[1], "y", DOWN)]

    slots = right_slots(
        ids, right_sector, rsector_other, term_on, on_other, thin, thin_other, right_folded
    )
    slots, theirs_now = lax.optimization_barrier((slots, theirs))
    arrived = lax.all_to_all(slots, COL, 0, 0, tiled=True)
    scalars = (ids, right_sector, rsector_other, left_sector, left_size, right_size)
    halves = lax.ppermute(arrived[:, :THIN, :], "c", SWAP)
    r_hi, r_lo, m_hi, m_lo, q1, stats = first_vector(scalars, halves, arrived)

    pieces = [mine, theirs] + above + far + below
    left_sent = left_slots(ids, left_sector, pieces)
    left_arrived = lax.all_to_all(left_sent, COL, 0, 0, tiled=True)
    l_hi, l_lo, part = image_one(left_arrived, m_hi, m_lo)
    stacks = (r_hi, r_lo, l_hi, l_lo)
    part, q2, stats = image_two(scalars, part, lax.ppermute(part, "c", SWAP), q1, stats, stacks)
    sent = image_three(scalars, part, lax.ppermute(part, "c", SWAP), q1, q2, stats, stacks)

    got = lax.all_to_all(sent, COL, 0, 0, tiled=True)
    plane_stats = got[:, COLS, :]
    turned = [
        lax.ppermute(plane_stats, "y", [(i, (i + k) % 4) for i in range(4)]) for k in (1, 2, 3)
    ]
    give = lax.dynamic_slice(got, ((1 - core) * 8, 0, 0), (8, COLS, HALF))
    back = lax.ppermute(give, "c", SWAP)
    own_stats = jnp.concatenate([plane_stats] + turned)
    other_stats = lax.ppermute(own_stats, "c", SWAP)
    out, energy = finish(
        ids, left_sector, right_sector, left_size, right_size,
        own_stats, other_stats, thin, got, back,
    )
    return jnp.swapaxes(out, 1, 2), energy[0, 0]


def solution(mesh):
    fine = Mesh(mesh.devices.reshape(4, 2, 4, 4), ALL)
    row = ("y", "c")
    placed = (
        P(row, None, COL),
        P(row, COL, None, None),
        P(None, COL, None, None),
        P(),
        P(row),
        P(row, COL),
        P(),
        P(),
    )
    return jax.shard_map(
        local, mesh=fine, in_specs=placed, out_specs=(P(row, None, COL), P()), check_vma=False
    )
```

```python
import jax
import jax.numpy as jnp
from jax import lax
from jax.experimental import pallas as pl
from jax.experimental.pallas import tpu as pltpu
from jax.sharding import Mesh, PartitionSpec as P

ITERS = 2
LEFT_FLOPS = 15_000_000_000
NEAR_FLOPS = 1_000_000_000
TILE = 256
HALF = 128
TERMS = 16
FOLDED = 264
THIN = 16
COLS = 32
SLOT = THIN + FOLDED
COL = ("x", "z")
ALL = ("y", "c", "x", "z")
SWAP = [(0, 1), (1, 0)]
UP = [(i, (i + 1) % 4) for i in range(4)]
DOWN = [(i, (i - 1) % 4) for i in range(4)]
f32 = jnp.float32
bf16 = jnp.bfloat16


def params(mib):
    return pltpu.CompilerParams(vmem_limit_bytes=mib * 1024 * 1024)


def hbm():
    return pl.BlockSpec(memory_space=pltpu.HBM)


def in_hbm(x):
    return pltpu.with_memory_space_constraint(x, pltpu.HBM)


def smem():
    return pl.BlockSpec(memory_space=pltpu.SMEM)


def cost(flops, nbytes):
    return pl.CostEstimate(flops=flops, transcendentals=0, bytes_accessed=nbytes)


def vmem():
    return pl.BlockSpec(memory_space=pltpu.VMEM)


def grids(rows, cols):
    i = lax.broadcasted_iota(jnp.int32, (rows, cols), 0)
    j = lax.broadcasted_iota(jnp.int32, (rows, cols), 1)
    return i, j


def fold_tile(tile):
    i, j = grids(HALF, HALF)
    a00 = tile[:HALF, :HALF]
    a11 = tile[HALF:, HALF:]
    fold = jnp.where(i >= j, a00, a11)
    diag = jnp.sum(jnp.where(i == j, a11, 0.0), axis=0, keepdims=True)
    return fold, tile[:HALF, HALF:], diag


def put_folded(dst, at, tile):
    fold, corner, diag = fold_tile(tile)
    dst[at, :HALF, :] = fold
    dst[at, HALF:TILE, :] = corner
    dst[at, TILE:, :] = jnp.broadcast_to(diag, (FOLDED - TILE, HALF))


def get_folded(src, at, row):
    return unfold_tile(
        src[at, row : row + HALF, :],
        src[at, row + HALF : row + TILE, :],
        src[at, row + TILE : row + TILE + 1, :],
    )


def unfold_tile(fold, corner, diag):
    i, j = grids(HALF, HALF)
    flip = fold.T
    a00 = jnp.where(i >= j, fold, flip)
    a11 = jnp.where(i == j, diag, jnp.where(i < j, fold, flip))
    top = jnp.concatenate([a00, corner], axis=1)
    low = jnp.concatenate([corner.T, a11], axis=1)
    return jnp.concatenate([top, low], axis=0)


def split(x):
    hi = x.astype(bf16)
    return hi, (x - hi.astype(f32)).astype(bf16)


def dot3(a_hi, a_lo, b_hi, b_lo):
    def dot(a, b):
        return jnp.dot(a, b, preferred_element_type=f32)

    return dot(a_hi, b_hi) + (dot(a_hi, b_lo) + dot(a_lo, b_hi))


def total(x):
    return jnp.sum(jnp.sum(x, axis=0, keepdims=True), axis=1, keepdims=True)


def inverse(norm):
    good = norm > 0.0
    return jnp.where(good, 1.0 / jnp.where(good, norm, 1.0), 0.0)


def put(stats, lane, value):
    _, j = grids(8, HALF)
    return jnp.where(j == lane, value, stats)


def fold_body(
    ids, left_env, right_env, keep, give, right, tiles, folded, others, sem_in, sem_out, sem_right
):
    def fetch(t):
        term = ids[1] if t else 1 - ids[1]
        return pltpu.make_async_copy(left_env.at[:, term], tiles.at[t], sem_in.at[t])

    def store(t):
        dst = keep if t else give
        return pltpu.make_async_copy(folded.at[t], dst, sem_out.at[t])

    rights = pltpu.make_async_copy(right_env.at[:, ids[1]], others, sem_right)
    for t in range(2):
        fetch(t).start()
    rights.start()
    right[8] = jnp.zeros((FOLDED, HALF), f32)
    for t in range(2):
        fetch(t).wait()
        for n in range(4):
            put_folded(folded.at[t], n, tiles[t, n])
        store(t).start()
    rights.wait()
    for n in range(8):
        put_folded(right, n, others[n])
    for t in range(2):
        store(t).wait()


def fold(ids, left_env, right_env):
    return pl.pallas_call(
        fold_body,
        in_specs=[smem(), hbm(), hbm()],
        out_specs=[hbm(), hbm(), vmem()],
        out_shape=[pltpu.HBM((4, FOLDED, HALF), f32)] * 2
        + [jax.ShapeDtypeStruct((9, FOLDED, HALF), f32)],
        scratch_shapes=[
            pltpu.VMEM((2, 4, TILE, TILE), f32),
            pltpu.VMEM((2, 4, FOLDED, HALF), f32),
            pltpu.VMEM((8, TILE, TILE), f32),
            pltpu.SemaphoreType.DMA((2,)),
            pltpu.SemaphoreType.DMA((2,)),
            pltpu.SemaphoreType.DMA(()),
        ],
        compiler_params=params(10),
        cost_estimate=cost(1_000_000, 6_000_000),
        name="fold",
    )(ids, in_hbm(left_env), in_hbm(right_env))


def sector_of(ids, rsector, rsector_other, slot):
    return jnp.where(slot // 8 == ids[1], rsector[slot % 8], rsector_other[slot % 8])


def right_slots_body(
    ids, rsector, rsector_other, on, on_other, thin, thin_other, folded, out, cols, sem
):
    for slot in range(TERMS):
        here = slot // 8 == ids[1]
        weight = jnp.where(here, on[slot % 8, ids[1]], on_other[slot % 8, ids[1]])
        sector = sector_of(ids, rsector, rsector_other, slot)
        src = folded.at[jnp.where(weight == 0, 8, sector)]
        pltpu.make_async_copy(src, out.at[slot, pl.ds(THIN, FOLDED), :], sem).start()
    for slot in range(TERMS):
        here = slot // 8 == ids[1]
        block = jnp.where(here, thin[slot % 8], thin_other[slot % 8])
        cols[slot] = jnp.where(ids[1] == 0, block[:, :HALF], block[:, HALF:])
    pltpu.make_async_copy(cols, out.at[:, pl.ds(0, THIN), :], sem).start()
    pltpu.make_async_copy(out, out, sem).wait()


def right_slots(ids, rsector, rsector_other, on, on_other, thin, thin_other, folded):
    return pl.pallas_call(
        right_slots_body,
        in_specs=[smem()] * 5 + [vmem()] * 3,
        out_specs=hbm(),
        out_shape=pltpu.HBM((TERMS, SLOT, HALF), f32),
        scratch_shapes=[
            pltpu.VMEM((TERMS, THIN, HALF), f32),
            pltpu.SemaphoreType.DMA(()),
        ],
        compiler_params=params(6),
        cost_estimate=cost(4_000_000, 6_000_000),
        name="right_slots",
    )(ids, rsector, rsector_other, on, on_other, thin, thin_other, folded)


def where_from(ids, left_sector, slot):
    sector = left_sector[ids[0] * 16 + slot]
    home = sector // 4
    return sector % 4, (home // 2 - ids[0] + 4) % 4, home % 2 == ids[1]


def send_tiles(out, sem, cases_of):
    def start(slot, carry):
        for case, src, tile in cases_of(slot):

            @pl.when(case)
            def _():
                pltpu.make_async_copy(src.at[tile], out.at[slot], sem).start()

        return carry

    def finish(slot, carry):
        for case, src, tile in cases_of(slot):

            @pl.when(case)
            def _():
                pltpu.make_async_copy(src.at[tile], out.at[slot], sem).wait()

        return carry

    lax.fori_loop(0, TERMS, start, 0)
    lax.fori_loop(0, TERMS, finish, 0)


def near_slots_body(ids, left_sector, mine, theirs, above_a, above_b, below_a, below_b, out, sem):
    def cases_of(slot):
        tile, away, same = where_from(ids, left_sector, slot)
        by_away = {0: (mine, theirs), 1: (above_a, above_b), 3: (below_a, below_b)}
        cases = []
        for planes, (first, second) in by_away.items():
            cases.append((same & (away == planes), first, tile))
            cases.append((~same & (away == planes), second, tile))
        return cases

    send_tiles(out, sem, cases_of)


def far_slots_body(ids, left_sector, far_a, far_b, near, out, sem):
    def cases_of(slot):
        tile, away, same = where_from(ids, left_sector, slot)
        return [(same & (away == 2), far_a, tile), (~same & (away == 2), far_b, tile)]

    send_tiles(out, sem, cases_of)


def left_slots(ids, left_sector, near, far):
    slots = pltpu.HBM((TERMS, FOLDED, HALF), f32)
    ready = pl.pallas_call(
        near_slots_body,
        in_specs=[smem(), smem()] + [vmem()] * 6,
        out_specs=hbm(),
        out_shape=slots,
        scratch_shapes=[pltpu.SemaphoreType.DMA(())],
        compiler_params=params(8),
        cost_estimate=cost(NEAR_FLOPS, 4_000_000),
        name="near_slots",
    )(ids, left_sector, *near)
    return pl.pallas_call(
        far_slots_body,
        in_specs=[smem(), smem()] + [vmem()] * 2 + [hbm()],
        out_specs=hbm(),
        out_shape=slots,
        scratch_shapes=[pltpu.SemaphoreType.DMA(())],
        input_output_aliases={4: 0},
        compiler_params=params(4),
        cost_estimate=cost(LEFT_FLOPS, 4_000_000),
        name="far_slots",
    )(ids, left_sector, *far, in_hbm(ready))


def live_sizes(ids, rsector, rsector_other, left_sector, left_size, right_size):
    live_left = left_size[left_sector[ids[0] * 16 + ids[2]]]
    live_right = right_size[sector_of(ids, rsector, rsector_other, ids[2])]
    return live_right, live_left


def mask_of(live_right, live_left):
    i, j = grids(TILE, TILE)
    return (i < live_right) & (j < live_left)


def first_body(
    ids, rsector, rsector_other, sector, lsize, rsize, halves, slots,
    r_hi, r_lo, m_hi, m_lo, q1, stats, arrived, sem,
):
    live_right, live_left = live_sizes(ids, rsector, rsector_other, sector, lsize, rsize)

    def fetch(n):
        return pltpu.make_async_copy(slots.at[n], arrived.at[n], sem.at[n])

    for n in range(TERMS):
        fetch(n).start()
    for n in range(TERMS):
        fetch(n).wait()
        full = get_folded(arrived, n, THIN)
        hi, lo = split(full)
        r_hi[n * TILE : (n + 1) * TILE, :] = hi
        r_lo[n * TILE : (n + 1) * TILE, :] = lo
    mine = jnp.concatenate([arrived[n, :THIN, :] for n in range(TERMS)], axis=0)
    theirs = jnp.concatenate([halves[n] for n in range(TERMS)], axis=0)
    first = ids[1] == 0
    block = jnp.concatenate(
        [jnp.where(first, mine, theirs), jnp.where(first, theirs, mine)], axis=1
    )
    start = jnp.where(mask_of(live_right, live_left), block, 0.0)
    norm = jnp.sqrt(total(start * start))
    vec = start * inverse(norm)
    q1[...] = vec
    stats[...] = put(jnp.zeros((8, HALF), f32), 0, norm)
    q_hi, q_lo = split(vec)
    for n in range(TERMS):
        rows = pl.ds(n * TILE, TILE)
        hi, lo = split(dot3(r_hi[rows, :], r_lo[rows, :], q_hi, q_lo))
        m_hi[:, rows] = hi
        m_lo[:, rows] = lo


def first_vector(scalars, halves, slots):
    return pl.pallas_call(
        first_body,
        in_specs=[smem()] * 6 + [vmem(), hbm()],
        out_specs=[vmem()] * 6,
        out_shape=[
            jax.ShapeDtypeStruct((TERMS * TILE, TILE), bf16),
            jax.ShapeDtypeStruct((TERMS * TILE, TILE), bf16),
            jax.ShapeDtypeStruct((TILE, TERMS * TILE), bf16),
            jax.ShapeDtypeStruct((TILE, TERMS * TILE), bf16),
            jax.ShapeDtypeStruct((TILE, TILE), f32),
            jax.ShapeDtypeStruct((8, HALF), f32),
        ],
        scratch_shapes=[
            pltpu.VMEM((TERMS, SLOT, HALF), f32),
            pltpu.SemaphoreType.DMA((TERMS,)),
        ],
        compiler_params=params(10),
        cost_estimate=cost(1_700_000_000, 12_000_000),
        name="first_vector",
    )(*scalars, halves, in_hbm(slots))


def image_one_body(arrived, m_hi, m_lo, l_hi, l_lo, part, here_hi, here_lo, sem):
    fetches = [
        pltpu.make_async_copy(m_hi, here_hi, sem.at[0]),
        pltpu.make_async_copy(m_lo, here_lo, sem.at[1]),
    ]
    for fetch in fetches:
        fetch.start()
    for n in range(TERMS):
        hi, lo = split(get_folded(arrived, n, 0))
        l_hi[n * TILE : (n + 1) * TILE, :] = hi
        l_lo[n * TILE : (n + 1) * TILE, :] = lo
    for fetch in fetches:
        fetch.wait()
    part[...] = dot3(here_hi[...], here_lo[...], l_hi[...], l_lo[...])


def image_one(arrived, m_hi, m_lo):
    stack = jax.ShapeDtypeStruct((TERMS * TILE, TILE), bf16)
    return pl.pallas_call(
        image_one_body,
        in_specs=[vmem(), hbm(), hbm()],
        out_specs=[vmem()] * 3,
        out_shape=[stack, stack, jax.ShapeDtypeStruct((TILE, TILE), f32)],
        scratch_shapes=[
            pltpu.VMEM((TILE, TERMS * TILE), bf16),
            pltpu.VMEM((TILE, TERMS * TILE), bf16),
            pltpu.SemaphoreType.DMA((2,)),
        ],
        compiler_params=params(10),
        cost_estimate=cost(1_700_000_000, 10_000_000),
        name="image_one",
    )(arrived, in_hbm(m_hi), in_hbm(m_lo))


def lanczos(image, last, before, beta):
    alpha = total(last * image)
    rest = image - alpha * last
    if before is not None:
        rest = rest - beta * before
    again = rest - total(last * rest) * last
    if before is not None:
        again = again - total(before * rest) * before
    norm = jnp.sqrt(total(again * again))
    return alpha, norm, again * inverse(norm)


def half_image(vec, r_hi, r_lo, l_hi, l_lo):
    q_hi, q_lo = split(vec)
    acc = jnp.zeros((TILE, TILE), f32)
    for n in range(TERMS):
        rows = pl.ds(n * TILE, TILE)
        hi, lo = split(dot3(r_hi[rows, :], r_lo[rows, :], q_hi, q_lo))
        acc = acc + dot3(hi, lo, l_hi[rows, :], l_lo[rows, :])
    return acc


def image_two_body(
    ids, rsector, rsector_other, sector, lsize, rsize,
    part_a, part_b, q1, stats_in, r_hi, r_lo, l_hi, l_lo,
    part, q2, stats,
):
    mask = mask_of(*live_sizes(ids, rsector, rsector_other, sector, lsize, rsize))
    image = jnp.where(mask, part_a[...] + part_b[...], 0.0)
    alpha, norm, vec = lanczos(image, q1[...], None, None)
    q2[...] = vec
    stats[...] = put(put(stats_in[...], 1, alpha), 2, norm)
    part[...] = half_image(vec, r_hi, r_lo, l_hi, l_lo)


def image_two(scalars, part, part_other, q1, stats, stacks):
    return pl.pallas_call(
        image_two_body,
        in_specs=[smem()] * 6 + [vmem()] * 8,
        out_specs=[vmem()] * 3,
        out_shape=[
            jax.ShapeDtypeStruct((TILE, TILE), f32),
            jax.ShapeDtypeStruct((TILE, TILE), f32),
            jax.ShapeDtypeStruct((8, HALF), f32),
        ],
        compiler_params=params(6),
        cost_estimate=cost(3_300_000_000, 9_000_000),
        name="image_two",
    )(*scalars, part, part_other, q1, stats, *stacks)


def image_three_body(
    ids, rsector, rsector_other, sector, lsize, rsize,
    part_a, part_b, q1, q2, stats_in, r_hi, r_lo, l_hi, l_lo, slots,
):
    mask = mask_of(*live_sizes(ids, rsector, rsector_other, sector, lsize, rsize))
    image = jnp.where(mask, part_a[...] + part_b[...], 0.0)
    i, j = grids(8, HALF)
    beta = total(jnp.where((j == 2) & (i == 0), stats_in[...], 0.0))
    alpha, norm, vec = lanczos(image, q2[...], q1[...], beta)
    pick = jnp.where(ids[1] == 0, q2[...], vec)
    for n in range(16):
        slots[n, :16, :] = pick[16 * n : 16 * n + 16, :HALF]
        slots[n, 16:COLS, :] = pick[16 * n : 16 * n + 16, HALF:]
    stats = put(put(stats_in[...], 3, alpha), 4, norm)
    alpha = total(vec * half_image(vec, r_hi, r_lo, l_hi, l_lo))
    stats = put(stats, 5, alpha)
    for n in range(16):
        slots[n, COLS:, :] = stats


def image_three(scalars, part, part_other, q1, q2, stats, stacks):
    return pl.pallas_call(
        image_three_body,
        in_specs=[smem()] * 6 + [vmem()] * 9,
        out_specs=vmem(),
        out_shape=jax.ShapeDtypeStruct((16, COLS + 8, HALF), f32),
        compiler_params=params(6),
        cost_estimate=cost(3_300_000_000, 9_000_000),
        name="image_three",
    )(*scalars, part, part_other, q1, q2, stats, *stacks)


def ritz_pair(norm, a1, b1, a2, b2, a3):
    def apply(x):
        return [a1 * x[0] + b1 * x[1], b1 * x[0] + a2 * x[1] + b2 * x[2], b2 * x[1] + a3 * x[2]]

    def dot(x, y):
        return jnp.sum(x[0] * y[0] + x[1] * y[1] + x[2] * y[2], axis=1, keepdims=True)

    zero = jnp.zeros_like(norm)
    start = [norm, zero, zero]
    image = apply(start)
    norm_sq = dot(start, start)
    correlation = dot(start, image)
    inv_norm = 1.0 / jnp.sqrt(norm_sq)
    basis = [x * inv_norm for x in start]
    applied = [x * inv_norm for x in image]
    ritz = correlation / norm_sq
    for _ in range(ITERS):
        residual = [x - ritz * y for x, y in zip(applied, basis)]
        res_sq = dot(residual, residual)
        length = jnp.sqrt(res_sq)
        fresh = [x / length for x in residual]
        fresh_applied = apply(fresh)
        curvature = dot(fresh, fresh_applied)
        half_gap = 0.5 * (ritz - curvature)
        root = jnp.sqrt(half_gap * half_gap + res_sq)
        lowest = 0.5 * (ritz + curvature) - root
        first = curvature - lowest
        pair = jnp.sqrt(first * first + res_sq)
        basis = [(first * x - length * y) / pair for x, y in zip(basis, fresh)]
        applied = [(first * x - length * y) / pair for x, y in zip(applied, fresh_applied)]
        ritz = lowest
    return basis, ritz


def finish_body(
    ids, sector, rsector, lsize, rsize, own_stats, other_stats, thin, got, back,
    out, energy, coef,
):
    _, lane = grids(64, HALF)
    stats = own_stats[...] + jnp.where(lane == 5, other_stats[...], 0.0)
    flip = jnp.concatenate([stats, jnp.zeros((64, HALF), f32)], axis=0).T
    norm, a1, b1, a2, b2, a3 = [flip[m : m + 1, :] for m in range(6)]
    basis, ritz = ritz_pair(norm, a1, b1, a2, b2, a3)
    energy[0, 0] = jnp.sum(ritz)
    scale = jnp.sqrt(jnp.full((1, HALF), 64 * TILE * TILE, f32))
    i, _ = grids(HALF, HALF)
    c1 = basis[0] * inverse(norm) * scale
    c2 = basis[1] * scale
    c3 = basis[2] * scale
    coef[...] = jnp.where(i == 0, c1, jnp.where(i == 1, c2, jnp.where(i == 2, c3, 0.0))).T
    core = ids[1]
    own = coef[pl.ds(pl.multiple_of(core * 8, 8), 8), :]
    jcol, irow = grids(16, TILE)
    for b in range(8):
        live_left = lsize[sector[ids[0] * 16 + core * 8 + b]]
        live_right = rsize[rsector[b]]
        live = (jcol + ids[2] * 16 < live_right) & (irow < live_left)
        at = core * 8 + b
        keep = jnp.concatenate([got[at, :16, :], got[at, 16:COLS, :]], axis=1)
        recv = jnp.concatenate([back[b, :16, :], back[b, 16:COLS, :]], axis=1)
        second = jnp.where(core == 0, keep, recv)
        third = jnp.where(core == 0, recv, keep)
        out[b] = (
            own[b : b + 1, 0:1] * jnp.where(live, thin[b], 0.0)
            + own[b : b + 1, 1:2] * second
            + own[b : b + 1, 2:3] * third
        )


def finish(ids, sector, rsector, lsize, rsize, own_stats, other_stats, thin, got, back):
    return pl.pallas_call(
        finish_body,
        in_specs=[smem()] * 5 + [vmem()] * 5,
        out_specs=[vmem(), smem()],
        out_shape=[
            jax.ShapeDtypeStruct(thin.shape, f32),
            jax.ShapeDtypeStruct((1, 1), f32),
        ],
        scratch_shapes=[pltpu.VMEM((HALF, HALF), f32)],
        compiler_params=params(4),
        name="finish",
    )(ids, sector, rsector, lsize, rsize, own_stats, other_stats, thin, got, back)


def local(theta, left_env, right_env, left_sector, right_sector, term_on, left_size, right_size):
    plane = lax.axis_index("y").astype(jnp.int32)
    core = lax.axis_index("c").astype(jnp.int32)
    place = lax.axis_index(COL).astype(jnp.int32)
    ids = jnp.stack([plane, core, place])
    thin = jnp.swapaxes(theta, 1, 2)

    rsector_other = lax.ppermute(right_sector, "c", SWAP)
    on_other = lax.ppermute(term_on, "c", SWAP)
    thin_other = lax.ppermute(thin, "c", SWAP)

    mine, folded, right_folded = fold(ids, left_env, right_env)
    theirs = lax.ppermute(folded, "c", SWAP)
    theirs, rsector_other, on_other, thin_other = lax.optimization_barrier(
        (theirs, rsector_other, on_other, thin_other)
    )
    below = [lax.ppermute(x, "y", UP) for x in (mine, theirs)]
    above = [lax.ppermute(x, "y", DOWN) for x in (mine, theirs)]
    far = [lax.ppermute(below[0], "y", UP), lax.ppermute(above[1], "y", DOWN)]

    slots = right_slots(
        ids, right_sector, rsector_other, term_on, on_other, thin, thin_other, right_folded
    )
    slots, theirs_now = lax.optimization_barrier((slots, theirs))
    arrived = lax.all_to_all(slots, COL, 0, 0, tiled=True)
    scalars = (ids, right_sector, rsector_other, left_sector, left_size, right_size)
    halves = lax.ppermute(arrived[:, :THIN, :], "c", SWAP)
    r_hi, r_lo, m_hi, m_lo, q1, stats = first_vector(scalars, halves, arrived)

    left_sent = left_slots(ids, left_sector, [mine, theirs] + above + below, far)
    left_arrived = lax.all_to_all(left_sent, COL, 0, 0, tiled=True)
    l_hi, l_lo, part = image_one(left_arrived, m_hi, m_lo)
    stacks = (r_hi, r_lo, l_hi, l_lo)
    part, q2, stats = image_two(scalars, part, lax.ppermute(part, "c", SWAP), q1, stats, stacks)
    sent = image_three(scalars, part, lax.ppermute(part, "c", SWAP), q1, q2, stats, stacks)

    got = lax.all_to_all(sent, COL, 0, 0, tiled=True)
    plane_stats = got[:, COLS, :]
    turned = [
        lax.ppermute(plane_stats, "y", [(i, (i + k) % 4) for i in range(4)]) for k in (1, 2, 3)
    ]
    give = lax.dynamic_slice(got, ((1 - core) * 8, 0, 0), (8, COLS, HALF))
    back = lax.ppermute(give, "c", SWAP)
    own_stats = jnp.concatenate([plane_stats] + turned)
    other_stats = lax.ppermute(own_stats, "c", SWAP)
    out, energy = finish(
        ids, left_sector, right_sector, left_size, right_size,
        own_stats, other_stats, thin, got, back,
    )
    return jnp.swapaxes(out, 1, 2), energy[0, 0]


def solution(mesh):
    fine = Mesh(mesh.devices.reshape(4, 2, 4, 4), ALL)
    row = ("y", "c")
    placed = (
        P(row, None, COL),
        P(row, COL, None, None),
        P(None, COL, None, None),
        P(),
        P(row),
        P(row, COL),
        P(),
        P(),
    )
    return jax.shard_map(
        local, mesh=fine, in_specs=placed, out_specs=(P(row, None, COL), P()), check_vma=False
    )
```

```python
import jax
import jax.numpy as jnp
from jax import lax
from jax.experimental import pallas as pl
from jax.experimental.pallas import tpu as pltpu
from jax.sharding import Mesh, PartitionSpec as P

ITERS = 2
LEFT_FLOPS = 15_000_000_000
NEAR_FLOPS = 1_000_000_000
TILE = 256
HALF = 128
TERMS = 16
FOLDED = 264
THIN = 16
COLS = 32
SLOT = THIN + FOLDED
COL = ("x", "z")
ALL = ("y", "c", "x", "z")
SWAP = [(0, 1), (1, 0)]
UP = [(i, (i + 1) % 4) for i in range(4)]
DOWN = [(i, (i - 1) % 4) for i in range(4)]
f32 = jnp.float32
bf16 = jnp.bfloat16


def params(mib):
    return pltpu.CompilerParams(vmem_limit_bytes=mib * 1024 * 1024)


def hbm():
    return pl.BlockSpec(memory_space=pltpu.HBM)


def in_hbm(x):
    return pltpu.with_memory_space_constraint(x, pltpu.HBM)


def smem():
    return pl.BlockSpec(memory_space=pltpu.SMEM)


def cost(flops, nbytes):
    return pl.CostEstimate(flops=flops, transcendentals=0, bytes_accessed=nbytes)


def vmem():
    return pl.BlockSpec(memory_space=pltpu.VMEM)


def grids(rows, cols):
    i = lax.broadcasted_iota(jnp.int32, (rows, cols), 0)
    j = lax.broadcasted_iota(jnp.int32, (rows, cols), 1)
    return i, j


def fold_tile(tile):
    i, j = grids(HALF, HALF)
    a00 = tile[:HALF, :HALF]
    a11 = tile[HALF:, HALF:]
    fold = jnp.where(i >= j, a00, a11)
    diag = jnp.sum(jnp.where(i == j, a11, 0.0), axis=0, keepdims=True)
    return fold, tile[:HALF, HALF:], diag


def put_folded(dst, at, tile):
    fold, corner, diag = fold_tile(tile)
    dst[at, :HALF, :] = fold
    dst[at, HALF:TILE, :] = corner
    dst[at, TILE:, :] = jnp.broadcast_to(diag, (FOLDED - TILE, HALF))


def get_folded(src, at, row):
    return unfold_tile(
        src[at, row : row + HALF, :],
        src[at, row + HALF : row + TILE, :],
        src[at, row + TILE : row + TILE + 1, :],
    )


def unfold_tile(fold, corner, diag):
    i, j = grids(HALF, HALF)
    flip = fold.T
    a00 = jnp.where(i >= j, fold, flip)
    a11 = jnp.where(i == j, diag, jnp.where(i < j, fold, flip))
    top = jnp.concatenate([a00, corner], axis=1)
    low = jnp.concatenate([corner.T, a11], axis=1)
    return jnp.concatenate([top, low], axis=0)


def split(x):
    hi = x.astype(bf16)
    return hi, (x - hi.astype(f32)).astype(bf16)


def dot3(a_hi, a_lo, b_hi, b_lo):
    def dot(a, b):
        return jnp.dot(a, b, preferred_element_type=f32)

    return dot(a_hi, b_hi) + (dot(a_hi, b_lo) + dot(a_lo, b_hi))


def total(x):
    return jnp.sum(jnp.sum(x, axis=0, keepdims=True), axis=1, keepdims=True)


def inverse(norm):
    good = norm > 0.0
    return jnp.where(good, 1.0 / jnp.where(good, norm, 1.0), 0.0)


def put(stats, lane, value):
    _, j = grids(8, HALF)
    return jnp.where(j == lane, value, stats)


def fold_body(
    ids, left_env, right_env, keep, give, right, tiles, folded, others, sem_in, sem_out, sem_right
):
    def fetch(t):
        term = ids[1] if t else 1 - ids[1]
        return pltpu.make_async_copy(left_env.at[:, term], tiles.at[t], sem_in.at[t])

    def store(t):
        dst = keep if t else give
        return pltpu.make_async_copy(folded.at[t], dst, sem_out.at[t])

    rights = pltpu.make_async_copy(right_env.at[:, ids[1]], others, sem_right)
    for t in range(2):
        fetch(t).start()
    rights.start()
    right[8] = jnp.zeros((FOLDED, HALF), f32)
    for t in range(2):
        fetch(t).wait()
        for n in range(4):
            put_folded(folded.at[t], n, tiles[t, n])
        store(t).start()
    rights.wait()
    for n in range(8):
        put_folded(right, n, others[n])
    for t in range(2):
        store(t).wait()


def fold(ids, left_env, right_env):
    return pl.pallas_call(
        fold_body,
        in_specs=[smem(), hbm(), hbm()],
        out_specs=[hbm(), hbm(), vmem()],
        out_shape=[pltpu.HBM((4, FOLDED, HALF), f32)] * 2
        + [jax.ShapeDtypeStruct((9, FOLDED, HALF), f32)],
        scratch_shapes=[
            pltpu.VMEM((2, 4, TILE, TILE), f32),
            pltpu.VMEM((2, 4, FOLDED, HALF), f32),
            pltpu.VMEM((8, TILE, TILE), f32),
            pltpu.SemaphoreType.DMA((2,)),
            pltpu.SemaphoreType.DMA((2,)),
            pltpu.SemaphoreType.DMA(()),
        ],
        compiler_params=params(10),
        cost_estimate=cost(1_000_000, 6_000_000),
        name="fold",
    )(ids, in_hbm(left_env), in_hbm(right_env))


def sector_of(ids, rsector, rsector_other, slot):
    return jnp.where(slot // 8 == ids[1], rsector[slot % 8], rsector_other[slot % 8])


def right_slots_body(
    ids, rsector, rsector_other, on, on_other, thin, thin_other, folded, out, cols, sem
):
    for slot in range(TERMS):
        here = slot // 8 == ids[1]
        weight = jnp.where(here, on[slot % 8, ids[1]], on_other[slot % 8, ids[1]])
        sector = sector_of(ids, rsector, rsector_other, slot)
        src = folded.at[jnp.where(weight == 0, 8, sector)]
        pltpu.make_async_copy(src, out.at[slot, pl.ds(THIN, FOLDED), :], sem).start()
    for slot in range(TERMS):
        here = slot // 8 == ids[1]
        block = jnp.where(here, thin[slot % 8], thin_other[slot % 8])
        cols[slot] = jnp.where(ids[1] == 0, block[:, :HALF], block[:, HALF:])
    pltpu.make_async_copy(cols, out.at[:, pl.ds(0, THIN), :], sem).start()
    pltpu.make_async_copy(out, out, sem).wait()


def right_slots(ids, rsector, rsector_other, on, on_other, thin, thin_other, folded):
    return pl.pallas_call(
        right_slots_body,
        in_specs=[smem()] * 5 + [vmem()] * 3,
        out_specs=hbm(),
        out_shape=pltpu.HBM((TERMS, SLOT, HALF), f32),
        scratch_shapes=[
            pltpu.VMEM((TERMS, THIN, HALF), f32),
            pltpu.SemaphoreType.DMA(()),
        ],
        compiler_params=params(6),
        cost_estimate=cost(4_000_000, 6_000_000),
        name="right_slots",
    )(ids, rsector, rsector_other, on, on_other, thin, thin_other, folded)


def where_from(ids, left_sector, slot):
    sector = left_sector[ids[0] * 16 + slot]
    home = sector // 4
    return sector % 4, (home // 2 - ids[0] + 4) % 4, home % 2 == ids[1]


def near_slots_body(ids, left_sector, mine, theirs, above_a, above_b, below_a, below_b, out, sem):
    for slot in range(TERMS):
        tile, away, same = where_from(ids, left_sector, slot)
        sources = [
            (same & (away % 2 == 0), mine),
            (~same & (away % 2 == 0), theirs),
            (same & (away == 1), above_a),
            (~same & (away == 1), above_b),
            (same & (away == 3), below_a),
            (~same & (away == 3), below_b),
        ]
        for case, src in sources:

            @pl.when(case)
            def _():
                pltpu.make_async_copy(src.at[tile], out.at[slot], sem).start()

    pltpu.make_async_copy(out, out, sem).wait()


def far_slots_body(ids, left_sector, far_a, far_b, near, out, sem):
    places = [where_from(ids, left_sector, slot) for slot in range(TERMS)]
    for slot, (tile, away, same) in enumerate(places):
        for case, src in ((same, far_a), (~same, far_b)):

            @pl.when(case & (away == 2))
            def _():
                pltpu.make_async_copy(src.at[tile], out.at[slot], sem).start()

    for slot, (tile, away, same) in enumerate(places):

        @pl.when(away == 2)
        def _():
            pltpu.make_async_copy(far_a.at[0], out.at[slot], sem).wait()


def left_slots(ids, left_sector, near, far):
    slots = pltpu.HBM((TERMS, FOLDED, HALF), f32)
    ready = pl.pallas_call(
        near_slots_body,
        in_specs=[smem(), smem()] + [vmem()] * 6,
        out_specs=hbm(),
        out_shape=slots,
        scratch_shapes=[pltpu.SemaphoreType.DMA(())],
        compiler_params=params(8),
        cost_estimate=cost(NEAR_FLOPS, 4_000_000),
        name="near_slots",
    )(ids, left_sector, *near)
    return pl.pallas_call(
        far_slots_body,
        in_specs=[smem(), smem()] + [vmem()] * 2 + [hbm()],
        out_specs=hbm(),
        out_shape=slots,
        scratch_shapes=[pltpu.SemaphoreType.DMA(())],
        input_output_aliases={4: 0},
        compiler_params=params(4),
        cost_estimate=cost(LEFT_FLOPS, 4_000_000),
        name="far_slots",
    )(ids, left_sector, *far, in_hbm(ready))


def live_sizes(ids, rsector, rsector_other, left_sector, left_size, right_size):
    live_left = left_size[left_sector[ids[0] * 16 + ids[2]]]
    live_right = right_size[sector_of(ids, rsector, rsector_other, ids[2])]
    return live_right, live_left


def mask_of(live_right, live_left):
    i, j = grids(TILE, TILE)
    return (i < live_right) & (j < live_left)


def first_body(
    ids, rsector, rsector_other, sector, lsize, rsize, halves, slots,
    r_hi, r_lo, m_hi, m_lo, q1, stats, arrived, sem,
):
    live_right, live_left = live_sizes(ids, rsector, rsector_other, sector, lsize, rsize)

    def fetch(n):
        return pltpu.make_async_copy(slots.at[n], arrived.at[n], sem.at[n])

    for n in range(TERMS):
        fetch(n).start()
    for n in range(TERMS):
        fetch(n).wait()
        full = get_folded(arrived, n, THIN)
        hi, lo = split(full)
        r_hi[n * TILE : (n + 1) * TILE, :] = hi
        r_lo[n * TILE : (n + 1) * TILE, :] = lo
    mine = jnp.concatenate([arrived[n, :THIN, :] for n in range(TERMS)], axis=0)
    theirs = jnp.concatenate([halves[n] for n in range(TERMS)], axis=0)
    first = ids[1] == 0
    block = jnp.concatenate(
        [jnp.where(first, mine, theirs), jnp.where(first, theirs, mine)], axis=1
    )
    start = jnp.where(mask_of(live_right, live_left), block, 0.0)
    norm = jnp.sqrt(total(start * start))
    vec = start * inverse(norm)
    q1[...] = vec
    stats[...] = put(jnp.zeros((8, HALF), f32), 0, norm)
    q_hi, q_lo = split(vec)
    for n in range(TERMS):
        rows = pl.ds(n * TILE, TILE)
        hi, lo = split(dot3(r_hi[rows, :], r_lo[rows, :], q_hi, q_lo))
        m_hi[:, rows] = hi
        m_lo[:, rows] = lo


def first_vector(scalars, halves, slots):
    return pl.pallas_call(
        first_body,
        in_specs=[smem()] * 6 + [vmem(), hbm()],
        out_specs=[vmem()] * 6,
        out_shape=[
            jax.ShapeDtypeStruct((TERMS * TILE, TILE), bf16),
            jax.ShapeDtypeStruct((TERMS * TILE, TILE), bf16),
            jax.ShapeDtypeStruct((TILE, TERMS * TILE), bf16),
            jax.ShapeDtypeStruct((TILE, TERMS * TILE), bf16),
            jax.ShapeDtypeStruct((TILE, TILE), f32),
            jax.ShapeDtypeStruct((8, HALF), f32),
        ],
        scratch_shapes=[
            pltpu.VMEM((TERMS, SLOT, HALF), f32),
            pltpu.SemaphoreType.DMA((TERMS,)),
        ],
        compiler_params=params(10),
        cost_estimate=cost(1_700_000_000, 12_000_000),
        name="first_vector",
    )(*scalars, halves, in_hbm(slots))


def image_one_body(arrived, m_hi, m_lo, l_hi, l_lo, part, here_hi, here_lo, sem):
    fetches = [
        pltpu.make_async_copy(m_hi, here_hi, sem.at[0]),
        pltpu.make_async_copy(m_lo, here_lo, sem.at[1]),
    ]
    for fetch in fetches:
        fetch.start()
    for n in range(TERMS):
        hi, lo = split(get_folded(arrived, n, 0))
        l_hi[n * TILE : (n + 1) * TILE, :] = hi
        l_lo[n * TILE : (n + 1) * TILE, :] = lo
    for fetch in fetches:
        fetch.wait()
    part[...] = dot3(here_hi[...], here_lo[...], l_hi[...], l_lo[...])


def image_one(arrived, m_hi, m_lo):
    stack = jax.ShapeDtypeStruct((TERMS * TILE, TILE), bf16)
    return pl.pallas_call(
        image_one_body,
        in_specs=[vmem(), hbm(), hbm()],
        out_specs=[vmem()] * 3,
        out_shape=[stack, stack, jax.ShapeDtypeStruct((TILE, TILE), f32)],
        scratch_shapes=[
            pltpu.VMEM((TILE, TERMS * TILE), bf16),
            pltpu.VMEM((TILE, TERMS * TILE), bf16),
            pltpu.SemaphoreType.DMA((2,)),
        ],
        compiler_params=params(10),
        cost_estimate=cost(1_700_000_000, 10_000_000),
        name="image_one",
    )(arrived, in_hbm(m_hi), in_hbm(m_lo))


def lanczos(image, last, before, beta):
    alpha = total(last * image)
    rest = image - alpha * last
    if before is not None:
        rest = rest - beta * before
    again = rest - total(last * rest) * last
    if before is not None:
        again = again - total(before * rest) * before
    norm = jnp.sqrt(total(again * again))
    return alpha, norm, again * inverse(norm)


def half_image(vec, r_hi, r_lo, l_hi, l_lo):
    q_hi, q_lo = split(vec)
    acc = jnp.zeros((TILE, TILE), f32)
    for n in range(TERMS):
        rows = pl.ds(n * TILE, TILE)
        hi, lo = split(dot3(r_hi[rows, :], r_lo[rows, :], q_hi, q_lo))
        acc = acc + dot3(hi, lo, l_hi[rows, :], l_lo[rows, :])
    return acc


def image_two_body(
    ids, rsector, rsector_other, sector, lsize, rsize,
    part_a, part_b, q1, stats_in, r_hi, r_lo, l_hi, l_lo,
    part, q2, stats,
):
    mask = mask_of(*live_sizes(ids, rsector, rsector_other, sector, lsize, rsize))
    image = jnp.where(mask, part_a[...] + part_b[...], 0.0)
    alpha, norm, vec = lanczos(image, q1[...], None, None)
    q2[...] = vec
    stats[...] = put(put(stats_in[...], 1, alpha), 2, norm)
    part[...] = half_image(vec, r_hi, r_lo, l_hi, l_lo)


def image_two(scalars, part, part_other, q1, stats, stacks):
    return pl.pallas_call(
        image_two_body,
        in_specs=[smem()] * 6 + [vmem()] * 8,
        out_specs=[vmem()] * 3,
        out_shape=[
            jax.ShapeDtypeStruct((TILE, TILE), f32),
            jax.ShapeDtypeStruct((TILE, TILE), f32),
            jax.ShapeDtypeStruct((8, HALF), f32),
        ],
        compiler_params=params(6),
        cost_estimate=cost(3_300_000_000, 9_000_000),
        name="image_two",
    )(*scalars, part, part_other, q1, stats, *stacks)


def image_three_body(
    ids, rsector, rsector_other, sector, lsize, rsize,
    part_a, part_b, q1, q2, stats_in, r_hi, r_lo, l_hi, l_lo, slots,
):
    mask = mask_of(*live_sizes(ids, rsector, rsector_other, sector, lsize, rsize))
    image = jnp.where(mask, part_a[...] + part_b[...], 0.0)
    i, j = grids(8, HALF)
    beta = total(jnp.where((j == 2) & (i == 0), stats_in[...], 0.0))
    alpha, norm, vec = lanczos(image, q2[...], q1[...], beta)
    pick = jnp.where(ids[1] == 0, q2[...], vec)
    for n in range(16):
        slots[n, :16, :] = pick[16 * n : 16 * n + 16, :HALF]
        slots[n, 16:COLS, :] = pick[16 * n : 16 * n + 16, HALF:]
    stats = put(put(stats_in[...], 3, alpha), 4, norm)
    alpha = total(vec * half_image(vec, r_hi, r_lo, l_hi, l_lo))
    stats = put(stats, 5, alpha)
    for n in range(16):
        slots[n, COLS:, :] = stats


def image_three(scalars, part, part_other, q1, q2, stats, stacks):
    return pl.pallas_call(
        image_three_body,
        in_specs=[smem()] * 6 + [vmem()] * 9,
        out_specs=vmem(),
        out_shape=jax.ShapeDtypeStruct((16, COLS + 8, HALF), f32),
        compiler_params=params(6),
        cost_estimate=cost(3_300_000_000, 9_000_000),
        name="image_three",
    )(*scalars, part, part_other, q1, q2, stats, *stacks)


def ritz_pair(norm, a1, b1, a2, b2, a3):
    def apply(x):
        return [a1 * x[0] + b1 * x[1], b1 * x[0] + a2 * x[1] + b2 * x[2], b2 * x[1] + a3 * x[2]]

    def dot(x, y):
        return jnp.sum(x[0] * y[0] + x[1] * y[1] + x[2] * y[2], axis=1, keepdims=True)

    zero = jnp.zeros_like(norm)
    start = [norm, zero, zero]
    image = apply(start)
    norm_sq = dot(start, start)
    correlation = dot(start, image)
    inv_norm = 1.0 / jnp.sqrt(norm_sq)
    basis = [x * inv_norm for x in start]
    applied = [x * inv_norm for x in image]
    ritz = correlation / norm_sq
    for _ in range(ITERS):
        residual = [x - ritz * y for x, y in zip(applied, basis)]
        res_sq = dot(residual, residual)
        length = jnp.sqrt(res_sq)
        fresh = [x / length for x in residual]
        fresh_applied = apply(fresh)
        curvature = dot(fresh, fresh_applied)
        half_gap = 0.5 * (ritz - curvature)
        root = jnp.sqrt(half_gap * half_gap + res_sq)
        lowest = 0.5 * (ritz + curvature) - root
        first = curvature - lowest
        pair = jnp.sqrt(first * first + res_sq)
        basis = [(first * x - length * y) / pair for x, y in zip(basis, fresh)]
        applied = [(first * x - length * y) / pair for x, y in zip(applied, fresh_applied)]
        ritz = lowest
    return basis, ritz


def finish_body(
    ids, sector, rsector, lsize, rsize, own_stats, other_stats, thin, got, back,
    out, energy, coef,
):
    _, lane = grids(64, HALF)
    stats = own_stats[...] + jnp.where(lane == 5, other_stats[...], 0.0)
    flip = jnp.concatenate([stats, jnp.zeros((64, HALF), f32)], axis=0).T
    norm, a1, b1, a2, b2, a3 = [flip[m : m + 1, :] for m in range(6)]
    basis, ritz = ritz_pair(norm, a1, b1, a2, b2, a3)
    energy[0, 0] = jnp.sum(ritz)
    scale = jnp.sqrt(jnp.full((1, HALF), 64 * TILE * TILE, f32))
    i, _ = grids(HALF, HALF)
    c1 = basis[0] * inverse(norm) * scale
    c2 = basis[1] * scale
    c3 = basis[2] * scale
    coef[...] = jnp.where(i == 0, c1, jnp.where(i == 1, c2, jnp.where(i == 2, c3, 0.0))).T
    core = ids[1]
    own = coef[pl.ds(pl.multiple_of(core * 8, 8), 8), :]
    jcol, irow = grids(16, TILE)
    for b in range(8):
        live_left = lsize[sector[ids[0] * 16 + core * 8 + b]]
        live_right = rsize[rsector[b]]
        live = (jcol + ids[2] * 16 < live_right) & (irow < live_left)
        at = core * 8 + b
        keep = jnp.concatenate([got[at, :16, :], got[at, 16:COLS, :]], axis=1)
        recv = jnp.concatenate([back[b, :16, :], back[b, 16:COLS, :]], axis=1)
        second = jnp.where(core == 0, keep, recv)
        third = jnp.where(core == 0, recv, keep)
        out[b] = (
            own[b : b + 1, 0:1] * jnp.where(live, thin[b], 0.0)
            + own[b : b + 1, 1:2] * second
            + own[b : b + 1, 2:3] * third
        )


def finish(ids, sector, rsector, lsize, rsize, own_stats, other_stats, thin, got, back):
    return pl.pallas_call(
        finish_body,
        in_specs=[smem()] * 5 + [vmem()] * 5,
        out_specs=[vmem(), smem()],
        out_shape=[
            jax.ShapeDtypeStruct(thin.shape, f32),
            jax.ShapeDtypeStruct((1, 1), f32),
        ],
        scratch_shapes=[pltpu.VMEM((HALF, HALF), f32)],
        compiler_params=params(4),
        name="finish",
    )(ids, sector, rsector, lsize, rsize, own_stats, other_stats, thin, got, back)


def local(theta, left_env, right_env, left_sector, right_sector, term_on, left_size, right_size):
    plane = lax.axis_index("y").astype(jnp.int32)
    core = lax.axis_index("c").astype(jnp.int32)
    place = lax.axis_index(COL).astype(jnp.int32)
    ids = jnp.stack([plane, core, place])
    thin = jnp.swapaxes(theta, 1, 2)

    rsector_other = lax.ppermute(right_sector, "c", SWAP)
    on_other = lax.ppermute(term_on, "c", SWAP)
    thin_other = lax.ppermute(thin, "c", SWAP)

    mine, folded, right_folded = fold(ids, left_env, right_env)
    theirs = lax.ppermute(folded, "c", SWAP)
    theirs, rsector_other, on_other, thin_other = lax.optimization_barrier(
        (theirs, rsector_other, on_other, thin_other)
    )
    below = [lax.ppermute(x, "y", UP) for x in (mine, theirs)]
    above = [lax.ppermute(x, "y", DOWN) for x in (mine, theirs)]
    far = [lax.ppermute(below[0], "y", UP), lax.ppermute(above[1], "y", DOWN)]

    slots = right_slots(
        ids, right_sector, rsector_other, term_on, on_other, thin, thin_other, right_folded
    )
    slots, theirs_now = lax.optimization_barrier((slots, theirs))
    arrived = lax.all_to_all(slots, COL, 0, 0, tiled=True)
    scalars = (ids, right_sector, rsector_other, left_sector, left_size, right_size)
    halves = lax.ppermute(arrived[:, :THIN, :], "c", SWAP)
    r_hi, r_lo, m_hi, m_lo, q1, stats = first_vector(scalars, halves, arrived)

    left_sent = left_slots(ids, left_sector, [mine, theirs] + above + below, far)
    left_arrived = lax.all_to_all(left_sent, COL, 0, 0, tiled=True)
    l_hi, l_lo, part = image_one(left_arrived, m_hi, m_lo)
    stacks = (r_hi, r_lo, l_hi, l_lo)
    part, q2, stats = image_two(scalars, part, lax.ppermute(part, "c", SWAP), q1, stats, stacks)
    sent = image_three(scalars, part, lax.ppermute(part, "c", SWAP), q1, q2, stats, stacks)

    got = lax.all_to_all(sent, COL, 0, 0, tiled=True)
    plane_stats = got[:, COLS, :]
    turned = [
        lax.ppermute(plane_stats, "y", [(i, (i + k) % 4) for i in range(4)]) for k in (1, 2, 3)
    ]
    give = lax.dynamic_slice(got, ((1 - core) * 8, 0, 0), (8, COLS, HALF))
    back = lax.ppermute(give, "c", SWAP)
    own_stats = jnp.concatenate([plane_stats] + turned)
    other_stats = lax.ppermute(own_stats, "c", SWAP)
    out, energy = finish(
        ids, left_sector, right_sector, left_size, right_size,
        own_stats, other_stats, thin, got, back,
    )
    return jnp.swapaxes(out, 1, 2), energy[0, 0]


def solution(mesh):
    fine = Mesh(mesh.devices.reshape(4, 2, 4, 4), ALL)
    row = ("y", "c")
    placed = (
        P(row, None, COL),
        P(row, COL, None, None),
        P(None, COL, None, None),
        P(),
        P(row),
        P(row, COL),
        P(),
        P(),
    )
    return jax.shard_map(
        local, mesh=fine, in_specs=placed, out_specs=(P(row, None, COL), P()), check_vma=False
    )
```

```python
import jax
import jax.numpy as jnp
from jax import lax
from jax.experimental import pallas as pl
from jax.experimental.pallas import tpu as pltpu
from jax.sharding import Mesh, PartitionSpec as P

ITERS = 2
LEFT_FLOPS = 15_000_000_000
NEAR_FLOPS = 1_000_000_000
TILE = 256
HALF = 128
TERMS = 16
FOLDED = 264
THIN = 16
COLS = 32
SLOT = THIN + FOLDED
COL = ("x", "z")
ALL = ("y", "c", "x", "z")
SWAP = [(0, 1), (1, 0)]
UP = [(i, (i + 1) % 4) for i in range(4)]
DOWN = [(i, (i - 1) % 4) for i in range(4)]
f32 = jnp.float32
bf16 = jnp.bfloat16


def params(mib):
    return pltpu.CompilerParams(vmem_limit_bytes=mib * 1024 * 1024)


def hbm():
    return pl.BlockSpec(memory_space=pltpu.HBM)


def in_hbm(x):
    return pltpu.with_memory_space_constraint(x, pltpu.HBM)


def smem():
    return pl.BlockSpec(memory_space=pltpu.SMEM)


def cost(flops, nbytes):
    return pl.CostEstimate(flops=flops, transcendentals=0, bytes_accessed=nbytes)


def vmem():
    return pl.BlockSpec(memory_space=pltpu.VMEM)


def grids(rows, cols):
    i = lax.broadcasted_iota(jnp.int32, (rows, cols), 0)
    j = lax.broadcasted_iota(jnp.int32, (rows, cols), 1)
    return i, j


def fold_tile(tile):
    i, j = grids(HALF, HALF)
    a00 = tile[:HALF, :HALF]
    a11 = tile[HALF:, HALF:]
    fold = jnp.where(i >= j, a00, a11)
    diag = jnp.sum(jnp.where(i == j, a11, 0.0), axis=0, keepdims=True)
    return fold, tile[:HALF, HALF:], diag


def put_folded(dst, at, tile):
    fold, corner, diag = fold_tile(tile)
    dst[at, :HALF, :] = fold
    dst[at, HALF:TILE, :] = corner
    dst[at, TILE:, :] = jnp.broadcast_to(diag, (FOLDED - TILE, HALF))


def get_folded(src, at, row):
    return unfold_tile(
        src[at, row : row + HALF, :],
        src[at, row + HALF : row + TILE, :],
        src[at, row + TILE : row + TILE + 1, :],
    )


def unfold_tile(fold, corner, diag):
    i, j = grids(HALF, HALF)
    flip = fold.T
    a00 = jnp.where(i >= j, fold, flip)
    a11 = jnp.where(i == j, diag, jnp.where(i < j, fold, flip))
    top = jnp.concatenate([a00, corner], axis=1)
    low = jnp.concatenate([corner.T, a11], axis=1)
    return jnp.concatenate([top, low], axis=0)


def split(x):
    hi = x.astype(bf16)
    return hi, (x - hi.astype(f32)).astype(bf16)


def dot3(a_hi, a_lo, b_hi, b_lo):
    def dot(a, b):
        return jnp.dot(a, b, preferred_element_type=f32)

    return dot(a_hi, b_hi) + (dot(a_hi, b_lo) + dot(a_lo, b_hi))


def total(x):
    return jnp.sum(jnp.sum(x, axis=0, keepdims=True), axis=1, keepdims=True)


def inverse(norm):
    good = norm > 0.0
    return jnp.where(good, 1.0 / jnp.where(good, norm, 1.0), 0.0)


def put(stats, lane, value):
    _, j = grids(8, HALF)
    return jnp.where(j == lane, value, stats)


def fold_body(
    ids, left_env, right_env, keep, give, right, tiles, folded, others, sem_in, sem_out, sem_right
):
    def fetch(t):
        term = ids[1] if t else 1 - ids[1]
        return pltpu.make_async_copy(left_env.at[:, term], tiles.at[t], sem_in.at[t])

    def store(t):
        dst = keep if t else give
        return pltpu.make_async_copy(folded.at[t], dst, sem_out.at[t])

    rights = pltpu.make_async_copy(right_env.at[:, ids[1]], others, sem_right)
    for t in range(2):
        fetch(t).start()
    rights.start()
    right[8] = jnp.zeros((FOLDED, HALF), f32)
    for t in range(2):
        fetch(t).wait()
        for n in range(4):
            put_folded(folded.at[t], n, tiles[t, n])
        store(t).start()
    rights.wait()
    for n in range(8):
        put_folded(right, n, others[n])
    for t in range(2):
        store(t).wait()


def fold(ids, left_env, right_env):
    return pl.pallas_call(
        fold_body,
        in_specs=[smem(), hbm(), hbm()],
        out_specs=[hbm(), hbm(), vmem()],
        out_shape=[pltpu.HBM((4, FOLDED, HALF), f32)] * 2
        + [jax.ShapeDtypeStruct((9, FOLDED, HALF), f32)],
        scratch_shapes=[
            pltpu.VMEM((2, 4, TILE, TILE), f32),
            pltpu.VMEM((2, 4, FOLDED, HALF), f32),
            pltpu.VMEM((8, TILE, TILE), f32),
            pltpu.SemaphoreType.DMA((2,)),
            pltpu.SemaphoreType.DMA((2,)),
            pltpu.SemaphoreType.DMA(()),
        ],
        compiler_params=params(10),
        cost_estimate=cost(1_000_000, 6_000_000),
        name="fold",
    )(ids, in_hbm(left_env), in_hbm(right_env))


def sector_of(ids, rsector, rsector_other, slot):
    return jnp.where(slot // 8 == ids[1], rsector[slot % 8], rsector_other[slot % 8])


def right_slots_body(
    ids, rsector, rsector_other, on, on_other, thin, thin_other, folded, out, cols, sem
):
    for slot in range(TERMS):
        here = slot // 8 == ids[1]
        weight = jnp.where(here, on[slot % 8, ids[1]], on_other[slot % 8, ids[1]])
        sector = sector_of(ids, rsector, rsector_other, slot)
        src = folded.at[jnp.where(weight == 0, 8, sector)]
        pltpu.make_async_copy(src, out.at[slot, pl.ds(THIN, FOLDED), :], sem).start()
    for slot in range(TERMS):
        here = slot // 8 == ids[1]
        block = jnp.where(here, thin[slot % 8], thin_other[slot % 8])
        cols[slot] = jnp.where(ids[1] == 0, block[:, :HALF], block[:, HALF:])
    pltpu.make_async_copy(cols, out.at[:, pl.ds(0, THIN), :], sem).start()
    pltpu.make_async_copy(out, out, sem).wait()


def right_slots(ids, rsector, rsector_other, on, on_other, thin, thin_other, folded):
    return pl.pallas_call(
        right_slots_body,
        in_specs=[smem()] * 5 + [vmem()] * 3,
        out_specs=hbm(),
        out_shape=pltpu.HBM((TERMS, SLOT, HALF), f32),
        scratch_shapes=[
            pltpu.VMEM((TERMS, THIN, HALF), f32),
            pltpu.SemaphoreType.DMA(()),
        ],
        compiler_params=params(6),
        cost_estimate=cost(4_000_000, 6_000_000),
        name="right_slots",
    )(ids, rsector, rsector_other, on, on_other, thin, thin_other, folded)


def where_from(ids, left_sector, slot):
    sector = left_sector[ids[0] * 16 + slot]
    home = sector // 4
    return sector % 4, (home // 2 - ids[0] + 4) % 4, home % 2 == ids[1]


def send_tiles(out, sem, cases_of):
    def start(slot, carry):
        for case, src, tile in cases_of(slot):

            @pl.when(case)
            def _():
                pltpu.make_async_copy(src.at[tile], out.at[slot], sem).start()

        return carry

    def finish(slot, carry):
        for case, src, tile in cases_of(slot):

            @pl.when(case)
            def _():
                pltpu.make_async_copy(src.at[tile], out.at[slot], sem).wait()

        return carry

    lax.fori_loop(0, TERMS, start, 0)
    lax.fori_loop(0, TERMS, finish, 0)


def near_slots_body(ids, left_sector, mine, theirs, above_a, above_b, below_a, below_b, out, sem):
    def cases_of(slot):
        tile, away, same = where_from(ids, left_sector, slot)
        by_away = {0: (mine, theirs), 1: (above_a, above_b), 3: (below_a, below_b)}
        cases = []
        for planes, (first, second) in by_away.items():
            cases.append((same & (away == planes), first, tile))
            cases.append((~same & (away == planes), second, tile))
        return cases

    send_tiles(out, sem, cases_of)


def far_slots_body(ids, left_sector, far_a, far_b, near, out, sem):
    def cases_of(slot):
        tile, away, same = where_from(ids, left_sector, slot)
        return [(same & (away == 2), far_a, tile), (~same & (away == 2), far_b, tile)]

    send_tiles(out, sem, cases_of)


def left_slots(ids, left_sector, near, far):
    slots = pltpu.HBM((TERMS, FOLDED, HALF), f32)
    ready = pl.pallas_call(
        near_slots_body,
        in_specs=[smem(), smem()] + [vmem()] * 6,
        out_specs=hbm(),
        out_shape=slots,
        scratch_shapes=[pltpu.SemaphoreType.DMA(())],
        compiler_params=params(8),
        cost_estimate=cost(NEAR_FLOPS, 4_000_000),
        name="near_slots",
    )(ids, left_sector, *near)
    return pl.pallas_call(
        far_slots_body,
        in_specs=[smem(), smem()] + [vmem()] * 2 + [hbm()],
        out_specs=hbm(),
        out_shape=slots,
        scratch_shapes=[pltpu.SemaphoreType.DMA(())],
        input_output_aliases={4: 0},
        compiler_params=params(4),
        cost_estimate=cost(LEFT_FLOPS, 4_000_000),
        name="far_slots",
    )(ids, left_sector, *far, in_hbm(ready))


def live_sizes(ids, rsector, rsector_other, left_sector, left_size, right_size):
    live_left = left_size[left_sector[ids[0] * 16 + ids[2]]]
    live_right = right_size[sector_of(ids, rsector, rsector_other, ids[2])]
    return live_right, live_left


def mask_of(live_right, live_left):
    i, j = grids(TILE, TILE)
    return (i < live_right) & (j < live_left)


def first_body(
    ids, rsector, rsector_other, sector, lsize, rsize, halves, slots,
    r_hi, r_lo, m_hi, m_lo, q1, stats, arrived, sem,
):
    live_right, live_left = live_sizes(ids, rsector, rsector_other, sector, lsize, rsize)

    def fetch(n):
        return pltpu.make_async_copy(slots.at[n], arrived.at[n], sem.at[n])

    for n in range(TERMS):
        fetch(n).start()
    for n in range(TERMS):
        fetch(n).wait()
        full = get_folded(arrived, n, THIN)
        hi, lo = split(full)
        r_hi[n * TILE : (n + 1) * TILE, :] = hi
        r_lo[n * TILE : (n + 1) * TILE, :] = lo
    mine = jnp.concatenate([arrived[n, :THIN, :] for n in range(TERMS)], axis=0)
    theirs = jnp.concatenate([halves[n] for n in range(TERMS)], axis=0)
    first = ids[1] == 0
    block = jnp.concatenate(
        [jnp.where(first, mine, theirs), jnp.where(first, theirs, mine)], axis=1
    )
    start = jnp.where(mask_of(live_right, live_left), block, 0.0)
    norm = jnp.sqrt(total(start * start))
    vec = start * inverse(norm)
    q1[...] = vec
    stats[...] = put(jnp.zeros((8, HALF), f32), 0, norm)
    q_hi, q_lo = split(vec)
    for n in range(TERMS):
        rows = pl.ds(n * TILE, TILE)
        hi, lo = split(dot3(r_hi[rows, :], r_lo[rows, :], q_hi, q_lo))
        m_hi[:, rows] = hi
        m_lo[:, rows] = lo


def first_vector(scalars, halves, slots):
    return pl.pallas_call(
        first_body,
        in_specs=[smem()] * 6 + [vmem(), hbm()],
        out_specs=[vmem()] * 6,
        out_shape=[
            jax.ShapeDtypeStruct((TERMS * TILE, TILE), bf16),
            jax.ShapeDtypeStruct((TERMS * TILE, TILE), bf16),
            jax.ShapeDtypeStruct((TILE, TERMS * TILE), bf16),
            jax.ShapeDtypeStruct((TILE, TERMS * TILE), bf16),
            jax.ShapeDtypeStruct((TILE, TILE), f32),
            jax.ShapeDtypeStruct((8, HALF), f32),
        ],
        scratch_shapes=[
            pltpu.VMEM((TERMS, SLOT, HALF), f32),
            pltpu.SemaphoreType.DMA((TERMS,)),
        ],
        compiler_params=params(10),
        cost_estimate=cost(1_700_000_000, 12_000_000),
        name="first_vector",
    )(*scalars, halves, in_hbm(slots))


def image_one_body(arrived, m_hi, m_lo, l_hi, l_lo, part, here_hi, here_lo, sem):
    fetches = [
        pltpu.make_async_copy(m_hi, here_hi, sem.at[0]),
        pltpu.make_async_copy(m_lo, here_lo, sem.at[1]),
    ]
    for fetch in fetches:
        fetch.start()
    for n in range(TERMS):
        hi, lo = split(get_folded(arrived, n, 0))
        l_hi[n * TILE : (n + 1) * TILE, :] = hi
        l_lo[n * TILE : (n + 1) * TILE, :] = lo
    for fetch in fetches:
        fetch.wait()
    part[...] = dot3(here_hi[...], here_lo[...], l_hi[...], l_lo[...])


def image_one(arrived, m_hi, m_lo):
    stack = jax.ShapeDtypeStruct((TERMS * TILE, TILE), bf16)
    return pl.pallas_call(
        image_one_body,
        in_specs=[vmem(), hbm(), hbm()],
        out_specs=[vmem()] * 3,
        out_shape=[stack, stack, jax.ShapeDtypeStruct((TILE, TILE), f32)],
        scratch_shapes=[
            pltpu.VMEM((TILE, TERMS * TILE), bf16),
            pltpu.VMEM((TILE, TERMS * TILE), bf16),
            pltpu.SemaphoreType.DMA((2,)),
        ],
        compiler_params=params(10),
        cost_estimate=cost(1_700_000_000, 10_000_000),
        name="image_one",
    )(arrived, in_hbm(m_hi), in_hbm(m_lo))


def lanczos(image, last, before, beta):
    alpha = total(last * image)
    rest = image - alpha * last
    if before is not None:
        rest = rest - beta * before
    again = rest - total(last * rest) * last
    if before is not None:
        again = again - total(before * rest) * before
    norm = jnp.sqrt(total(again * again))
    return alpha, norm, again * inverse(norm)


def half_image(vec, r_hi, r_lo, l_hi, l_lo):
    q_hi, q_lo = split(vec)
    acc = jnp.zeros((TILE, TILE), f32)
    for n in range(TERMS):
        rows = pl.ds(n * TILE, TILE)
        hi, lo = split(dot3(r_hi[rows, :], r_lo[rows, :], q_hi, q_lo))
        acc = acc + dot3(hi, lo, l_hi[rows, :], l_lo[rows, :])
    return acc


def image_two_body(
    ids, rsector, rsector_other, sector, lsize, rsize,
    part_a, part_b, q1, stats_in, r_hi, r_lo, l_hi, l_lo,
    part, q2, stats,
):
    mask = mask_of(*live_sizes(ids, rsector, rsector_other, sector, lsize, rsize))
    image = jnp.where(mask, part_a[...] + part_b[...], 0.0)
    alpha, norm, vec = lanczos(image, q1[...], None, None)
    q2[...] = vec
    stats[...] = put(put(stats_in[...], 1, alpha), 2, norm)
    part[...] = half_image(vec, r_hi, r_lo, l_hi, l_lo)


def image_two(scalars, part, part_other, q1, stats, stacks):
    return pl.pallas_call(
        image_two_body,
        in_specs=[smem()] * 6 + [vmem()] * 8,
        out_specs=[vmem()] * 3,
        out_shape=[
            jax.ShapeDtypeStruct((TILE, TILE), f32),
            jax.ShapeDtypeStruct((TILE, TILE), f32),
            jax.ShapeDtypeStruct((8, HALF), f32),
        ],
        compiler_params=params(6),
        cost_estimate=cost(3_300_000_000, 9_000_000),
        name="image_two",
    )(*scalars, part, part_other, q1, stats, *stacks)


def image_three_body(
    ids, rsector, rsector_other, sector, lsize, rsize,
    part_a, part_b, q1, q2, stats_in, r_hi, r_lo, l_hi, l_lo, slots,
):
    mask = mask_of(*live_sizes(ids, rsector, rsector_other, sector, lsize, rsize))
    image = jnp.where(mask, part_a[...] + part_b[...], 0.0)
    i, j = grids(8, HALF)
    beta = total(jnp.where((j == 2) & (i == 0), stats_in[...], 0.0))
    alpha, norm, vec = lanczos(image, q2[...], q1[...], beta)
    pick = jnp.where(ids[1] == 0, q2[...], vec)
    for n in range(16):
        slots[n, :16, :] = pick[16 * n : 16 * n + 16, :HALF]
        slots[n, 16:COLS, :] = pick[16 * n : 16 * n + 16, HALF:]
    stats = put(put(stats_in[...], 3, alpha), 4, norm)
    alpha = total(vec * half_image(vec, r_hi, r_lo, l_hi, l_lo))
    stats = put(stats, 5, alpha)
    for n in range(16):
        slots[n, COLS:, :] = stats


def image_three(scalars, part, part_other, q1, q2, stats, stacks):
    return pl.pallas_call(
        image_three_body,
        in_specs=[smem()] * 6 + [vmem()] * 9,
        out_specs=vmem(),
        out_shape=jax.ShapeDtypeStruct((16, COLS + 8, HALF), f32),
        compiler_params=params(6),
        cost_estimate=cost(3_300_000_000, 9_000_000),
        name="image_three",
    )(*scalars, part, part_other, q1, q2, stats, *stacks)


def ritz_pair(norm, a1, b1, a2, b2, a3):
    def apply(x):
        return [a1 * x[0] + b1 * x[1], b1 * x[0] + a2 * x[1] + b2 * x[2], b2 * x[1] + a3 * x[2]]

    def dot(x, y):
        return jnp.sum(x[0] * y[0] + x[1] * y[1] + x[2] * y[2], axis=1, keepdims=True)

    zero = jnp.zeros_like(norm)
    start = [norm, zero, zero]
    image = apply(start)
    norm_sq = dot(start, start)
    correlation = dot(start, image)
    inv_norm = 1.0 / jnp.sqrt(norm_sq)
    basis = [x * inv_norm for x in start]
    applied = [x * inv_norm for x in image]
    ritz = correlation / norm_sq
    for _ in range(ITERS):
        residual = [x - ritz * y for x, y in zip(applied, basis)]
        res_sq = dot(residual, residual)
        length = jnp.sqrt(res_sq)
        fresh = [x / length for x in residual]
        fresh_applied = apply(fresh)
        curvature = dot(fresh, fresh_applied)
        half_gap = 0.5 * (ritz - curvature)
        root = jnp.sqrt(half_gap * half_gap + res_sq)
        lowest = 0.5 * (ritz + curvature) - root
        first = curvature - lowest
        pair = jnp.sqrt(first * first + res_sq)
        basis = [(first * x - length * y) / pair for x, y in zip(basis, fresh)]
        applied = [(first * x - length * y) / pair for x, y in zip(applied, fresh_applied)]
        ritz = lowest
    return basis, ritz


def finish_body(
    ids, sector, rsector, lsize, rsize, own_stats, other_stats, thin, got, back,
    out, energy, coef,
):
    _, lane = grids(64, HALF)
    stats = own_stats[...] + jnp.where(lane == 5, other_stats[...], 0.0)
    flip = jnp.concatenate([stats, jnp.zeros((64, HALF), f32)], axis=0).T
    norm, a1, b1, a2, b2, a3 = [flip[m : m + 1, :] for m in range(6)]
    basis, ritz = ritz_pair(norm, a1, b1, a2, b2, a3)
    energy[0, 0] = jnp.sum(ritz)
    scale = jnp.sqrt(jnp.full((1, HALF), 64 * TILE * TILE, f32))
    i, _ = grids(HALF, HALF)
    c1 = basis[0] * inverse(norm) * scale
    c2 = basis[1] * scale
    c3 = basis[2] * scale
    coef[...] = jnp.where(i == 0, c1, jnp.where(i == 1, c2, jnp.where(i == 2, c3, 0.0))).T
    core = ids[1]
    own = coef[pl.ds(pl.multiple_of(core * 8, 8), 8), :]
    jcol, irow = grids(16, TILE)
    for b in range(8):
        live_left = lsize[sector[ids[0] * 16 + core * 8 + b]]
        live_right = rsize[rsector[b]]
        live = (jcol + ids[2] * 16 < live_right) & (irow < live_left)
        at = core * 8 + b
        keep = jnp.concatenate([got[at, :16, :], got[at, 16:COLS, :]], axis=1)
        recv = jnp.concatenate([back[b, :16, :], back[b, 16:COLS, :]], axis=1)
        second = jnp.where(core == 0, keep, recv)
        third = jnp.where(core == 0, recv, keep)
        out[b] = (
            own[b : b + 1, 0:1] * jnp.where(live, thin[b], 0.0)
            + own[b : b + 1, 1:2] * second
            + own[b : b + 1, 2:3] * third
        )


def finish(ids, sector, rsector, lsize, rsize, own_stats, other_stats, thin, got, back):
    return pl.pallas_call(
        finish_body,
        in_specs=[smem()] * 5 + [vmem()] * 5,
        out_specs=[vmem(), smem()],
        out_shape=[
            jax.ShapeDtypeStruct(thin.shape, f32),
            jax.ShapeDtypeStruct((1, 1), f32),
        ],
        scratch_shapes=[pltpu.VMEM((HALF, HALF), f32)],
        compiler_params=params(4),
        name="finish",
    )(ids, sector, rsector, lsize, rsize, own_stats, other_stats, thin, got, back)


def local(theta, left_env, right_env, left_sector, right_sector, term_on, left_size, right_size):
    plane = lax.axis_index("y").astype(jnp.int32)
    core = lax.axis_index("c").astype(jnp.int32)
    place = lax.axis_index(COL).astype(jnp.int32)
    ids = jnp.stack([plane, core, place])
    thin = jnp.swapaxes(theta, 1, 2)

    rsector_other = lax.ppermute(right_sector, "c", SWAP)
    on_other = lax.ppermute(term_on, "c", SWAP)
    thin_other = lax.ppermute(thin, "c", SWAP)

    mine, folded, right_folded = fold(ids, left_env, right_env)
    theirs = lax.ppermute(folded, "c", SWAP)
    theirs, rsector_other, on_other, thin_other = lax.optimization_barrier(
        (theirs, rsector_other, on_other, thin_other)
    )
    below = [lax.ppermute(mine, "y", UP)]
    above = [lax.ppermute(mine, "y", DOWN)]

    slots = right_slots(
        ids, right_sector, rsector_other, term_on, on_other, thin, thin_other, right_folded
    )
    slots, theirs = lax.optimization_barrier((slots, theirs))
    below.append(lax.ppermute(theirs, "y", UP))
    above.append(lax.ppermute(theirs, "y", DOWN))
    far = [lax.ppermute(below[0], "y", UP), lax.ppermute(above[1], "y", DOWN)]
    arrived = lax.all_to_all(slots, COL, 0, 0, tiled=True)
    scalars = (ids, right_sector, rsector_other, left_sector, left_size, right_size)
    halves = lax.ppermute(arrived[:, :THIN, :], "c", SWAP)
    r_hi, r_lo, m_hi, m_lo, q1, stats = first_vector(scalars, halves, arrived)

    left_sent = left_slots(ids, left_sector, [mine, theirs] + above + below, far)
    left_arrived = lax.all_to_all(left_sent, COL, 0, 0, tiled=True)
    l_hi, l_lo, part = image_one(left_arrived, m_hi, m_lo)
    stacks = (r_hi, r_lo, l_hi, l_lo)
    part, q2, stats = image_two(scalars, part, lax.ppermute(part, "c", SWAP), q1, stats, stacks)
    sent = image_three(scalars, part, lax.ppermute(part, "c", SWAP), q1, q2, stats, stacks)

    got = lax.all_to_all(sent, COL, 0, 0, tiled=True)
    plane_stats = got[:, COLS, :]
    turned = [
        lax.ppermute(plane_stats, "y", [(i, (i + k) % 4) for i in range(4)]) for k in (1, 2, 3)
    ]
    give = lax.dynamic_slice(got, ((1 - core) * 8, 0, 0), (8, COLS, HALF))
    back = lax.ppermute(give, "c", SWAP)
    own_stats = jnp.concatenate([plane_stats] + turned)
    other_stats = lax.ppermute(own_stats, "c", SWAP)
    out, energy = finish(
        ids, left_sector, right_sector, left_size, right_size,
        own_stats, other_stats, thin, got, back,
    )
    return jnp.swapaxes(out, 1, 2), energy[0, 0]


def solution(mesh):
    fine = Mesh(mesh.devices.reshape(4, 2, 4, 4), ALL)
    row = ("y", "c")
    placed = (
        P(row, None, COL),
        P(row, COL, None, None),
        P(None, COL, None, None),
        P(),
        P(row),
        P(row, COL),
        P(),
        P(),
    )
    return jax.shard_map(
        local, mesh=fine, in_specs=placed, out_specs=(P(row, None, COL), P()), check_vma=False
    )
```

```python
import jax
import jax.numpy as jnp
from jax import lax
from jax.experimental import pallas as pl
from jax.experimental.pallas import tpu as pltpu
from jax.sharding import Mesh, PartitionSpec as P

ITERS = 2
LEFT_FLOPS = 15_000_000_000
NEAR_FLOPS = 3_000_000_000
TILE = 256
HALF = 128
TERMS = 16
FOLDED = 264
THIN = 16
COLS = 32
SLOT = THIN + FOLDED
COL = ("x", "z")
ALL = ("y", "c", "x", "z")
SWAP = [(0, 1), (1, 0)]
UP = [(i, (i + 1) % 4) for i in range(4)]
DOWN = [(i, (i - 1) % 4) for i in range(4)]
f32 = jnp.float32
bf16 = jnp.bfloat16


def params(mib):
    return pltpu.CompilerParams(vmem_limit_bytes=mib * 1024 * 1024)


def hbm():
    return pl.BlockSpec(memory_space=pltpu.HBM)


def in_hbm(x):
    return pltpu.with_memory_space_constraint(x, pltpu.HBM)


def smem():
    return pl.BlockSpec(memory_space=pltpu.SMEM)


def cost(flops, nbytes):
    return pl.CostEstimate(flops=flops, transcendentals=0, bytes_accessed=nbytes)


def vmem():
    return pl.BlockSpec(memory_space=pltpu.VMEM)


def grids(rows, cols):
    i = lax.broadcasted_iota(jnp.int32, (rows, cols), 0)
    j = lax.broadcasted_iota(jnp.int32, (rows, cols), 1)
    return i, j


def fold_tile(tile):
    i, j = grids(HALF, HALF)
    a00 = tile[:HALF, :HALF]
    a11 = tile[HALF:, HALF:]
    fold = jnp.where(i >= j, a00, a11)
    diag = jnp.sum(jnp.where(i == j, a11, 0.0), axis=0, keepdims=True)
    return fold, tile[:HALF, HALF:], diag


def put_folded(dst, at, tile):
    fold, corner, diag = fold_tile(tile)
    dst[at, :HALF, :] = fold
    dst[at, HALF:TILE, :] = corner
    dst[at, TILE:, :] = jnp.broadcast_to(diag, (FOLDED - TILE, HALF))


def get_folded(src, at, row):
    return unfold_tile(
        src[at, row : row + HALF, :],
        src[at, row + HALF : row + TILE, :],
        src[at, row + TILE : row + TILE + 1, :],
    )


def unfold_tile(fold, corner, diag):
    i, j = grids(HALF, HALF)
    flip = fold.T
    a00 = jnp.where(i >= j, fold, flip)
    a11 = jnp.where(i == j, diag, jnp.where(i < j, fold, flip))
    top = jnp.concatenate([a00, corner], axis=1)
    low = jnp.concatenate([corner.T, a11], axis=1)
    return jnp.concatenate([top, low], axis=0)


def split(x):
    hi = x.astype(bf16)
    return hi, (x - hi.astype(f32)).astype(bf16)


def dot3(a_hi, a_lo, b_hi, b_lo):
    def dot(a, b):
        return jnp.dot(a, b, preferred_element_type=f32)

    return dot(a_hi, b_hi) + (dot(a_hi, b_lo) + dot(a_lo, b_hi))


def total(x):
    return jnp.sum(jnp.sum(x, axis=0, keepdims=True), axis=1, keepdims=True)


def inverse(norm):
    good = norm > 0.0
    return jnp.where(good, 1.0 / jnp.where(good, norm, 1.0), 0.0)


def put(stats, lane, value):
    _, j = grids(8, HALF)
    return jnp.where(j == lane, value, stats)


def fold_body(
    ids, left_env, right_env, keep, give, right, tiles, folded, others, sem_in, sem_out, sem_right
):
    def fetch(t):
        term = ids[1] if t else 1 - ids[1]
        return pltpu.make_async_copy(left_env.at[:, term], tiles.at[t], sem_in.at[t])

    def store(t):
        dst = keep if t else give
        return pltpu.make_async_copy(folded.at[t], dst, sem_out.at[t])

    rights = pltpu.make_async_copy(right_env.at[:, ids[1]], others, sem_right)
    for t in range(2):
        fetch(t).start()
    rights.start()
    right[8] = jnp.zeros((FOLDED, HALF), f32)
    for t in range(2):
        fetch(t).wait()
        for n in range(4):
            put_folded(folded.at[t], n, tiles[t, n])
        store(t).start()
    rights.wait()
    for n in range(8):
        put_folded(right, n, others[n])
    for t in range(2):
        store(t).wait()


def fold(ids, left_env, right_env):
    return pl.pallas_call(
        fold_body,
        in_specs=[smem(), hbm(), hbm()],
        out_specs=[hbm(), hbm(), vmem()],
        out_shape=[pltpu.HBM((4, FOLDED, HALF), f32)] * 2
        + [jax.ShapeDtypeStruct((9, FOLDED, HALF), f32)],
        scratch_shapes=[
            pltpu.VMEM((2, 4, TILE, TILE), f32),
            pltpu.VMEM((2, 4, FOLDED, HALF), f32),
            pltpu.VMEM((8, TILE, TILE), f32),
            pltpu.SemaphoreType.DMA((2,)),
            pltpu.SemaphoreType.DMA((2,)),
            pltpu.SemaphoreType.DMA(()),
        ],
        compiler_params=params(10),
        cost_estimate=cost(1_000_000, 6_000_000),
        name="fold",
    )(ids, in_hbm(left_env), in_hbm(right_env))


def sector_of(ids, rsector, rsector_other, slot):
    return jnp.where(slot // 8 == ids[1], rsector[slot % 8], rsector_other[slot % 8])


def right_slots_body(
    ids, rsector, rsector_other, on, on_other, thin, thin_other, folded, out, cols, sem
):
    for slot in range(TERMS):
        here = slot // 8 == ids[1]
        weight = jnp.where(here, on[slot % 8, ids[1]], on_other[slot % 8, ids[1]])
        sector = sector_of(ids, rsector, rsector_other, slot)
        src = folded.at[jnp.where(weight == 0, 8, sector)]
        pltpu.make_async_copy(src, out.at[slot, pl.ds(THIN, FOLDED), :], sem).start()
    for slot in range(TERMS):
        here = slot // 8 == ids[1]
        block = jnp.where(here, thin[slot % 8], thin_other[slot % 8])
        cols[slot] = jnp.where(ids[1] == 0, block[:, :HALF], block[:, HALF:])
    pltpu.make_async_copy(cols, out.at[:, pl.ds(0, THIN), :], sem).start()
    pltpu.make_async_copy(out, out, sem).wait()


def right_slots(ids, rsector, rsector_other, on, on_other, thin, thin_other, folded):
    return pl.pallas_call(
        right_slots_body,
        in_specs=[smem()] * 5 + [vmem()] * 3,
        out_specs=hbm(),
        out_shape=pltpu.HBM((TERMS, SLOT, HALF), f32),
        scratch_shapes=[
            pltpu.VMEM((TERMS, THIN, HALF), f32),
            pltpu.SemaphoreType.DMA(()),
        ],
        compiler_params=params(6),
        cost_estimate=cost(4_000_000, 6_000_000),
        name="right_slots",
    )(ids, rsector, rsector_other, on, on_other, thin, thin_other, folded)


def where_from(ids, left_sector, slot):
    sector = left_sector[ids[0] * 16 + slot]
    home = sector // 4
    return sector % 4, (home // 2 - ids[0] + 4) % 4, home % 2 == ids[1]


def send_tiles(out, sem, cases_of):
    def start(slot, carry):
        for case, src, tile in cases_of(slot):

            @pl.when(case)
            def _():
                pltpu.make_async_copy(src.at[tile], out.at[slot], sem).start()

        return carry

    def finish(slot, carry):
        for case, src, tile in cases_of(slot):

            @pl.when(case)
            def _():
                pltpu.make_async_copy(src.at[tile], out.at[slot], sem).wait()

        return carry

    lax.fori_loop(0, TERMS, start, 0)
    lax.fori_loop(0, TERMS, finish, 0)


def near_slots_body(ids, left_sector, mine, theirs, above_a, above_b, below_a, below_b, out, sem):
    def cases_of(slot):
        tile, away, same = where_from(ids, left_sector, slot)
        by_away = {0: (mine, theirs), 1: (above_a, above_b), 3: (below_a, below_b)}
        cases = []
        for planes, (first, second) in by_away.items():
            cases.append((same & (away == planes), first, tile))
            cases.append((~same & (away == planes), second, tile))
        return cases

    send_tiles(out, sem, cases_of)


def far_slots_body(ids, left_sector, far_a, far_b, near, out, sem):
    def cases_of(slot):
        tile, away, same = where_from(ids, left_sector, slot)
        return [(same & (away == 2), far_a, tile), (~same & (away == 2), far_b, tile)]

    send_tiles(out, sem, cases_of)


def left_slots(ids, left_sector, near, far):
    slots = pltpu.HBM((TERMS, FOLDED, HALF), f32)
    ready = pl.pallas_call(
        near_slots_body,
        in_specs=[smem(), smem()] + [vmem()] * 6,
        out_specs=hbm(),
        out_shape=slots,
        scratch_shapes=[pltpu.SemaphoreType.DMA(())],
        compiler_params=params(8),
        cost_estimate=cost(NEAR_FLOPS, 4_000_000),
        name="near_slots",
    )(ids, left_sector, *near)
    return pl.pallas_call(
        far_slots_body,
        in_specs=[smem(), smem()] + [vmem()] * 2 + [hbm()],
        out_specs=hbm(),
        out_shape=slots,
        scratch_shapes=[pltpu.SemaphoreType.DMA(())],
        input_output_aliases={4: 0},
        compiler_params=params(4),
        cost_estimate=cost(LEFT_FLOPS, 4_000_000),
        name="far_slots",
    )(ids, left_sector, *far, in_hbm(ready))


def live_sizes(ids, rsector, rsector_other, left_sector, left_size, right_size):
    live_left = left_size[left_sector[ids[0] * 16 + ids[2]]]
    live_right = right_size[sector_of(ids, rsector, rsector_other, ids[2])]
    return live_right, live_left


def mask_of(live_right, live_left):
    i, j = grids(TILE, TILE)
    return (i < live_right) & (j < live_left)


def first_body(
    ids, rsector, rsector_other, sector, lsize, rsize, halves, slots,
    r_hi, r_lo, m_hi, m_lo, q1, stats, arrived, sem,
):
    live_right, live_left = live_sizes(ids, rsector, rsector_other, sector, lsize, rsize)

    def fetch(n):
        return pltpu.make_async_copy(slots.at[n], arrived.at[n], sem.at[n])

    for n in range(TERMS):
        fetch(n).start()
    for n in range(TERMS):
        fetch(n).wait()
        full = get_folded(arrived, n, THIN)
        hi, lo = split(full)
        r_hi[n * TILE : (n + 1) * TILE, :] = hi
        r_lo[n * TILE : (n + 1) * TILE, :] = lo
    mine = jnp.concatenate([arrived[n, :THIN, :] for n in range(TERMS)], axis=0)
    theirs = jnp.concatenate([halves[n] for n in range(TERMS)], axis=0)
    first = ids[1] == 0
    block = jnp.concatenate(
        [jnp.where(first, mine, theirs), jnp.where(first, theirs, mine)], axis=1
    )
    start = jnp.where(mask_of(live_right, live_left), block, 0.0)
    norm = jnp.sqrt(total(start * start))
    vec = start * inverse(norm)
    q1[...] = vec
    stats[...] = put(jnp.zeros((8, HALF), f32), 0, norm)
    q_hi, q_lo = split(vec)
    for n in range(TERMS):
        rows = pl.ds(n * TILE, TILE)
        hi, lo = split(dot3(r_hi[rows, :], r_lo[rows, :], q_hi, q_lo))
        m_hi[:, rows] = hi
        m_lo[:, rows] = lo


def first_vector(scalars, halves, slots):
    return pl.pallas_call(
        first_body,
        in_specs=[smem()] * 6 + [vmem(), hbm()],
        out_specs=[vmem()] * 6,
        out_shape=[
            jax.ShapeDtypeStruct((TERMS * TILE, TILE), bf16),
            jax.ShapeDtypeStruct((TERMS * TILE, TILE), bf16),
            jax.ShapeDtypeStruct((TILE, TERMS * TILE), bf16),
            jax.ShapeDtypeStruct((TILE, TERMS * TILE), bf16),
            jax.ShapeDtypeStruct((TILE, TILE), f32),
            jax.ShapeDtypeStruct((8, HALF), f32),
        ],
        scratch_shapes=[
            pltpu.VMEM((TERMS, SLOT, HALF), f32),
            pltpu.SemaphoreType.DMA((TERMS,)),
        ],
        compiler_params=params(10),
        cost_estimate=cost(1_700_000_000, 12_000_000),
        name="first_vector",
    )(*scalars, halves, in_hbm(slots))


def image_one_body(arrived, m_hi, m_lo, l_hi, l_lo, part, here_hi, here_lo, sem):
    fetches = [
        pltpu.make_async_copy(m_hi, here_hi, sem.at[0]),
        pltpu.make_async_copy(m_lo, here_lo, sem.at[1]),
    ]
    for fetch in fetches:
        fetch.start()
    for n in range(TERMS):
        hi, lo = split(get_folded(arrived, n, 0))
        l_hi[n * TILE : (n + 1) * TILE, :] = hi
        l_lo[n * TILE : (n + 1) * TILE, :] = lo
    for fetch in fetches:
        fetch.wait()
    part[...] = dot3(here_hi[...], here_lo[...], l_hi[...], l_lo[...])


def image_one(arrived, m_hi, m_lo):
    stack = jax.ShapeDtypeStruct((TERMS * TILE, TILE), bf16)
    return pl.pallas_call(
        image_one_body,
        in_specs=[vmem(), hbm(), hbm()],
        out_specs=[vmem()] * 3,
        out_shape=[stack, stack, jax.ShapeDtypeStruct((TILE, TILE), f32)],
        scratch_shapes=[
            pltpu.VMEM((TILE, TERMS * TILE), bf16),
            pltpu.VMEM((TILE, TERMS * TILE), bf16),
            pltpu.SemaphoreType.DMA((2,)),
        ],
        compiler_params=params(10),
        cost_estimate=cost(1_700_000_000, 10_000_000),
        name="image_one",
    )(arrived, in_hbm(m_hi), in_hbm(m_lo))


def lanczos(image, last, before, beta):
    alpha = total(last * image)
    rest = image - alpha * last
    if before is not None:
        rest = rest - beta * before
    again = rest - total(last * rest) * last
    if before is not None:
        again = again - total(before * rest) * before
    norm = jnp.sqrt(total(again * again))
    return alpha, norm, again * inverse(norm)


def half_image(vec, r_hi, r_lo, l_hi, l_lo):
    q_hi, q_lo = split(vec)
    acc = jnp.zeros((TILE, TILE), f32)
    for n in range(TERMS):
        rows = pl.ds(n * TILE, TILE)
        hi, lo = split(dot3(r_hi[rows, :], r_lo[rows, :], q_hi, q_lo))
        acc = acc + dot3(hi, lo, l_hi[rows, :], l_lo[rows, :])
    return acc


def image_two_body(
    ids, rsector, rsector_other, sector, lsize, rsize,
    part_a, part_b, q1, stats_in, r_hi, r_lo, l_hi, l_lo,
    part, q2, stats,
):
    mask = mask_of(*live_sizes(ids, rsector, rsector_other, sector, lsize, rsize))
    image = jnp.where(mask, part_a[...] + part_b[...], 0.0)
    alpha, norm, vec = lanczos(image, q1[...], None, None)
    q2[...] = vec
    stats[...] = put(put(stats_in[...], 1, alpha), 2, norm)
    part[...] = half_image(vec, r_hi, r_lo, l_hi, l_lo)


def image_two(scalars, part, part_other, q1, stats, stacks):
    return pl.pallas_call(
        image_two_body,
        in_specs=[smem()] * 6 + [vmem()] * 8,
        out_specs=[vmem()] * 3,
        out_shape=[
            jax.ShapeDtypeStruct((TILE, TILE), f32),
            jax.ShapeDtypeStruct((TILE, TILE), f32),
            jax.ShapeDtypeStruct((8, HALF), f32),
        ],
        compiler_params=params(6),
        cost_estimate=cost(3_300_000_000, 9_000_000),
        name="image_two",
    )(*scalars, part, part_other, q1, stats, *stacks)


def image_three_body(
    ids, rsector, rsector_other, sector, lsize, rsize,
    part_a, part_b, q1, q2, stats_in, r_hi, r_lo, l_hi, l_lo, slots,
):
    mask = mask_of(*live_sizes(ids, rsector, rsector_other, sector, lsize, rsize))
    image = jnp.where(mask, part_a[...] + part_b[...], 0.0)
    i, j = grids(8, HALF)
    beta = total(jnp.where((j == 2) & (i == 0), stats_in[...], 0.0))
    alpha, norm, vec = lanczos(image, q2[...], q1[...], beta)
    pick = jnp.where(ids[1] == 0, q2[...], vec)
    for n in range(16):
        slots[n, :16, :] = pick[16 * n : 16 * n + 16, :HALF]
        slots[n, 16:COLS, :] = pick[16 * n : 16 * n + 16, HALF:]
    stats = put(put(stats_in[...], 3, alpha), 4, norm)
    alpha = total(vec * half_image(vec, r_hi, r_lo, l_hi, l_lo))
    stats = put(stats, 5, alpha)
    for n in range(16):
        slots[n, COLS:, :] = stats


def image_three(scalars, part, part_other, q1, q2, stats, stacks):
    return pl.pallas_call(
        image_three_body,
        in_specs=[smem()] * 6 + [vmem()] * 9,
        out_specs=vmem(),
        out_shape=jax.ShapeDtypeStruct((16, COLS + 8, HALF), f32),
        compiler_params=params(6),
        cost_estimate=cost(3_300_000_000, 9_000_000),
        name="image_three",
    )(*scalars, part, part_other, q1, q2, stats, *stacks)


def ritz_pair(norm, a1, b1, a2, b2, a3):
    def apply(x):
        return [a1 * x[0] + b1 * x[1], b1 * x[0] + a2 * x[1] + b2 * x[2], b2 * x[1] + a3 * x[2]]

    def dot(x, y):
        return jnp.sum(x[0] * y[0] + x[1] * y[1] + x[2] * y[2], axis=1, keepdims=True)

    zero = jnp.zeros_like(norm)
    start = [norm, zero, zero]
    image = apply(start)
    norm_sq = dot(start, start)
    correlation = dot(start, image)
    inv_norm = 1.0 / jnp.sqrt(norm_sq)
    basis = [x * inv_norm for x in start]
    applied = [x * inv_norm for x in image]
    ritz = correlation / norm_sq
    for _ in range(ITERS):
        residual = [x - ritz * y for x, y in zip(applied, basis)]
        res_sq = dot(residual, residual)
        length = jnp.sqrt(res_sq)
        fresh = [x / length for x in residual]
        fresh_applied = apply(fresh)
        curvature = dot(fresh, fresh_applied)
        half_gap = 0.5 * (ritz - curvature)
        root = jnp.sqrt(half_gap * half_gap + res_sq)
        lowest = 0.5 * (ritz + curvature) - root
        first = curvature - lowest
        pair = jnp.sqrt(first * first + res_sq)
        basis = [(first * x - length * y) / pair for x, y in zip(basis, fresh)]
        applied = [(first * x - length * y) / pair for x, y in zip(applied, fresh_applied)]
        ritz = lowest
    return basis, ritz


def finish_body(
    ids, sector, rsector, lsize, rsize, own_stats, other_stats, thin, got, back,
    out, energy, coef,
):
    _, lane = grids(64, HALF)
    stats = own_stats[...] + jnp.where(lane == 5, other_stats[...], 0.0)
    flip = jnp.concatenate([stats, jnp.zeros((64, HALF), f32)], axis=0).T
    norm, a1, b1, a2, b2, a3 = [flip[m : m + 1, :] for m in range(6)]
    basis, ritz = ritz_pair(norm, a1, b1, a2, b2, a3)
    energy[0, 0] = jnp.sum(ritz)
    scale = jnp.sqrt(jnp.full((1, HALF), 64 * TILE * TILE, f32))
    i, _ = grids(HALF, HALF)
    c1 = basis[0] * inverse(norm) * scale
    c2 = basis[1] * scale
    c3 = basis[2] * scale
    coef[...] = jnp.where(i == 0, c1, jnp.where(i == 1, c2, jnp.where(i == 2, c3, 0.0))).T
    core = ids[1]
    own = coef[pl.ds(pl.multiple_of(core * 8, 8), 8), :]
    jcol, irow = grids(16, TILE)
    for b in range(8):
        live_left = lsize[sector[ids[0] * 16 + core * 8 + b]]
        live_right = rsize[rsector[b]]
        live = (jcol + ids[2] * 16 < live_right) & (irow < live_left)
        at = core * 8 + b
        keep = jnp.concatenate([got[at, :16, :], got[at, 16:COLS, :]], axis=1)
        recv = jnp.concatenate([back[b, :16, :], back[b, 16:COLS, :]], axis=1)
        second = jnp.where(core == 0, keep, recv)
        third = jnp.where(core == 0, recv, keep)
        out[b] = (
            own[b : b + 1, 0:1] * jnp.where(live, thin[b], 0.0)
            + own[b : b + 1, 1:2] * second
            + own[b : b + 1, 2:3] * third
        )


def finish(ids, sector, rsector, lsize, rsize, own_stats, other_stats, thin, got, back):
    return pl.pallas_call(
        finish_body,
        in_specs=[smem()] * 5 + [vmem()] * 5,
        out_specs=[vmem(), smem()],
        out_shape=[
            jax.ShapeDtypeStruct(thin.shape, f32),
            jax.ShapeDtypeStruct((1, 1), f32),
        ],
        scratch_shapes=[pltpu.VMEM((HALF, HALF), f32)],
        compiler_params=params(4),
        name="finish",
    )(ids, sector, rsector, lsize, rsize, own_stats, other_stats, thin, got, back)


def local(theta, left_env, right_env, left_sector, right_sector, term_on, left_size, right_size):
    plane = lax.axis_index("y").astype(jnp.int32)
    core = lax.axis_index("c").astype(jnp.int32)
    place = lax.axis_index(COL).astype(jnp.int32)
    ids = jnp.stack([plane, core, place])
    thin = jnp.swapaxes(theta, 1, 2)

    rsector_other = lax.ppermute(right_sector, "c", SWAP)
    on_other = lax.ppermute(term_on, "c", SWAP)
    thin_other = lax.ppermute(thin, "c", SWAP)

    mine, folded, right_folded = fold(ids, left_env, right_env)
    theirs = lax.ppermute(folded, "c", SWAP)
    theirs, rsector_other, on_other, thin_other = lax.optimization_barrier(
        (theirs, rsector_other, on_other, thin_other)
    )
    below = [lax.ppermute(x, "y", UP) for x in (mine, theirs)]
    above = [lax.ppermute(x, "y", DOWN) for x in (mine, theirs)]
    far = [lax.ppermute(below[0], "y", UP), lax.ppermute(above[1], "y", DOWN)]

    slots = right_slots(
        ids, right_sector, rsector_other, term_on, on_other, thin, thin_other, right_folded
    )
    slots, theirs_now = lax.optimization_barrier((slots, theirs))
    arrived = lax.all_to_all(slots, COL, 0, 0, tiled=True)
    scalars = (ids, right_sector, rsector_other, left_sector, left_size, right_size)
    halves = lax.ppermute(arrived[:, :THIN, :], "c", SWAP)
    r_hi, r_lo, m_hi, m_lo, q1, stats = first_vector(scalars, halves, arrived)

    left_sent = left_slots(ids, left_sector, [mine, theirs] + above + below, far)
    left_arrived = lax.all_to_all(left_sent, COL, 0, 0, tiled=True)
    l_hi, l_lo, part = image_one(left_arrived, m_hi, m_lo)
    stacks = (r_hi, r_lo, l_hi, l_lo)
    part, q2, stats = image_two(scalars, part, lax.ppermute(part, "c", SWAP), q1, stats, stacks)
    sent = image_three(scalars, part, lax.ppermute(part, "c", SWAP), q1, q2, stats, stacks)

    got = lax.all_to_all(sent, COL, 0, 0, tiled=True)
    plane_stats = got[:, COLS, :]
    turned = [
        lax.ppermute(plane_stats, "y", [(i, (i + k) % 4) for i in range(4)]) for k in (1, 2, 3)
    ]
    give = lax.dynamic_slice(got, ((1 - core) * 8, 0, 0), (8, COLS, HALF))
    back = lax.ppermute(give, "c", SWAP)
    own_stats = jnp.concatenate([plane_stats] + turned)
    other_stats = lax.ppermute(own_stats, "c", SWAP)
    out, energy = finish(
        ids, left_sector, right_sector, left_size, right_size,
        own_stats, other_stats, thin, got, back,
    )
    return jnp.swapaxes(out, 1, 2), energy[0, 0]


def solution(mesh):
    fine = Mesh(mesh.devices.reshape(4, 2, 4, 4), ALL)
    row = ("y", "c")
    placed = (
        P(row, None, COL),
        P(row, COL, None, None),
        P(None, COL, None, None),
        P(),
        P(row),
        P(row, COL),
        P(),
        P(),
    )
    return jax.shard_map(
        local, mesh=fine, in_specs=placed, out_specs=(P(row, None, COL), P()), check_vma=False
    )
```

```python
import jax
import jax.numpy as jnp
from jax import lax
from jax.experimental import pallas as pl
from jax.experimental.pallas import tpu as pltpu
from jax.sharding import Mesh, PartitionSpec as P

ITERS = 2
LEFT_FLOPS = 15_000_000_000
NEAR_FLOPS = 1_000_000_000
TILE = 256
HALF = 128
TERMS = 16
FOLDED = 264
THIN = 16
COLS = 32
SLOT = THIN + FOLDED
COL = ("x", "z")
ALL = ("y", "c", "x", "z")
SWAP = [(0, 1), (1, 0)]
UP = [(i, (i + 1) % 4) for i in range(4)]
DOWN = [(i, (i - 1) % 4) for i in range(4)]
f32 = jnp.float32
bf16 = jnp.bfloat16


def params(mib):
    return pltpu.CompilerParams(vmem_limit_bytes=mib * 1024 * 1024)


def hbm():
    return pl.BlockSpec(memory_space=pltpu.HBM)


def in_hbm(x):
    return pltpu.with_memory_space_constraint(x, pltpu.HBM)


def smem():
    return pl.BlockSpec(memory_space=pltpu.SMEM)


def cost(flops, nbytes):
    return pl.CostEstimate(flops=flops, transcendentals=0, bytes_accessed=nbytes)


def vmem():
    return pl.BlockSpec(memory_space=pltpu.VMEM)


def grids(rows, cols):
    i = lax.broadcasted_iota(jnp.int32, (rows, cols), 0)
    j = lax.broadcasted_iota(jnp.int32, (rows, cols), 1)
    return i, j


def fold_tile(tile):
    i, j = grids(HALF, HALF)
    a00 = tile[:HALF, :HALF]
    a11 = tile[HALF:, HALF:]
    fold = jnp.where(i >= j, a00, a11)
    diag = jnp.sum(jnp.where(i == j, a11, 0.0), axis=0, keepdims=True)
    return fold, tile[:HALF, HALF:], diag


def put_folded(dst, at, tile):
    fold, corner, diag = fold_tile(tile)
    dst[at, :HALF, :] = fold
    dst[at, HALF:TILE, :] = corner
    dst[at, TILE:, :] = jnp.broadcast_to(diag, (FOLDED - TILE, HALF))


def get_folded(src, at, row):
    return unfold_tile(
        src[at, row : row + HALF, :],
        src[at, row + HALF : row + TILE, :],
        src[at, row + TILE : row + TILE + 1, :],
    )


def unfold_tile(fold, corner, diag):
    i, j = grids(HALF, HALF)
    flip = fold.T
    a00 = jnp.where(i >= j, fold, flip)
    a11 = jnp.where(i == j, diag, jnp.where(i < j, fold, flip))
    top = jnp.concatenate([a00, corner], axis=1)
    low = jnp.concatenate([corner.T, a11], axis=1)
    return jnp.concatenate([top, low], axis=0)


def split(x):
    hi = x.astype(bf16)
    return hi, (x - hi.astype(f32)).astype(bf16)


def dot3(a_hi, a_lo, b_hi, b_lo):
    def dot(a, b):
        return jnp.dot(a, b, preferred_element_type=f32)

    return dot(a_hi, b_hi) + (dot(a_hi, b_lo) + dot(a_lo, b_hi))


def total(x):
    return jnp.sum(jnp.sum(x, axis=0, keepdims=True), axis=1, keepdims=True)


def inverse(norm):
    good = norm > 0.0
    return jnp.where(good, 1.0 / jnp.where(good, norm, 1.0), 0.0)


def put(stats, lane, value):
    _, j = grids(8, HALF)
    return jnp.where(j == lane, value, stats)


def fold_body(
    ids, left_env, right_env, keep, give, right, tiles, folded, others, sem_in, sem_out, sem_right
):
    def fetch(t):
        term = ids[1] if t else 1 - ids[1]
        return pltpu.make_async_copy(left_env.at[:, term], tiles.at[t], sem_in.at[t])

    def store(t):
        dst = keep if t else give
        return pltpu.make_async_copy(folded.at[t], dst, sem_out.at[t])

    rights = pltpu.make_async_copy(right_env.at[:, ids[1]], others, sem_right)
    for t in range(2):
        fetch(t).start()
    rights.start()
    right[8] = jnp.zeros((FOLDED, HALF), f32)
    for t in range(2):
        fetch(t).wait()
        for n in range(4):
            put_folded(folded.at[t], n, tiles[t, n])
        store(t).start()
    rights.wait()
    for n in range(8):
        put_folded(right, n, others[n])
    for t in range(2):
        store(t).wait()


def fold(ids, left_env, right_env):
    return pl.pallas_call(
        fold_body,
        in_specs=[smem(), hbm(), hbm()],
        out_specs=[hbm(), hbm(), vmem()],
        out_shape=[pltpu.HBM((4, FOLDED, HALF), f32)] * 2
        + [jax.ShapeDtypeStruct((9, FOLDED, HALF), f32)],
        scratch_shapes=[
            pltpu.VMEM((2, 4, TILE, TILE), f32),
            pltpu.VMEM((2, 4, FOLDED, HALF), f32),
            pltpu.VMEM((8, TILE, TILE), f32),
            pltpu.SemaphoreType.DMA((2,)),
            pltpu.SemaphoreType.DMA((2,)),
            pltpu.SemaphoreType.DMA(()),
        ],
        compiler_params=params(10),
        cost_estimate=cost(1_000_000, 6_000_000),
        name="fold",
    )(ids, in_hbm(left_env), in_hbm(right_env))


def sector_of(ids, rsector, rsector_other, slot):
    return jnp.where(slot // 8 == ids[1], rsector[slot % 8], rsector_other[slot % 8])


def right_slots_body(
    ids, rsector, rsector_other, on, on_other, thin, thin_other, folded, out, cols, sem
):
    for slot in range(TERMS):
        here = slot // 8 == ids[1]
        weight = jnp.where(here, on[slot % 8, ids[1]], on_other[slot % 8, ids[1]])
        sector = sector_of(ids, rsector, rsector_other, slot)
        src = folded.at[jnp.where(weight == 0, 8, sector)]
        pltpu.make_async_copy(src, out.at[slot, pl.ds(THIN, FOLDED), :], sem).start()
    for slot in range(TERMS):
        here = slot // 8 == ids[1]
        block = jnp.where(here, thin[slot % 8], thin_other[slot % 8])
        cols[slot] = jnp.where(ids[1] == 0, block[:, :HALF], block[:, HALF:])
    pltpu.make_async_copy(cols, out.at[:, pl.ds(0, THIN), :], sem).start()
    pltpu.make_async_copy(out, out, sem).wait()


def right_slots(ids, rsector, rsector_other, on, on_other, thin, thin_other, folded):
    return pl.pallas_call(
        right_slots_body,
        in_specs=[smem()] * 5 + [vmem()] * 3,
        out_specs=hbm(),
        out_shape=pltpu.HBM((TERMS, SLOT, HALF), f32),
        scratch_shapes=[
            pltpu.VMEM((TERMS, THIN, HALF), f32),
            pltpu.SemaphoreType.DMA(()),
        ],
        compiler_params=params(6),
        cost_estimate=cost(4_000_000, 6_000_000),
        name="right_slots",
    )(ids, rsector, rsector_other, on, on_other, thin, thin_other, folded)


def where_from(ids, left_sector, slot):
    sector = left_sector[ids[0] * 16 + slot]
    home = sector // 4
    return sector % 4, (home // 2 - ids[0] + 4) % 4, home % 2 == ids[1]


def send_tiles(out, sem, cases_of):
    def start(slot, carry):
        for case, src, tile in cases_of(slot):

            @pl.when(case)
            def _():
                pltpu.make_async_copy(src.at[tile], out.at[slot], sem).start()

        return carry

    def finish(slot, carry):
        for case, src, tile in cases_of(slot):

            @pl.when(case)
            def _():
                pltpu.make_async_copy(src.at[tile], out.at[slot], sem).wait()

        return carry

    lax.fori_loop(0, TERMS, start, 0)
    lax.fori_loop(0, TERMS, finish, 0)


def near_slots_body(ids, left_sector, mine, theirs, above_a, above_b, below_a, below_b, out, sem):
    def cases_of(slot):
        tile, away, same = where_from(ids, left_sector, slot)
        by_away = {0: (mine, theirs), 1: (above_a, above_b), 3: (below_a, below_b)}
        cases = []
        for planes, (first, second) in by_away.items():
            cases.append((same & (away == planes), first, tile))
            cases.append((~same & (away == planes), second, tile))
        return cases

    send_tiles(out, sem, cases_of)


def far_slots_body(ids, left_sector, far_a, far_b, near, out, sem):
    def cases_of(slot):
        tile, away, same = where_from(ids, left_sector, slot)
        return [(same & (away == 2), far_a, tile), (~same & (away == 2), far_b, tile)]

    send_tiles(out, sem, cases_of)


def left_slots(ids, left_sector, near, far):
    slots = pltpu.HBM((TERMS, FOLDED, HALF), f32)
    ready = pl.pallas_call(
        near_slots_body,
        in_specs=[smem(), smem()] + [vmem()] * 6,
        out_specs=hbm(),
        out_shape=slots,
        scratch_shapes=[pltpu.SemaphoreType.DMA(())],
        compiler_params=params(8),
        cost_estimate=cost(NEAR_FLOPS, 4_000_000),
        name="near_slots",
    )(ids, left_sector, *near)
    return pl.pallas_call(
        far_slots_body,
        in_specs=[smem(), smem()] + [vmem()] * 2 + [hbm()],
        out_specs=hbm(),
        out_shape=slots,
        scratch_shapes=[pltpu.SemaphoreType.DMA(())],
        input_output_aliases={4: 0},
        compiler_params=params(4),
        cost_estimate=cost(LEFT_FLOPS, 4_000_000),
        name="far_slots",
    )(ids, left_sector, *far, in_hbm(ready))


def live_sizes(ids, rsector, rsector_other, left_sector, left_size, right_size):
    live_left = left_size[left_sector[ids[0] * 16 + ids[2]]]
    live_right = right_size[sector_of(ids, rsector, rsector_other, ids[2])]
    return live_right, live_left


def mask_of(live_right, live_left):
    i, j = grids(TILE, TILE)
    return (i < live_right) & (j < live_left)


def first_body(
    ids, rsector, rsector_other, sector, lsize, rsize, halves, slots,
    r_hi, r_lo, m_hi, m_lo, q1, stats, arrived, sem,
):
    live_right, live_left = live_sizes(ids, rsector, rsector_other, sector, lsize, rsize)

    def fetch(n):
        return pltpu.make_async_copy(slots.at[n], arrived.at[n], sem.at[n])

    for n in range(TERMS):
        fetch(n).start()
    for n in range(TERMS):
        fetch(n).wait()
        full = get_folded(arrived, n, THIN)
        hi, lo = split(full)
        r_hi[n * TILE : (n + 1) * TILE, :] = hi
        r_lo[n * TILE : (n + 1) * TILE, :] = lo
    mine = jnp.concatenate([arrived[n, :THIN, :] for n in range(TERMS)], axis=0)
    theirs = jnp.concatenate([halves[n] for n in range(TERMS)], axis=0)
    first = ids[1] == 0
    block = jnp.concatenate(
        [jnp.where(first, mine, theirs), jnp.where(first, theirs, mine)], axis=1
    )
    start = jnp.where(mask_of(live_right, live_left), block, 0.0)
    norm = jnp.sqrt(total(start * start))
    vec = start * inverse(norm)
    q1[...] = vec
    stats[...] = put(jnp.zeros((8, HALF), f32), 0, norm)
    q_hi, q_lo = split(vec)
    for n in range(TERMS):
        rows = pl.ds(n * TILE, TILE)
        hi, lo = split(dot3(r_hi[rows, :], r_lo[rows, :], q_hi, q_lo))
        m_hi[:, rows] = hi
        m_lo[:, rows] = lo


def first_vector(scalars, halves, slots):
    return pl.pallas_call(
        first_body,
        in_specs=[smem()] * 6 + [vmem(), hbm()],
        out_specs=[vmem()] * 6,
        out_shape=[
            jax.ShapeDtypeStruct((TERMS * TILE, TILE), bf16),
            jax.ShapeDtypeStruct((TERMS * TILE, TILE), bf16),
            jax.ShapeDtypeStruct((TILE, TERMS * TILE), bf16),
            jax.ShapeDtypeStruct((TILE, TERMS * TILE), bf16),
            jax.ShapeDtypeStruct((TILE, TILE), f32),
            jax.ShapeDtypeStruct((8, HALF), f32),
        ],
        scratch_shapes=[
            pltpu.VMEM((TERMS, SLOT, HALF), f32),
            pltpu.SemaphoreType.DMA((TERMS,)),
        ],
        compiler_params=params(10),
        cost_estimate=cost(1_700_000_000, 12_000_000),
        name="first_vector",
    )(*scalars, halves, in_hbm(slots))


def image_one_body(arrived, m_hi, m_lo, l_hi, l_lo, part, here_hi, here_lo, sem):
    fetches = [
        pltpu.make_async_copy(m_hi, here_hi, sem.at[0]),
        pltpu.make_async_copy(m_lo, here_lo, sem.at[1]),
    ]
    for fetch in fetches:
        fetch.start()
    for n in range(TERMS):
        hi, lo = split(get_folded(arrived, n, 0))
        l_hi[n * TILE : (n + 1) * TILE, :] = hi
        l_lo[n * TILE : (n + 1) * TILE, :] = lo
    for fetch in fetches:
        fetch.wait()
    part[...] = dot3(here_hi[...], here_lo[...], l_hi[...], l_lo[...])


def image_one(arrived, m_hi, m_lo):
    stack = jax.ShapeDtypeStruct((TERMS * TILE, TILE), bf16)
    return pl.pallas_call(
        image_one_body,
        in_specs=[vmem(), hbm(), hbm()],
        out_specs=[vmem()] * 3,
        out_shape=[stack, stack, jax.ShapeDtypeStruct((TILE, TILE), f32)],
        scratch_shapes=[
            pltpu.VMEM((TILE, TERMS * TILE), bf16),
            pltpu.VMEM((TILE, TERMS * TILE), bf16),
            pltpu.SemaphoreType.DMA((2,)),
        ],
        compiler_params=params(10),
        cost_estimate=cost(1_700_000_000, 10_000_000),
        name="image_one",
    )(arrived, in_hbm(m_hi), in_hbm(m_lo))


def lanczos(image, last, before, beta):
    alpha = total(last * image)
    rest = image - alpha * last
    if before is not None:
        rest = rest - beta * before
    again = rest - total(last * rest) * last
    if before is not None:
        again = again - total(before * rest) * before
    norm = jnp.sqrt(total(again * again))
    return alpha, norm, again * inverse(norm)


def half_image(vec, r_hi, r_lo, l_hi, l_lo):
    q_hi, q_lo = split(vec)
    acc = jnp.zeros((TILE, TILE), f32)
    for n in range(TERMS):
        rows = pl.ds(n * TILE, TILE)
        hi, lo = split(dot3(r_hi[rows, :], r_lo[rows, :], q_hi, q_lo))
        acc = acc + dot3(hi, lo, l_hi[rows, :], l_lo[rows, :])
    return acc


def image_two_body(
    ids, rsector, rsector_other, sector, lsize, rsize,
    part_a, part_b, q1, stats_in, r_hi, r_lo, l_hi, l_lo,
    part, q2, stats,
):
    mask = mask_of(*live_sizes(ids, rsector, rsector_other, sector, lsize, rsize))
    image = jnp.where(mask, part_a[...] + part_b[...], 0.0)
    alpha, norm, vec = lanczos(image, q1[...], None, None)
    q2[...] = vec
    stats[...] = put(put(stats_in[...], 1, alpha), 2, norm)
    part[...] = half_image(vec, r_hi, r_lo, l_hi, l_lo)


def image_two(scalars, part, part_other, q1, stats, stacks):
    return pl.pallas_call(
        image_two_body,
        in_specs=[smem()] * 6 + [vmem()] * 8,
        out_specs=[vmem()] * 3,
        out_shape=[
            jax.ShapeDtypeStruct((TILE, TILE), f32),
            jax.ShapeDtypeStruct((TILE, TILE), f32),
            jax.ShapeDtypeStruct((8, HALF), f32),
        ],
        compiler_params=params(6),
        cost_estimate=cost(3_300_000_000, 9_000_000),
        name="image_two",
    )(*scalars, part, part_other, q1, stats, *stacks)


def image_three_body(
    ids, rsector, rsector_other, sector, lsize, rsize,
    part_a, part_b, q1, q2, stats_in, r_hi, r_lo, l_hi, l_lo, slots,
):
    mask = mask_of(*live_sizes(ids, rsector, rsector_other, sector, lsize, rsize))
    image = jnp.where(mask, part_a[...] + part_b[...], 0.0)
    beta = stats_in[0:1, 2:3]
    alpha, norm, vec = lanczos(image, q2[...], q1[...], beta)
    pick = jnp.where(ids[1] == 0, q2[...], vec)
    for n in range(16):
        slots[n, :16, :] = pick[16 * n : 16 * n + 16, :HALF]
        slots[n, 16:COLS, :] = pick[16 * n : 16 * n + 16, HALF:]
    stats = put(put(stats_in[...], 3, alpha), 4, norm)
    alpha = total(vec * half_image(vec, r_hi, r_lo, l_hi, l_lo))
    stats = put(stats, 5, alpha)
    for n in range(16):
        slots[n, COLS:, :] = stats


def image_three(scalars, part, part_other, q1, q2, stats, stacks):
    return pl.pallas_call(
        image_three_body,
        in_specs=[smem()] * 6 + [vmem()] * 9,
        out_specs=vmem(),
        out_shape=jax.ShapeDtypeStruct((16, COLS + 8, HALF), f32),
        compiler_params=params(6),
        cost_estimate=cost(3_300_000_000, 9_000_000),
        name="image_three",
    )(*scalars, part, part_other, q1, q2, stats, *stacks)


def ritz_pair(norm, a1, b1, a2, b2, a3):
    def apply(x):
        return [a1 * x[0] + b1 * x[1], b1 * x[0] + a2 * x[1] + b2 * x[2], b2 * x[1] + a3 * x[2]]

    def dot(x, y):
        return jnp.sum(x[0] * y[0] + x[1] * y[1] + x[2] * y[2], axis=1, keepdims=True)

    zero = jnp.zeros_like(norm)
    start = [norm, zero, zero]
    image = apply(start)
    norm_sq = dot(start, start)
    correlation = dot(start, image)
    inv_norm = 1.0 / jnp.sqrt(norm_sq)
    basis = [x * inv_norm for x in start]
    applied = [x * inv_norm for x in image]
    ritz = correlation / norm_sq
    for _ in range(ITERS):
        residual = [x - ritz * y for x, y in zip(applied, basis)]
        res_sq = dot(residual, residual)
        length = jnp.sqrt(res_sq)
        fresh = [x / length for x in residual]
        fresh_applied = apply(fresh)
        curvature = dot(fresh, fresh_applied)
        half_gap = 0.5 * (ritz - curvature)
        root = jnp.sqrt(half_gap * half_gap + res_sq)
        lowest = 0.5 * (ritz + curvature) - root
        first = curvature - lowest
        pair = jnp.sqrt(first * first + res_sq)
        basis = [(first * x - length * y) / pair for x, y in zip(basis, fresh)]
        applied = [(first * x - length * y) / pair for x, y in zip(applied, fresh_applied)]
        ritz = lowest
    return basis, ritz


def finish_body(
    ids, sector, rsector, lsize, rsize, own_stats, other_stats, thin, got, back,
    out, energy, coef,
):
    _, lane = grids(64, HALF)
    stats = own_stats[...] + jnp.where(lane == 5, other_stats[...], 0.0)
    flip = jnp.concatenate([stats, jnp.zeros((64, HALF), f32)], axis=0).T
    norm, a1, b1, a2, b2, a3 = [flip[m : m + 1, :] for m in range(6)]
    basis, ritz = ritz_pair(norm, a1, b1, a2, b2, a3)
    energy[0, 0] = jnp.sum(ritz)
    scale = jnp.sqrt(jnp.full((1, HALF), 64 * TILE * TILE, f32))
    i, _ = grids(HALF, HALF)
    c1 = basis[0] * inverse(norm) * scale
    c2 = basis[1] * scale
    c3 = basis[2] * scale
    coef[...] = jnp.where(i == 0, c1, jnp.where(i == 1, c2, jnp.where(i == 2, c3, 0.0))).T
    core = ids[1]
    own = coef[pl.ds(pl.multiple_of(core * 8, 8), 8), :]
    jcol, irow = grids(16, TILE)
    for b in range(8):
        live_left = lsize[sector[ids[0] * 16 + core * 8 + b]]
        live_right = rsize[rsector[b]]
        live = (jcol + ids[2] * 16 < live_right) & (irow < live_left)
        at = core * 8 + b
        keep = jnp.concatenate([got[at, :16, :], got[at, 16:COLS, :]], axis=1)
        recv = jnp.concatenate([back[b, :16, :], back[b, 16:COLS, :]], axis=1)
        second = jnp.where(core == 0, keep, recv)
        third = jnp.where(core == 0, recv, keep)
        out[b] = (
            own[b : b + 1, 0:1] * jnp.where(live, thin[b], 0.0)
            + own[b : b + 1, 1:2] * second
            + own[b : b + 1, 2:3] * third
        )


def finish(ids, sector, rsector, lsize, rsize, own_stats, other_stats, thin, got, back):
    return pl.pallas_call(
        finish_body,
        in_specs=[smem()] * 5 + [vmem()] * 5,
        out_specs=[vmem(), smem()],
        out_shape=[
            jax.ShapeDtypeStruct(thin.shape, f32),
            jax.ShapeDtypeStruct((1, 1), f32),
        ],
        scratch_shapes=[pltpu.VMEM((HALF, HALF), f32)],
        compiler_params=params(4),
        name="finish",
    )(ids, sector, rsector, lsize, rsize, own_stats, other_stats, thin, got, back)


def local(theta, left_env, right_env, left_sector, right_sector, term_on, left_size, right_size):
    plane = lax.axis_index("y").astype(jnp.int32)
    core = lax.axis_index("c").astype(jnp.int32)
    place = lax.axis_index(COL).astype(jnp.int32)
    ids = jnp.stack([plane, core, place])
    thin = jnp.swapaxes(theta, 1, 2)

    rsector_other = lax.ppermute(right_sector, "c", SWAP)
    on_other = lax.ppermute(term_on, "c", SWAP)
    thin_other = lax.ppermute(thin, "c", SWAP)

    mine, folded, right_folded = fold(ids, left_env, right_env)
    theirs = lax.ppermute(folded, "c", SWAP)
    theirs, rsector_other, on_other, thin_other = lax.optimization_barrier(
        (theirs, rsector_other, on_other, thin_other)
    )
    below = [lax.ppermute(x, "y", UP) for x in (mine, theirs)]
    above = [lax.ppermute(x, "y", DOWN) for x in (mine, theirs)]
    far = [lax.ppermute(below[0], "y", UP), lax.ppermute(above[1], "y", DOWN)]

    slots = right_slots(
        ids, right_sector, rsector_other, term_on, on_other, thin, thin_other, right_folded
    )
    slots, theirs_now = lax.optimization_barrier((slots, theirs))
    arrived = lax.all_to_all(slots, COL, 0, 0, tiled=True)
    scalars = (ids, right_sector, rsector_other, left_sector, left_size, right_size)
    halves = lax.ppermute(arrived[:, :THIN, :], "c", SWAP)
    r_hi, r_lo, m_hi, m_lo, q1, stats = first_vector(scalars, halves, arrived)

    left_sent = left_slots(ids, left_sector, [mine, theirs] + above + below, far)
    left_arrived = lax.all_to_all(left_sent, COL, 0, 0, tiled=True)
    l_hi, l_lo, part = image_one(left_arrived, m_hi, m_lo)
    stacks = (r_hi, r_lo, l_hi, l_lo)
    part, q2, stats = image_two(scalars, part, lax.ppermute(part, "c", SWAP), q1, stats, stacks)
    sent = image_three(scalars, part, lax.ppermute(part, "c", SWAP), q1, q2, stats, stacks)

    got = lax.all_to_all(sent, COL, 0, 0, tiled=True)
    plane_stats = got[:, COLS, :]
    turned = [
        lax.ppermute(plane_stats, "y", [(i, (i + k) % 4) for i in range(4)]) for k in (1, 2, 3)
    ]
    give = lax.dynamic_slice(got, ((1 - core) * 8, 0, 0), (8, COLS, HALF))
    back = lax.ppermute(give, "c", SWAP)
    own_stats = jnp.concatenate([plane_stats] + turned)
    other_stats = lax.ppermute(own_stats, "c", SWAP)
    out, energy = finish(
        ids, left_sector, right_sector, left_size, right_size,
        own_stats, other_stats, thin, got, back,
    )
    return jnp.swapaxes(out, 1, 2), energy[0, 0]


def solution(mesh):
    fine = Mesh(mesh.devices.reshape(4, 2, 4, 4), ALL)
    row = ("y", "c")
    placed = (
        P(row, None, COL),
        P(row, COL, None, None),
        P(None, COL, None, None),
        P(),
        P(row),
        P(row, COL),
        P(),
        P(),
    )
    return jax.shard_map(
        local, mesh=fine, in_specs=placed, out_specs=(P(row, None, COL), P()), check_vma=False
    )
```
